32 devices in a mesh: dp: 8 (over z, x), tensor: 4 (over y, core).
Axes of the slice: x: 2, y: 2, z: 4, core: 2. Of those that a mesh axis runs over, the one named last changes fastest.
Arguments:
- tokens: bfloat16 [16384, 1024], P('dp'), may hold values from -6 to 6
- segments: int32 [16, 1024], P('dp'), may hold values from 0 to 7, never falling along the last dimension, each value on 1 to 512 neighbouring positions
- w_qkv: bfloat16 [1024, 3, 1024], P(None, None, 'tensor'), may hold values from -0.1875 to 0.1875
- head_bias: float32 [2, 1024], P(None, 'tensor'), may hold values from -3 to 3
- w_out: bfloat16 [1024, 1024], P('tensor'), may hold values from -0.75 to 0.75
- w_in: bfloat16 [1024, 4096], P(None, 'tensor'), may hold values from -0.1875 to 0.1875
- unit_bias: float32 [4096], P('tensor'), may hold values from -3 to 3
- w_down: bfloat16 [4096, 1024], P('tensor'), may hold values from -0.09375 to 0.09375
- vectors: float32 [6, 1024], replicated, may hold values from 0.5 to 1.5
- cotangent: bfloat16 [16384, 1024], P('dp'), may hold values from -6 to 6
- err_qkv: float32 [8, 1024, 3, 1024], P('dp', None, None, 'tensor'), may hold values from -80 to 80
- err_out: float32 [8, 1024, 1024], P('dp', 'tensor'), may hold values from -80 to 80
- err_in: float32 [8, 1024, 4096], P('dp', None, 'tensor'), may hold values from -80 to 80
- err_down: float32 [8, 4096, 1024], P('dp', 'tensor'), may hold values from -80 to 80
- basis_qkv: float32 [8, 3, 1024], P(None, None, 'tensor'), may hold values from -6 to 6
- basis_out: float32 [32, 1024], P('tensor'), may hold values from -6 to 6
- basis_in: float32 [8, 4096], P(None, 'tensor'), may hold values from -6 to 6
- basis_down: float32 [32, 1024], P('tensor'), may hold values from -6 to 6
- mom_qkv: float32 [1024, 3, 1024], P(None, None, 'tensor'), may hold values from -5 to 5
- mom_head_bias: float32 [2, 1024], P(None, 'tensor'), may hold values from -10 to 10
- mom_out: float32 [1024, 1024], P('tensor'), may hold values from -5 to 5
- mom_in: float32 [1024, 4096], P(None, 'tensor'), may hold values from -5 to 5
- mom_unit_bias: float32 [4096], P('tensor'), may hold values from -10 to 10
- mom_down: float32 [4096, 1024], P('tensor'), may hold values from -5 to 5
- mom_vectors: float32 [6, 1024], replicated, may hold values from -28 to 28
Outputs:
- layer_out: bfloat16 [16384, 1024], P(('dp', 'tensor'))
- grad_tokens: float32 [16384, 1024], P(('dp', 'tensor'))
- grad_w_qkv: float32 [1024, 3, 1024], P(None, None, 'tensor')
- grad_head_bias: float32 [2, 1024], P(None, 'tensor')
- grad_w_out: float32 [1024, 1024], P('tensor')
- grad_w_in: float32 [1024, 4096], P(None, 'tensor')
- grad_unit_bias: float32 [4096], P('tensor')
- grad_w_down: float32 [4096, 1024], P('tensor')
- grad_vectors: float32 [6, 1024], replicated
- new_err_qkv: float32 [8, 1024, 3, 1024], P('dp', None, None, 'tensor')
- new_err_out: float32 [8, 1024, 1024], P('dp', 'tensor')
- new_err_in: float32 [8, 1024, 4096], P('dp', None, 'tensor')
- new_err_down: float32 [8, 4096, 1024], P('dp', 'tensor')
- new_basis_qkv: float32 [8, 3, 1024], P(None, None, 'tensor')
- new_basis_out: float32 [32, 1024], P('tensor')
- new_basis_in: float32 [8, 4096], P(None, 'tensor')
- new_basis_down: float32 [32, 1024], P('tensor')
- new_mom_qkv: float32 [1024, 3, 1024], P(None, None, 'tensor')
- new_mom_head_bias: float32 [2, 1024], P(None, 'tensor')
- new_mom_out: float32 [1024, 1024], P('tensor')
- new_mom_in: float32 [1024, 4096], P(None, 'tensor')
- new_mom_unit_bias: float32 [4096], P('tensor')
- new_mom_down: float32 [4096, 1024], P('tensor')
- new_mom_vectors: float32 [6, 1024], replicated
- new_w_qkv: float32 [1024, 3, 1024], P(None, None, 'tensor')
- new_head_bias: float32 [2, 1024], P(None, 'tensor')
- new_w_out: float32 [1024, 1024], P('tensor')
- new_w_in: float32 [1024, 4096], P(None, 'tensor')
- new_unit_bias: float32 [4096], P('tensor')
- new_w_down: float32 [4096, 1024], P('tensor')
- new_vectors: float32 [6, 1024], replicated
The draws below stay inside these ranges and needn't reach their ends.
Inputs may be any that keep to these rules, and one draw needn't show every extreme that they name: `segments`: along a sequence the numbers never fall; each of its 8 documents holds 1 to 512 tokens, and one of them exactly 512.
All inputs are finite; a program needn't handle non-finite values.
Results may differ from the reference program's by a relative error of at most 0.02.
Values may be sent and summed in bfloat16 or wider, within the bound.
A program may use at most 256 MiB of HBM per device.

```python
import math
import jax
import jax.numpy as jnp
import numpy as np
from jax import lax

D = 1024
HEADS = 16
DH = 64
FF = 4096
LEN = 1024
SEQ_DEV = 2
RANK = 8
HD = 1024
PIECES = 4
REPLICAS = 8
TOK_DEV = 2048
SEQS = 16
TOKENS = 16384
QROWS = 32


def steps_of(rng, shape, split, least, largest):
    level = 1.0
    for dim, parts in split:
        draws = jax.random.uniform(jax.random.fold_in(jax.random.fold_in(rng, 6), dim), (parts,), jnp.float32, least / len(split), largest / len(split))
        level = level * jnp.repeat(jnp.exp(draws), shape[dim] // parts).reshape((-1,) + (1,) * (len(shape) - 1 - dim))
    return level


def length_profile(number_of, total, most, slope):
    weights = [(1 << 20) // math.isqrt(standing ** slope) + 1 for standing in range(2, number_of + 1)]
    surplus, given = total - most - (number_of - 1), [1] * (number_of - 1)
    while surplus > 0:
        free = [i for i in range(number_of - 1) if given[i] < most]
        whole, budget = sum([weights[i] for i in free]), surplus
        for i in free:
            more = min(most - given[i], max(1, budget * weights[i] // whole), surplus)
            given[i] = given[i] + more
            surplus = surplus - more
    return np.array([most] + given)


def uneven_parts(rng, number_of, total, limit, lean):
    if number_of == 2:
        one = jax.random.randint(rng, (), max(1, total - limit), min(limit, total - 1) + 1)
        return jnp.stack([one, total - one])
    lengths = jnp.asarray(length_profile(number_of, total, limit, lean), jnp.int32)
    pairs = (number_of - 1) // 2
    source_of, receiver = lengths[1:1 + 2 * pairs:2], lengths[2:2 + 2 * pairs:2]
    slack = jnp.minimum(source_of - 1, limit - receiver)
    shifted = jax.random.randint(jax.random.fold_in(rng, 1), (pairs,), 0, 1 << 20) % (slack + 1)
    lengths = lengths.at[1:1 + 2 * pairs:2].set(source_of - shifted).at[2:2 + 2 * pairs:2].set(receiver + shifted)
    return lengths[jax.random.permutation(jax.random.fold_in(rng, 2), number_of)]


def normal_values(rng, extent, width, limit, shards=(), dtype=jnp.bfloat16):
    drawn = jax.random.normal(rng, extent, jnp.float32) * width
    if len(shards) > 0:
        drawn = steps_of(rng, extent, shards, -0.22, 0.18) * drawn
    return jnp.clip(drawn, min=-limit, max=limit).astype(dtype)


def setup_inputs(seed: int = 0) -> dict:
    key_list = jax.random.split(jax.random.key(seed), 26)
    tokens = normal_values(key_list[0], (TOKENS, D), 1.0, 6.0, ((0, 8),))
    segments = jax.vmap(lambda own: jnp.searchsorted(jnp.cumsum(uneven_parts(own, 8, LEN, LEN // 2, 2)), jnp.arange(LEN), side="right"))(jax.random.split(key_list[1], SEQS)).reshape((SEQS, LEN)).astype(jnp.int32)
    w_qkv = normal_values(key_list[2], (D, 3, HD), D ** -0.5, 0.1875, ((2, 4),))
    head_bias = normal_values(key_list[3], (2, HD), 0.5, 3.0, ((1, 4),), jnp.float32)
    w_out = normal_values(key_list[4], (HD, D), (HD // 16) ** -0.5, 0.75, ((0, 4),))
    w_in = normal_values(key_list[5], (D, FF), D ** -0.5, 0.1875, ((1, 4),))
    unit_bias = normal_values(key_list[6], (FF,), 0.5, 3.0, ((0, 4),), jnp.float32)
    w_down = normal_values(key_list[7], (FF, D), FF ** -0.5, 0.09375, ((0, 4),))
    vectors = jnp.clip(jax.random.uniform(key_list[8], (6, D), jnp.float32, 0.5, 1.5), 0.5, 1.5)
    cotangent = normal_values(key_list[9], (TOKENS, D), 1.0, 6.0, ((0, 8),))
    err_qkv = normal_values(key_list[10], (REPLICAS, D, 3, HD), (0.3 * TOK_DEV ** 0.5), 80.0, ((0, 8), (3, 4)), jnp.float32)
    err_out = normal_values(key_list[11], (REPLICAS, HD, D), (0.3 * TOK_DEV ** 0.5), 80.0, ((0, 8), (1, 4)), jnp.float32)
    err_in = normal_values(key_list[12], (REPLICAS, D, FF), (0.3 * TOK_DEV ** 0.5), 80.0, ((0, 8), (2, 4)), jnp.float32)
    err_down = normal_values(key_list[13], (REPLICAS, FF, D), (0.3 * TOK_DEV ** 0.5), 80.0, ((0, 8), (1, 4)), jnp.float32)
    basis_qkv = normal_values(key_list[14], (RANK, 3, HD), 1.0, 6.0, ((2, 4),), jnp.float32)
    basis_out = normal_values(key_list[15], (QROWS, D), 1.0, 6.0, ((0, 4),), jnp.float32)
    basis_in = normal_values(key_list[16], (RANK, FF), 1.0, 6.0, ((1, 4),), jnp.float32)
    basis_down = normal_values(key_list[17], (QROWS, D), 1.0, 6.0, ((0, 4),), jnp.float32)
    mom_qkv = normal_values(key_list[18], (D, 3, HD), (0.05 * (TOK_DEV // REPLICAS) ** 0.5), 5.0, ((2, 4),), jnp.float32)
    mom_head_bias = normal_values(key_list[19], (2, HD), (0.1 * (TOK_DEV // REPLICAS) ** 0.5), 10.0, ((1, 4),), jnp.float32)
    mom_out = normal_values(key_list[20], (HD, D), (0.05 * (TOK_DEV // REPLICAS) ** 0.5), 5.0, ((0, 4),), jnp.float32)
    mom_in = normal_values(key_list[21], (D, FF), (0.05 * (TOK_DEV // REPLICAS) ** 0.5), 5.0, ((1, 4),), jnp.float32)
    mom_unit_bias = normal_values(key_list[22], (FF,), (0.1 * (TOK_DEV // REPLICAS) ** 0.5), 10.0, ((0, 4),), jnp.float32)
    mom_down = normal_values(key_list[23], (FF, D), (0.05 * (TOK_DEV // REPLICAS) ** 0.5), 5.0, ((0, 4),), jnp.float32)
    mom_vectors = normal_values(key_list[24], (6, D), (0.3 * (TOK_DEV // REPLICAS) ** 0.5), 28.0, (), jnp.float32)
    return dict(tokens=tokens, segments=segments, w_qkv=w_qkv, head_bias=head_bias, w_out=w_out, w_in=w_in, unit_bias=unit_bias, w_down=w_down, vectors=vectors, cotangent=cotangent, err_qkv=err_qkv, err_out=err_out, err_in=err_in, err_down=err_down, basis_qkv=basis_qkv, basis_out=basis_out, basis_in=basis_in, basis_down=basis_down, mom_qkv=mom_qkv, mom_head_bias=mom_head_bias, mom_out=mom_out, mom_in=mom_in, mom_unit_bias=mom_unit_bias, mom_down=mom_down, mom_vectors=mom_vectors)


PRECISE = lax.Precision.HIGHEST
EPS_NORM = 1e-05
EPS_BASIS = 1e-08
MASKED = -1000000000.0

@jax.custom_vjp
def low(v):
    return lax.optimization_barrier(v.astype(jnp.bfloat16)).astype(jnp.float32)

@jax.custom_vjp
def low_back(v):
    return v

def low_keep(v):
    return (low(v), None)

def low_pass(kept, grad):
    return (grad,)

def back_keep(v):
    return (v, None)

def back_low(kept, grad):
    return (low(grad),)
low.defvjp(low_keep, low_pass)
low_back.defvjp(back_keep, back_low)

def both_ways(values):
    return low_back(low(values))

def layer_norm(values, gain, shift):
    row_mean = lax.optimization_barrier(jnp.mean(values, axis=-1, keepdims=True))
    centred = values - row_mean
    variance = lax.optimization_barrier(jnp.mean(centred * centred, axis=-1, keepdims=True))
    return centred * lax.rsqrt(variance + EPS_NORM) * gain + shift

def attend(inputs_of):
    queries, key_heads, value_heads, seg_ids = inputs_of
    scores = low_back(jnp.einsum('qhd,khd->hqk', queries, key_heads, precision=PRECISE))
    same_doc = seg_ids[:, None] == seg_ids[None, :]
    scores = jnp.where(same_doc[None], scores, MASKED)
    weights = low(jax.nn.softmax(scores, axis=-1))
    return jnp.einsum('hqk,khd->qhd', weights, value_heads, precision=PRECISE)

def layer_forward(tokens, w_qkv, head_bias, w_out, w_in, unit_bias, w_down, vectors, segments):
    token_count = tokens.shape[0]
    seq_count = segments.shape[0]
    projected = jnp.dot(tokens, w_qkv.reshape(D, 3 * HD), precision=PRECISE).reshape(token_count, 3, HD)
    head_scale = 1.0 / math.sqrt(DH)
    queries = both_ways((projected[:, 0] + head_bias[0]) * head_scale)
    key_rows = both_ways(projected[:, 1])
    value_rows = both_ways(projected[:, 2] + head_bias[1])
    head_shape = (seq_count, LEN, HEADS, DH)
    mixed = lax.map(jax.checkpoint(attend), (queries.reshape(head_shape), key_rows.reshape(head_shape), value_rows.reshape(head_shape), segments))
    mixed = both_ways(mixed.reshape(token_count, HD))
    attn_out = low_back(jnp.dot(mixed, w_out, precision=PRECISE) + vectors[0])
    first_norm = layer_norm(tokens + attn_out, vectors[2], vectors[3])
    hidden = low_back(jnp.dot(low(first_norm), w_in, precision=PRECISE) + unit_bias)
    active = low(jax.nn.gelu(hidden, approximate=False))
    branch = low_back(jnp.dot(active, w_down, precision=PRECISE) + vectors[1])
    return layer_norm(first_norm + branch, vectors[4], vectors[5])

def orthonormal(factor):
    columns = []
    for position in range(factor.shape[-1]):
        column = factor[..., position]
        for earlier in columns:
            column = column - lax.optimization_barrier(jnp.sum(earlier * column, axis=-1, keepdims=True)) * earlier
        column = column / (jnp.sqrt(lax.optimization_barrier(jnp.sum(column * column, axis=-1, keepdims=True))) + EPS_BASIS)
        columns.append(column)
    return jnp.stack(columns, axis=-1)

def compress(stacked, factor):
    left_side = lax.optimization_barrier(jnp.mean(jnp.einsum('trmn,tkn->trmk', stacked, factor, precision=PRECISE), axis=1))
    basis = orthonormal(left_side)
    right_side = lax.optimization_barrier(jnp.mean(jnp.einsum('trmn,tmk->trkn', stacked, basis, precision=PRECISE), axis=1))
    low_rank = jnp.einsum('tmk,tkn->tmn', basis, right_side, precision=PRECISE)
    return (low_rank, right_side, stacked - low_rank[:, None])

def reference(tokens, segments, w_qkv, head_bias, w_out, w_in, unit_bias, w_down, vectors, cotangent, err_qkv, err_out, err_in, err_down, basis_qkv, basis_out, basis_in, basis_down, mom_qkv, mom_head_bias, mom_out, mom_in, mom_unit_bias, mom_down, mom_vectors):
    params = (w_qkv.astype(jnp.float32), head_bias, w_out.astype(jnp.float32), w_in.astype(jnp.float32), unit_bias, w_down.astype(jnp.float32), vectors)
    tok_rep = tokens.astype(jnp.float32).reshape(REPLICAS, TOK_DEV, D)
    cot_rep = cotangent.astype(jnp.float32).reshape(REPLICAS, TOK_DEV, D)
    seg_rep = segments.reshape(REPLICAS, SEQ_DEV, LEN)

    def replica(inputs_of):
        tok_rows, cot_rows, seg_rows = inputs_of

        def forward_fn(*values):
            return layer_forward(*values, seg_rows)
        result, pullback = jax.vjp(forward_fn, tok_rows, *params)
        return (result,) + tuple(pullback(cot_rows))
    per_replica = lax.map(replica, (tok_rep, cot_rep, seg_rep))
    layer_out = per_replica[0].reshape(TOKENS, D).astype(jnp.bfloat16)
    grad_tokens = per_replica[1].reshape(TOKENS, D)
    grads_all = per_replica[2:]
    head_slab = HD // PIECES
    unit_slab = FF // PIECES
    stack_qkv = (grads_all[0] + err_qkv).reshape(REPLICAS, D, 3, PIECES, head_slab).transpose(3, 0, 1, 2, 4).reshape(PIECES, REPLICAS, D, 3 * head_slab)
    factor_qkv = basis_qkv.reshape(RANK, 3, PIECES, head_slab).transpose(2, 0, 1, 3).reshape(PIECES, RANK, 3 * head_slab)
    rank_qkv, right_qkv, error_qkv = compress(stack_qkv, factor_qkv)
    grad_w_qkv = rank_qkv.reshape(PIECES, D, 3, head_slab).transpose(1, 2, 0, 3).reshape(D, 3, HD)
    new_err_qkv = error_qkv.reshape(PIECES, REPLICAS, D, 3, head_slab).transpose(1, 2, 3, 0, 4).reshape(REPLICAS, D, 3, HD)
    new_basis_qkv = right_qkv.reshape(PIECES, RANK, 3, head_slab).transpose(1, 2, 0, 3).reshape(RANK, 3, HD)
    stack_out = (grads_all[2] + err_out).reshape(REPLICAS, PIECES, head_slab, D).transpose(1, 0, 2, 3)
    rank_out, right_out, error_out = compress(stack_out, basis_out.reshape(PIECES, RANK, D))
    grad_w_out = rank_out.reshape(HD, D)
    new_err_out = error_out.transpose(1, 0, 2, 3).reshape(REPLICAS, HD, D)
    new_basis_out = right_out.reshape(QROWS, D)
    stack_in = (grads_all[3] + err_in).reshape(REPLICAS, D, PIECES, unit_slab).transpose(2, 0, 1, 3)
    factor_in = basis_in.reshape(RANK, PIECES, unit_slab).transpose(1, 0, 2)
    rank_in, right_in, error_in = compress(stack_in, factor_in)
    grad_w_in = rank_in.transpose(1, 0, 2).reshape(D, FF)
    new_err_in = error_in.transpose(1, 2, 0, 3).reshape(REPLICAS, D, FF)
    new_basis_in = right_in.transpose(1, 0, 2).reshape(RANK, FF)
    stack_down = (grads_all[5] + err_down).reshape(REPLICAS, PIECES, unit_slab, D).transpose(1, 0, 2, 3)
    rank_down, right_down, error_down = compress(stack_down, basis_down.reshape(PIECES, RANK, D))
    grad_w_down = rank_down.reshape(FF, D)
    new_err_down = error_down.transpose(1, 0, 2, 3).reshape(REPLICAS, FF, D)
    new_basis_down = right_down.reshape(QROWS, D)
    grad_head_bias = lax.optimization_barrier(jnp.mean(grads_all[1], axis=0))
    grad_unit_bias = lax.optimization_barrier(jnp.mean(grads_all[4], axis=0))
    grad_vectors = lax.optimization_barrier(jnp.mean(grads_all[6], axis=0))
    step_rate = 0.3 * math.sqrt(REPLICAS / TOK_DEV)
    reduced = (grad_w_qkv, grad_head_bias, grad_w_out, grad_w_in, grad_unit_bias, grad_w_down, grad_vectors)
    momenta = (mom_qkv, mom_head_bias, mom_out, mom_in, mom_unit_bias, mom_down, mom_vectors)
    new_moms = tuple((0.9 * old + grad for old, grad in zip(momenta, reduced)))
    new_params = tuple((weight - step_rate * moment for weight, moment in zip(params, new_moms)))
    return (layer_out, grad_tokens, grad_w_qkv, grad_head_bias, grad_w_out, grad_w_in, grad_unit_bias, grad_w_down, grad_vectors, new_err_qkv, new_err_out, new_err_in, new_err_down, new_basis_qkv, new_basis_out, new_basis_in, new_basis_down, new_moms[0], new_moms[1], new_moms[2], new_moms[3], new_moms[4], new_moms[5], new_moms[6], new_params[0], new_params[1], new_params[2], new_params[3], new_params[4], new_params[5], new_params[6])
```

```python
from functools import partial
import math

import jax
import jax.numpy as jnp
from jax import lax
from jax.experimental import pallas as pl
from jax.experimental.pallas import tpu as pltpu
from jax.sharding import PartitionSpec as P

DH = 64
LANES = 128
MESH = pl.DeviceIdType.MESH


PRECISE = lax.Precision.HIGHEST
EPS_NORM = 1e-05
EPS_BASIS = 1e-08
MASKED = -1000000000.0


def norm_forward(values, gain, shift):
    row_mean = jnp.mean(values, axis=-1, keepdims=True)
    centred = values - row_mean
    variance = jnp.mean(centred * centred, axis=-1, keepdims=True)
    inverse = lax.rsqrt(variance + EPS_NORM)
    normed = centred * inverse
    return (normed * gain + shift, normed, inverse)


def norm_backward(grad_norm, normed, inverse, gain):
    scaled_grad = grad_norm * gain
    grad_mean = jnp.mean(scaled_grad, axis=-1, keepdims=True)
    along_norm = jnp.mean(scaled_grad * normed, axis=-1, keepdims=True)
    return inverse * (scaled_grad - grad_mean - normed * along_norm)


def times_trans(left_side, right_side):
    return lax.dot_general(
        left_side, right_side, (((1,), (1,)), ((), ())), preferred_element_type=jnp.float32
    )


def trans_times(left_side, right_side):
    return lax.dot_general(
        left_side, right_side, (((0,), (0,)), ((), ())), preferred_element_type=jnp.float32
    )


def split_bf16(values):
    high = values.astype(jnp.bfloat16)
    low = (values - high.astype(jnp.float32)).astype(jnp.bfloat16)
    return high, low


def dot_nt(left_side, right_side):
    return lax.dot_general(
        left_side, right_side, (((1,), (1,)), ((), ())), preferred_element_type=jnp.float32
    )


def dot_nn(left_side, right_side):
    return lax.dot_general(
        left_side, right_side, (((1,), (0,)), ((), ())), preferred_element_type=jnp.float32
    )


def dot_tn(left_side, right_side):
    return lax.dot_general(
        left_side, right_side, (((0,), (0,)), ((), ())), preferred_element_type=jnp.float32
    )


def left_factor(factor, matrix):
    rank_size = factor.shape[0]
    factor_high, factor_low = split_bf16(factor)
    matrix_high, matrix_low = split_bf16(matrix)
    both = dot_nt(jnp.concatenate([factor_high, factor_low], axis=0), matrix_high)
    return both[:rank_size] + both[rank_size:] + dot_nt(factor_high, matrix_low)


def right_factor(basis_rows, matrix):
    rank_size = basis_rows.shape[0]
    basis_high, basis_low = split_bf16(basis_rows)
    matrix_high, matrix_low = split_bf16(matrix)
    both = dot_nn(jnp.concatenate([basis_high, basis_low], axis=0), matrix_high)
    return both[:rank_size] + both[rank_size:] + dot_nn(basis_high, matrix_low)


def lefts_kernel(qkv_ref, out_ref, in_ref, down_ref, fq_ref, fo_ref, fi_ref, fd_ref,
                 lq_ref, lo_ref, li_ref, ld_ref):
    lq_ref[...] = (
        left_factor(fq_ref[0], qkv_ref[0])
        + left_factor(fq_ref[1], qkv_ref[1])
        + left_factor(fq_ref[2], qkv_ref[2])
    )
    li_ref[...] = left_factor(fi_ref[...], in_ref[...])
    ld_ref[...] = left_factor(fd_ref[...], down_ref[...])

    @pl.when(pl.program_id(0) == 0)
    def _():
        lo_ref[...] = left_factor(fo_ref[...], out_ref[...])


def lefts_of(matrices, factors):
    steps = 4
    qkv, out, inw, down = matrices
    rank_size = factors[1].shape[0]

    def whole(array):
        return pl.BlockSpec(array.shape, lambda i: (0,) * array.ndim)

    def rows(array):
        return pl.BlockSpec((array.shape[0] // steps, array.shape[1]), lambda i: (i, 0))

    def lanes(size):
        return pl.BlockSpec((rank_size, size // steps), lambda i: (0, i))

    return pl.pallas_call(
        lefts_kernel,
        grid=(steps,),
        in_specs=[
            pl.BlockSpec((3, qkv.shape[1] // steps, qkv.shape[2]), lambda i: (0, i, 0)),
            whole(out),
            rows(inw),
            rows(down),
        ]
        + [whole(factor) for factor in factors],
        out_specs=[
            lanes(qkv.shape[1]),
            pl.BlockSpec((rank_size, out.shape[0]), lambda i: (0, 0)),
            lanes(inw.shape[0]),
            lanes(down.shape[0]),
        ],
        out_shape=[
            jax.ShapeDtypeStruct((rank_size, size), jnp.float32)
            for size in (qkv.shape[1], out.shape[0], inw.shape[0], down.shape[0])
        ],
        compiler_params=pltpu.CompilerParams(vmem_limit_bytes=40 << 20),
        name="left_factors",
    )(qkv, out, inw, down, *factors)


def rights_kernel(qkv_ref, out_ref, in_ref, down_ref, bq_ref, bo_ref, bi_ref, bd_ref,
                  rq_ref, ro_ref, ri_ref, rd_ref):
    first = pl.program_id(0) == 0

    @pl.when(first)
    def _():
        ro_ref[...] = right_factor(bo_ref[...], out_ref[...])
        rq_ref[...] = jnp.zeros_like(rq_ref)
        ri_ref[...] = jnp.zeros_like(ri_ref)
        rd_ref[...] = jnp.zeros_like(rd_ref)

    for part in range(3):
        rq_ref[part] += right_factor(bq_ref[...], qkv_ref[part])
    ri_ref[...] += right_factor(bi_ref[...], in_ref[...])
    rd_ref[...] += right_factor(bd_ref[...], down_ref[...])


def rights_of(matrices, bases):
    steps = 4
    qkv, out, inw, down = matrices
    rank_size = bases[0].shape[0]

    def whole(shape):
        return pl.BlockSpec(shape, lambda i: (0,) * len(shape))

    def rows(array):
        return pl.BlockSpec((array.shape[0] // steps, array.shape[1]), lambda i: (i, 0))

    def lanes(array):
        return pl.BlockSpec((rank_size, array.shape[1] // steps), lambda i: (0, i))

    shapes = [(3, rank_size, qkv.shape[2])] + [(rank_size, one.shape[1]) for one in (out, inw, down)]
    return pl.pallas_call(
        rights_kernel,
        grid=(steps,),
        in_specs=[
            pl.BlockSpec((3, qkv.shape[1] // steps, qkv.shape[2]), lambda i: (0, i, 0)),
            whole(out.shape),
            rows(inw),
            rows(down),
            lanes(bases[0]),
            whole(bases[1].shape),
            lanes(bases[2]),
            lanes(bases[3]),
        ],
        out_specs=[whole(shape) for shape in shapes],
        out_shape=[jax.ShapeDtypeStruct(shape, jnp.float32) for shape in shapes],
        compiler_params=pltpu.CompilerParams(vmem_limit_bytes=40 << 20),
        name="right_factors",
    )(qkv, out, inw, down, *bases)


def peer_ids(replicas, place):
    dp_place = lax.axis_index("dp")
    tensor_place = lax.axis_index("tensor")
    return dp_place, tensor_place


def greet(replicas, tensor_size):
    dp_place = lax.axis_index("dp")
    tensor_place = lax.axis_index("tensor")
    barrier = pltpu.get_barrier_semaphore()

    def greet_dp(step, carry):
        pl.semaphore_signal(
            barrier,
            inc=1,
            device_id=(lax.rem(dp_place + step, replicas), tensor_place),
            device_id_type=MESH,
        )
        return carry

    def greet_tensor(step, carry):
        pl.semaphore_signal(
            barrier,
            inc=1,
            device_id=(dp_place, lax.rem(tensor_place + step, tensor_size)),
            device_id_type=MESH,
        )
        return carry

    lax.fori_loop(1, replicas, greet_dp, 0)
    if tensor_size > 1:
        lax.fori_loop(1, tensor_size, greet_tensor, 0)
    pl.semaphore_wait(barrier, replicas - 1 + tensor_size - 1)


def dp_sum(replicas, mine, wire, arrived, total, send_one, recv_one, send_two, recv_two):
    dp_place = lax.axis_index("dp")
    tensor_place = lax.axis_index("tensor")

    def scatter_to(step):
        peer = lax.rem(dp_place + step, replicas)
        return pltpu.make_async_remote_copy(
            src_ref=wire.at[peer],
            dst_ref=arrived.at[dp_place],
            send_sem=send_one.at[step],
            recv_sem=recv_one.at[dp_place],
            device_id=(peer, tensor_place),
            device_id_type=MESH,
        )

    def scatter_from(step):
        peer = lax.rem(dp_place + step, replicas)
        return pltpu.make_async_remote_copy(
            src_ref=wire.at[peer],
            dst_ref=arrived.at[peer],
            send_sem=send_one.at[step],
            recv_sem=recv_one.at[peer],
            device_id=(peer, tensor_place),
            device_id_type=MESH,
        )

    def gather_to(step):
        peer = lax.rem(dp_place + step, replicas)
        return pltpu.make_async_remote_copy(
            src_ref=total.at[dp_place],
            dst_ref=total.at[dp_place],
            send_sem=send_two.at[step],
            recv_sem=recv_two.at[dp_place],
            device_id=(peer, tensor_place),
            device_id_type=MESH,
        )

    def gather_from(step):
        peer = lax.rem(dp_place + step, replicas)
        return pltpu.make_async_remote_copy(
            src_ref=total.at[dp_place],
            dst_ref=total.at[peer],
            send_sem=send_two.at[step],
            recv_sem=recv_two.at[peer],
            device_id=(peer, tensor_place),
            device_id_type=MESH,
        )

    def start_scatter(step, carry):
        scatter_to(step).start()
        return carry

    def add_arrived(step, carry):
        scatter_from(step).wait_recv()
        peer = lax.rem(dp_place + step, replicas)
        return carry + arrived[peer].astype(jnp.float32)

    def start_gather(step, carry):
        gather_to(step).start()
        return carry

    def finish(step, carry):
        scatter_to(step).wait_send()
        gather_to(step).wait_send()
        gather_from(step).wait_recv()
        return carry

    wire[...] = mine[...].astype(wire.dtype)
    lax.fori_loop(1, replicas, start_scatter, 0)
    total[dp_place] = lax.fori_loop(1, replicas, add_arrived, mine[dp_place])
    lax.fori_loop(1, replicas, start_gather, 0)
    lax.fori_loop(1, replicas, finish, 0)


def place_tiles(target, offset, values):
    per_chunk = target.shape[2] // LANES
    for tile in range(values.shape[1] // LANES):
        spot = offset + tile
        target[spot // per_chunk, :, pl.ds(spot % per_chunk * LANES, LANES)] = values[
            :, tile * LANES : (tile + 1) * LANES
        ]
    return offset + values.shape[1] // LANES


def take_tiles(source, offset, size):
    per_chunk = source.shape[2] // LANES
    pieces = []
    for tile in range(size // LANES):
        spot = offset + tile
        pieces.append(source[spot // per_chunk, :, pl.ds(spot % per_chunk * LANES, LANES)])
    return jnp.concatenate(pieces, axis=1) if len(pieces) > 1 else pieces[0]


def orthonormal_rows(rows):
    rank_size = rows.shape[0]
    row_number = lax.broadcasted_iota(jnp.int32, (rank_size, 1), 0)
    for position in range(rank_size):
        row = rows[position : position + 1]
        length = jnp.sqrt(jnp.sum(row * row, axis=1, keepdims=True)) + EPS_BASIS
        unit = row / length
        along = jnp.sum(rows * unit, axis=1, keepdims=True)
        later = jnp.where(row_number > position, along, 0.0)
        rows = jnp.where(row_number == position, unit, rows - later * unit)
    return rows


def basis_kernel(replicas, tensor_size, lq_ref, lo_ref, li_ref, ld_ref, small_ref,
                 bq_ref, bo_ref, bi_ref, bd_ref, sum_ref,
                 mine, wire, arrived, total, small_slots,
                 send_one, recv_one, send_two, recv_two, send_three, recv_three):
    dp_place = lax.axis_index("dp")
    tensor_place = lax.axis_index("tensor")
    mine[...] = jnp.zeros_like(mine)
    greet(replicas, tensor_size)
    lefts = (lq_ref, lo_ref, li_ref, ld_ref)
    offset = 0
    for ref in lefts + (small_ref,):
        offset = place_tiles(mine, offset, ref[...])
    dp_sum(replicas, mine, wire, arrived, total, send_one, recv_one, send_two, recv_two)

    def slot_copy(step, slot):
        peer = lax.rem(tensor_place + step, tensor_size)
        return pltpu.make_async_remote_copy(
            src_ref=small_slots.at[tensor_place],
            dst_ref=small_slots.at[slot],
            send_sem=send_three.at[step],
            recv_sem=recv_three.at[slot],
            device_id=(dp_place, peer),
            device_id_type=MESH,
        )

    def start(step, carry):
        slot_copy(step, tensor_place).start()
        return carry

    small_at = sum(ref.shape[1] for ref in lefts) // LANES
    own_small = take_tiles(total, small_at, small_ref.shape[1])
    small_slots[tensor_place] = own_small
    lax.fori_loop(1, tensor_size, start, 0)
    offset = 0
    for ref, basis_ref in zip(lefts, (bq_ref, bo_ref, bi_ref, bd_ref)):
        rows = take_tiles(total, offset, ref.shape[1]) * (1.0 / replicas)
        basis_ref[...] = orthonormal_rows(rows)
        offset += ref.shape[1] // LANES

    def collect(step, carry):
        peer = lax.rem(tensor_place + step, tensor_size)
        slot_copy(step, peer).wait_recv()
        slot_copy(step, tensor_place).wait_send()
        return carry + small_slots[peer]

    everyone = lax.fori_loop(1, tensor_size, collect, own_small)
    row_number = lax.broadcasted_iota(jnp.int32, everyone.shape, 0)
    sum_ref[...] = jnp.where(row_number < 6, everyone, own_small) * (1.0 / replicas)


def bases_of(lefts, small, replicas, tensor_size):
    rank_size = small.shape[0]
    lanes = sum(left.shape[1] for left in lefts) + small.shape[1]
    width = -(-lanes // (LANES * replicas)) * LANES
    shapes = [left.shape for left in lefts] + [small.shape]
    vmem = pl.BlockSpec(memory_space=pltpu.VMEM)
    return pl.pallas_call(
        partial(basis_kernel, replicas, tensor_size),
        in_specs=[vmem] * 5,
        out_specs=[vmem] * 5,
        out_shape=[jax.ShapeDtypeStruct(shape, jnp.float32) for shape in shapes],
        scratch_shapes=[
            pltpu.VMEM((replicas, rank_size, width), jnp.float32),
            pltpu.VMEM((replicas, rank_size, width), jnp.bfloat16),
            pltpu.VMEM((replicas, rank_size, width), jnp.bfloat16),
            pltpu.VMEM((replicas, rank_size, width), jnp.float32),
            pltpu.VMEM((tensor_size,) + small.shape, jnp.float32),
            pltpu.SemaphoreType.DMA((replicas,)),
            pltpu.SemaphoreType.DMA((replicas,)),
            pltpu.SemaphoreType.DMA((replicas,)),
            pltpu.SemaphoreType.DMA((replicas,)),
            pltpu.SemaphoreType.DMA((tensor_size,)),
            pltpu.SemaphoreType.DMA((tensor_size,)),
        ],
        compiler_params=pltpu.CompilerParams(collective_id=1, has_side_effects=True),
        name="bases",
    )(*lefts, small)


def right_sum_kernel(replicas, rq_ref, ro_ref, ri_ref, rd_ref, sq_ref, so_ref, si_ref, sd_ref,
                     mine, wire, arrived, total, send_one, recv_one, send_two, recv_two):
    mine[...] = jnp.zeros_like(mine)
    greet(replicas, 1)
    offset = 0
    for part in range(3):
        offset = place_tiles(mine, offset, rq_ref[part])
    for ref in (ro_ref, ri_ref, rd_ref):
        offset = place_tiles(mine, offset, ref[...])
    dp_sum(replicas, mine, wire, arrived, total, send_one, recv_one, send_two, recv_two)
    offset = 0
    for part in range(3):
        sq_ref[part] = take_tiles(total, offset, sq_ref.shape[2]) * (1.0 / replicas)
        offset += sq_ref.shape[2] // LANES
    for ref in (so_ref, si_ref, sd_ref):
        ref[...] = take_tiles(total, offset, ref.shape[1]) * (1.0 / replicas)
        offset += ref.shape[1] // LANES


def right_sums(rights, replicas):
    rank_size = rights[1].shape[0]
    lanes = 3 * rights[0].shape[2] + sum(right.shape[1] for right in rights[1:])
    width = -(-lanes // (LANES * replicas)) * LANES
    vmem = pl.BlockSpec(memory_space=pltpu.VMEM)
    return pl.pallas_call(
        partial(right_sum_kernel, replicas),
        in_specs=[vmem] * 4,
        out_specs=[vmem] * 4,
        out_shape=[jax.ShapeDtypeStruct(right.shape, jnp.float32) for right in rights],
        scratch_shapes=[
            pltpu.VMEM((replicas, rank_size, width), jnp.float32),
            pltpu.VMEM((replicas, rank_size, width), jnp.bfloat16),
            pltpu.VMEM((replicas, rank_size, width), jnp.bfloat16),
            pltpu.VMEM((replicas, rank_size, width), jnp.float32),
            pltpu.SemaphoreType.DMA((replicas,)),
            pltpu.SemaphoreType.DMA((replicas,)),
            pltpu.SemaphoreType.DMA((replicas,)),
            pltpu.SemaphoreType.DMA((replicas,)),
        ],
        compiler_params=pltpu.CompilerParams(collective_id=2, has_side_effects=True),
        name="right_sums",
    )(*rights)


def outer_of(basis_rows, right):
    basis_high, basis_low = split_bf16(basis_rows)
    right_high, right_low = split_bf16(right)
    return dot_tn(
        jnp.concatenate([basis_high, basis_low, basis_high], axis=0),
        jnp.concatenate([right_high, right_high, right_low], axis=0),
    )


def update_kernel(step_rate, out_steps, *refs):
    (mq, mo, mi, md, oq, oo, oi, od, wq, wo, wi, wd, bq, bo, bi, bd, rq, ro, ri, rd,
     gq, go, gi, gd, eq, eo, ei, ed, nq, no, ni, nd, vq, vo, vi, vd) = refs
    step = pl.program_id(0)

    def one(matrix, old, weight, rank, grad_ref, err_ref, mom_ref, new_ref, place):
        moment = 0.9 * old + rank
        grad_ref[place] = rank
        err_ref[place] = matrix - rank
        mom_ref[place] = moment
        new_ref[place] = weight.astype(jnp.float32) - step_rate * moment

    def lanes_of(ref, rows):
        return ref[:, pl.ds(pl.multiple_of(step * rows, LANES), rows)]

    rows = mq.shape[1]
    for part in range(3):
        rank = outer_of(lanes_of(bq, rows), rq[part])
        one(mq[part], oq[part], wq[part], rank, gq, eq, nq, vq, part)
    rank = outer_of(lanes_of(bi, mi.shape[0]), ri[...])
    one(mi[...], oi[...], wi[...], rank, gi, ei, ni, vi, slice(None))
    rank = outer_of(lanes_of(bd, md.shape[0]), rd[...])
    one(md[...], od[...], wd[...], rank, gd, ed, nd, vd, slice(None))

    @pl.when(step < out_steps)
    def _():
        rank = outer_of(lanes_of(bo, mo.shape[0]), ro[...])
        one(mo[...], oo[...], wo[...], rank, go, eo, no, vo, slice(None))


def update(matrices, momenta, weights, bases, rights, step_rate):
    qkv, out, inw, down = matrices
    rows = LANES
    steps = inw.shape[0] // rows
    down_rows = down.shape[0] // steps
    if down_rows < LANES:
        steps = down.shape[0] // LANES
        rows, down_rows = inw.shape[0] // steps, LANES
    out_steps = out.shape[0] // LANES

    def whole(array):
        return pl.BlockSpec(array.shape, lambda i: (0,) * array.ndim)

    def specs():
        return [
            pl.BlockSpec((3, rows, qkv.shape[2]), lambda i: (0, i, 0)),
            pl.BlockSpec((LANES, out.shape[1]), lambda i: (jnp.minimum(i, out_steps - 1), 0)),
            pl.BlockSpec((rows, inw.shape[1]), lambda i: (i, 0)),
            pl.BlockSpec((down_rows, down.shape[1]), lambda i: (i, 0)),
        ]

    shapes = [jax.ShapeDtypeStruct(one.shape, jnp.float32) for one in matrices]
    outputs = pl.pallas_call(
        partial(update_kernel, step_rate, out_steps),
        grid=(steps,),
        in_specs=specs() * 3 + [whole(one) for one in bases] + [whole(one) for one in rights],
        out_specs=specs() * 4,
        out_shape=shapes * 4,
        compiler_params=pltpu.CompilerParams(vmem_limit_bytes=48 << 20),
        name="update",
    )(*matrices, *momenta, *weights, *bases, *rights)
    return outputs[0:4], outputs[4:8], outputs[8:12], outputs[12:16]


def masked_scores(queries, key_heads, seg_ids):
    scores = jnp.einsum("qhd,khd->hqk", queries, key_heads, preferred_element_type=jnp.float32)
    same_doc = seg_ids[:, None] == seg_ids[None, :]
    return jnp.where(same_doc[None], scores, MASKED)


def attend_forward(inputs_of):
    queries, key_heads, value_heads, seg_ids = inputs_of
    scores = masked_scores(queries, key_heads, seg_ids)
    highest = jnp.max(scores, axis=-1, keepdims=True)
    powers = jnp.exp(scores - highest)
    denominator = jnp.sum(powers, axis=-1, keepdims=True)
    weights = (powers / denominator).astype(jnp.bfloat16)
    mixed_heads = jnp.einsum(
        "hqk,khd->qhd", weights, value_heads, preferred_element_type=jnp.float32
    )
    return (mixed_heads.astype(jnp.bfloat16), highest[..., 0] + jnp.log(denominator[..., 0]))


def attend_backward(inputs_of):
    queries, key_heads, value_heads, seg_ids, grad_mixed, log_total = inputs_of
    scores = masked_scores(queries, key_heads, seg_ids)
    probability = jnp.exp(scores - log_total[..., None])
    grad_probs = jnp.einsum(
        "qhd,khd->hqk", grad_mixed, value_heads, preferred_element_type=jnp.float32
    )
    centre = jnp.sum(probability * grad_probs, axis=-1, keepdims=True)
    grad_scores = (probability * (grad_probs - centre)).astype(jnp.bfloat16)
    grad_query = jnp.einsum(
        "hqk,khd->qhd", grad_scores, key_heads, preferred_element_type=jnp.float32
    )
    grad_key = jnp.einsum("hqk,qhd->khd", grad_scores, queries, preferred_element_type=jnp.float32)
    grad_value = jnp.einsum(
        "hqk,qhd->khd",
        probability.astype(jnp.bfloat16),
        grad_mixed,
        preferred_element_type=jnp.float32,
    )
    return (
        grad_query.astype(jnp.bfloat16),
        grad_key.astype(jnp.bfloat16),
        grad_value.astype(jnp.bfloat16),
    )


def local(
    tokens,
    segments,
    w_qkv,
    head_bias,
    w_out,
    w_in,
    unit_bias,
    w_down,
    vectors,
    cotangent,
    err_qkv,
    err_out,
    err_in,
    err_down,
    basis_qkv,
    basis_out,
    basis_in,
    basis_down,
    mom_qkv,
    mom_head_bias,
    mom_out,
    mom_in,
    mom_unit_bias,
    mom_down,
    mom_vectors,
):
    token_count, model_width = tokens.shape
    seq_count, length = segments.shape
    head_slab = w_qkv.shape[2]
    head_count = head_slab // DH
    unit_slab = w_in.shape[1]
    tensor_size = lax.axis_size("tensor")
    replicas = lax.axis_size("dp")
    share_rows = token_count // tensor_size
    tensor_place = lax.axis_index("tensor")
    row_start = tensor_place * share_rows
    head_scale = 1.0 / math.sqrt(DH)

    def own_rows(values):
        return lax.dynamic_slice_in_dim(values, row_start, share_rows, 0)

    flat_qkv = w_qkv.reshape(model_width, 3 * head_slab)
    projected = jnp.dot(tokens, flat_qkv, preferred_element_type=jnp.float32).reshape(
        token_count, 3, head_slab
    )
    head_shape = (seq_count, length, head_count, DH)
    queries = (
        ((projected[:, 0] + head_bias[0]) * head_scale).astype(jnp.bfloat16).reshape(head_shape)
    )
    key_heads = projected[:, 1].astype(jnp.bfloat16).reshape(head_shape)
    value_heads = (projected[:, 2] + head_bias[1]).astype(jnp.bfloat16).reshape(head_shape)
    mixed_heads, log_total = lax.map(attend_forward, (queries, key_heads, value_heads, segments))
    mixed_flat = mixed_heads.reshape(token_count, head_slab)
    attn_out = (
        lax.psum(jnp.dot(mixed_flat, w_out, preferred_element_type=jnp.float32), "tensor")
        + vectors[0]
    )
    first_norm, first_normed, first_inverse = norm_forward(
        tokens.astype(jnp.float32) + attn_out, vectors[2], vectors[3]
    )
    first_low = first_norm.astype(jnp.bfloat16)
    hidden = jnp.dot(first_low, w_in, preferred_element_type=jnp.float32) + unit_bias
    active, gelu_back = jax.vjp(partial(jax.nn.gelu, approximate=False), hidden)
    active_low = active.astype(jnp.bfloat16)
    grad_out_share = own_rows(cotangent).astype(jnp.float32)
    summed_input = (
        first_norm
        + lax.psum(jnp.dot(active_low, w_down, preferred_element_type=jnp.float32), "tensor")
        + vectors[1]
    )
    second_norm, second_normed, second_inverse = norm_forward(summed_input, vectors[4], vectors[5])
    layer_out = own_rows(second_norm).astype(jnp.bfloat16)
    grad_sum = norm_backward(
        cotangent.astype(jnp.float32), second_normed, second_inverse, vectors[4]
    )
    grad_branch = grad_sum.astype(jnp.bfloat16)
    second_share = own_rows(second_normed)
    grad_w_down = trans_times(active_low, grad_branch)
    grad_active = times_trans(grad_branch, w_down)
    grad_hidden = gelu_back(grad_active)[0].astype(jnp.bfloat16)
    grad_w_in = trans_times(first_low, grad_hidden)
    grad_units = jnp.sum(grad_hidden.astype(jnp.float32), axis=0)
    grad_first = lax.psum(times_trans(grad_hidden, w_in), "tensor") + grad_sum
    grad_h1 = norm_backward(grad_first, first_normed, first_inverse, vectors[2])
    grad_attn = grad_h1.astype(jnp.bfloat16)
    grad_first_share = own_rows(grad_first)
    first_normed_share = own_rows(first_normed)
    grad_h1_share = own_rows(grad_h1)
    grad_w_out = trans_times(mixed_flat, grad_attn)
    grad_mixed = times_trans(grad_attn, w_out).astype(jnp.bfloat16).reshape(head_shape)
    grad_query, grad_key, grad_value = lax.map(
        attend_backward, (queries, key_heads, value_heads, segments, grad_mixed, log_total)
    )
    grad_query = (
        grad_query.reshape(token_count, head_slab).astype(jnp.float32) * head_scale
    ).astype(jnp.bfloat16)
    grad_key = grad_key.reshape(token_count, head_slab)
    grad_value = grad_value.reshape(token_count, head_slab)
    grad_projected = jnp.stack([grad_query, grad_key, grad_value], axis=1).reshape(
        token_count, 3 * head_slab
    )
    grad_w_qkv = trans_times(tokens, grad_projected)
    grad_heads = jnp.stack(
        [
            jnp.sum(grad_query.astype(jnp.float32), axis=0),
            jnp.sum(grad_value.astype(jnp.float32), axis=0),
        ]
    )
    grad_tokens = (
        lax.psum_scatter(
            times_trans(grad_projected, flat_qkv).astype(jnp.bfloat16),
            "tensor",
            scatter_dimension=0,
            tiled=True,
        ).astype(jnp.float32)
        + grad_h1_share
    )
    local_vectors = jnp.stack(
        [
            jnp.sum(own_rows(grad_attn).astype(jnp.float32), axis=0),
            jnp.sum(own_rows(grad_branch).astype(jnp.float32), axis=0),
            jnp.sum(grad_first_share * first_normed_share, axis=0),
            jnp.sum(grad_first_share, axis=0),
            jnp.sum(grad_out_share * second_share, axis=0),
            jnp.sum(grad_out_share, axis=0),
        ]
    )
    small = jnp.concatenate(
        [
            local_vectors,
            jnp.pad(grad_units, (0, model_width - unit_slab))[None],
            jnp.pad(grad_heads.reshape(1, 2 * head_slab), ((0, 0), (0, model_width - 2 * head_slab))),
        ],
        axis=0,
    )
    planes = (1, 0, 2)
    combined_qkv = grad_w_qkv.reshape(model_width, 3, head_slab).transpose(planes) + err_qkv[
        0
    ].transpose(planes)
    combined_out = grad_w_out + err_out[0]
    combined_in = grad_w_in + err_in[0]
    combined_down = grad_w_down + err_down[0]
    matrices = (combined_qkv, combined_out, combined_in, combined_down)
    lefts = lefts_of(matrices, (basis_qkv.transpose(planes), basis_out, basis_in, basis_down))
    *bases, small_sum = bases_of(lefts, small, replicas, tensor_size)
    rights = right_sums(rights_of(matrices, bases), replicas)
    step_rate = 0.3 * math.sqrt(replicas / token_count)
    grads, errors, moments, news = update(
        matrices,
        (mom_qkv.transpose(planes), mom_out, mom_in, mom_down),
        (w_qkv.transpose(planes), w_out, w_in, w_down),
        bases,
        rights,
        step_rate,
    )
    reduced_qkv, rank_out, rank_in, rank_down = (grads[0].transpose(planes),) + tuple(grads[1:])
    new_err_qkv, new_err_out, new_err_in, new_err_down = (
        errors[0].transpose(planes)[None],
        errors[1][None],
        errors[2][None],
        errors[3][None],
    )
    new_mom_qkv, new_mom_out, new_mom_in, new_mom_down = (moments[0].transpose(planes),) + tuple(
        moments[1:]
    )
    new_w_qkv, new_w_out, new_w_in, new_w_down = (news[0].transpose(planes),) + tuple(news[1:])
    right_qkv, right_out, right_in, right_down = rights
    new_basis_qkv = right_qkv.transpose(planes)
    grad_vectors = small_sum[:6]
    grad_unit_bias = small_sum[6, :unit_slab]
    grad_head_bias = small_sum[7, : 2 * head_slab].reshape(2, head_slab)
    new_mom_head_bias = 0.9 * mom_head_bias + grad_head_bias
    new_mom_unit_bias = 0.9 * mom_unit_bias + grad_unit_bias
    new_mom_vectors = 0.9 * mom_vectors + grad_vectors
    new_head_bias = head_bias - step_rate * new_mom_head_bias
    new_unit_bias = unit_bias - step_rate * new_mom_unit_bias
    new_vectors = vectors - step_rate * new_mom_vectors
    return (
        layer_out,
        grad_tokens,
        reduced_qkv,
        grad_head_bias,
        rank_out,
        rank_in,
        grad_unit_bias,
        rank_down,
        grad_vectors,
        new_err_qkv,
        new_err_out,
        new_err_in,
        new_err_down,
        new_basis_qkv,
        right_out,
        right_in,
        right_down,
        new_mom_qkv,
        new_mom_head_bias,
        new_mom_out,
        new_mom_in,
        new_mom_unit_bias,
        new_mom_down,
        new_mom_vectors,
        new_w_qkv,
        new_head_bias,
        new_w_out,
        new_w_in,
        new_unit_bias,
        new_w_down,
        new_vectors,
    )


def solution(mesh):
    in_specs = (
        P("dp", None),
        P("dp", None),
        P(None, None, "tensor"),
        P(None, "tensor"),
        P("tensor", None),
        P(None, "tensor"),
        P("tensor"),
        P("tensor", None),
        P(),
        P("dp", None),
        P("dp", None, None, "tensor"),
        P("dp", "tensor", None),
        P("dp", None, "tensor"),
        P("dp", "tensor", None),
        P(None, None, "tensor"),
        P("tensor", None),
        P(None, "tensor"),
        P("tensor", None),
        P(None, None, "tensor"),
        P(None, "tensor"),
        P("tensor", None),
        P(None, "tensor"),
        P("tensor"),
        P("tensor", None),
        P(),
    )
    out_specs = (
        P(("dp", "tensor"), None),
        P(("dp", "tensor"), None),
        P(None, None, "tensor"),
        P(None, "tensor"),
        P("tensor", None),
        P(None, "tensor"),
        P("tensor"),
        P("tensor", None),
        P(),
        P("dp", None, None, "tensor"),
        P("dp", "tensor", None),
        P("dp", None, "tensor"),
        P("dp", "tensor", None),
        P(None, None, "tensor"),
        P("tensor", None),
        P(None, "tensor"),
        P("tensor", None),
        P(None, None, "tensor"),
        P(None, "tensor"),
        P("tensor", None),
        P(None, "tensor"),
        P("tensor"),
        P("tensor", None),
        P(),
        P(None, None, "tensor"),
        P(None, "tensor"),
        P("tensor", None),
        P(None, "tensor"),
        P("tensor"),
        P("tensor", None),
        P(),
    )
    return jax.shard_map(local, mesh=mesh, in_specs=in_specs, out_specs=out_specs, check_vma=False)
```

```python
from functools import partial
import math

import jax
import jax.numpy as jnp
from jax import lax
from jax.experimental import pallas as pl
from jax.experimental.pallas import tpu as pltpu
from jax.sharding import PartitionSpec as P

DH = 64
LANES = 128
MESH = pl.DeviceIdType.MESH


PRECISE = lax.Precision.HIGHEST
EPS_NORM = 1e-05
EPS_BASIS = 1e-08
MASKED = -1000000000.0


def norm_forward(values, gain, shift):
    row_mean = jnp.mean(values, axis=-1, keepdims=True)
    centred = values - row_mean
    variance = jnp.mean(centred * centred, axis=-1, keepdims=True)
    inverse = lax.rsqrt(variance + EPS_NORM)
    normed = centred * inverse
    return (normed * gain + shift, normed, inverse)


def norm_backward(grad_norm, normed, inverse, gain):
    scaled_grad = grad_norm * gain
    grad_mean = jnp.mean(scaled_grad, axis=-1, keepdims=True)
    along_norm = jnp.mean(scaled_grad * normed, axis=-1, keepdims=True)
    return inverse * (scaled_grad - grad_mean - normed * along_norm)


def times_trans(left_side, right_side):
    return lax.dot_general(
        left_side, right_side, (((1,), (1,)), ((), ())), preferred_element_type=jnp.float32
    )


def trans_times(left_side, right_side):
    return lax.dot_general(
        left_side, right_side, (((0,), (0,)), ((), ())), preferred_element_type=jnp.float32
    )


def split_bf16(values):
    high = values.astype(jnp.bfloat16)
    low = (values - high.astype(jnp.float32)).astype(jnp.bfloat16)
    return high, low


def dot_nt(left_side, right_side):
    return lax.dot_general(
        left_side, right_side, (((1,), (1,)), ((), ())), preferred_element_type=jnp.float32
    )


def dot_nn(left_side, right_side):
    return lax.dot_general(
        left_side, right_side, (((1,), (0,)), ((), ())), preferred_element_type=jnp.float32
    )


def dot_tn(left_side, right_side):
    return lax.dot_general(
        left_side, right_side, (((0,), (0,)), ((), ())), preferred_element_type=jnp.float32
    )


def left_factor(factor, matrix):
    rank_size = factor.shape[0]
    factor_high, factor_low = split_bf16(factor)
    matrix_high, matrix_low = split_bf16(matrix)
    both = dot_nt(jnp.concatenate([factor_high, factor_low], axis=0), matrix_high)
    return both[:rank_size] + both[rank_size:] + dot_nt(factor_high, matrix_low)


def right_factor(basis_rows, matrix):
    rank_size = basis_rows.shape[0]
    basis_high, basis_low = split_bf16(basis_rows)
    matrix_high, matrix_low = split_bf16(matrix)
    both = dot_nn(jnp.concatenate([basis_high, basis_low], axis=0), matrix_high)
    return both[:rank_size] + both[rank_size:] + dot_nn(basis_high, matrix_low)


def lefts_kernel(qkv_ref, out_ref, in_ref, down_ref, fq_ref, fo_ref, fi_ref, fd_ref,
                 lq_ref, lo_ref, li_ref, ld_ref):
    lq_ref[...] = (
        left_factor(fq_ref[0], qkv_ref[0])
        + left_factor(fq_ref[1], qkv_ref[1])
        + left_factor(fq_ref[2], qkv_ref[2])
    )
    li_ref[...] = left_factor(fi_ref[...], in_ref[...])
    ld_ref[...] = left_factor(fd_ref[...], down_ref[...])

    @pl.when(pl.program_id(0) == 0)
    def _():
        lo_ref[...] = left_factor(fo_ref[...], out_ref[...])


def lefts_of(matrices, factors):
    steps = 4
    qkv, out, inw, down = matrices
    rank_size = factors[1].shape[0]

    def whole(array):
        return pl.BlockSpec(array.shape, lambda i: (0,) * array.ndim)

    def rows(array):
        return pl.BlockSpec((array.shape[0] // steps, array.shape[1]), lambda i: (i, 0))

    def lanes(size):
        return pl.BlockSpec((rank_size, size // steps), lambda i: (0, i))

    return pl.pallas_call(
        lefts_kernel,
        grid=(steps,),
        in_specs=[
            pl.BlockSpec((3, qkv.shape[1] // steps, qkv.shape[2]), lambda i: (0, i, 0)),
            whole(out),
            rows(inw),
            rows(down),
        ]
        + [whole(factor) for factor in factors],
        out_specs=[
            lanes(qkv.shape[1]),
            pl.BlockSpec((rank_size, out.shape[0]), lambda i: (0, 0)),
            lanes(inw.shape[0]),
            lanes(down.shape[0]),
        ],
        out_shape=[
            jax.ShapeDtypeStruct((rank_size, size), jnp.float32)
            for size in (qkv.shape[1], out.shape[0], inw.shape[0], down.shape[0])
        ],
        compiler_params=pltpu.CompilerParams(vmem_limit_bytes=40 << 20),
        name="left_factors",
    )(qkv, out, inw, down, *factors)


def rights_kernel(qkv_ref, out_ref, in_ref, down_ref, bq_ref, bo_ref, bi_ref, bd_ref,
                  rq_ref, ro_ref, ri_ref, rd_ref):
    first = pl.program_id(0) == 0

    @pl.when(first)
    def _():
        ro_ref[...] = right_factor(bo_ref[...], out_ref[...])
        rq_ref[...] = jnp.zeros_like(rq_ref)
        ri_ref[...] = jnp.zeros_like(ri_ref)
        rd_ref[...] = jnp.zeros_like(rd_ref)

    for part in range(3):
        rq_ref[part] += right_factor(bq_ref[...], qkv_ref[part])
    ri_ref[...] += right_factor(bi_ref[...], in_ref[...])
    rd_ref[...] += right_factor(bd_ref[...], down_ref[...])


def rights_of(matrices, bases):
    steps = 4
    qkv, out, inw, down = matrices
    rank_size = bases[0].shape[0]

    def whole(shape):
        return pl.BlockSpec(shape, lambda i: (0,) * len(shape))

    def rows(array):
        return pl.BlockSpec((array.shape[0] // steps, array.shape[1]), lambda i: (i, 0))

    def lanes(array):
        return pl.BlockSpec((rank_size, array.shape[1] // steps), lambda i: (0, i))

    shapes = [(3, rank_size, qkv.shape[2])] + [(rank_size, one.shape[1]) for one in (out, inw, down)]
    return pl.pallas_call(
        rights_kernel,
        grid=(steps,),
        in_specs=[
            pl.BlockSpec((3, qkv.shape[1] // steps, qkv.shape[2]), lambda i: (0, i, 0)),
            whole(out.shape),
            rows(inw),
            rows(down),
            lanes(bases[0]),
            whole(bases[1].shape),
            lanes(bases[2]),
            lanes(bases[3]),
        ],
        out_specs=[whole(shape) for shape in shapes],
        out_shape=[jax.ShapeDtypeStruct(shape, jnp.float32) for shape in shapes],
        compiler_params=pltpu.CompilerParams(vmem_limit_bytes=40 << 20),
        name="right_factors",
    )(qkv, out, inw, down, *bases)


def peer_ids(replicas, place):
    dp_place = lax.axis_index("dp")
    tensor_place = lax.axis_index("tensor")
    return dp_place, tensor_place


def greet(replicas, tensor_size):
    dp_place = lax.axis_index("dp")
    tensor_place = lax.axis_index("tensor")
    barrier = pltpu.get_barrier_semaphore()

    def greet_dp(step, carry):
        pl.semaphore_signal(
            barrier,
            inc=1,
            device_id=(lax.rem(dp_place + step, replicas), tensor_place),
            device_id_type=MESH,
        )
        return carry

    def greet_tensor(step, carry):
        pl.semaphore_signal(
            barrier,
            inc=1,
            device_id=(dp_place, lax.rem(tensor_place + step, tensor_size)),
            device_id_type=MESH,
        )
        return carry

    lax.fori_loop(1, replicas, greet_dp, 0)
    if tensor_size > 1:
        lax.fori_loop(1, tensor_size, greet_tensor, 0)
    pl.semaphore_wait(barrier, replicas - 1 + tensor_size - 1)


def dp_sum(replicas, mine, wire, arrived, total, send_one, recv_one, send_two, recv_two):
    dp_place = lax.axis_index("dp")
    tensor_place = lax.axis_index("tensor")

    def scatter_to(step):
        peer = lax.rem(dp_place + step, replicas)
        return pltpu.make_async_remote_copy(
            src_ref=wire.at[peer],
            dst_ref=arrived.at[dp_place],
            send_sem=send_one.at[step],
            recv_sem=recv_one.at[dp_place],
            device_id=(peer, tensor_place),
            device_id_type=MESH,
        )

    def scatter_from(step):
        peer = lax.rem(dp_place + step, replicas)
        return pltpu.make_async_remote_copy(
            src_ref=wire.at[peer],
            dst_ref=arrived.at[peer],
            send_sem=send_one.at[step],
            recv_sem=recv_one.at[peer],
            device_id=(peer, tensor_place),
            device_id_type=MESH,
        )

    def gather_to(step):
        peer = lax.rem(dp_place + step, replicas)
        return pltpu.make_async_remote_copy(
            src_ref=total.at[dp_place],
            dst_ref=total.at[dp_place],
            send_sem=send_two.at[step],
            recv_sem=recv_two.at[dp_place],
            device_id=(peer, tensor_place),
            device_id_type=MESH,
        )

    def gather_from(step):
        peer = lax.rem(dp_place + step, replicas)
        return pltpu.make_async_remote_copy(
            src_ref=total.at[dp_place],
            dst_ref=total.at[peer],
            send_sem=send_two.at[step],
            recv_sem=recv_two.at[peer],
            device_id=(peer, tensor_place),
            device_id_type=MESH,
        )

    def start_scatter(step, carry):
        scatter_to(step).start()
        return carry

    def add_arrived(step, carry):
        scatter_from(step).wait_recv()
        peer = lax.rem(dp_place + step, replicas)
        return carry + arrived[peer].astype(jnp.float32)

    def start_gather(step, carry):
        gather_to(step).start()
        return carry

    def finish(step, carry):
        scatter_to(step).wait_send()
        gather_to(step).wait_send()
        gather_from(step).wait_recv()
        return carry

    wire[...] = mine[...].astype(wire.dtype)
    lax.fori_loop(1, replicas, start_scatter, 0)
    total[dp_place] = lax.fori_loop(1, replicas, add_arrived, mine[dp_place])
    lax.fori_loop(1, replicas, start_gather, 0)
    lax.fori_loop(1, replicas, finish, 0)


def place_tiles(target, offset, values):
    per_chunk = target.shape[2] // LANES
    for tile in range(values.shape[1] // LANES):
        spot = offset + tile
        target[spot // per_chunk, :, pl.ds(spot % per_chunk * LANES, LANES)] = values[
            :, tile * LANES : (tile + 1) * LANES
        ]
    return offset + values.shape[1] // LANES


def take_tiles(source, offset, size):
    per_chunk = source.shape[2] // LANES
    pieces = []
    for tile in range(size // LANES):
        spot = offset + tile
        pieces.append(source[spot // per_chunk, :, pl.ds(spot % per_chunk * LANES, LANES)])
    return jnp.concatenate(pieces, axis=1) if len(pieces) > 1 else pieces[0]


def orthonormal_rows(rows):
    rank_size = rows.shape[0]
    row_number = lax.broadcasted_iota(jnp.int32, (rank_size, 1), 0)
    for position in range(rank_size):
        row = rows[position : position + 1]
        length = jnp.sqrt(jnp.sum(row * row, axis=1, keepdims=True)) + EPS_BASIS
        unit = row / length
        along = jnp.sum(rows * unit, axis=1, keepdims=True)
        later = jnp.where(row_number > position, along, 0.0)
        rows = jnp.where(row_number == position, unit, rows - later * unit)
    return rows


def basis_kernel(replicas, tensor_size, lq_ref, lo_ref, li_ref, ld_ref, small_ref,
                 bq_ref, bo_ref, bi_ref, bd_ref, sum_ref,
                 mine, wire, arrived, total, small_slots,
                 send_one, recv_one, send_two, recv_two, send_three, recv_three):
    dp_place = lax.axis_index("dp")
    tensor_place = lax.axis_index("tensor")
    mine[...] = jnp.zeros_like(mine)
    greet(replicas, tensor_size)
    lefts = (lq_ref, lo_ref, li_ref, ld_ref)
    offset = 0
    for ref in lefts + (small_ref,):
        offset = place_tiles(mine, offset, ref[...])
    dp_sum(replicas, mine, wire, arrived, total, send_one, recv_one, send_two, recv_two)

    def slot_copy(step, slot):
        peer = lax.rem(tensor_place + step, tensor_size)
        return pltpu.make_async_remote_copy(
            src_ref=small_slots.at[tensor_place],
            dst_ref=small_slots.at[slot],
            send_sem=send_three.at[step],
            recv_sem=recv_three.at[slot],
            device_id=(dp_place, peer),
            device_id_type=MESH,
        )

    def start(step, carry):
        slot_copy(step, tensor_place).start()
        return carry

    small_at = sum(ref.shape[1] for ref in lefts) // LANES
    own_small = take_tiles(total, small_at, small_ref.shape[1])
    small_slots[tensor_place] = own_small
    lax.fori_loop(1, tensor_size, start, 0)
    offset = 0
    for ref, basis_ref in zip(lefts, (bq_ref, bo_ref, bi_ref, bd_ref)):
        rows = take_tiles(total, offset, ref.shape[1]) * (1.0 / replicas)
        basis_ref[...] = orthonormal_rows(rows)
        offset += ref.shape[1] // LANES

    def collect(step, carry):
        peer = lax.rem(tensor_place + step, tensor_size)
        slot_copy(step, peer).wait_recv()
        slot_copy(step, tensor_place).wait_send()
        return carry + small_slots[peer]

    everyone = lax.fori_loop(1, tensor_size, collect, own_small)
    row_number = lax.broadcasted_iota(jnp.int32, everyone.shape, 0)
    sum_ref[...] = jnp.where(row_number < 6, everyone, own_small) * (1.0 / replicas)


def bases_of(lefts, small, replicas, tensor_size):
    rank_size = small.shape[0]
    lanes = sum(left.shape[1] for left in lefts) + small.shape[1]
    width = -(-lanes // (LANES * replicas)) * LANES
    shapes = [left.shape for left in lefts] + [small.shape]
    vmem = pl.BlockSpec(memory_space=pltpu.VMEM)
    return pl.pallas_call(
        partial(basis_kernel, replicas, tensor_size),
        in_specs=[vmem] * 5,
        out_specs=[vmem] * 5,
        out_shape=[jax.ShapeDtypeStruct(shape, jnp.float32) for shape in shapes],
        scratch_shapes=[
            pltpu.VMEM((replicas, rank_size, width), jnp.float32),
            pltpu.VMEM((replicas, rank_size, width), jnp.bfloat16),
            pltpu.VMEM((replicas, rank_size, width), jnp.bfloat16),
            pltpu.VMEM((replicas, rank_size, width), jnp.float32),
            pltpu.VMEM((tensor_size,) + small.shape, jnp.float32),
            pltpu.SemaphoreType.DMA((replicas,)),
            pltpu.SemaphoreType.DMA((replicas,)),
            pltpu.SemaphoreType.DMA((replicas,)),
            pltpu.SemaphoreType.DMA((replicas,)),
            pltpu.SemaphoreType.DMA((tensor_size,)),
            pltpu.SemaphoreType.DMA((tensor_size,)),
        ],
        compiler_params=pltpu.CompilerParams(collective_id=1, has_side_effects=True),
        name="bases",
    )(*lefts, small)


def right_sum_kernel(replicas, rq_ref, ro_ref, ri_ref, rd_ref, sq_ref, so_ref, si_ref, sd_ref,
                     mine, wire, arrived, total, send_one, recv_one, send_two, recv_two):
    mine[...] = jnp.zeros_like(mine)
    greet(replicas, 1)
    offset = 0
    for part in range(3):
        offset = place_tiles(mine, offset, rq_ref[part])
    for ref in (ro_ref, ri_ref, rd_ref):
        offset = place_tiles(mine, offset, ref[...])
    dp_sum(replicas, mine, wire, arrived, total, send_one, recv_one, send_two, recv_two)
    offset = 0
    for part in range(3):
        sq_ref[part] = take_tiles(total, offset, sq_ref.shape[2]) * (1.0 / replicas)
        offset += sq_ref.shape[2] // LANES
    for ref in (so_ref, si_ref, sd_ref):
        ref[...] = take_tiles(total, offset, ref.shape[1]) * (1.0 / replicas)
        offset += ref.shape[1] // LANES


def right_sums(rights, replicas):
    rank_size = rights[1].shape[0]
    lanes = 3 * rights[0].shape[2] + sum(right.shape[1] for right in rights[1:])
    width = -(-lanes // (LANES * replicas)) * LANES
    vmem = pl.BlockSpec(memory_space=pltpu.VMEM)
    return pl.pallas_call(
        partial(right_sum_kernel, replicas),
        in_specs=[vmem] * 4,
        out_specs=[vmem] * 4,
        out_shape=[jax.ShapeDtypeStruct(right.shape, jnp.float32) for right in rights],
        scratch_shapes=[
            pltpu.VMEM((replicas, rank_size, width), jnp.float32),
            pltpu.VMEM((replicas, rank_size, width), jnp.bfloat16),
            pltpu.VMEM((replicas, rank_size, width), jnp.bfloat16),
            pltpu.VMEM((replicas, rank_size, width), jnp.float32),
            pltpu.SemaphoreType.DMA((replicas,)),
            pltpu.SemaphoreType.DMA((replicas,)),
            pltpu.SemaphoreType.DMA((replicas,)),
            pltpu.SemaphoreType.DMA((replicas,)),
        ],
        compiler_params=pltpu.CompilerParams(collective_id=2, has_side_effects=True),
        name="right_sums",
    )(*rights)


def outer_of(basis_rows, right):
    basis_high, basis_low = split_bf16(basis_rows)
    right_high, right_low = split_bf16(right)
    return dot_tn(
        jnp.concatenate([basis_high, basis_low, basis_high], axis=0),
        jnp.concatenate([right_high, right_high, right_low], axis=0),
    )


def update_kernel(step_rate, out_steps, *refs):
    (mq, mo, mi, md, oq, oo, oi, od, wq, wo, wi, wd, bq, bo, bi, bd, rq, ro, ri, rd,
     gq, go, gi, gd, eq, eo, ei, ed, nq, no, ni, nd, vq, vo, vi, vd) = refs
    step = pl.program_id(0)

    def one(matrix, old, weight, rank, grad_ref, err_ref, mom_ref, new_ref, place):
        moment = 0.9 * old + rank
        grad_ref[place] = rank
        err_ref[place] = matrix - rank
        mom_ref[place] = moment
        new_ref[place] = weight.astype(jnp.float32) - step_rate * moment

    def lanes_of(ref, rows):
        return ref[:, pl.ds(pl.multiple_of(step * rows, LANES), rows)]

    rows = mq.shape[1]
    for part in range(3):
        rank = outer_of(lanes_of(bq, rows), rq[part])
        one(mq[part], oq[part], wq[part], rank, gq, eq, nq, vq, part)
    rank = outer_of(lanes_of(bi, mi.shape[0]), ri[...])
    one(mi[...], oi[...], wi[...], rank, gi, ei, ni, vi, slice(None))
    rank = outer_of(lanes_of(bd, md.shape[0]), rd[...])
    one(md[...], od[...], wd[...], rank, gd, ed, nd, vd, slice(None))

    @pl.when(step < out_steps)
    def _():
        rank = outer_of(lanes_of(bo, mo.shape[0]), ro[...])
        one(mo[...], oo[...], wo[...], rank, go, eo, no, vo, slice(None))


def update(matrices, momenta, weights, bases, rights, step_rate):
    qkv, out, inw, down = matrices
    rows = LANES
    steps = inw.shape[0] // rows
    down_rows = down.shape[0] // steps
    if down_rows < LANES:
        steps = down.shape[0] // LANES
        rows, down_rows = inw.shape[0] // steps, LANES
    out_steps = out.shape[0] // LANES

    def whole(array):
        return pl.BlockSpec(array.shape, lambda i: (0,) * array.ndim)

    def specs():
        return [
            pl.BlockSpec((3, rows, qkv.shape[2]), lambda i: (0, i, 0)),
            pl.BlockSpec((LANES, out.shape[1]), lambda i: (jnp.minimum(i, out_steps - 1), 0)),
            pl.BlockSpec((rows, inw.shape[1]), lambda i: (i, 0)),
            pl.BlockSpec((down_rows, down.shape[1]), lambda i: (i, 0)),
        ]

    shapes = [jax.ShapeDtypeStruct(one.shape, jnp.float32) for one in matrices]
    outputs = pl.pallas_call(
        partial(update_kernel, step_rate, out_steps),
        grid=(steps,),
        in_specs=specs() * 3 + [whole(one) for one in bases] + [whole(one) for one in rights],
        out_specs=specs() * 4,
        out_shape=shapes * 4,
        compiler_params=pltpu.CompilerParams(vmem_limit_bytes=48 << 20),
        name="update",
    )(*matrices, *momenta, *weights, *bases, *rights)
    return outputs[0:4], outputs[4:8], outputs[8:12], outputs[12:16]


def masked_scores(queries, key_heads, seg_ids):
    scores = jnp.einsum("qhd,khd->hqk", queries, key_heads, preferred_element_type=jnp.float32)
    same_doc = seg_ids[:, None] == seg_ids[None, :]
    return jnp.where(same_doc[None], scores, MASKED)


def attend_forward(inputs_of):
    queries, key_heads, value_heads, seg_ids = inputs_of
    scores = masked_scores(queries, key_heads, seg_ids)
    highest = jnp.max(scores, axis=-1, keepdims=True)
    powers = jnp.exp(scores - highest)
    denominator = jnp.sum(powers, axis=-1, keepdims=True)
    weights = (powers / denominator).astype(jnp.bfloat16)
    mixed_heads = jnp.einsum(
        "hqk,khd->qhd", weights, value_heads, preferred_element_type=jnp.float32
    )
    return (mixed_heads.astype(jnp.bfloat16), highest[..., 0] + jnp.log(denominator[..., 0]))


def attend_backward(inputs_of):
    queries, key_heads, value_heads, seg_ids, grad_mixed, log_total = inputs_of
    scores = masked_scores(queries, key_heads, seg_ids)
    probability = jnp.exp(scores - log_total[..., None])
    grad_probs = jnp.einsum(
        "qhd,khd->hqk", grad_mixed, value_heads, preferred_element_type=jnp.float32
    )
    centre = jnp.sum(probability * grad_probs, axis=-1, keepdims=True)
    grad_scores = (probability * (grad_probs - centre)).astype(jnp.bfloat16)
    grad_query = jnp.einsum(
        "hqk,khd->qhd", grad_scores, key_heads, preferred_element_type=jnp.float32
    )
    grad_key = jnp.einsum("hqk,qhd->khd", grad_scores, queries, preferred_element_type=jnp.float32)
    grad_value = jnp.einsum(
        "hqk,qhd->khd",
        probability.astype(jnp.bfloat16),
        grad_mixed,
        preferred_element_type=jnp.float32,
    )
    return (
        grad_query.astype(jnp.bfloat16),
        grad_key.astype(jnp.bfloat16),
        grad_value.astype(jnp.bfloat16),
    )


def stacked_heads(pair, lane_is_low):
    zero = jnp.zeros_like(pair)
    return jnp.concatenate(
        [jnp.where(lane_is_low, pair, zero), jnp.where(lane_is_low, zero, pair)], axis=0
    )


def own_blocks(both):
    rows = both.shape[1] // 2
    return jnp.concatenate([both[:DH, :rows], both[DH:, rows:]], axis=0).T


def mask_bias(seg_key_ref, seg_query_ref):
    same = seg_key_ref[...] == seg_query_ref[...]
    bias = jnp.where(same, 0.0, MASKED)
    return jnp.concatenate([bias, bias], axis=1)


def attend_kernel(place_ref, q_ref, k_ref, v_ref, seg_key_ref, seg_query_ref, mixed_ref, log_ref,
                  value_t):
    @pl.when(pl.program_id(0) == 0)
    def _():
        value_t[...] = v_ref[...].T

    pairs = q_ref.shape[1] // LANES
    lane_is_low = lax.broadcasted_iota(jnp.int32, (1, LANES), 1) < DH
    bias = mask_bias(seg_key_ref, seg_query_ref)
    for pair in range(pairs):
        lanes = slice(pair * LANES, (pair + 1) * LANES)
        queries = stacked_heads(q_ref[:, lanes], lane_is_low)
        scores = dot_nt(k_ref[:, lanes], queries) + bias
        highest = jnp.max(scores, axis=0, keepdims=True)
        powers = jnp.exp(scores - highest)
        denominator = jnp.sum(powers, axis=0, keepdims=True)
        weights = (powers * (1.0 / denominator)).astype(jnp.bfloat16)
        mixed_ref[:, lanes] = own_blocks(dot_nn(value_t[lanes], weights)).astype(jnp.bfloat16)
        log_total = highest + jnp.log(denominator)
        log_ref[2 * pair : 2 * pair + 1] = log_total[:, :LANES]
        log_ref[2 * pair + 1 : 2 * pair + 2] = log_total[:, LANES:]


def attend(projected, seg_keys, seg_queries, place):
    length = seg_keys.shape[1]
    slab = projected.shape[2]
    blocks = length // LANES
    grid_spec = pltpu.PrefetchScalarGridSpec(
        num_scalar_prefetch=1,
        grid=(blocks,),
        in_specs=[
            pl.BlockSpec((None, LANES, slab), lambda i, at: (0, at[0] * blocks + i, 0)),
            pl.BlockSpec((None, length, slab), lambda i, at: (1, at[0], 0)),
            pl.BlockSpec((None, length, slab), lambda i, at: (2, at[0], 0)),
            pl.BlockSpec((None, length, LANES), lambda i, at: (at[0], 0, 0)),
            pl.BlockSpec((None, 1, LANES), lambda i, at: (at[0], 0, i)),
        ],
        out_specs=[
            pl.BlockSpec((LANES, slab), lambda i, at: (i, 0)),
            pl.BlockSpec((slab // DH, LANES), lambda i, at: (0, i)),
        ],
        scratch_shapes=[pltpu.VMEM((slab, length), jnp.bfloat16)],
    )
    return pl.pallas_call(
        attend_kernel,
        grid_spec=grid_spec,
        out_shape=[
            jax.ShapeDtypeStruct((length, slab), jnp.bfloat16),
            jax.ShapeDtypeStruct((slab // DH, length), jnp.float32),
        ],
        compiler_params=pltpu.CompilerParams(vmem_limit_bytes=32 << 20),
        cost_estimate=pl.CostEstimate(
            flops=16 * length * length * slab, bytes_accessed=8 * length * slab,
            transcendentals=length * length * slab // DH,
        ),
        name="attend",
    )(place.reshape(1), projected, projected, projected, seg_keys, seg_queries)


def attend_back_kernel(place_ref, q_ref, k_ref, v_ref, seg_key_ref, seg_query_ref, gm_ref, log_ref,
                       old_ref, grad_ref, sums_ref, key_t, grad_key, grad_value):
    del old_ref
    step = pl.program_id(0)

    @pl.when(step == 0)
    def _():
        key_t[...] = k_ref[...].T
        grad_key[...] = jnp.zeros_like(grad_key)
        grad_value[...] = jnp.zeros_like(grad_value)

    pairs = q_ref.shape[1] // LANES
    lane_is_low = lax.broadcasted_iota(jnp.int32, (1, LANES), 1) < DH
    bias = mask_bias(seg_key_ref, seg_query_ref)
    head_scale = 1.0 / math.sqrt(DH)
    here = pl.ds(pl.multiple_of(step * LANES, LANES), LANES)
    for pair in range(pairs):
        lanes = slice(pair * LANES, (pair + 1) * LANES)
        queries = stacked_heads(q_ref[:, lanes], lane_is_low)
        grads = stacked_heads(gm_ref[:, lanes], lane_is_low)
        log_total = jnp.concatenate(
            [log_ref[2 * pair : 2 * pair + 1], log_ref[2 * pair + 1 : 2 * pair + 2]], axis=1
        )
        probs = jnp.exp(dot_nt(k_ref[:, lanes], queries) + (bias - log_total))
        grad_probs = dot_nt(v_ref[:, lanes], grads)
        centre = jnp.sum(probs * grad_probs, axis=0, keepdims=True)
        grad_scores = (probs * (grad_probs - centre)).astype(jnp.bfloat16)
        grad_value[:, lanes] += dot_nn(probs.astype(jnp.bfloat16), grads)
        grad_key[:, lanes] += dot_nn(grad_scores, queries)
        grad_query = own_blocks(dot_nn(key_t[lanes], grad_scores)).astype(jnp.bfloat16)
        grad_ref[0, here, lanes] = (grad_query.astype(jnp.float32) * head_scale).astype(
            jnp.bfloat16
        )

    @pl.when(step == pl.num_programs(0) - 1)
    def _():
        grad_ref[1] = grad_key[...].astype(jnp.bfloat16)
        low_value = grad_value[...].astype(jnp.bfloat16)
        grad_ref[2] = low_value
        sums_ref[0:1] = jnp.sum(grad_ref[0].astype(jnp.float32), axis=0, keepdims=True)
        sums_ref[1:2] = jnp.sum(low_value.astype(jnp.float32), axis=0, keepdims=True)


def attend_back(projected, seg_keys, seg_queries, grad_halves, log_total, old, place, core):
    length = seg_keys.shape[1]
    slab = projected.shape[2]
    blocks = length // LANES
    half = blocks // 2
    grid_spec = pltpu.PrefetchScalarGridSpec(
        num_scalar_prefetch=1,
        grid=(blocks,),
        in_specs=[
            pl.BlockSpec((None, LANES, slab), lambda i, at: (0, at[0] * blocks + i, 0)),
            pl.BlockSpec((None, length, slab), lambda i, at: (1, at[0], 0)),
            pl.BlockSpec((None, length, slab), lambda i, at: (2, at[0], 0)),
            pl.BlockSpec((None, length, LANES), lambda i, at: (at[0], 0, 0)),
            pl.BlockSpec((None, 1, LANES), lambda i, at: (at[0], 0, i)),
            pl.BlockSpec(
                (None, LANES, slab), lambda i, at: (lax.rem(i // half + at[1], 2), lax.rem(i, half), 0)
            ),
            pl.BlockSpec((slab // DH, LANES), lambda i, at: (0, i)),
            pl.BlockSpec(memory_space=pl.ANY),
        ],
        out_specs=[
            pl.BlockSpec((3, length, slab), lambda i, at: (0, at[0], 0)),
            pl.BlockSpec((2, slab), lambda i, at: (0, 0)),
        ],
        scratch_shapes=[
            pltpu.VMEM((slab, length), jnp.bfloat16),
            pltpu.VMEM((length, slab), jnp.float32),
            pltpu.VMEM((length, slab), jnp.float32),
        ],
    )
    return pl.pallas_call(
        attend_back_kernel,
        grid_spec=grid_spec,
        out_shape=[
            jax.ShapeDtypeStruct(projected.shape, jnp.bfloat16),
            jax.ShapeDtypeStruct((2, slab), jnp.float32),
        ],
        input_output_aliases={8: 0},
        compiler_params=pltpu.CompilerParams(vmem_limit_bytes=40 << 20),
        cost_estimate=pl.CostEstimate(
            flops=40 * length * length * slab, bytes_accessed=16 * length * slab,
            transcendentals=length * length * slab // DH,
        ),
        name="attend_back",
    )(jnp.stack([place, core]), projected, projected, projected, seg_keys, seg_queries, grad_halves,
      log_total, old)


def row_mean(values):
    return jnp.mean(values, axis=-1, keepdims=True)


def ffn_kernel(mixed_own, mixed_one, mixed_two, mixed_three, tokens, cotangent, out_own, out_one,
               out_two, out_three, in_own, in_near, in_far, down_own, down_near, down_far,
               bias_ref, vec_ref,
               result_ref, low_out, active_out, branch_out, hidden_out, norm_out, attn_out,
               mixed_out, unit_ref, sums_ref,
               w_out, w_in, w_down, tok, cot, first, normed, inverse, low, slope, active, part,
               other, other_two, acc, wide, branch, hidden, result, grad_h1, attn, mixed,
               load_sem, store_sem, send_sem, recv_sem):
    dp_place = lax.axis_index("dp")
    tensor_place = lax.axis_index("tensor")
    core = lax.rem(tensor_place, 2)
    sibling = (dp_place, tensor_place + 1 - 2 * core)
    side = lax.rem(dp_place, 2)
    share, width = tok.shape
    slab = in_own.shape[1]
    own_rows = pl.ds(pl.multiple_of(tensor_place * share, LANES), share)
    near_rows = pl.ds(pl.multiple_of(side * (width // 2), LANES), width // 2)
    far_rows = pl.ds(pl.multiple_of((1 - side) * (width // 2), LANES), width // 2)
    near_units = pl.ds(pl.multiple_of(slab + side * (slab // 2), LANES), slab // 2)
    far_units = pl.ds(pl.multiple_of(slab + (1 - side) * (slab // 2), LANES), slab // 2)

    loads = [
        (out_own, w_out.at[0]), (out_one, w_out.at[1]), (out_two, w_out.at[2]),
        (out_three, w_out.at[3]), (tokens.at[own_rows], tok),
        (in_own, w_in.at[0]), (in_near, w_in.at[1, near_rows]), (in_far, w_in.at[1, far_rows]),
        (down_own, w_down.at[pl.ds(0, slab)]), (down_near, w_down.at[near_units]),
        (down_far, w_down.at[far_units]), (cotangent.at[own_rows], cot),
    ]
    loads = [
        pltpu.make_async_copy(source, target, load_sem.at[number])
        for number, (source, target) in enumerate(loads)
    ]
    for load in loads:
        load.start()
    stores = []

    def store(source, target):
        copy = pltpu.make_async_copy(source, target, store_sem.at[len(stores)])
        copy.start()
        stores.append(copy)

    def send(number, source, target):
        return pltpu.make_async_remote_copy(
            src_ref=source,
            dst_ref=target,
            send_sem=send_sem.at[number],
            recv_sem=recv_sem.at[number],
            device_id=sibling,
            device_id_type=MESH,
        )

    barrier = pltpu.get_barrier_semaphore()
    pl.semaphore_signal(barrier, inc=1, device_id=sibling, device_id_type=MESH)
    pl.semaphore_wait(barrier, 1)
    sums_ref[...] = jnp.zeros_like(sums_ref)
    unit_ref[...] = jnp.zeros_like(unit_ref)
    pieces = (mixed_own, mixed_one, mixed_two, mixed_three)
    for load in loads[:5]:
        load.wait()
    big = 256
    small = 64

    def attn_rows(step, carry):
        rows = pl.ds(pl.multiple_of(step * big, big), big)
        total = dot_nn(pieces[0][rows], w_out[0])
        for piece in range(1, 4):
            total += dot_nn(pieces[piece][rows], w_out[piece])
        acc[rows] = total
        return carry

    def first_rows(step, carry):
        rows = pl.ds(pl.multiple_of(step * small, small), small)
        values = tok[rows].astype(jnp.float32) + (acc[rows] + vec_ref[0:1])
        centred = values - row_mean(values)
        scale = lax.rsqrt(row_mean(centred * centred) + EPS_NORM)
        unit = centred * scale
        normed[rows] = unit
        inverse[rows] = scale
        shifted = unit * vec_ref[2:3] + vec_ref[3:4]
        first[rows] = shifted
        low[0, rows] = shifted.astype(jnp.bfloat16)
        return carry

    lax.fori_loop(0, share // big, attn_rows, 0)
    lax.fori_loop(0, share // small, first_rows, 0)
    low_send = send(0, low.at[0], low.at[1])
    low_send.start()
    for load in loads[5:8]:
        load.wait()
    chunk = 256
    half_chunks = slab // chunk

    def hidden_of(slot):
        def units(step, carry):
            part_of = step // half_chunks
            inner = pl.ds(pl.multiple_of(lax.rem(step, half_chunks) * chunk, chunk), chunk)
            outer = pl.ds(pl.multiple_of(step * chunk, chunk), chunk)
            values = dot_nn(low[slot], w_in[part_of, :, inner]) + bias_ref[:, outer]
            share_of = 0.5 * (1.0 + lax.erf(values * math.sqrt(0.5)))
            density = jnp.exp(-0.5 * values * values) * (1.0 / math.sqrt(2.0 * math.pi))
            active[slot, :, outer] = (values * share_of).astype(jnp.bfloat16)
            slope[slot, :, outer] = share_of + values * density
            return carry

        lax.fori_loop(0, 2 * half_chunks, units, 0)

    def branch_of(slot, target):
        def columns(step, carry):
            at = pl.ds(pl.multiple_of(step * chunk, chunk), chunk)
            target[:, at] = dot_nn(active[slot], w_down[:, at])
            return carry

        lax.fori_loop(0, width // chunk, columns, 0)

    hidden_of(0)
    low_send.wait_recv()
    hidden_of(1)
    store(low, low_out)
    store(active, active_out)
    for load in loads[8:]:
        load.wait()
    branch_of(1, part)
    part_send = send(1, part, other)
    part_send.start()
    branch_of(0, acc)
    part_send.wait_recv()

    def second_rows(step, carry):
        rows = pl.ds(pl.multiple_of(step * small, small), small)
        values = first[rows] + (acc[rows] + other[rows]) + vec_ref[1:2]
        centred = values - row_mean(values)
        scale = lax.rsqrt(row_mean(centred * centred) + EPS_NORM)
        unit = centred * scale
        result[rows] = (unit * vec_ref[4:5] + vec_ref[5:6]).astype(jnp.bfloat16)
        upper = cot[rows].astype(jnp.float32)
        scaled = upper * vec_ref[4:5]
        grad = scale * (scaled - row_mean(scaled) - unit * row_mean(scaled * unit))
        wide[rows] = grad
        grad_low = grad.astype(jnp.bfloat16)
        branch[0, rows] = grad_low
        sums_ref[1:2] += jnp.sum(grad_low.astype(jnp.float32), axis=0, keepdims=True)
        sums_ref[4:5] += jnp.sum(upper * unit, axis=0, keepdims=True)
        sums_ref[5:6] += jnp.sum(upper, axis=0, keepdims=True)
        return carry

    lax.fori_loop(0, share // small, second_rows, 0)
    branch_send = send(2, branch.at[0], branch.at[1])
    branch_send.start()
    store(result, result_ref)

    def grad_hidden_of(slot):
        def units(step, carry):
            outer = pl.ds(pl.multiple_of(step * chunk, chunk), chunk)
            grad = dot_nt(branch[slot], w_down[outer]) * slope[slot, :, outer]
            grad_low = grad.astype(jnp.bfloat16)
            hidden[slot, :, outer] = grad_low
            unit_ref[:, outer] += jnp.sum(grad_low.astype(jnp.float32), axis=0, keepdims=True)
            return carry

        lax.fori_loop(0, 2 * half_chunks, units, 0)

    def grad_first_of(slot, target):
        def columns(step, carry):
            at = pl.ds(pl.multiple_of(step * chunk, chunk), chunk)
            target[:, at] = dot_nt(hidden[slot, :, :slab], w_in[0, at]) + dot_nt(
                hidden[slot, :, slab:], w_in[1, at]
            )
            return carry

        lax.fori_loop(0, width // chunk, columns, 0)

    grad_hidden_of(0)
    branch_send.wait_recv()
    store(branch, branch_out)
    grad_hidden_of(1)
    store(hidden, hidden_out)
    part_send.wait_send()
    grad_first_of(1, part)
    first_send = send(3, part, other_two)
    first_send.start()
    grad_first_of(0, acc)
    first_send.wait_recv()

    def back_rows(step, carry):
        rows = pl.ds(pl.multiple_of(step * small, small), small)
        grad = acc[rows] + other_two[rows] + wide[rows]
        unit = normed[rows]
        scaled = grad * vec_ref[2:3]
        back = inverse[rows] * (scaled - row_mean(scaled) - unit * row_mean(scaled * unit))
        grad_h1[rows] = back
        back_low = back.astype(jnp.bfloat16)
        attn[rows] = back_low
        sums_ref[0:1] += jnp.sum(back_low.astype(jnp.float32), axis=0, keepdims=True)
        sums_ref[2:3] += jnp.sum(grad * unit, axis=0, keepdims=True)
        sums_ref[3:4] += jnp.sum(grad, axis=0, keepdims=True)
        return carry

    lax.fori_loop(0, share // small, back_rows, 0)
    store(grad_h1, norm_out)
    store(attn, attn_out)

    def mixed_rows(step, carry):
        rows = pl.ds(pl.multiple_of(step * big, big), big)
        for piece in range(4):
            mixed[piece, rows] = dot_nt(attn[rows], w_out[piece]).astype(jnp.bfloat16)
        return carry

    lax.fori_loop(0, share // big, mixed_rows, 0)
    store(mixed, mixed_out)
    low_send.wait_send()
    branch_send.wait_send()
    first_send.wait_send()
    for copy in stores:
        copy.wait()


def ffn(pieces, tokens, cotangent, w_out, w_in, w_down, bias, vectors):
    share, piece_width = pieces[0].shape
    width = tokens.shape[1]
    slab = w_in[0].shape[1]
    units = 2 * slab
    low_type, full_type = jnp.bfloat16, jnp.float32
    vmem = pl.BlockSpec(memory_space=pltpu.VMEM)
    anywhere = pl.BlockSpec(memory_space=pl.ANY)
    shapes = [
        jax.ShapeDtypeStruct((share, width), low_type),
        jax.ShapeDtypeStruct((2, share, width), low_type),
        jax.ShapeDtypeStruct((2, share, units), low_type),
        jax.ShapeDtypeStruct((2, share, width), low_type),
        jax.ShapeDtypeStruct((2, share, units), low_type),
        jax.ShapeDtypeStruct((share, width), full_type),
        jax.ShapeDtypeStruct((share, width), low_type),
        jax.ShapeDtypeStruct((4, share, piece_width), low_type),
        jax.ShapeDtypeStruct((1, units), full_type),
        jax.ShapeDtypeStruct((6, width), full_type),
    ]
    return pl.pallas_call(
        ffn_kernel,
        in_specs=[vmem] * 4 + [anywhere] * 12 + [vmem] * 2,
        out_specs=[anywhere] * 8 + [vmem] * 2,
        out_shape=shapes,
        scratch_shapes=[
            pltpu.VMEM((4, piece_width, width), low_type),
            pltpu.VMEM((2, width, slab), low_type),
            pltpu.VMEM((units, width), low_type),
            pltpu.VMEM((share, width), low_type),
            pltpu.VMEM((share, width), low_type),
            pltpu.VMEM((share, width), full_type),
            pltpu.VMEM((share, width), full_type),
            pltpu.VMEM((share, 1), full_type),
            pltpu.VMEM((2, share, width), low_type),
            pltpu.VMEM((2, share, units), full_type),
            pltpu.VMEM((2, share, units), low_type),
            pltpu.VMEM((share, width), full_type),
            pltpu.VMEM((share, width), full_type),
            pltpu.VMEM((share, width), full_type),
            pltpu.VMEM((share, width), full_type),
            pltpu.VMEM((share, width), full_type),
            pltpu.VMEM((2, share, width), low_type),
            pltpu.VMEM((2, share, units), low_type),
            pltpu.VMEM((share, width), low_type),
            pltpu.VMEM((share, width), full_type),
            pltpu.VMEM((share, width), low_type),
            pltpu.VMEM((4, share, piece_width), low_type),
            pltpu.SemaphoreType.DMA((12,)),
            pltpu.SemaphoreType.DMA((8,)),
            pltpu.SemaphoreType.DMA((4,)),
            pltpu.SemaphoreType.DMA((4,)),
        ],
        compiler_params=pltpu.CompilerParams(
            collective_id=3, has_side_effects=True, vmem_limit_bytes=60 << 20
        ),
        cost_estimate=pl.CostEstimate(
            flops=2 * share * width * (8 * units + 8 * piece_width),
            bytes_accessed=60 * share * width, transcendentals=4 * share * units,
        ),
        name="ffn",
    )(*pieces, tokens, cotangent, *w_out, *w_in, *w_down, bias, vectors)


def layer_general(tokens, segments, w_qkv, head_bias, w_out, w_in, unit_bias, w_down, vectors,
                  cotangent):
    token_count, model_width = tokens.shape
    seq_count, length = segments.shape
    head_slab = w_qkv.shape[2]
    head_count = head_slab // DH
    tensor_size = lax.axis_size("tensor")
    share_rows = token_count // tensor_size
    tensor_place = lax.axis_index("tensor")
    row_start = tensor_place * share_rows
    head_scale = 1.0 / math.sqrt(DH)

    def own_rows(values):
        return lax.dynamic_slice_in_dim(values, row_start, share_rows, 0)

    flat_qkv = w_qkv.reshape(model_width, 3 * head_slab)
    projected = jnp.dot(tokens, flat_qkv, preferred_element_type=jnp.float32).reshape(
        token_count, 3, head_slab
    )
    head_shape = (seq_count, length, head_count, DH)
    queries = (
        ((projected[:, 0] + head_bias[0]) * head_scale).astype(jnp.bfloat16).reshape(head_shape)
    )
    key_heads = projected[:, 1].astype(jnp.bfloat16).reshape(head_shape)
    value_heads = (projected[:, 2] + head_bias[1]).astype(jnp.bfloat16).reshape(head_shape)
    mixed_heads, log_total = lax.map(attend_forward, (queries, key_heads, value_heads, segments))
    mixed_flat = mixed_heads.reshape(token_count, head_slab)
    attn_out = (
        lax.psum(jnp.dot(mixed_flat, w_out, preferred_element_type=jnp.float32), "tensor")
        + vectors[0]
    )
    first_norm, first_normed, first_inverse = norm_forward(
        tokens.astype(jnp.float32) + attn_out, vectors[2], vectors[3]
    )
    first_low = first_norm.astype(jnp.bfloat16)
    hidden = jnp.dot(first_low, w_in, preferred_element_type=jnp.float32) + unit_bias
    active, gelu_back = jax.vjp(partial(jax.nn.gelu, approximate=False), hidden)
    active_low = active.astype(jnp.bfloat16)
    grad_out_share = own_rows(cotangent).astype(jnp.float32)
    summed_input = (
        first_norm
        + lax.psum(jnp.dot(active_low, w_down, preferred_element_type=jnp.float32), "tensor")
        + vectors[1]
    )
    second_norm, second_normed, second_inverse = norm_forward(summed_input, vectors[4], vectors[5])
    layer_out = own_rows(second_norm).astype(jnp.bfloat16)
    grad_sum = norm_backward(
        cotangent.astype(jnp.float32), second_normed, second_inverse, vectors[4]
    )
    grad_branch = grad_sum.astype(jnp.bfloat16)
    second_share = own_rows(second_normed)
    grad_w_down = trans_times(active_low, grad_branch)
    grad_active = times_trans(grad_branch, w_down)
    grad_hidden = gelu_back(grad_active)[0].astype(jnp.bfloat16)
    grad_w_in = trans_times(first_low, grad_hidden)
    grad_units = jnp.sum(grad_hidden.astype(jnp.float32), axis=0)
    grad_first = lax.psum(times_trans(grad_hidden, w_in), "tensor") + grad_sum
    grad_h1 = norm_backward(grad_first, first_normed, first_inverse, vectors[2])
    grad_attn = grad_h1.astype(jnp.bfloat16)
    grad_first_share = own_rows(grad_first)
    first_normed_share = own_rows(first_normed)
    grad_h1_share = own_rows(grad_h1)
    grad_w_out = trans_times(mixed_flat, grad_attn)
    grad_mixed = times_trans(grad_attn, w_out).astype(jnp.bfloat16).reshape(head_shape)
    grad_query, grad_key, grad_value = lax.map(
        attend_backward, (queries, key_heads, value_heads, segments, grad_mixed, log_total)
    )
    grad_query = (
        grad_query.reshape(token_count, head_slab).astype(jnp.float32) * head_scale
    ).astype(jnp.bfloat16)
    grad_key = grad_key.reshape(token_count, head_slab)
    grad_value = grad_value.reshape(token_count, head_slab)
    grad_projected = jnp.stack([grad_query, grad_key, grad_value], axis=1).reshape(
        token_count, 3 * head_slab
    )
    grad_w_qkv = trans_times(tokens, grad_projected)
    grad_heads = jnp.stack(
        [
            jnp.sum(grad_query.astype(jnp.float32), axis=0),
            jnp.sum(grad_value.astype(jnp.float32), axis=0),
        ]
    )
    grad_tokens = (
        lax.psum_scatter(
            times_trans(grad_projected, flat_qkv).astype(jnp.bfloat16),
            "tensor",
            scatter_dimension=0,
            tiled=True,
        ).astype(jnp.float32)
        + grad_h1_share
    )
    local_vectors = jnp.stack(
        [
            jnp.sum(own_rows(grad_attn).astype(jnp.float32), axis=0),
            jnp.sum(own_rows(grad_branch).astype(jnp.float32), axis=0),
            jnp.sum(grad_first_share * first_normed_share, axis=0),
            jnp.sum(grad_first_share, axis=0),
            jnp.sum(grad_out_share * second_share, axis=0),
            jnp.sum(grad_out_share, axis=0),
        ]
    )
    return (
        layer_out,
        grad_tokens,
        (
            grad_w_qkv.reshape(model_width, 3, head_slab).transpose(1, 0, 2),
            grad_w_out,
            grad_w_in,
            grad_w_down,
        ),
        local_vectors,
        grad_heads,
        grad_units,
    )


def layer_split(tokens, segments, w_qkv, head_bias, w_out, w_in, unit_bias, w_down, vectors,
                cotangent):
    token_count, model_width = tokens.shape
    seq_count, length = segments.shape
    head_slab = w_qkv.shape[2]
    unit_slab = w_in.shape[1]
    tensor_size = lax.axis_size("tensor")
    replicas = lax.axis_size("dp")
    share = token_count // tensor_size
    tensor_place = lax.axis_index("tensor")
    core = lax.rem(tensor_place, 2)
    seq = tensor_place // 2
    side = lax.rem(lax.axis_index("dp"), 2)
    head_scale = 1.0 / math.sqrt(DH)

    def to(values, step):
        return lax.ppermute(
            values, "tensor", [(place, place ^ step) for place in range(tensor_size)]
        )

    def across(values):
        return lax.ppermute(values, "dp", [(place, place ^ 1) for place in range(replicas)])

    def rows_at(values, number, size):
        return lax.dynamic_slice_in_dim(values, number * size, size, 0)

    in_near = to(rows_at(w_in, side, model_width // 2), 2)
    out_two = to(w_out, 2)
    down_near = to(rows_at(w_down, side, unit_slab // 2), 2)
    in_far = across(in_near)
    down_far = across(down_near)
    bias_two = to(unit_bias, 2)
    out_one, out_three = to(jnp.stack([w_out, out_two]), 1)

    planes = w_qkv.transpose(1, 0, 2)
    shift = jnp.stack([head_bias[0], jnp.zeros_like(head_bias[0]), head_bias[1]])
    scale = jnp.array([head_scale, 1.0, 1.0], jnp.float32)
    projected = jnp.einsum("td,gdn->gtn", tokens, planes, preferred_element_type=jnp.float32)
    projected = ((projected + shift[:, None]) * scale[:, None, None]).astype(jnp.bfloat16)
    seg_keys = jnp.broadcast_to(segments[:, :, None], (seq_count, length, LANES))
    seg_queries = segments[:, None, :]
    mixed_far, log_far = attend(projected, seg_keys, seg_queries, 1 - seq)
    piece_two = to(rows_at(mixed_far, core, share), 2)
    piece_three = to(rows_at(mixed_far, 1 - core, share), 3)
    mixed_near, log_near = attend(projected, seg_keys, seg_queries, seq)
    piece_one = to(rows_at(mixed_near, 1 - core, share), 1)
    pieces = (rows_at(mixed_near, core, share), piece_one, piece_two, piece_three)

    (layer_out, low, active, grad_branch, grad_hidden, grad_h1, grad_attn, grad_mixed, units, sums
     ) = ffn(
        pieces,
        tokens,
        cotangent,
        (w_out, out_one, out_two, out_three),
        (w_in, in_near, in_far),
        (w_down, down_near, down_far),
        jnp.concatenate([unit_bias, bias_two])[None],
        vectors,
    )
    low = low.reshape(2 * share, model_width)
    active = active.reshape(2 * share, 2 * unit_slab)
    grad_branch = grad_branch.reshape(2 * share, model_width)
    grad_hidden = grad_hidden.reshape(2 * share, 2 * unit_slab)
    mixed_one = to(grad_mixed[1], 1)
    mixed_two = to(grad_mixed[2], 2)
    mixed_three = to(grad_mixed[3], 3)
    down_two = to(trans_times(active[:, unit_slab:], grad_branch).astype(jnp.bfloat16), 2)
    in_two = to(trans_times(low, grad_hidden[:, unit_slab:]).astype(jnp.bfloat16), 2)
    outs = [trans_times(piece, grad_attn) for piece in pieces]
    back_one, back_three = to(jnp.stack([outs[1], outs[3]]), 1)
    out_back = to((outs[2] + back_three).astype(jnp.bfloat16), 2)
    unit_two = to(units[0, unit_slab:], 2)

    grad_projected = jnp.zeros_like(projected)
    grad_projected, heads_near = attend_back(
        projected, seg_keys, seg_queries, jnp.stack([grad_mixed[0], mixed_one]), log_near,
        grad_projected, seq, core,
    )
    grad_projected, heads_far = attend_back(
        projected, seg_keys, seg_queries, jnp.stack([mixed_two, mixed_three]), log_far,
        grad_projected, 1 - seq, core,
    )
    token_part = jnp.einsum(
        "gtn,gdn->td", grad_projected, planes, preferred_element_type=jnp.float32
    ).astype(jnp.bfloat16)
    other_one = to(
        jnp.stack([rows_at(token_part, 2 * at + 1 - core, share) for at in (seq, 1 - seq)]), 1
    ).astype(jnp.float32)
    across_part = rows_at(token_part, 2 * (1 - seq) + core, share).astype(jnp.float32)
    from_two = to((across_part + other_one[1]).astype(jnp.bfloat16), 2)
    grad_tokens = (
        rows_at(token_part, 2 * seq + core, share).astype(jnp.float32)
        + other_one[0]
        + from_two.astype(jnp.float32)
        + grad_h1
    )
    grad_w_qkv = jnp.einsum(
        "td,gtn->gdn", tokens, grad_projected, preferred_element_type=jnp.float32
    )
    grad_w_down = trans_times(active[:, :unit_slab], grad_branch) + down_two.astype(jnp.float32)
    grad_w_in = trans_times(low, grad_hidden[:, :unit_slab]) + in_two.astype(jnp.float32)
    grad_w_out = outs[0] + back_one + out_back.astype(jnp.float32)
    return (
        layer_out,
        grad_tokens,
        (grad_w_qkv, grad_w_out, grad_w_in, grad_w_down),
        sums,
        heads_near + heads_far,
        units[0, :unit_slab] + unit_two,
    )


def local(
    tokens,
    segments,
    w_qkv,
    head_bias,
    w_out,
    w_in,
    unit_bias,
    w_down,
    vectors,
    cotangent,
    err_qkv,
    err_out,
    err_in,
    err_down,
    basis_qkv,
    basis_out,
    basis_in,
    basis_down,
    mom_qkv,
    mom_head_bias,
    mom_out,
    mom_in,
    mom_unit_bias,
    mom_down,
    mom_vectors,
):
    token_count, model_width = tokens.shape
    head_slab = w_qkv.shape[2]
    unit_slab = w_in.shape[1]
    tensor_size = lax.axis_size("tensor")
    replicas = lax.axis_size("dp")
    one_sequence_per_chip = 2 * segments.shape[0] == tensor_size and replicas % 2 == 0
    layer = layer_split if one_sequence_per_chip else layer_general
    layer_out, grad_tokens, grads, local_vectors, grad_heads, grad_units = layer(
        tokens, segments, w_qkv, head_bias, w_out, w_in, unit_bias, w_down, vectors, cotangent
    )
    grad_w_qkv, grad_w_out, grad_w_in, grad_w_down = grads
    small = jnp.concatenate(
        [
            local_vectors,
            jnp.pad(grad_units, (0, model_width - unit_slab))[None],
            jnp.pad(grad_heads.reshape(1, 2 * head_slab), ((0, 0), (0, model_width - 2 * head_slab))),
        ],
        axis=0,
    )
    planes = (1, 0, 2)
    combined_qkv = grad_w_qkv + err_qkv[0].transpose(planes)
    combined_out = grad_w_out + err_out[0]
    combined_in = grad_w_in + err_in[0]
    combined_down = grad_w_down + err_down[0]
    matrices = (combined_qkv, combined_out, combined_in, combined_down)
    lefts = lefts_of(matrices, (basis_qkv.transpose(planes), basis_out, basis_in, basis_down))
    *bases, small_sum = bases_of(lefts, small, replicas, tensor_size)
    rights = right_sums(rights_of(matrices, bases), replicas)
    step_rate = 0.3 * math.sqrt(replicas / token_count)
    grads, errors, moments, news = update(
        matrices,
        (mom_qkv.transpose(planes), mom_out, mom_in, mom_down),
        (w_qkv.transpose(planes), w_out, w_in, w_down),
        bases,
        rights,
        step_rate,
    )
    reduced_qkv, rank_out, rank_in, rank_down = (grads[0].transpose(planes),) + tuple(grads[1:])
    new_err_qkv, new_err_out, new_err_in, new_err_down = (
        errors[0].transpose(planes)[None],
        errors[1][None],
        errors[2][None],
        errors[3][None],
    )
    new_mom_qkv, new_mom_out, new_mom_in, new_mom_down = (moments[0].transpose(planes),) + tuple(
        moments[1:]
    )
    new_w_qkv, new_w_out, new_w_in, new_w_down = (news[0].transpose(planes),) + tuple(news[1:])
    right_qkv, right_out, right_in, right_down = rights
    new_basis_qkv = right_qkv.transpose(planes)
    grad_vectors = small_sum[:6]
    grad_unit_bias = small_sum[6, :unit_slab]
    grad_head_bias = small_sum[7, : 2 * head_slab].reshape(2, head_slab)
    new_mom_head_bias = 0.9 * mom_head_bias + grad_head_bias
    new_mom_unit_bias = 0.9 * mom_unit_bias + grad_unit_bias
    new_mom_vectors = 0.9 * mom_vectors + grad_vectors
    new_head_bias = head_bias - step_rate * new_mom_head_bias
    new_unit_bias = unit_bias - step_rate * new_mom_unit_bias
    new_vectors = vectors - step_rate * new_mom_vectors
    return (
        layer_out,
        grad_tokens,
        reduced_qkv,
        grad_head_bias,
        rank_out,
        rank_in,
        grad_unit_bias,
        rank_down,
        grad_vectors,
        new_err_qkv,
        new_err_out,
        new_err_in,
        new_err_down,
        new_basis_qkv,
        right_out,
        right_in,
        right_down,
        new_mom_qkv,
        new_mom_head_bias,
        new_mom_out,
        new_mom_in,
        new_mom_unit_bias,
        new_mom_down,
        new_mom_vectors,
        new_w_qkv,
        new_head_bias,
        new_w_out,
        new_w_in,
        new_unit_bias,
        new_w_down,
        new_vectors,
    )


def solution(mesh):
    in_specs = (
        P("dp", None),
        P("dp", None),
        P(None, None, "tensor"),
        P(None, "tensor"),
        P("tensor", None),
        P(None, "tensor"),
        P("tensor"),
        P("tensor", None),
        P(),
        P("dp", None),
        P("dp", None, None, "tensor"),
        P("dp", "tensor", None),
        P("dp", None, "tensor"),
        P("dp", "tensor", None),
        P(None, None, "tensor"),
        P("tensor", None),
        P(None, "tensor"),
        P("tensor", None),
        P(None, None, "tensor"),
        P(None, "tensor"),
        P("tensor", None),
        P(None, "tensor"),
        P("tensor"),
        P("tensor", None),
        P(),
    )
    out_specs = (
        P(("dp", "tensor"), None),
        P(("dp", "tensor"), None),
        P(None, None, "tensor"),
        P(None, "tensor"),
        P("tensor", None),
        P(None, "tensor"),
        P("tensor"),
        P("tensor", None),
        P(),
        P("dp", None, None, "tensor"),
        P("dp", "tensor", None),
        P("dp", None, "tensor"),
        P("dp", "tensor", None),
        P(None, None, "tensor"),
        P("tensor", None),
        P(None, "tensor"),
        P("tensor", None),
        P(None, None, "tensor"),
        P(None, "tensor"),
        P("tensor", None),
        P(None, "tensor"),
        P("tensor"),
        P("tensor", None),
        P(),
        P(None, None, "tensor"),
        P(None, "tensor"),
        P("tensor", None),
        P(None, "tensor"),
        P("tensor"),
        P("tensor", None),
        P(),
    )
    return jax.shard_map(local, mesh=mesh, in_specs=in_specs, out_specs=out_specs, check_vma=False)
```

```python
from functools import partial
import math

import jax
import jax.numpy as jnp
from jax import lax
from jax.experimental import pallas as pl
from jax.experimental.pallas import tpu as pltpu
from jax.sharding import PartitionSpec as P

DH = 64
LANES = 128
MESH = pl.DeviceIdType.MESH
VMEM_GRANT = 60 << 20


PRECISE = lax.Precision.HIGHEST
EPS_NORM = 1e-05
EPS_BASIS = 1e-08
MASKED = -1000000000.0


def norm_forward(values, gain, shift):
    row_mean = jnp.mean(values, axis=-1, keepdims=True)
    centred = values - row_mean
    variance = jnp.mean(centred * centred, axis=-1, keepdims=True)
    inverse = lax.rsqrt(variance + EPS_NORM)
    normed = centred * inverse
    return (normed * gain + shift, normed, inverse)


def norm_backward(grad_norm, normed, inverse, gain):
    scaled_grad = grad_norm * gain
    grad_mean = jnp.mean(scaled_grad, axis=-1, keepdims=True)
    along_norm = jnp.mean(scaled_grad * normed, axis=-1, keepdims=True)
    return inverse * (scaled_grad - grad_mean - normed * along_norm)


def times_trans(left_side, right_side):
    return lax.dot_general(
        left_side, right_side, (((1,), (1,)), ((), ())), preferred_element_type=jnp.float32
    )


def trans_times(left_side, right_side):
    return lax.dot_general(
        left_side, right_side, (((0,), (0,)), ((), ())), preferred_element_type=jnp.float32
    )


def split_bf16(values):
    high = values.astype(jnp.bfloat16)
    low = (values - high.astype(jnp.float32)).astype(jnp.bfloat16)
    return high, low


def dot_nt(left_side, right_side):
    return lax.dot_general(
        left_side, right_side, (((1,), (1,)), ((), ())), preferred_element_type=jnp.float32
    )


def dot_nn(left_side, right_side):
    return lax.dot_general(
        left_side, right_side, (((1,), (0,)), ((), ())), preferred_element_type=jnp.float32
    )


def dot_tn(left_side, right_side):
    return lax.dot_general(
        left_side, right_side, (((0,), (0,)), ((), ())), preferred_element_type=jnp.float32
    )


def left_factor(factor, matrix):
    rank_size = factor.shape[0]
    factor_high, factor_low = split_bf16(factor)
    matrix_high, matrix_low = split_bf16(matrix)
    both = dot_nt(jnp.concatenate([factor_high, factor_low], axis=0), matrix_high)
    return both[:rank_size] + both[rank_size:] + dot_nt(factor_high, matrix_low)


def right_factor(basis_rows, matrix):
    rank_size = basis_rows.shape[0]
    basis_high, basis_low = split_bf16(basis_rows)
    matrix_high, matrix_low = split_bf16(matrix)
    both = dot_nn(jnp.concatenate([basis_high, basis_low], axis=0), matrix_high)
    return both[:rank_size] + both[rank_size:] + dot_nn(basis_high, matrix_low)


def place_tiles(target, offset, values):
    per_chunk = target.shape[2] // LANES
    for tile in range(values.shape[1] // LANES):
        spot = offset + tile
        target[spot // per_chunk, :, pl.ds(spot % per_chunk * LANES, LANES)] = values[
            :, tile * LANES : (tile + 1) * LANES
        ]
    return offset + values.shape[1] // LANES


def take_tiles(source, offset, size):
    per_chunk = source.shape[2] // LANES
    pieces = []
    for tile in range(size // LANES):
        spot = offset + tile
        pieces.append(source[spot // per_chunk, :, pl.ds(spot % per_chunk * LANES, LANES)])
    return jnp.concatenate(pieces, axis=1) if len(pieces) > 1 else pieces[0]


def orthonormal_rows(rows):
    rank_size = rows.shape[0]
    row_number = lax.broadcasted_iota(jnp.int32, (rank_size, 1), 0)
    for position in range(rank_size):
        row = rows[position : position + 1]
        length = jnp.sqrt(jnp.sum(row * row, axis=1, keepdims=True)) + EPS_BASIS
        unit = row / length
        along = jnp.sum(rows * unit, axis=1, keepdims=True)
        later = jnp.where(row_number > position, along, 0.0)
        rows = jnp.where(row_number == position, unit, rows - later * unit)
    return rows


def dp_exchange(replicas, mine, wire, arrived, total, sems, meanwhile=None):
    send_one, recv_one, send_two, recv_two = sems
    dp_place = lax.axis_index("dp")
    tensor_place = lax.axis_index("tensor")

    def peer_of(step):
        return lax.rem(dp_place + step, replicas)

    def scatter(step, slot):
        return pltpu.make_async_remote_copy(
            src_ref=wire.at[peer_of(step)],
            dst_ref=arrived.at[slot],
            send_sem=send_one.at[step],
            recv_sem=recv_one.at[slot],
            device_id=(peer_of(step), tensor_place),
            device_id_type=MESH,
        )

    def gather(step, slot):
        return pltpu.make_async_remote_copy(
            src_ref=total.at[dp_place],
            dst_ref=total.at[slot],
            send_sem=send_two.at[step],
            recv_sem=recv_two.at[slot],
            device_id=(peer_of(step), tensor_place),
            device_id_type=MESH,
        )

    def start_scatter(step, carry):
        scatter(step, dp_place).start()
        return carry

    def add_arrived(step, carry):
        scatter(step, peer_of(step)).wait_recv()
        return carry + arrived[peer_of(step)].astype(jnp.float32)

    def start_gather(step, carry):
        gather(step, dp_place).start()
        return carry

    def finish(step, carry):
        gather(step, peer_of(step)).wait_recv()
        return carry

    wire[...] = mine[...].astype(wire.dtype)
    lax.fori_loop(1, replicas, start_scatter, 0)
    total[dp_place] = lax.fori_loop(1, replicas, add_arrived, mine[dp_place])
    lax.fori_loop(1, replicas, start_gather, 0)
    lax.fori_loop(1, replicas, finish, 0)

    def drain(step, carry):
        scatter(step, dp_place).wait_send()
        gather(step, dp_place).wait_send()
        return carry

    return lambda: lax.fori_loop(1, replicas, drain, 0)


def compress_kernel(replicas, tensor_size, qkv_ref, out_ref, in_ref, down_ref,
                    fq_ref, fo_ref, fi_ref, fd_ref, small_ref,
                    bq_ref, bo_ref, bi_ref, bd_ref, rq_ref, ro_ref, ri_ref, rd_ref, sum_ref,
                    qkv, out, inw, down, mine, wire, arrived, total,
                    mine_two, wire_two, arrived_two, total_two, small_slots,
                    load_sem, *sems):
    first_sems, second_sems, (send_small, recv_small) = sems[:4], sems[4:8], sems[8:]
    dp_place = lax.axis_index("dp")
    tensor_place = lax.axis_index("tensor")
    loads = [
        pltpu.make_async_copy(source, target, load_sem.at[number])
        for number, (source, target) in enumerate(
            [(qkv_ref, qkv), (out_ref, out), (down_ref, down), (in_ref, inw)]
        )
    ]
    for load in loads:
        load.start()
    barrier = pltpu.get_barrier_semaphore()

    def greet_dp(step, carry):
        pl.semaphore_signal(
            barrier,
            inc=1,
            device_id=(lax.rem(dp_place + step, replicas), tensor_place),
            device_id_type=MESH,
        )
        return carry

    def greet_tensor(step, carry):
        pl.semaphore_signal(
            barrier,
            inc=1,
            device_id=(dp_place, lax.rem(tensor_place + step, tensor_size)),
            device_id_type=MESH,
        )
        return carry

    lax.fori_loop(1, replicas, greet_dp, 0)
    lax.fori_loop(1, tensor_size, greet_tensor, 0)
    mine[...] = jnp.zeros_like(mine)
    mine_two[...] = jnp.zeros_like(mine_two)
    block = 2 * LANES
    offset = 0
    loads[0].wait()
    for start in range(0, qkv.shape[1], block):
        rows = slice(start, start + block)
        left = left_factor(fq_ref[0], qkv[0, rows])
        for part in range(1, 3):
            left += left_factor(fq_ref[part], qkv[part, rows])
        offset = place_tiles(mine, offset, left)
    for load, factor_ref, matrix in zip(loads[1:], (fo_ref, fd_ref, fi_ref), (out, down, inw)):
        load.wait()
        rows_of = min(block, matrix.shape[0])
        for start in range(0, matrix.shape[0], rows_of):
            left = left_factor(factor_ref[...], matrix[start : start + rows_of])
            offset = place_tiles(mine, offset, left)
    place_tiles(mine, offset, small_ref[...])
    pl.semaphore_wait(barrier, replicas - 1 + tensor_size - 1)
    drain_one = dp_exchange(replicas, mine, wire, arrived, total, first_sems)

    def slot_copy(step, slot):
        peer = lax.rem(tensor_place + step, tensor_size)
        return pltpu.make_async_remote_copy(
            src_ref=small_slots.at[tensor_place],
            dst_ref=small_slots.at[slot],
            send_sem=send_small.at[step],
            recv_sem=recv_small.at[slot],
            device_id=(dp_place, peer),
            device_id_type=MESH,
        )

    def start_small(step, carry):
        slot_copy(step, tensor_place).start()
        return carry

    own_small = take_tiles(total, offset, small_ref.shape[1])
    small_slots[tensor_place] = own_small
    lax.fori_loop(1, tensor_size, start_small, 0)
    offset = 0
    offset_two = 0
    for basis_ref in (bq_ref, bo_ref, bd_ref, bi_ref):
        rows = take_tiles(total, offset, basis_ref.shape[1]) * (1.0 / replicas)
        basis_ref[...] = orthonormal_rows(rows)
        offset += basis_ref.shape[1] // LANES
    drain_one()
    for part in range(3):
        right = right_factor(bq_ref[:, :block], qkv[part, :block])
        for start in range(block, qkv.shape[1], block):
            rows = slice(start, start + block)
            right += right_factor(bq_ref[:, rows], qkv[part, rows])
        offset_two = place_tiles(mine_two, offset_two, right)
    for basis_ref, matrix in zip((bo_ref, bd_ref, bi_ref), (out, down, inw)):
        rows_of = min(block, matrix.shape[0])
        right = right_factor(basis_ref[:, :rows_of], matrix[:rows_of])
        for start in range(rows_of, matrix.shape[0], rows_of):
            rows = slice(start, start + rows_of)
            right += right_factor(basis_ref[:, rows], matrix[rows])
        offset_two = place_tiles(mine_two, offset_two, right)
    drain_two = dp_exchange(
        replicas, mine_two, wire_two, arrived_two, total_two, second_sems
    )

    def collect(step, carry):
        peer = lax.rem(tensor_place + step, tensor_size)
        slot_copy(step, peer).wait_recv()
        slot_copy(step, tensor_place).wait_send()
        return carry + small_slots[peer]

    everyone = lax.fori_loop(1, tensor_size, collect, own_small)
    row_number = lax.broadcasted_iota(jnp.int32, everyone.shape, 0)
    sum_ref[...] = jnp.where(row_number < 6, everyone, own_small) * (1.0 / replicas)
    offset = 0
    for part in range(3):
        rq_ref[part] = take_tiles(total_two, offset, rq_ref.shape[2]) * (1.0 / replicas)
        offset += rq_ref.shape[2] // LANES
    for ref in (ro_ref, rd_ref, ri_ref):
        ref[...] = take_tiles(total_two, offset, ref.shape[1]) * (1.0 / replicas)
        offset += ref.shape[1] // LANES
    drain_two()


def compress(matrices, factors, small, replicas, tensor_size):
    qkv, out, inw, down = matrices
    rank_size = small.shape[0]
    sizes = (qkv.shape[1], out.shape[0], inw.shape[0], down.shape[0])
    right_shapes = [(3, rank_size, qkv.shape[2])] + [(rank_size, one.shape[1]) for one in matrices[1:]]
    lanes_one = sum(sizes) + small.shape[1]
    lanes_two = 3 * qkv.shape[2] + sum(one.shape[1] for one in matrices[1:])
    scratch = [pltpu.VMEM(one.shape, jnp.float32) for one in matrices]
    for lanes in (lanes_one, lanes_two):
        shape = (replicas, rank_size, -(-lanes // (LANES * replicas)) * LANES)
        scratch += [
            pltpu.VMEM(shape, jnp.float32),
            pltpu.VMEM(shape, jnp.bfloat16),
            pltpu.VMEM(shape, jnp.bfloat16),
            pltpu.VMEM(shape, jnp.float32),
        ]
    scratch += [pltpu.VMEM((tensor_size,) + small.shape, jnp.float32), pltpu.SemaphoreType.DMA((4,))]
    scratch += [pltpu.SemaphoreType.DMA((replicas,))] * 8
    scratch += [pltpu.SemaphoreType.DMA((tensor_size,))] * 2
    vmem = pl.BlockSpec(memory_space=pltpu.VMEM)
    shapes = [(rank_size, size) for size in sizes] + right_shapes + [small.shape]
    outputs = pl.pallas_call(
        partial(compress_kernel, replicas, tensor_size),
        in_specs=[pl.BlockSpec(memory_space=pl.ANY)] * 4 + [vmem] * 5,
        out_specs=[vmem] * 9,
        out_shape=[jax.ShapeDtypeStruct(shape, jnp.float32) for shape in shapes],
        scratch_shapes=scratch,
        compiler_params=pltpu.CompilerParams(
            collective_id=1, has_side_effects=True, vmem_limit_bytes=VMEM_GRANT
        ),
        name="compress",
    )(*matrices, *factors, small)
    return outputs[:4], outputs[4:8], outputs[8]


def outer_of(basis_rows, right):
    basis_high, basis_low = split_bf16(basis_rows)
    right_high, right_low = split_bf16(right)
    return dot_tn(
        jnp.concatenate([basis_high, basis_low, basis_high], axis=0),
        jnp.concatenate([right_high, right_high, right_low], axis=0),
    )


def update_kernel(step_rate, out_steps, *refs):
    (mq, mo, mi, md, oq, oo, oi, od, wq, wo, wi, wd, bq, bo, bi, bd, rq, ro, ri, rd,
     gq, go, gi, gd, eq, eo, ei, ed, nq, no, ni, nd, vq, vo, vi, vd) = refs
    step = pl.program_id(0)

    def one(matrix, old, weight, rank, grad_ref, err_ref, mom_ref, new_ref, place):
        moment = 0.9 * old + rank
        grad_ref[place] = rank
        err_ref[place] = matrix - rank
        mom_ref[place] = moment
        new_ref[place] = weight.astype(jnp.float32) - step_rate * moment

    def lanes_of(ref, rows):
        return ref[:, pl.ds(pl.multiple_of(step * rows, LANES), rows)]

    rows = mq.shape[1]
    for part in range(3):
        rank = outer_of(lanes_of(bq, rows), rq[part])
        one(mq[part], oq[part], wq[part], rank, gq, eq, nq, vq, part)
    rank = outer_of(lanes_of(bi, mi.shape[0]), ri[...])
    one(mi[...], oi[...], wi[...], rank, gi, ei, ni, vi, slice(None))
    rank = outer_of(lanes_of(bd, md.shape[0]), rd[...])
    one(md[...], od[...], wd[...], rank, gd, ed, nd, vd, slice(None))

    @pl.when(step < out_steps)
    def _():
        rank = outer_of(lanes_of(bo, mo.shape[0]), ro[...])
        one(mo[...], oo[...], wo[...], rank, go, eo, no, vo, slice(None))


def update(matrices, momenta, weights, bases, rights, step_rate):
    qkv, out, inw, down = matrices
    rows = LANES
    steps = inw.shape[0] // rows
    down_rows = down.shape[0] // steps
    if down_rows < LANES:
        steps = down.shape[0] // LANES
        rows, down_rows = inw.shape[0] // steps, LANES
    out_steps = out.shape[0] // LANES

    def whole(array):
        return pl.BlockSpec(array.shape, lambda i: (0,) * array.ndim)

    def specs():
        return [
            pl.BlockSpec((3, rows, qkv.shape[2]), lambda i: (0, i, 0)),
            pl.BlockSpec((LANES, out.shape[1]), lambda i: (jnp.minimum(i, out_steps - 1), 0)),
            pl.BlockSpec((rows, inw.shape[1]), lambda i: (i, 0)),
            pl.BlockSpec((down_rows, down.shape[1]), lambda i: (i, 0)),
        ]

    shapes = [jax.ShapeDtypeStruct(one.shape, jnp.float32) for one in matrices]
    outputs = pl.pallas_call(
        partial(update_kernel, step_rate, out_steps),
        grid=(steps,),
        in_specs=specs() * 3 + [whole(one) for one in bases] + [whole(one) for one in rights],
        out_specs=specs() * 4,
        out_shape=shapes * 4,
        compiler_params=pltpu.CompilerParams(vmem_limit_bytes=VMEM_GRANT),
        name="update",
    )(*matrices, *momenta, *weights, *bases, *rights)
    return outputs[0:4], outputs[4:8], outputs[8:12], outputs[12:16]


def masked_scores(queries, key_heads, seg_ids):
    scores = jnp.einsum("qhd,khd->hqk", queries, key_heads, preferred_element_type=jnp.float32)
    same_doc = seg_ids[:, None] == seg_ids[None, :]
    return jnp.where(same_doc[None], scores, MASKED)


def attend_forward(inputs_of):
    queries, key_heads, value_heads, seg_ids = inputs_of
    scores = masked_scores(queries, key_heads, seg_ids)
    highest = jnp.max(scores, axis=-1, keepdims=True)
    powers = jnp.exp(scores - highest)
    denominator = jnp.sum(powers, axis=-1, keepdims=True)
    weights = (powers / denominator).astype(jnp.bfloat16)
    mixed_heads = jnp.einsum(
        "hqk,khd->qhd", weights, value_heads, preferred_element_type=jnp.float32
    )
    return (mixed_heads.astype(jnp.bfloat16), highest[..., 0] + jnp.log(denominator[..., 0]))


def attend_backward(inputs_of):
    queries, key_heads, value_heads, seg_ids, grad_mixed, log_total = inputs_of
    scores = masked_scores(queries, key_heads, seg_ids)
    probability = jnp.exp(scores - log_total[..., None])
    grad_probs = jnp.einsum(
        "qhd,khd->hqk", grad_mixed, value_heads, preferred_element_type=jnp.float32
    )
    centre = jnp.sum(probability * grad_probs, axis=-1, keepdims=True)
    grad_scores = (probability * (grad_probs - centre)).astype(jnp.bfloat16)
    grad_query = jnp.einsum(
        "hqk,khd->qhd", grad_scores, key_heads, preferred_element_type=jnp.float32
    )
    grad_key = jnp.einsum("hqk,qhd->khd", grad_scores, queries, preferred_element_type=jnp.float32)
    grad_value = jnp.einsum(
        "hqk,qhd->khd",
        probability.astype(jnp.bfloat16),
        grad_mixed,
        preferred_element_type=jnp.float32,
    )
    return (
        grad_query.astype(jnp.bfloat16),
        grad_key.astype(jnp.bfloat16),
        grad_value.astype(jnp.bfloat16),
    )


def stacked_heads(pair, lane_is_low):
    zero = jnp.zeros_like(pair)
    return jnp.concatenate(
        [jnp.where(lane_is_low, pair, zero), jnp.where(lane_is_low, zero, pair)], axis=0
    )


def own_blocks(both):
    rows = both.shape[1] // 2
    return jnp.concatenate([both[:DH, :rows], both[DH:, rows:]], axis=0).T


def mask_bias(seg_key_ref, seg_query_ref):
    same = seg_key_ref[...] == seg_query_ref[...]
    bias = jnp.where(same, 0.0, MASKED)
    return jnp.concatenate([bias, bias], axis=1)


def attend_kernel(place_ref, q_ref, k_ref, v_ref, seg_key_ref, seg_query_ref, mixed_ref, log_ref,
                  value_t):
    @pl.when(pl.program_id(0) == 0)
    def _():
        value_t[...] = v_ref[...].T

    pairs = q_ref.shape[1] // LANES
    lane_is_low = lax.broadcasted_iota(jnp.int32, (1, LANES), 1) < DH
    bias = mask_bias(seg_key_ref, seg_query_ref)
    for pair in range(pairs):
        lanes = slice(pair * LANES, (pair + 1) * LANES)
        queries = stacked_heads(q_ref[:, lanes], lane_is_low)
        scores = dot_nt(k_ref[:, lanes], queries) + bias
        highest = jnp.max(scores, axis=0, keepdims=True)
        powers = jnp.exp(scores - highest)
        denominator = jnp.sum(powers, axis=0, keepdims=True)
        weights = (powers * (1.0 / denominator)).astype(jnp.bfloat16)
        mixed_ref[:, lanes] = own_blocks(dot_nn(value_t[lanes], weights)).astype(jnp.bfloat16)
        log_total = highest + jnp.log(denominator)
        log_ref[2 * pair : 2 * pair + 1] = log_total[:, :LANES]
        log_ref[2 * pair + 1 : 2 * pair + 2] = log_total[:, LANES:]


def attend(projected, seg_keys, seg_queries, place):
    length = seg_keys.shape[1]
    slab = projected.shape[2]
    blocks = length // LANES
    grid_spec = pltpu.PrefetchScalarGridSpec(
        num_scalar_prefetch=1,
        grid=(blocks,),
        in_specs=[
            pl.BlockSpec((None, LANES, slab), lambda i, at: (0, at[0] * blocks + i, 0)),
            pl.BlockSpec((None, length, slab), lambda i, at: (1, at[0], 0)),
            pl.BlockSpec((None, length, slab), lambda i, at: (2, at[0], 0)),
            pl.BlockSpec((None, length, LANES), lambda i, at: (at[0], 0, 0)),
            pl.BlockSpec((None, 1, LANES), lambda i, at: (at[0], 0, i)),
        ],
        out_specs=[
            pl.BlockSpec((LANES, slab), lambda i, at: (i, 0)),
            pl.BlockSpec((slab // DH, LANES), lambda i, at: (0, i)),
        ],
        scratch_shapes=[pltpu.VMEM((slab, length), jnp.bfloat16)],
    )
    return pl.pallas_call(
        attend_kernel,
        grid_spec=grid_spec,
        out_shape=[
            jax.ShapeDtypeStruct((length, slab), jnp.bfloat16),
            jax.ShapeDtypeStruct((slab // DH, length), jnp.float32),
        ],
        compiler_params=pltpu.CompilerParams(vmem_limit_bytes=VMEM_GRANT),
        cost_estimate=pl.CostEstimate(
            flops=16 * length * length * slab, bytes_accessed=8 * length * slab,
            transcendentals=length * length * slab // DH,
        ),
        name="attend",
    )(place.reshape(1), projected, projected, projected, seg_keys, seg_queries)


def attend_back_kernel(place_ref, q_ref, k_ref, v_ref, seg_key_ref, seg_query_ref, gm_ref, log_ref,
                       old_ref, grad_ref, sums_ref, key_t, grad_key, grad_value):
    del old_ref
    step = pl.program_id(0)

    @pl.when(step == 0)
    def _():
        key_t[...] = k_ref[...].T
        grad_key[...] = jnp.zeros_like(grad_key)
        grad_value[...] = jnp.zeros_like(grad_value)

    pairs = q_ref.shape[1] // LANES
    lane_is_low = lax.broadcasted_iota(jnp.int32, (1, LANES), 1) < DH
    bias = mask_bias(seg_key_ref, seg_query_ref)
    head_scale = 1.0 / math.sqrt(DH)
    here = pl.ds(pl.multiple_of(step * LANES, LANES), LANES)
    for pair in range(pairs):
        lanes = slice(pair * LANES, (pair + 1) * LANES)
        queries = stacked_heads(q_ref[:, lanes], lane_is_low)
        grads = stacked_heads(gm_ref[:, lanes], lane_is_low)
        log_total = jnp.concatenate(
            [log_ref[2 * pair : 2 * pair + 1], log_ref[2 * pair + 1 : 2 * pair + 2]], axis=1
        )
        probs = jnp.exp(dot_nt(k_ref[:, lanes], queries) + (bias - log_total))
        grad_probs = dot_nt(v_ref[:, lanes], grads)
        centre = jnp.sum(probs * grad_probs, axis=0, keepdims=True)
        grad_scores = (probs * (grad_probs - centre)).astype(jnp.bfloat16)
        grad_value[:, lanes] += dot_nn(probs.astype(jnp.bfloat16), grads)
        grad_key[:, lanes] += dot_nn(grad_scores, queries)
        grad_query = own_blocks(dot_nn(key_t[lanes], grad_scores)).astype(jnp.bfloat16)
        grad_ref[0, here, lanes] = (grad_query.astype(jnp.float32) * head_scale).astype(
            jnp.bfloat16
        )

    @pl.when(step == pl.num_programs(0) - 1)
    def _():
        grad_ref[1] = grad_key[...].astype(jnp.bfloat16)
        low_value = grad_value[...].astype(jnp.bfloat16)
        grad_ref[2] = low_value
        sums_ref[0:1] = jnp.sum(grad_ref[0].astype(jnp.float32), axis=0, keepdims=True)
        sums_ref[1:2] = jnp.sum(low_value.astype(jnp.float32), axis=0, keepdims=True)


def attend_back(projected, seg_keys, seg_queries, grad_halves, log_total, old, place, core):
    length = seg_keys.shape[1]
    slab = projected.shape[2]
    blocks = length // LANES
    half = blocks // 2
    grid_spec = pltpu.PrefetchScalarGridSpec(
        num_scalar_prefetch=1,
        grid=(blocks,),
        in_specs=[
            pl.BlockSpec((None, LANES, slab), lambda i, at: (0, at[0] * blocks + i, 0)),
            pl.BlockSpec((None, length, slab), lambda i, at: (1, at[0], 0)),
            pl.BlockSpec((None, length, slab), lambda i, at: (2, at[0], 0)),
            pl.BlockSpec((None, length, LANES), lambda i, at: (at[0], 0, 0)),
            pl.BlockSpec((None, 1, LANES), lambda i, at: (at[0], 0, i)),
            pl.BlockSpec(
                (None, LANES, slab), lambda i, at: (lax.rem(i // half + at[1], 2), lax.rem(i, half), 0)
            ),
            pl.BlockSpec((slab // DH, LANES), lambda i, at: (0, i)),
            pl.BlockSpec(memory_space=pl.ANY),
        ],
        out_specs=[
            pl.BlockSpec((3, length, slab), lambda i, at: (0, at[0], 0)),
            pl.BlockSpec((2, slab), lambda i, at: (0, 0)),
        ],
        scratch_shapes=[
            pltpu.VMEM((slab, length), jnp.bfloat16),
            pltpu.VMEM((length, slab), jnp.float32),
            pltpu.VMEM((length, slab), jnp.float32),
        ],
    )
    return pl.pallas_call(
        attend_back_kernel,
        grid_spec=grid_spec,
        out_shape=[
            jax.ShapeDtypeStruct(projected.shape, jnp.bfloat16),
            jax.ShapeDtypeStruct((2, slab), jnp.float32),
        ],
        input_output_aliases={8: 0},
        compiler_params=pltpu.CompilerParams(vmem_limit_bytes=VMEM_GRANT),
        cost_estimate=pl.CostEstimate(
            flops=40 * length * length * slab, bytes_accessed=16 * length * slab,
            transcendentals=length * length * slab // DH,
        ),
        name="attend_back",
    )(jnp.stack([place, core]), projected, projected, projected, seg_keys, seg_queries, grad_halves,
      log_total, old)


def row_mean(values):
    return jnp.mean(values, axis=-1, keepdims=True)


def ffn_kernel(mixed_own, mixed_one, mixed_two, mixed_three, tokens, cotangent, out_own, out_one,
               out_two, out_three, in_own, in_near, in_far, down_own, down_near, down_far,
               bias_ref, vec_ref,
               result_ref, low_out, active_out, branch_out, hidden_out, norm_out, attn_out,
               mixed_out, unit_ref, sums_ref,
               w_out, w_in, w_down, tok, cot, first, normed, inverse, low, slope, active, part,
               other, other_two, acc, wide, branch, hidden, result, grad_h1, attn, mixed,
               load_sem, store_sem, send_sem, recv_sem):
    dp_place = lax.axis_index("dp")
    tensor_place = lax.axis_index("tensor")
    core = lax.rem(tensor_place, 2)
    sibling = (dp_place, tensor_place + 1 - 2 * core)
    side = lax.rem(dp_place, 2)
    share, width = tok.shape
    slab = in_own.shape[1]
    own_rows = pl.ds(pl.multiple_of(tensor_place * share, LANES), share)
    near_rows = pl.ds(pl.multiple_of(side * (width // 2), LANES), width // 2)
    far_rows = pl.ds(pl.multiple_of((1 - side) * (width // 2), LANES), width // 2)
    near_units = pl.ds(pl.multiple_of(slab + side * (slab // 2), LANES), slab // 2)
    far_units = pl.ds(pl.multiple_of(slab + (1 - side) * (slab // 2), LANES), slab // 2)

    loads = [
        (out_own, w_out.at[0]), (out_one, w_out.at[1]), (out_two, w_out.at[2]),
        (out_three, w_out.at[3]), (tokens.at[own_rows], tok),
        (in_own, w_in.at[0]), (in_near, w_in.at[1, near_rows]), (in_far, w_in.at[1, far_rows]),
        (down_own, w_down.at[pl.ds(0, slab)]), (down_near, w_down.at[near_units]),
        (down_far, w_down.at[far_units]), (cotangent.at[own_rows], cot),
    ]
    loads = [
        pltpu.make_async_copy(source, target, load_sem.at[number])
        for number, (source, target) in enumerate(loads)
    ]
    for load in loads:
        load.start()
    stores = []

    def store(source, target):
        copy = pltpu.make_async_copy(source, target, store_sem.at[len(stores)])
        copy.start()
        stores.append(copy)

    def send(number, source, target):
        return pltpu.make_async_remote_copy(
            src_ref=source,
            dst_ref=target,
            send_sem=send_sem.at[number],
            recv_sem=recv_sem.at[number],
            device_id=sibling,
            device_id_type=MESH,
        )

    barrier = pltpu.get_barrier_semaphore()
    pl.semaphore_signal(barrier, inc=1, device_id=sibling, device_id_type=MESH)
    pl.semaphore_wait(barrier, 1)
    sums_ref[...] = jnp.zeros_like(sums_ref)
    unit_ref[...] = jnp.zeros_like(unit_ref)
    pieces = (mixed_own, mixed_one, mixed_two, mixed_three)
    for load in loads[:5]:
        load.wait()
    big = 256
    small = 64

    def attn_rows(step, carry):
        rows = pl.ds(pl.multiple_of(step * big, big), big)
        total = dot_nn(pieces[0][rows], w_out[0])
        for piece in range(1, 4):
            total += dot_nn(pieces[piece][rows], w_out[piece])
        acc[rows] = total
        return carry

    def first_rows(step, carry):
        rows = pl.ds(pl.multiple_of(step * small, small), small)
        values = tok[rows].astype(jnp.float32) + (acc[rows] + vec_ref[0:1])
        centred = values - row_mean(values)
        scale = lax.rsqrt(row_mean(centred * centred) + EPS_NORM)
        unit = centred * scale
        normed[rows] = unit
        inverse[rows] = scale
        shifted = unit * vec_ref[2:3] + vec_ref[3:4]
        first[rows] = shifted
        low[0, rows] = shifted.astype(jnp.bfloat16)
        return carry

    lax.fori_loop(0, share // big, attn_rows, 0)
    lax.fori_loop(0, share // small, first_rows, 0)
    low_send = send(0, low.at[0], low.at[1])
    low_send.start()
    for load in loads[5:8]:
        load.wait()
    chunk = 256
    half_chunks = slab // chunk

    def hidden_of(slot):
        def units(step, carry):
            part_of = step // half_chunks
            inner = pl.ds(pl.multiple_of(lax.rem(step, half_chunks) * chunk, chunk), chunk)
            outer = pl.ds(pl.multiple_of(step * chunk, chunk), chunk)
            values = dot_nn(low[slot], w_in[part_of, :, inner]) + bias_ref[:, outer]
            share_of = 0.5 * (1.0 + lax.erf(values * math.sqrt(0.5)))
            density = jnp.exp(-0.5 * values * values) * (1.0 / math.sqrt(2.0 * math.pi))
            active[slot, :, outer] = (values * share_of).astype(jnp.bfloat16)
            slope[slot, :, outer] = share_of + values * density
            return carry

        lax.fori_loop(0, 2 * half_chunks, units, 0)

    def branch_of(slot, target):
        def columns(step, carry):
            at = pl.ds(pl.multiple_of(step * chunk, chunk), chunk)
            target[:, at] = dot_nn(active[slot], w_down[:, at])
            return carry

        lax.fori_loop(0, width // chunk, columns, 0)

    hidden_of(0)
    low_send.wait_recv()
    hidden_of(1)
    store(low, low_out)
    store(active, active_out)
    for load in loads[8:]:
        load.wait()
    branch_of(1, part)
    part_send = send(1, part, other)
    part_send.start()
    branch_of(0, acc)
    part_send.wait_recv()

    def second_rows(step, carry):
        rows = pl.ds(pl.multiple_of(step * small, small), small)
        values = first[rows] + (acc[rows] + other[rows]) + vec_ref[1:2]
        centred = values - row_mean(values)
        scale = lax.rsqrt(row_mean(centred * centred) + EPS_NORM)
        unit = centred * scale
        result[rows] = (unit * vec_ref[4:5] + vec_ref[5:6]).astype(jnp.bfloat16)
        upper = cot[rows].astype(jnp.float32)
        scaled = upper * vec_ref[4:5]
        grad = scale * (scaled - row_mean(scaled) - unit * row_mean(scaled * unit))
        wide[rows] = grad
        grad_low = grad.astype(jnp.bfloat16)
        branch[0, rows] = grad_low
        sums_ref[1:2] += jnp.sum(grad_low.astype(jnp.float32), axis=0, keepdims=True)
        sums_ref[4:5] += jnp.sum(upper * unit, axis=0, keepdims=True)
        sums_ref[5:6] += jnp.sum(upper, axis=0, keepdims=True)
        return carry

    lax.fori_loop(0, share // small, second_rows, 0)
    branch_send = send(2, branch.at[0], branch.at[1])
    branch_send.start()
    store(result, result_ref)

    def grad_hidden_of(slot):
        def units(step, carry):
            outer = pl.ds(pl.multiple_of(step * chunk, chunk), chunk)
            grad = dot_nt(branch[slot], w_down[outer]) * slope[slot, :, outer]
            grad_low = grad.astype(jnp.bfloat16)
            hidden[slot, :, outer] = grad_low
            unit_ref[:, outer] += jnp.sum(grad_low.astype(jnp.float32), axis=0, keepdims=True)
            return carry

        lax.fori_loop(0, 2 * half_chunks, units, 0)

    def grad_first_of(slot, target):
        def columns(step, carry):
            at = pl.ds(pl.multiple_of(step * chunk, chunk), chunk)
            target[:, at] = dot_nt(hidden[slot, :, :slab], w_in[0, at]) + dot_nt(
                hidden[slot, :, slab:], w_in[1, at]
            )
            return carry

        lax.fori_loop(0, width // chunk, columns, 0)

    grad_hidden_of(0)
    branch_send.wait_recv()
    store(branch, branch_out)
    grad_hidden_of(1)
    store(hidden, hidden_out)
    part_send.wait_send()
    grad_first_of(1, part)
    first_send = send(3, part, other_two)
    first_send.start()
    grad_first_of(0, acc)
    first_send.wait_recv()

    def back_rows(step, carry):
        rows = pl.ds(pl.multiple_of(step * small, small), small)
        grad = acc[rows] + other_two[rows] + wide[rows]
        unit = normed[rows]
        scaled = grad * vec_ref[2:3]
        back = inverse[rows] * (scaled - row_mean(scaled) - unit * row_mean(scaled * unit))
        grad_h1[rows] = back
        back_low = back.astype(jnp.bfloat16)
        attn[rows] = back_low
        sums_ref[0:1] += jnp.sum(back_low.astype(jnp.float32), axis=0, keepdims=True)
        sums_ref[2:3] += jnp.sum(grad * unit, axis=0, keepdims=True)
        sums_ref[3:4] += jnp.sum(grad, axis=0, keepdims=True)
        return carry

    lax.fori_loop(0, share // small, back_rows, 0)
    store(grad_h1, norm_out)
    store(attn, attn_out)

    def mixed_rows(step, carry):
        rows = pl.ds(pl.multiple_of(step * big, big), big)
        for piece in range(4):
            mixed[piece, rows] = dot_nt(attn[rows], w_out[piece]).astype(jnp.bfloat16)
        return carry

    lax.fori_loop(0, share // big, mixed_rows, 0)
    store(mixed, mixed_out)
    low_send.wait_send()
    branch_send.wait_send()
    first_send.wait_send()
    for copy in stores:
        copy.wait()


def ffn(pieces, tokens, cotangent, w_out, w_in, w_down, bias, vectors):
    share, piece_width = pieces[0].shape
    width = tokens.shape[1]
    slab = w_in[0].shape[1]
    units = 2 * slab
    low_type, full_type = jnp.bfloat16, jnp.float32
    vmem = pl.BlockSpec(memory_space=pltpu.VMEM)
    anywhere = pl.BlockSpec(memory_space=pl.ANY)
    shapes = [
        jax.ShapeDtypeStruct((share, width), low_type),
        jax.ShapeDtypeStruct((2, share, width), low_type),
        jax.ShapeDtypeStruct((2, share, units), low_type),
        jax.ShapeDtypeStruct((2, share, width), low_type),
        jax.ShapeDtypeStruct((2, share, units), low_type),
        jax.ShapeDtypeStruct((share, width), full_type),
        jax.ShapeDtypeStruct((share, width), low_type),
        jax.ShapeDtypeStruct((4, share, piece_width), low_type),
        jax.ShapeDtypeStruct((1, units), full_type),
        jax.ShapeDtypeStruct((6, width), full_type),
    ]
    return pl.pallas_call(
        ffn_kernel,
        in_specs=[vmem] * 4 + [anywhere] * 12 + [vmem] * 2,
        out_specs=[anywhere] * 8 + [vmem] * 2,
        out_shape=shapes,
        scratch_shapes=[
            pltpu.VMEM((4, piece_width, width), low_type),
            pltpu.VMEM((2, width, slab), low_type),
            pltpu.VMEM((units, width), low_type),
            pltpu.VMEM((share, width), low_type),
            pltpu.VMEM((share, width), low_type),
            pltpu.VMEM((share, width), full_type),
            pltpu.VMEM((share, width), full_type),
            pltpu.VMEM((share, 1), full_type),
            pltpu.VMEM((2, share, width), low_type),
            pltpu.VMEM((2, share, units), full_type),
            pltpu.VMEM((2, share, units), low_type),
            pltpu.VMEM((share, width), full_type),
            pltpu.VMEM((share, width), full_type),
            pltpu.VMEM((share, width), full_type),
            pltpu.VMEM((share, width), full_type),
            pltpu.VMEM((share, width), full_type),
            pltpu.VMEM((2, share, width), low_type),
            pltpu.VMEM((2, share, units), low_type),
            pltpu.VMEM((share, width), low_type),
            pltpu.VMEM((share, width), full_type),
            pltpu.VMEM((share, width), low_type),
            pltpu.VMEM((4, share, piece_width), low_type),
            pltpu.SemaphoreType.DMA((12,)),
            pltpu.SemaphoreType.DMA((8,)),
            pltpu.SemaphoreType.DMA((4,)),
            pltpu.SemaphoreType.DMA((4,)),
        ],
        compiler_params=pltpu.CompilerParams(
            collective_id=3, has_side_effects=True, vmem_limit_bytes=VMEM_GRANT
        ),
        cost_estimate=pl.CostEstimate(
            flops=2 * share * width * (8 * units + 8 * piece_width),
            bytes_accessed=60 * share * width, transcendentals=4 * share * units,
        ),
        name="ffn",
    )(*pieces, tokens, cotangent, *w_out, *w_in, *w_down, bias, vectors)


def layer_general(tokens, segments, w_qkv, head_bias, w_out, w_in, unit_bias, w_down, vectors,
                  cotangent):
    token_count, model_width = tokens.shape
    seq_count, length = segments.shape
    head_slab = w_qkv.shape[2]
    head_count = head_slab // DH
    tensor_size = lax.axis_size("tensor")
    share_rows = token_count // tensor_size
    tensor_place = lax.axis_index("tensor")
    row_start = tensor_place * share_rows
    head_scale = 1.0 / math.sqrt(DH)

    def own_rows(values):
        return lax.dynamic_slice_in_dim(values, row_start, share_rows, 0)

    flat_qkv = w_qkv.reshape(model_width, 3 * head_slab)
    projected = jnp.dot(tokens, flat_qkv, preferred_element_type=jnp.float32).reshape(
        token_count, 3, head_slab
    )
    head_shape = (seq_count, length, head_count, DH)
    queries = (
        ((projected[:, 0] + head_bias[0]) * head_scale).astype(jnp.bfloat16).reshape(head_shape)
    )
    key_heads = projected[:, 1].astype(jnp.bfloat16).reshape(head_shape)
    value_heads = (projected[:, 2] + head_bias[1]).astype(jnp.bfloat16).reshape(head_shape)
    mixed_heads, log_total = lax.map(attend_forward, (queries, key_heads, value_heads, segments))
    mixed_flat = mixed_heads.reshape(token_count, head_slab)
    attn_out = (
        lax.psum(jnp.dot(mixed_flat, w_out, preferred_element_type=jnp.float32), "tensor")
        + vectors[0]
    )
    first_norm, first_normed, first_inverse = norm_forward(
        tokens.astype(jnp.float32) + attn_out, vectors[2], vectors[3]
    )
    first_low = first_norm.astype(jnp.bfloat16)
    hidden = jnp.dot(first_low, w_in, preferred_element_type=jnp.float32) + unit_bias
    active, gelu_back = jax.vjp(partial(jax.nn.gelu, approximate=False), hidden)
    active_low = active.astype(jnp.bfloat16)
    grad_out_share = own_rows(cotangent).astype(jnp.float32)
    summed_input = (
        first_norm
        + lax.psum(jnp.dot(active_low, w_down, preferred_element_type=jnp.float32), "tensor")
        + vectors[1]
    )
    second_norm, second_normed, second_inverse = norm_forward(summed_input, vectors[4], vectors[5])
    layer_out = own_rows(second_norm).astype(jnp.bfloat16)
    grad_sum = norm_backward(
        cotangent.astype(jnp.float32), second_normed, second_inverse, vectors[4]
    )
    grad_branch = grad_sum.astype(jnp.bfloat16)
    second_share = own_rows(second_normed)
    grad_w_down = trans_times(active_low, grad_branch)
    grad_active = times_trans(grad_branch, w_down)
    grad_hidden = gelu_back(grad_active)[0].astype(jnp.bfloat16)
    grad_w_in = trans_times(first_low, grad_hidden)
    grad_units = jnp.sum(grad_hidden.astype(jnp.float32), axis=0)
    grad_first = lax.psum(times_trans(grad_hidden, w_in), "tensor") + grad_sum
    grad_h1 = norm_backward(grad_first, first_normed, first_inverse, vectors[2])
    grad_attn = grad_h1.astype(jnp.bfloat16)
    grad_first_share = own_rows(grad_first)
    first_normed_share = own_rows(first_normed)
    grad_h1_share = own_rows(grad_h1)
    grad_w_out = trans_times(mixed_flat, grad_attn)
    grad_mixed = times_trans(grad_attn, w_out).astype(jnp.bfloat16).reshape(head_shape)
    grad_query, grad_key, grad_value = lax.map(
        attend_backward, (queries, key_heads, value_heads, segments, grad_mixed, log_total)
    )
    grad_query = (
        grad_query.reshape(token_count, head_slab).astype(jnp.float32) * head_scale
    ).astype(jnp.bfloat16)
    grad_key = grad_key.reshape(token_count, head_slab)
    grad_value = grad_value.reshape(token_count, head_slab)
    grad_projected = jnp.stack([grad_query, grad_key, grad_value], axis=1).reshape(
        token_count, 3 * head_slab
    )
    grad_w_qkv = trans_times(tokens, grad_projected)
    grad_heads = jnp.stack(
        [
            jnp.sum(grad_query.astype(jnp.float32), axis=0),
            jnp.sum(grad_value.astype(jnp.float32), axis=0),
        ]
    )
    grad_tokens = (
        lax.psum_scatter(
            times_trans(grad_projected, flat_qkv).astype(jnp.bfloat16),
            "tensor",
            scatter_dimension=0,
            tiled=True,
        ).astype(jnp.float32)
        + grad_h1_share
    )
    local_vectors = jnp.stack(
        [
            jnp.sum(own_rows(grad_attn).astype(jnp.float32), axis=0),
            jnp.sum(own_rows(grad_branch).astype(jnp.float32), axis=0),
            jnp.sum(grad_first_share * first_normed_share, axis=0),
            jnp.sum(grad_first_share, axis=0),
            jnp.sum(grad_out_share * second_share, axis=0),
            jnp.sum(grad_out_share, axis=0),
        ]
    )
    return (
        layer_out,
        grad_tokens,
        (
            grad_w_qkv.reshape(model_width, 3, head_slab).transpose(1, 0, 2),
            grad_w_out,
            grad_w_in,
            grad_w_down,
        ),
        local_vectors,
        grad_heads,
        grad_units,
    )


def layer_split(tokens, segments, w_qkv, head_bias, w_out, w_in, unit_bias, w_down, vectors,
                cotangent):
    token_count, model_width = tokens.shape
    seq_count, length = segments.shape
    head_slab = w_qkv.shape[2]
    unit_slab = w_in.shape[1]
    tensor_size = lax.axis_size("tensor")
    replicas = lax.axis_size("dp")
    share = token_count // tensor_size
    tensor_place = lax.axis_index("tensor")
    core = lax.rem(tensor_place, 2)
    seq = tensor_place // 2
    side = lax.rem(lax.axis_index("dp"), 2)
    head_scale = 1.0 / math.sqrt(DH)

    def to(values, step):
        return lax.ppermute(
            values, "tensor", [(place, place ^ step) for place in range(tensor_size)]
        )

    def across(values):
        return lax.ppermute(values, "dp", [(place, place ^ 1) for place in range(replicas)])

    def rows_at(values, number, size):
        return lax.dynamic_slice_in_dim(values, number * size, size, 0)

    in_near = to(rows_at(w_in, side, model_width // 2), 2)
    out_two = to(w_out, 2)
    down_near = to(rows_at(w_down, side, unit_slab // 2), 2)
    in_far = across(in_near)
    down_far = across(down_near)
    bias_two = to(unit_bias, 2)
    out_one, out_three = to(jnp.stack([w_out, out_two]), 1)

    planes = w_qkv.transpose(1, 0, 2)
    shift = jnp.stack([head_bias[0], jnp.zeros_like(head_bias[0]), head_bias[1]])
    scale = jnp.array([head_scale, 1.0, 1.0], jnp.float32)
    projected = jnp.einsum("td,gdn->gtn", tokens, planes, preferred_element_type=jnp.float32)
    projected = ((projected + shift[:, None]) * scale[:, None, None]).astype(jnp.bfloat16)
    seg_keys = jnp.broadcast_to(segments[:, :, None], (seq_count, length, LANES))
    seg_queries = segments[:, None, :]
    mixed_far, log_far = attend(projected, seg_keys, seg_queries, 1 - seq)
    piece_two = to(rows_at(mixed_far, core, share), 2)
    piece_three = to(rows_at(mixed_far, 1 - core, share), 3)
    mixed_near, log_near = attend(projected, seg_keys, seg_queries, seq)
    piece_one = to(rows_at(mixed_near, 1 - core, share), 1)
    pieces = (rows_at(mixed_near, core, share), piece_one, piece_two, piece_three)

    (layer_out, low, active, grad_branch, grad_hidden, grad_h1, grad_attn, grad_mixed, units, sums
     ) = ffn(
        pieces,
        tokens,
        cotangent,
        (w_out, out_one, out_two, out_three),
        (w_in, in_near, in_far),
        (w_down, down_near, down_far),
        jnp.concatenate([unit_bias, bias_two])[None],
        vectors,
    )
    low = low.reshape(2 * share, model_width)
    active = active.reshape(2 * share, 2 * unit_slab)
    grad_branch = grad_branch.reshape(2 * share, model_width)
    grad_hidden = grad_hidden.reshape(2 * share, 2 * unit_slab)
    mixed_one = to(grad_mixed[1], 1)
    mixed_two = to(grad_mixed[2], 2)
    mixed_three = to(grad_mixed[3], 3)
    down_two = to(trans_times(active[:, unit_slab:], grad_branch).astype(jnp.bfloat16), 2)
    in_two = to(trans_times(low, grad_hidden[:, unit_slab:]).astype(jnp.bfloat16), 2)
    outs = [trans_times(piece, grad_attn) for piece in pieces]
    back_one, back_three = to(jnp.stack([outs[1], outs[3]]), 1)
    out_back = to((outs[2] + back_three).astype(jnp.bfloat16), 2)
    unit_two = to(units[0, unit_slab:], 2)

    grad_projected = jnp.zeros_like(projected)
    grad_projected, heads_near = attend_back(
        projected, seg_keys, seg_queries, jnp.stack([grad_mixed[0], mixed_one]), log_near,
        grad_projected, seq, core,
    )
    grad_projected, heads_far = attend_back(
        projected, seg_keys, seg_queries, jnp.stack([mixed_two, mixed_three]), log_far,
        grad_projected, 1 - seq, core,
    )
    token_part = jnp.einsum(
        "gtn,gdn->td", grad_projected, planes, preferred_element_type=jnp.float32
    ).astype(jnp.bfloat16)
    other_one = to(
        jnp.stack([rows_at(token_part, 2 * at + 1 - core, share) for at in (seq, 1 - seq)]), 1
    ).astype(jnp.float32)
    across_part = rows_at(token_part, 2 * (1 - seq) + core, share).astype(jnp.float32)
    from_two = to((across_part + other_one[1]).astype(jnp.bfloat16), 2)
    grad_tokens = (
        rows_at(token_part, 2 * seq + core, share).astype(jnp.float32)
        + other_one[0]
        + from_two.astype(jnp.float32)
        + grad_h1
    )
    grad_w_qkv = jnp.einsum(
        "td,gtn->gdn", tokens, grad_projected, preferred_element_type=jnp.float32
    )
    grad_w_down = trans_times(active[:, :unit_slab], grad_branch) + down_two.astype(jnp.float32)
    grad_w_in = trans_times(low, grad_hidden[:, :unit_slab]) + in_two.astype(jnp.float32)
    grad_w_out = outs[0] + back_one + out_back.astype(jnp.float32)
    return (
        layer_out,
        grad_tokens,
        (grad_w_qkv, grad_w_out, grad_w_in, grad_w_down),
        sums,
        heads_near + heads_far,
        units[0, :unit_slab] + unit_two,
    )


def local(
    tokens,
    segments,
    w_qkv,
    head_bias,
    w_out,
    w_in,
    unit_bias,
    w_down,
    vectors,
    cotangent,
    err_qkv,
    err_out,
    err_in,
    err_down,
    basis_qkv,
    basis_out,
    basis_in,
    basis_down,
    mom_qkv,
    mom_head_bias,
    mom_out,
    mom_in,
    mom_unit_bias,
    mom_down,
    mom_vectors,
):
    token_count, model_width = tokens.shape
    head_slab = w_qkv.shape[2]
    unit_slab = w_in.shape[1]
    tensor_size = lax.axis_size("tensor")
    replicas = lax.axis_size("dp")
    one_sequence_per_chip = 2 * segments.shape[0] == tensor_size and replicas % 2 == 0
    layer = layer_split if one_sequence_per_chip else layer_general
    layer_out, grad_tokens, grads, local_vectors, grad_heads, grad_units = layer(
        tokens, segments, w_qkv, head_bias, w_out, w_in, unit_bias, w_down, vectors, cotangent
    )
    grad_w_qkv, grad_w_out, grad_w_in, grad_w_down = grads
    small = jnp.concatenate(
        [
            local_vectors,
            jnp.pad(grad_units, (0, model_width - unit_slab))[None],
            jnp.pad(grad_heads.reshape(1, 2 * head_slab), ((0, 0), (0, model_width - 2 * head_slab))),
        ],
        axis=0,
    )
    planes = (1, 0, 2)
    combined_qkv = grad_w_qkv + err_qkv[0].transpose(planes)
    combined_out = grad_w_out + err_out[0]
    combined_in = grad_w_in + err_in[0]
    combined_down = grad_w_down + err_down[0]
    matrices = (combined_qkv, combined_out, combined_in, combined_down)
    bases, rights, small_sum = compress(
        matrices,
        (basis_qkv.transpose(planes), basis_out, basis_in, basis_down),
        small,
        replicas,
        tensor_size,
    )
    step_rate = 0.3 * math.sqrt(replicas / token_count)
    grads, errors, moments, news = update(
        matrices,
        (mom_qkv.transpose(planes), mom_out, mom_in, mom_down),
        (w_qkv.transpose(planes), w_out, w_in, w_down),
        bases,
        rights,
        step_rate,
    )
    reduced_qkv, rank_out, rank_in, rank_down = (grads[0].transpose(planes),) + tuple(grads[1:])
    new_err_qkv, new_err_out, new_err_in, new_err_down = (
        errors[0].transpose(planes)[None],
        errors[1][None],
        errors[2][None],
        errors[3][None],
    )
    new_mom_qkv, new_mom_out, new_mom_in, new_mom_down = (moments[0].transpose(planes),) + tuple(
        moments[1:]
    )
    new_w_qkv, new_w_out, new_w_in, new_w_down = (news[0].transpose(planes),) + tuple(news[1:])
    right_qkv, right_out, right_in, right_down = rights
    new_basis_qkv = right_qkv.transpose(planes)
    grad_vectors = small_sum[:6]
    grad_unit_bias = small_sum[6, :unit_slab]
    grad_head_bias = small_sum[7, : 2 * head_slab].reshape(2, head_slab)
    new_mom_head_bias = 0.9 * mom_head_bias + grad_head_bias
    new_mom_unit_bias = 0.9 * mom_unit_bias + grad_unit_bias
    new_mom_vectors = 0.9 * mom_vectors + grad_vectors
    new_head_bias = head_bias - step_rate * new_mom_head_bias
    new_unit_bias = unit_bias - step_rate * new_mom_unit_bias
    new_vectors = vectors - step_rate * new_mom_vectors
    return (
        layer_out,
        grad_tokens,
        reduced_qkv,
        grad_head_bias,
        rank_out,
        rank_in,
        grad_unit_bias,
        rank_down,
        grad_vectors,
        new_err_qkv,
        new_err_out,
        new_err_in,
        new_err_down,
        new_basis_qkv,
        right_out,
        right_in,
        right_down,
        new_mom_qkv,
        new_mom_head_bias,
        new_mom_out,
        new_mom_in,
        new_mom_unit_bias,
        new_mom_down,
        new_mom_vectors,
        new_w_qkv,
        new_head_bias,
        new_w_out,
        new_w_in,
        new_unit_bias,
        new_w_down,
        new_vectors,
    )


def solution(mesh):
    in_specs = (
        P("dp", None),
        P("dp", None),
        P(None, None, "tensor"),
        P(None, "tensor"),
        P("tensor", None),
        P(None, "tensor"),
        P("tensor"),
        P("tensor", None),
        P(),
        P("dp", None),
        P("dp", None, None, "tensor"),
        P("dp", "tensor", None),
        P("dp", None, "tensor"),
        P("dp", "tensor", None),
        P(None, None, "tensor"),
        P("tensor", None),
        P(None, "tensor"),
        P("tensor", None),
        P(None, None, "tensor"),
        P(None, "tensor"),
        P("tensor", None),
        P(None, "tensor"),
        P("tensor"),
        P("tensor", None),
        P(),
    )
    out_specs = (
        P(("dp", "tensor"), None),
        P(("dp", "tensor"), None),
        P(None, None, "tensor"),
        P(None, "tensor"),
        P("tensor", None),
        P(None, "tensor"),
        P("tensor"),
        P("tensor", None),
        P(),
        P("dp", None, None, "tensor"),
        P("dp", "tensor", None),
        P("dp", None, "tensor"),
        P("dp", "tensor", None),
        P(None, None, "tensor"),
        P("tensor", None),
        P(None, "tensor"),
        P("tensor", None),
        P(None, None, "tensor"),
        P(None, "tensor"),
        P("tensor", None),
        P(None, "tensor"),
        P("tensor"),
        P("tensor", None),
        P(),
        P(None, None, "tensor"),
        P(None, "tensor"),
        P("tensor", None),
        P(None, "tensor"),
        P("tensor"),
        P("tensor", None),
        P(),
    )
    return jax.shard_map(local, mesh=mesh, in_specs=in_specs, out_specs=out_specs, check_vma=False)
```

```python
from functools import partial
import math

import jax
import jax.numpy as jnp
from jax import lax
from jax.experimental import pallas as pl
from jax.experimental.pallas import tpu as pltpu
from jax.sharding import PartitionSpec as P

DH = 64
LANES = 128
MESH = pl.DeviceIdType.MESH
VMEM_GRANT = 60 << 20


PRECISE = lax.Precision.HIGHEST
EPS_NORM = 1e-05
EPS_BASIS = 1e-08
MASKED = -1000000000.0


def norm_forward(values, gain, shift):
    row_mean = jnp.mean(values, axis=-1, keepdims=True)
    centred = values - row_mean
    variance = jnp.mean(centred * centred, axis=-1, keepdims=True)
    inverse = lax.rsqrt(variance + EPS_NORM)
    normed = centred * inverse
    return (normed * gain + shift, normed, inverse)


def norm_backward(grad_norm, normed, inverse, gain):
    scaled_grad = grad_norm * gain
    grad_mean = jnp.mean(scaled_grad, axis=-1, keepdims=True)
    along_norm = jnp.mean(scaled_grad * normed, axis=-1, keepdims=True)
    return inverse * (scaled_grad - grad_mean - normed * along_norm)


def times_trans(left_side, right_side):
    return lax.dot_general(
        left_side, right_side, (((1,), (1,)), ((), ())), preferred_element_type=jnp.float32
    )


def trans_times(left_side, right_side):
    return lax.dot_general(
        left_side, right_side, (((0,), (0,)), ((), ())), preferred_element_type=jnp.float32
    )


def split_bf16(values):
    high = values.astype(jnp.bfloat16)
    low = (values - high.astype(jnp.float32)).astype(jnp.bfloat16)
    return high, low


def dot_nt(left_side, right_side):
    return lax.dot_general(
        left_side, right_side, (((1,), (1,)), ((), ())), preferred_element_type=jnp.float32
    )


def dot_nn(left_side, right_side):
    return lax.dot_general(
        left_side, right_side, (((1,), (0,)), ((), ())), preferred_element_type=jnp.float32
    )


def dot_tn(left_side, right_side):
    return lax.dot_general(
        left_side, right_side, (((0,), (0,)), ((), ())), preferred_element_type=jnp.float32
    )


def left_factor(factor, matrix):
    rank_size = factor.shape[0]
    factor_high, factor_low = split_bf16(factor)
    matrix_high, matrix_low = split_bf16(matrix)
    both = dot_nt(jnp.concatenate([factor_high, factor_low], axis=0), matrix_high)
    return both[:rank_size] + both[rank_size:] + dot_nt(factor_high, matrix_low)


def right_factor(basis_rows, matrix):
    rank_size = basis_rows.shape[0]
    basis_high, basis_low = split_bf16(basis_rows)
    matrix_high, matrix_low = split_bf16(matrix)
    both = dot_nn(jnp.concatenate([basis_high, basis_low], axis=0), matrix_high)
    return both[:rank_size] + both[rank_size:] + dot_nn(basis_high, matrix_low)


def place_tiles(target, offset, values):
    per_chunk = target.shape[2] // LANES
    for tile in range(values.shape[1] // LANES):
        spot = offset + tile
        target[spot // per_chunk, :, pl.ds(spot % per_chunk * LANES, LANES)] = values[
            :, tile * LANES : (tile + 1) * LANES
        ]
    return offset + values.shape[1] // LANES


def take_tiles(source, offset, size):
    per_chunk = source.shape[2] // LANES
    pieces = []
    for tile in range(size // LANES):
        spot = offset + tile
        pieces.append(source[spot // per_chunk, :, pl.ds(spot % per_chunk * LANES, LANES)])
    return jnp.concatenate(pieces, axis=1) if len(pieces) > 1 else pieces[0]


def orthonormal_rows(rows):
    rank_size = rows.shape[0]
    row_number = lax.broadcasted_iota(jnp.int32, (rank_size, 1), 0)
    for position in range(rank_size):
        row = rows[position : position + 1]
        length = jnp.sqrt(jnp.sum(row * row, axis=1, keepdims=True)) + EPS_BASIS
        unit = row / length
        along = jnp.sum(rows * unit, axis=1, keepdims=True)
        later = jnp.where(row_number > position, along, 0.0)
        rows = jnp.where(row_number == position, unit, rows - later * unit)
    return rows


def dp_exchange(replicas, mine, wire, arrived, total, sems, meanwhile=None):
    send_one, recv_one, send_two, recv_two = sems
    dp_place = lax.axis_index("dp")
    tensor_place = lax.axis_index("tensor")

    def peer_of(step):
        return lax.rem(dp_place + step, replicas)

    def scatter(step, slot):
        return pltpu.make_async_remote_copy(
            src_ref=wire.at[peer_of(step)],
            dst_ref=arrived.at[slot],
            send_sem=send_one.at[step],
            recv_sem=recv_one.at[slot],
            device_id=(peer_of(step), tensor_place),
            device_id_type=MESH,
        )

    def gather(step, slot):
        return pltpu.make_async_remote_copy(
            src_ref=total.at[dp_place],
            dst_ref=total.at[slot],
            send_sem=send_two.at[step],
            recv_sem=recv_two.at[slot],
            device_id=(peer_of(step), tensor_place),
            device_id_type=MESH,
        )

    def start_scatter(step, carry):
        scatter(step, dp_place).start()
        return carry

    def add_arrived(step, carry):
        scatter(step, peer_of(step)).wait_recv()
        return carry + arrived[peer_of(step)].astype(jnp.float32)

    def start_gather(step, carry):
        gather(step, dp_place).start()
        return carry

    def finish(step, carry):
        gather(step, peer_of(step)).wait_recv()
        return carry

    wire[...] = mine[...].astype(wire.dtype)
    lax.fori_loop(1, replicas, start_scatter, 0)
    total[dp_place] = lax.fori_loop(1, replicas, add_arrived, mine[dp_place])
    lax.fori_loop(1, replicas, start_gather, 0)
    lax.fori_loop(1, replicas, finish, 0)

    def drain(step, carry):
        scatter(step, dp_place).wait_send()
        gather(step, dp_place).wait_send()
        return carry

    return lambda: lax.fori_loop(1, replicas, drain, 0)


def compress_kernel(replicas, tensor_size, qkv_ref, out_ref, in_ref, down_ref,
                    fq_ref, fo_ref, fi_ref, fd_ref, small_ref,
                    bq_ref, bo_ref, bi_ref, bd_ref, rq_ref, ro_ref, ri_ref, rd_ref, sum_ref,
                    qkv, out, inw, down, mine, wire, arrived, total,
                    mine_two, wire_two, arrived_two, total_two, small_slots,
                    load_sem, *sems):
    first_sems, second_sems, (send_small, recv_small) = sems[:4], sems[4:8], sems[8:]
    dp_place = lax.axis_index("dp")
    tensor_place = lax.axis_index("tensor")
    loads = [
        pltpu.make_async_copy(source, target, load_sem.at[number])
        for number, (source, target) in enumerate(
            [(qkv_ref, qkv), (out_ref, out), (down_ref, down), (in_ref, inw)]
        )
    ]
    for load in loads:
        load.start()
    barrier = pltpu.get_barrier_semaphore()

    def greet_dp(step, carry):
        pl.semaphore_signal(
            barrier,
            inc=1,
            device_id=(lax.rem(dp_place + step, replicas), tensor_place),
            device_id_type=MESH,
        )
        return carry

    def greet_tensor(step, carry):
        pl.semaphore_signal(
            barrier,
            inc=1,
            device_id=(dp_place, lax.rem(tensor_place + step, tensor_size)),
            device_id_type=MESH,
        )
        return carry

    lax.fori_loop(1, replicas, greet_dp, 0)
    lax.fori_loop(1, tensor_size, greet_tensor, 0)
    mine[...] = jnp.zeros_like(mine)
    mine_two[...] = jnp.zeros_like(mine_two)
    block = 2 * LANES
    offset = 0
    loads[0].wait()
    for start in range(0, qkv.shape[1], block):
        rows = slice(start, start + block)
        left = left_factor(fq_ref[0], qkv[0, rows])
        for part in range(1, 3):
            left += left_factor(fq_ref[part], qkv[part, rows])
        offset = place_tiles(mine, offset, left)
    for load, factor_ref, matrix in zip(loads[1:], (fo_ref, fd_ref, fi_ref), (out, down, inw)):
        load.wait()
        rows_of = min(block, matrix.shape[0])
        for start in range(0, matrix.shape[0], rows_of):
            left = left_factor(factor_ref[...], matrix[start : start + rows_of])
            offset = place_tiles(mine, offset, left)
    place_tiles(mine, offset, small_ref[...])
    pl.semaphore_wait(barrier, replicas - 1 + tensor_size - 1)
    drain_one = dp_exchange(replicas, mine, wire, arrived, total, first_sems)

    def slot_copy(step, slot):
        peer = lax.rem(tensor_place + step, tensor_size)
        return pltpu.make_async_remote_copy(
            src_ref=small_slots.at[tensor_place],
            dst_ref=small_slots.at[slot],
            send_sem=send_small.at[step],
            recv_sem=recv_small.at[slot],
            device_id=(dp_place, peer),
            device_id_type=MESH,
        )

    def start_small(step, carry):
        slot_copy(step, tensor_place).start()
        return carry

    own_small = take_tiles(total, offset, small_ref.shape[1])
    small_slots[tensor_place] = own_small
    lax.fori_loop(1, tensor_size, start_small, 0)
    offset = 0
    offset_two = 0
    for basis_ref in (bq_ref, bo_ref, bd_ref, bi_ref):
        rows = take_tiles(total, offset, basis_ref.shape[1]) * (1.0 / replicas)
        basis_ref[...] = orthonormal_rows(rows)
        offset += basis_ref.shape[1] // LANES
    drain_one()
    for part in range(3):
        right = right_factor(bq_ref[:, :block], qkv[part, :block])
        for start in range(block, qkv.shape[1], block):
            rows = slice(start, start + block)
            right += right_factor(bq_ref[:, rows], qkv[part, rows])
        offset_two = place_tiles(mine_two, offset_two, right)
    for basis_ref, matrix in zip((bo_ref, bd_ref, bi_ref), (out, down, inw)):
        rows_of = min(block, matrix.shape[0])
        right = right_factor(basis_ref[:, :rows_of], matrix[:rows_of])
        for start in range(rows_of, matrix.shape[0], rows_of):
            rows = slice(start, start + rows_of)
            right += right_factor(basis_ref[:, rows], matrix[rows])
        offset_two = place_tiles(mine_two, offset_two, right)
    drain_two = dp_exchange(
        replicas, mine_two, wire_two, arrived_two, total_two, second_sems
    )

    def collect(step, carry):
        peer = lax.rem(tensor_place + step, tensor_size)
        slot_copy(step, peer).wait_recv()
        slot_copy(step, tensor_place).wait_send()
        return carry + small_slots[peer]

    everyone = lax.fori_loop(1, tensor_size, collect, own_small)
    row_number = lax.broadcasted_iota(jnp.int32, everyone.shape, 0)
    sum_ref[...] = jnp.where(row_number < 6, everyone, own_small) * (1.0 / replicas)
    offset = 0
    for part in range(3):
        rq_ref[part] = take_tiles(total_two, offset, rq_ref.shape[2]) * (1.0 / replicas)
        offset += rq_ref.shape[2] // LANES
    for ref in (ro_ref, rd_ref, ri_ref):
        ref[...] = take_tiles(total_two, offset, ref.shape[1]) * (1.0 / replicas)
        offset += ref.shape[1] // LANES
    drain_two()


def compress(matrices, factors, small, replicas, tensor_size):
    qkv, out, inw, down = matrices
    rank_size = small.shape[0]
    sizes = (qkv.shape[1], out.shape[0], inw.shape[0], down.shape[0])
    right_shapes = [(3, rank_size, qkv.shape[2])] + [(rank_size, one.shape[1]) for one in matrices[1:]]
    lanes_one = sum(sizes) + small.shape[1]
    lanes_two = 3 * qkv.shape[2] + sum(one.shape[1] for one in matrices[1:])
    scratch = [pltpu.VMEM(one.shape, jnp.float32) for one in matrices]
    for lanes in (lanes_one, lanes_two):
        shape = (replicas, rank_size, -(-lanes // (LANES * replicas)) * LANES)
        scratch += [
            pltpu.VMEM(shape, jnp.float32),
            pltpu.VMEM(shape, jnp.bfloat16),
            pltpu.VMEM(shape, jnp.bfloat16),
            pltpu.VMEM(shape, jnp.float32),
        ]
    scratch += [pltpu.VMEM((tensor_size,) + small.shape, jnp.float32), pltpu.SemaphoreType.DMA((4,))]
    scratch += [pltpu.SemaphoreType.DMA((replicas,))] * 8
    scratch += [pltpu.SemaphoreType.DMA((tensor_size,))] * 2
    vmem = pl.BlockSpec(memory_space=pltpu.VMEM)
    shapes = [(rank_size, size) for size in sizes] + right_shapes + [small.shape]
    outputs = pl.pallas_call(
        partial(compress_kernel, replicas, tensor_size),
        in_specs=[pl.BlockSpec(memory_space=pl.ANY)] * 4 + [vmem] * 5,
        out_specs=[vmem] * 9,
        out_shape=[jax.ShapeDtypeStruct(shape, jnp.float32) for shape in shapes],
        scratch_shapes=scratch,
        compiler_params=pltpu.CompilerParams(
            collective_id=1, has_side_effects=True, vmem_limit_bytes=VMEM_GRANT
        ),
        name="compress",
    )(*matrices, *factors, small)
    return outputs[:4], outputs[4:8], outputs[8]


def outer_of(basis_rows, right):
    basis_high, basis_low = split_bf16(basis_rows)
    right_high, right_low = split_bf16(right)
    return dot_tn(
        jnp.concatenate([basis_high, basis_low, basis_high], axis=0),
        jnp.concatenate([right_high, right_high, right_low], axis=0),
    )


def update_kernel(step_rate, out_steps, *refs):
    (mq, mo, mi, md, oq, oo, oi, od, wq, wo, wi, wd, bq, bo, bi, bd, rq, ro, ri, rd,
     gq, go, gi, gd, eq, eo, ei, ed, nq, no, ni, nd, vq, vo, vi, vd) = refs
    step = pl.program_id(0)

    def one(matrix, old, weight, rank, grad_ref, err_ref, mom_ref, new_ref, place):
        moment = 0.9 * old + rank
        grad_ref[place] = rank
        err_ref[place] = matrix - rank
        mom_ref[place] = moment
        new_ref[place] = weight.astype(jnp.float32) - step_rate * moment

    def lanes_of(ref, rows):
        return ref[:, pl.ds(pl.multiple_of(step * rows, LANES), rows)]

    rows = mq.shape[1]
    for part in range(3):
        rank = outer_of(lanes_of(bq, rows), rq[part])
        one(mq[part], oq[part], wq[part], rank, gq, eq, nq, vq, part)
    rank = outer_of(lanes_of(bi, mi.shape[0]), ri[...])
    one(mi[...], oi[...], wi[...], rank, gi, ei, ni, vi, slice(None))
    rank = outer_of(lanes_of(bd, md.shape[0]), rd[...])
    one(md[...], od[...], wd[...], rank, gd, ed, nd, vd, slice(None))

    @pl.when(step < out_steps)
    def _():
        rank = outer_of(lanes_of(bo, mo.shape[0]), ro[...])
        one(mo[...], oo[...], wo[...], rank, go, eo, no, vo, slice(None))


def update(matrices, momenta, weights, bases, rights, step_rate):
    qkv, out, inw, down = matrices
    rows = LANES
    steps = inw.shape[0] // rows
    down_rows = down.shape[0] // steps
    if down_rows < LANES:
        steps = down.shape[0] // LANES
        rows, down_rows = inw.shape[0] // steps, LANES
    out_steps = out.shape[0] // LANES

    def whole(array):
        return pl.BlockSpec(array.shape, lambda i: (0,) * array.ndim)

    def specs():
        return [
            pl.BlockSpec((3, rows, qkv.shape[2]), lambda i: (0, i, 0)),
            pl.BlockSpec((LANES, out.shape[1]), lambda i: (jnp.minimum(i, out_steps - 1), 0)),
            pl.BlockSpec((rows, inw.shape[1]), lambda i: (i, 0)),
            pl.BlockSpec((down_rows, down.shape[1]), lambda i: (i, 0)),
        ]

    shapes = [jax.ShapeDtypeStruct(one.shape, jnp.float32) for one in matrices]
    outputs = pl.pallas_call(
        partial(update_kernel, step_rate, out_steps),
        grid=(steps,),
        in_specs=specs() * 3 + [whole(one) for one in bases] + [whole(one) for one in rights],
        out_specs=specs() * 4,
        out_shape=shapes * 4,
        compiler_params=pltpu.CompilerParams(vmem_limit_bytes=VMEM_GRANT),
        name="update",
    )(*matrices, *momenta, *weights, *bases, *rights)
    return outputs[0:4], outputs[4:8], outputs[8:12], outputs[12:16]


def masked_scores(queries, key_heads, seg_ids):
    scores = jnp.einsum("qhd,khd->hqk", queries, key_heads, preferred_element_type=jnp.float32)
    same_doc = seg_ids[:, None] == seg_ids[None, :]
    return jnp.where(same_doc[None], scores, MASKED)


def attend_forward(inputs_of):
    queries, key_heads, value_heads, seg_ids = inputs_of
    scores = masked_scores(queries, key_heads, seg_ids)
    highest = jnp.max(scores, axis=-1, keepdims=True)
    powers = jnp.exp(scores - highest)
    denominator = jnp.sum(powers, axis=-1, keepdims=True)
    weights = (powers / denominator).astype(jnp.bfloat16)
    mixed_heads = jnp.einsum(
        "hqk,khd->qhd", weights, value_heads, preferred_element_type=jnp.float32
    )
    return (mixed_heads.astype(jnp.bfloat16), highest[..., 0] + jnp.log(denominator[..., 0]))


def attend_backward(inputs_of):
    queries, key_heads, value_heads, seg_ids, grad_mixed, log_total = inputs_of
    scores = masked_scores(queries, key_heads, seg_ids)
    probability = jnp.exp(scores - log_total[..., None])
    grad_probs = jnp.einsum(
        "qhd,khd->hqk", grad_mixed, value_heads, preferred_element_type=jnp.float32
    )
    centre = jnp.sum(probability * grad_probs, axis=-1, keepdims=True)
    grad_scores = (probability * (grad_probs - centre)).astype(jnp.bfloat16)
    grad_query = jnp.einsum(
        "hqk,khd->qhd", grad_scores, key_heads, preferred_element_type=jnp.float32
    )
    grad_key = jnp.einsum("hqk,qhd->khd", grad_scores, queries, preferred_element_type=jnp.float32)
    grad_value = jnp.einsum(
        "hqk,qhd->khd",
        probability.astype(jnp.bfloat16),
        grad_mixed,
        preferred_element_type=jnp.float32,
    )
    return (
        grad_query.astype(jnp.bfloat16),
        grad_key.astype(jnp.bfloat16),
        grad_value.astype(jnp.bfloat16),
    )


def stacked_heads(pair, lane_is_low):
    zero = jnp.zeros_like(pair)
    return jnp.concatenate(
        [jnp.where(lane_is_low, pair, zero), jnp.where(lane_is_low, zero, pair)], axis=0
    )


def own_blocks(both):
    rows = both.shape[1] // 2
    return jnp.concatenate([both[:DH, :rows], both[DH:, rows:]], axis=0).T


def mask_bias(seg_key_ref, seg_query_ref):
    same = seg_key_ref[...] == seg_query_ref[...]
    bias = jnp.where(same, 0.0, MASKED)
    return jnp.concatenate([bias, bias], axis=1)


def attend_back_kernel(place_ref, q_ref, k_ref, v_ref, seg_key_ref, seg_query_ref, gm_own_ref,
                       gm_other_ref, log_ref, old_ref, grad_ref, sums_ref, key_t, grad_key, grad_value):
    del old_ref
    step = pl.program_id(0)

    @pl.when(step == 0)
    def _():
        key_t[...] = k_ref[...].T
        grad_key[...] = jnp.zeros_like(grad_key)
        grad_value[...] = jnp.zeros_like(grad_value)

    pairs = q_ref.shape[1] // LANES
    lane_is_low = lax.broadcasted_iota(jnp.int32, (1, LANES), 1) < DH
    bias = mask_bias(seg_key_ref, seg_query_ref)
    head_scale = 1.0 / math.sqrt(DH)
    here = pl.ds(pl.multiple_of(step * LANES, LANES), LANES)
    is_own = lax.rem(step // (pl.num_programs(0) // 2) + place_ref[1], 2) == 0
    gm = jnp.where(is_own, gm_own_ref[...], gm_other_ref[...])
    for pair in range(pairs):
        lanes = slice(pair * LANES, (pair + 1) * LANES)
        queries = stacked_heads(q_ref[:, lanes], lane_is_low)
        grads = stacked_heads(gm[:, lanes], lane_is_low)
        log_total = jnp.concatenate(
            [log_ref[2 * pair : 2 * pair + 1], log_ref[2 * pair + 1 : 2 * pair + 2]], axis=1
        )
        probs = jnp.exp(dot_nt(k_ref[:, lanes], queries) + (bias - log_total))
        grad_probs = dot_nt(v_ref[:, lanes], grads)
        centre = jnp.sum(probs * grad_probs, axis=0, keepdims=True)
        grad_scores = (probs * (grad_probs - centre)).astype(jnp.bfloat16)
        grad_value[:, lanes] += dot_nn(probs.astype(jnp.bfloat16), grads)
        grad_key[:, lanes] += dot_nn(grad_scores, queries)
        grad_query = own_blocks(dot_nn(key_t[lanes], grad_scores)).astype(jnp.bfloat16)
        grad_ref[0, here, lanes] = (grad_query.astype(jnp.float32) * head_scale).astype(
            jnp.bfloat16
        )

    @pl.when(step == pl.num_programs(0) - 1)
    def _():
        grad_ref[1] = grad_key[...].astype(jnp.bfloat16)
        low_value = grad_value[...].astype(jnp.bfloat16)
        grad_ref[2] = low_value
        sums_ref[0:1] = jnp.sum(grad_ref[0].astype(jnp.float32), axis=0, keepdims=True)
        sums_ref[1:2] = jnp.sum(low_value.astype(jnp.float32), axis=0, keepdims=True)


def attend_back(projected, seg_keys, seg_queries, grad_own, grad_other, logs, slot, old, place, core):
    length = seg_keys.shape[1]
    slab = projected.shape[2]
    blocks = length // LANES
    half = blocks // 2
    grid_spec = pltpu.PrefetchScalarGridSpec(
        num_scalar_prefetch=1,
        grid=(blocks,),
        in_specs=[
            pl.BlockSpec((None, LANES, slab), lambda i, at: (0, at[0] * blocks + i, 0)),
            pl.BlockSpec((None, length, slab), lambda i, at: (1, at[0], 0)),
            pl.BlockSpec((None, length, slab), lambda i, at: (2, at[0], 0)),
            pl.BlockSpec((None, length, LANES), lambda i, at: (at[0], 0, 0)),
            pl.BlockSpec((None, 1, LANES), lambda i, at: (at[0], 0, i)),
            pl.BlockSpec((None, LANES, slab), lambda i, at: (grad_own[1], lax.rem(i, half), 0)),
            pl.BlockSpec((None, LANES, slab), lambda i, at: (grad_other[1], lax.rem(i, half), 0)),
            pl.BlockSpec((None, slab // DH, LANES), lambda i, at: (slot, 0, i)),
            pl.BlockSpec(memory_space=pl.ANY),
        ],
        out_specs=[
            pl.BlockSpec((3, length, slab), lambda i, at: (0, at[0], 0)),
            pl.BlockSpec((2, slab), lambda i, at: (0, 0)),
        ],
        scratch_shapes=[
            pltpu.VMEM((slab, length), jnp.bfloat16),
            pltpu.VMEM((length, slab), jnp.float32),
            pltpu.VMEM((length, slab), jnp.float32),
        ],
    )
    return pl.pallas_call(
        attend_back_kernel,
        grid_spec=grid_spec,
        out_shape=[
            jax.ShapeDtypeStruct(projected.shape, jnp.bfloat16),
            jax.ShapeDtypeStruct((2, slab), jnp.float32),
        ],
        input_output_aliases={9: 0},
        compiler_params=pltpu.CompilerParams(vmem_limit_bytes=VMEM_GRANT),
        cost_estimate=pl.CostEstimate(
            flops=40 * length * length * slab, bytes_accessed=16 * length * slab,
            transcendentals=length * length * slab // DH,
        ),
        name="attend_back",
    )(jnp.stack([place, core]), projected, projected, projected, seg_keys, seg_queries, grad_own[0],
      grad_other[0], logs, old)


def row_mean(values):
    return jnp.mean(values, axis=-1, keepdims=True)


def front_kernel(tokens, cotangent, w_qkv_ref, out_ref, in_ref, down_ref,
                 head_ref, bias_ref, vec_ref, seg_keys, seg_queries,
                 projected_out, log_out, in_two, down_two, out_rest, bias_two, pieces_out,
                 result_out, low_out, active_out, branch_out, slope_out, normed_out, inverse_out,
                 wide_out, sums_ref,
                 rows_in, w_qkv, projected, value_t, log_total, mixed, pieces,
                 w_out, w_in, w_down, bias, tok, cot, first, normed, inverse, low, slope, active,
                 part, other, acc, wide, branch, result,
                 load_sem, store_sem, fetch_sem, send_sem, recv_sem):
    dp_place = lax.axis_index("dp")
    tensor_place = lax.axis_index("tensor")
    core = lax.rem(tensor_place, 2)
    seq = tensor_place // 2
    far = 1 - seq
    side = lax.rem(dp_place, 2)
    sibling = (dp_place, tensor_place + 1 - 2 * core)
    opposite = (dp_place, core + 2 * far)
    diagonal = (dp_place, 1 - core + 2 * far)
    beside = (dp_place + 1 - 2 * side, tensor_place)
    share, width = tok.shape
    slab = in_ref.shape[1]
    length = rows_in.shape[1]
    head_slab = w_qkv.shape[2]
    head_count = head_slab // DH
    stores = []
    sends = []

    def load(number, source, target):
        copy = pltpu.make_async_copy(source, target, load_sem.at[number])
        copy.start()
        return copy

    def store(source, target):
        copy = pltpu.make_async_copy(source, target, store_sem.at[len(stores)])
        copy.start()
        stores.append(copy)

    def send(source, target, device):
        number = len(sends)
        copy = pltpu.make_async_remote_copy(
            src_ref=source,
            dst_ref=target,
            send_sem=send_sem.at[number],
            recv_sem=recv_sem.at[number],
            device_id=device,
            device_id_type=MESH,
        )
        copy.start()
        sends.append(copy)
        return copy

    def rows_of(number, size):
        return pl.ds(pl.multiple_of(number * size, LANES), size)

    load_qkv = load(0, w_qkv_ref, w_qkv)
    load_far = load(1, tokens.at[rows_of(far, length)], rows_in.at[0])
    load_near = load(2, tokens.at[rows_of(seq, length)], rows_in.at[1])
    load_out = load(3, out_ref, w_out.at[0])
    load_in = load(4, in_ref, w_in.at[0])
    load_down = load(5, down_ref, w_down.at[pl.ds(0, slab)])
    load_tok = load(6, tokens.at[rows_of(tensor_place, share)], tok)
    load_cot = load(7, cotangent.at[rows_of(tensor_place, share)], cot)

    barrier = pltpu.get_barrier_semaphore()
    for device in (sibling, opposite, diagonal, beside):
        pl.semaphore_signal(barrier, inc=1, device_id=device, device_id_type=MESH)
    pl.semaphore_wait(barrier, 4)
    sums_ref[...] = jnp.zeros_like(sums_ref)

    quarter = slab // 4

    def quarter_rows(number):
        return rows_of(2 * side + number, quarter)

    bias_send = send(bias_ref, bias_two, opposite)
    out_send = send(out_ref, out_rest.at[1], opposite)
    in_sends = [send(in_ref.at[quarter_rows(0)], in_two.at[quarter_rows(0)], opposite)]
    in_passes = []
    down_sends = []
    down_passes = []

    def pass_on(arrived, whole, number, passes):
        arrived.wait_recv()
        passes.append(send(whole.at[quarter_rows(number)], whole.at[quarter_rows(number)], beside))

    chunk = 256
    scale = 1.0 / math.sqrt(DH)

    def project(slot):
        def rows_step(step, carry):
            rows = rows_of(step, chunk)
            values = rows_in[slot, rows]
            projected[slot, 0, rows] = (
                (dot_nn(values, w_qkv[0]) + head_ref[0:1]) * scale
            ).astype(jnp.bfloat16)
            projected[slot, 1, rows] = dot_nn(values, w_qkv[1]).astype(jnp.bfloat16)
            projected[slot, 2, rows] = (dot_nn(values, w_qkv[2]) + head_ref[1:2]).astype(
                jnp.bfloat16
            )
            return carry

        lax.fori_loop(0, length // chunk, rows_step, 0)
        value_t[...] = projected[slot, 2].T

    lane_is_low = lax.broadcasted_iota(jnp.int32, (1, LANES), 1) < DH

    def attend_rows(slot, place, start, stop):
        def block(step, carry):
            rows = rows_of(step, LANES)
            same = seg_keys[place] == seg_queries[place, :, rows]
            mask = jnp.where(same, 0.0, MASKED)
            mask = jnp.concatenate([mask, mask], axis=1)
            for pair in range(head_count // 2):
                lanes = slice(pair * LANES, (pair + 1) * LANES)
                queries = stacked_heads(projected[slot, 0, rows, lanes], lane_is_low)
                scores = dot_nt(projected[slot, 1, :, lanes], queries) + mask
                highest = jnp.max(scores, axis=0, keepdims=True)
                powers = jnp.exp(scores - highest)
                denominator = jnp.sum(powers, axis=0, keepdims=True)
                weights = (powers * (1.0 / denominator)).astype(jnp.bfloat16)
                mixed[slot, rows, lanes] = own_blocks(dot_nn(value_t[lanes], weights)).astype(
                    jnp.bfloat16
                )
                total = highest + jnp.log(denominator)
                log_total[slot, 2 * pair : 2 * pair + 1, rows] = total[:, :LANES]
                log_total[slot, 2 * pair + 1 : 2 * pair + 2, rows] = total[:, LANES:]
            return carry

        lax.fori_loop(start, stop, block, 0)

    blocks = length // LANES
    load_qkv.wait()
    load_far.wait()
    project(0)
    attend_rows(0, far, 0, blocks // 4)
    pass_on(in_sends[0], in_two, 0, in_passes)
    in_sends.append(send(in_ref.at[quarter_rows(1)], in_two.at[quarter_rows(1)], opposite))
    out_send.wait_recv()
    fetch_out = pltpu.make_async_copy(out_rest.at[1], w_out.at[2], fetch_sem.at[0])
    fetch_out.start()
    out_pass = [
        send(out_ref, out_rest.at[0], sibling),
        send(out_rest.at[1], out_rest.at[2], sibling),
    ]
    attend_rows(0, far, blocks // 4, blocks)
    own_rows = rows_of(core, share)
    sibling_rows = rows_of(1 - core, share)
    piece_two = send(mixed.at[0, own_rows], pieces.at[1], opposite)
    piece_three = send(mixed.at[0, sibling_rows], pieces.at[2], diagonal)
    pass_on(in_sends[1], in_two, 1, in_passes)
    down_sends.append(send(down_ref.at[quarter_rows(0)], down_two.at[quarter_rows(0)], opposite))
    store(projected.at[0, 0], projected_out.at[0, rows_of(far, length)])
    store(projected.at[0, 1], projected_out.at[1, rows_of(far, length)])
    store(projected.at[0, 2], projected_out.at[2, rows_of(far, length)])
    load_near.wait()
    project(1)
    attend_rows(1, seq, 0, blocks // 2)
    pass_on(down_sends[0], down_two, 0, down_passes)
    down_sends.append(send(down_ref.at[quarter_rows(1)], down_two.at[quarter_rows(1)], opposite))
    attend_rows(1, seq, blocks // 2, blocks)
    piece_one = send(mixed.at[1, sibling_rows], pieces.at[0], sibling)
    store(projected.at[1, 0], projected_out.at[0, rows_of(seq, length)])
    store(projected.at[1, 1], projected_out.at[1, rows_of(seq, length)])
    store(projected.at[1, 2], projected_out.at[2, rows_of(seq, length)])
    store(log_total, log_out)
    for copy in out_pass:
        copy.wait_recv()
    fetch_one = pltpu.make_async_copy(out_rest.at[0], w_out.at[1], fetch_sem.at[1])
    fetch_three = pltpu.make_async_copy(out_rest.at[2], w_out.at[3], fetch_sem.at[2])
    fetch_one.start()
    fetch_three.start()
    store(mixed.at[1, own_rows], pieces_out.at[0])
    for copy in (load_out, load_tok, fetch_out, fetch_one, fetch_three):
        copy.wait()
    for copy in (piece_two, piece_three, piece_one):
        copy.wait_recv()
    for number in range(3):
        store(pieces.at[number], pieces_out.at[number + 1])
    small = 64

    def attn_rows(step, carry):
        rows = rows_of(step, chunk)
        total = dot_nn(mixed[1, pl.ds(pl.multiple_of(core * share + step * chunk, LANES), chunk)],
                       w_out[0])
        for piece in range(3):
            total += dot_nn(pieces[piece, rows], w_out[piece + 1])
        acc[rows] = total
        return carry

    def first_rows(step, carry):
        rows = pl.ds(pl.multiple_of(step * small, small), small)
        values = tok[rows].astype(jnp.float32) + (acc[rows] + vec_ref[0:1])
        centred = values - row_mean(values)
        spread = lax.rsqrt(row_mean(centred * centred) + EPS_NORM)
        unit = centred * spread
        normed[rows] = unit
        inverse[rows] = spread
        shifted = unit * vec_ref[2:3] + vec_ref[3:4]
        first[rows] = shifted
        low[0, rows] = shifted.astype(jnp.bfloat16)
        return carry

    lax.fori_loop(0, share // chunk, attn_rows, 0)
    lax.fori_loop(0, share // small, first_rows, 0)
    low_send = send(low.at[0], low.at[1], sibling)
    store(normed, normed_out)
    store(inverse, inverse_out)
    load_in.wait()

    def hidden_of(slot, owner):
        def units(step, carry):
            inner = rows_of(step, chunk)
            outer = pl.ds(pl.multiple_of(owner * slab + step * chunk, chunk), chunk)
            values = dot_nn(low[slot], w_in[owner, :, inner]) + bias[owner, :, inner]
            share_of = 0.5 * (1.0 + lax.erf(values * math.sqrt(0.5)))
            density = jnp.exp(-0.5 * values * values) * (1.0 / math.sqrt(2.0 * math.pi))
            active[slot, :, outer] = (values * share_of).astype(jnp.bfloat16)
            slope[slot, :, outer] = share_of + values * density
            return carry

        lax.fori_loop(0, slab // chunk, units, 0)

    def branch_of(slot, owner, target):
        units = slice(owner * slab, (owner + 1) * slab)

        def columns(step, carry):
            at = rows_of(step, chunk)
            values = dot_nn(active[slot, :, units], w_down[units, at])
            target[:, at] = values if owner == 0 else target[:, at] + values
            return carry

        lax.fori_loop(0, width // chunk, columns, 0)

    bias_send.wait_recv()
    bias[0] = bias_ref[...]
    fetch_bias = pltpu.make_async_copy(bias_two, bias.at[1], fetch_sem.at[3])
    fetch_bias.start()
    hidden_of(0, 0)
    low_send.wait_recv()
    store(low, low_out)
    hidden_of(1, 0)
    for copy in in_passes:
        copy.wait_recv()
    fetch_in = pltpu.make_async_copy(in_two, w_in.at[1], fetch_sem.at[4])
    fetch_in.start()
    pass_on(down_sends[1], down_two, 1, down_passes)
    load_down.wait()
    branch_of(1, 0, part)
    branch_of(0, 0, acc)
    fetch_bias.wait()
    fetch_in.wait()
    hidden_of(1, 1)
    hidden_of(0, 1)
    store(active, active_out)
    store(slope, slope_out)
    for copy in down_passes:
        copy.wait_recv()
    fetch_down = pltpu.make_async_copy(down_two, w_down.at[pl.ds(slab, slab)], fetch_sem.at[5])
    fetch_down.start()
    fetch_down.wait()
    branch_of(1, 1, part)
    part_send = send(part, other, sibling)
    branch_of(0, 1, acc)
    load_cot.wait()
    part_send.wait_recv()

    def second_rows(step, carry):
        rows = pl.ds(pl.multiple_of(step * small, small), small)
        values = first[rows] + (acc[rows] + other[rows]) + vec_ref[1:2]
        centred = values - row_mean(values)
        spread = lax.rsqrt(row_mean(centred * centred) + EPS_NORM)
        unit = centred * spread
        result[rows] = (unit * vec_ref[4:5] + vec_ref[5:6]).astype(jnp.bfloat16)
        upper = cot[rows].astype(jnp.float32)
        scaled = upper * vec_ref[4:5]
        grad = spread * (scaled - row_mean(scaled) - unit * row_mean(scaled * unit))
        wide[rows] = grad
        grad_low = grad.astype(jnp.bfloat16)
        branch[0, rows] = grad_low
        sums_ref[1:2] += jnp.sum(grad_low.astype(jnp.float32), axis=0, keepdims=True)
        sums_ref[4:5] += jnp.sum(upper * unit, axis=0, keepdims=True)
        sums_ref[5:6] += jnp.sum(upper, axis=0, keepdims=True)
        return carry

    lax.fori_loop(0, share // small, second_rows, 0)
    branch_send = send(branch.at[0], branch.at[1], sibling)
    store(result, result_out)
    store(wide, wide_out)
    branch_send.wait_recv()
    store(branch, branch_out)
    for copy in sends:
        copy.wait_send()
    for copy in stores:
        copy.wait()


def front(tokens, cotangent, planes, w_out, w_in, w_down, head_bias, unit_bias, vectors, seg_keys,
          seg_queries):
    token_count, width = tokens.shape
    seq_count, length = seg_keys.shape[:2]
    share = token_count // (2 * seq_count)
    head_slab = planes.shape[2]
    slab = w_in.shape[1]
    low_type, full_type = jnp.bfloat16, jnp.float32
    vmem = pl.BlockSpec(memory_space=pltpu.VMEM)
    anywhere = pl.BlockSpec(memory_space=pl.ANY)
    shapes = [
        jax.ShapeDtypeStruct((3, token_count, head_slab), low_type),
        jax.ShapeDtypeStruct((2, head_slab // DH, length), full_type),
        jax.ShapeDtypeStruct(w_in.shape, low_type),
        jax.ShapeDtypeStruct(w_down.shape, low_type),
        jax.ShapeDtypeStruct((3,) + w_out.shape, low_type),
        jax.ShapeDtypeStruct((1, slab), full_type),
        jax.ShapeDtypeStruct((4, share, head_slab), low_type),
        jax.ShapeDtypeStruct((share, width), low_type),
        jax.ShapeDtypeStruct((2, share, width), low_type),
        jax.ShapeDtypeStruct((2, share, 2 * slab), low_type),
        jax.ShapeDtypeStruct((2, share, width), low_type),
        jax.ShapeDtypeStruct((2, share, 2 * slab), full_type),
        jax.ShapeDtypeStruct((share, width), full_type),
        jax.ShapeDtypeStruct((share, 1), full_type),
        jax.ShapeDtypeStruct((share, width), full_type),
        jax.ShapeDtypeStruct((6, width), full_type),
    ]
    return pl.pallas_call(
        front_kernel,
        in_specs=[anywhere] * 6 + [vmem] * 5,
        out_specs=[anywhere] * 15 + [vmem],
        out_shape=shapes,
        scratch_shapes=[
            pltpu.VMEM((2, length, width), low_type),
            pltpu.VMEM(planes.shape, low_type),
            pltpu.VMEM((2, 3, length, head_slab), low_type),
            pltpu.VMEM((head_slab, length), low_type),
            pltpu.VMEM((2, head_slab // DH, length), full_type),
            pltpu.VMEM((2, length, head_slab), low_type),
            pltpu.VMEM((3, share, head_slab), low_type),
            pltpu.VMEM((4,) + w_out.shape, low_type),
            pltpu.VMEM((2,) + w_in.shape, low_type),
            pltpu.VMEM((2 * slab, width), low_type),
            pltpu.VMEM((2, 1, slab), full_type),
            pltpu.VMEM((share, width), low_type),
            pltpu.VMEM((share, width), low_type),
            pltpu.VMEM((share, width), full_type),
            pltpu.VMEM((share, width), full_type),
            pltpu.VMEM((share, 1), full_type),
            pltpu.VMEM((2, share, width), low_type),
            pltpu.VMEM((2, share, 2 * slab), full_type),
            pltpu.VMEM((2, share, 2 * slab), low_type),
            pltpu.VMEM((share, width), full_type),
            pltpu.VMEM((share, width), full_type),
            pltpu.VMEM((share, width), full_type),
            pltpu.VMEM((share, width), full_type),
            pltpu.VMEM((2, share, width), low_type),
            pltpu.VMEM((share, width), low_type),
            pltpu.SemaphoreType.DMA((8,)),
            pltpu.SemaphoreType.DMA((20,)),
            pltpu.SemaphoreType.DMA((6,)),
            pltpu.SemaphoreType.DMA((18,)),
            pltpu.SemaphoreType.DMA((18,)),
        ],
        compiler_params=pltpu.CompilerParams(
            collective_id=3, has_side_effects=True, vmem_limit_bytes=VMEM_GRANT
        ),
        name="front",
    )(tokens, cotangent, planes, w_out, w_in, w_down, head_bias, unit_bias, vectors, seg_keys,
      seg_queries)


def middle_kernel(in_ref, in_two, down_ref, down_two, out_ref, out_rest, branch_ref, slope_ref,
                  normed_ref, inverse_ref, wide_ref, pieces_ref, vec_ref,
                  hidden_out, norm_out, attn_out, near_out, far_out, out_sum, out_far,
                  unit_ref, unit_two, sums_ref,
                  w_in, w_down, w_out, branch, slope, normed, inverse, wide, hidden, part, other,
                  acc, attn, near, far_mixed, pieces, outs, outs_two,
                  load_sem, store_sem, send_sem, recv_sem):
    dp_place = lax.axis_index("dp")
    tensor_place = lax.axis_index("tensor")
    core = lax.rem(tensor_place, 2)
    far = 1 - tensor_place // 2
    sibling = (dp_place, tensor_place + 1 - 2 * core)
    opposite = (dp_place, core + 2 * far)
    share, width = normed.shape
    slab = in_ref.shape[1]
    loads = [
        pltpu.make_async_copy(source, target, load_sem.at[number])
        for number, (source, target) in enumerate(
            [
                (branch_ref, branch), (down_ref, w_down.at[pl.ds(0, slab)]),
                (slope_ref.at[0], slope.at[0]), (down_two, w_down.at[pl.ds(slab, slab)]),
                (slope_ref.at[1], slope.at[1]), (in_ref, w_in.at[0]), (in_two, w_in.at[1]),
                (wide_ref, wide), (normed_ref, normed), (inverse_ref, inverse),
                (out_ref, w_out.at[0]), (out_rest, w_out.at[pl.ds(1, 3)]), (pieces_ref, pieces),
            ]
        )
    ]
    for load in loads:
        load.start()
    barrier = pltpu.get_barrier_semaphore()
    for device in (sibling, opposite):
        pl.semaphore_signal(barrier, inc=1, device_id=device, device_id_type=MESH)
    pl.semaphore_wait(barrier, 2)
    sums_ref[...] = jnp.zeros_like(sums_ref)
    unit_ref[...] = jnp.zeros_like(unit_ref)
    stores = []
    sends = []

    def store(source, target):
        copy = pltpu.make_async_copy(source, target, store_sem.at[len(stores)])
        copy.start()
        stores.append(copy)

    def send(source, target, device):
        number = len(sends)
        copy = pltpu.make_async_remote_copy(
            src_ref=source,
            dst_ref=target,
            send_sem=send_sem.at[number],
            recv_sem=recv_sem.at[number],
            device_id=device,
            device_id_type=MESH,
        )
        copy.start()
        sends.append(copy)
        return copy

    chunk = 256
    small = 64

    def rows_of(number, size):
        return pl.ds(pl.multiple_of(number * size, size), size)

    def grad_hidden_of(slot, owner):
        def units(step, carry):
            outer = pl.ds(pl.multiple_of(owner * slab + step * chunk, chunk), chunk)
            grad = dot_nt(branch[slot], w_down[outer]) * slope[slot, :, outer]
            grad_low = grad.astype(jnp.bfloat16)
            hidden[slot, :, outer] = grad_low
            unit_ref[:, outer] += jnp.sum(grad_low.astype(jnp.float32), axis=0, keepdims=True)
            return carry

        lax.fori_loop(0, slab // chunk, units, 0)

    def grad_first_of(slot, target):
        def columns(step, carry):
            at = rows_of(step, chunk)
            target[:, at] = dot_nt(hidden[slot, :, :slab], w_in[0, at]) + dot_nt(
                hidden[slot, :, slab:], w_in[1, at]
            )
            return carry

        lax.fori_loop(0, width // chunk, columns, 0)

    for load in loads[:3]:
        load.wait()
    grad_hidden_of(0, 0)
    loads[3].wait()
    grad_hidden_of(0, 1)
    loads[4].wait()
    grad_hidden_of(1, 0)
    grad_hidden_of(1, 1)
    unit_send = send(unit_ref.at[:, pl.ds(slab, slab)], unit_two, opposite)
    store(hidden, hidden_out)
    loads[5].wait()
    loads[6].wait()
    grad_first_of(1, part)
    first_send = send(part, other, sibling)
    grad_first_of(0, acc)
    for load in loads[7:]:
        load.wait()
    first_send.wait_recv()

    def back_rows(step, carry):
        rows = rows_of(step, small)
        grad = acc[rows] + other[rows] + wide[rows]
        unit = normed[rows]
        scaled = grad * vec_ref[2:3]
        back = inverse[rows] * (scaled - row_mean(scaled) - unit * row_mean(scaled * unit))
        acc[rows] = back
        back_low = back.astype(jnp.bfloat16)
        attn[rows] = back_low
        sums_ref[0:1] += jnp.sum(back_low.astype(jnp.float32), axis=0, keepdims=True)
        sums_ref[2:3] += jnp.sum(grad * unit, axis=0, keepdims=True)
        sums_ref[3:4] += jnp.sum(grad, axis=0, keepdims=True)
        return carry

    lax.fori_loop(0, share // small, back_rows, 0)
    store(acc, norm_out)
    near[1] = dot_nt(attn[...], w_out[1]).astype(jnp.bfloat16)
    near_send = send(near.at[1], near.at[2], sibling)
    far_mixed[0] = dot_nt(attn[...], w_out[2]).astype(jnp.bfloat16)
    far_mixed[1] = dot_nt(attn[...], w_out[3]).astype(jnp.bfloat16)
    store(far_mixed, far_out)
    near[0] = dot_nt(attn[...], w_out[0]).astype(jnp.bfloat16)
    store(near.at[0], near_out.at[0])
    outs[1] = dot_tn(pieces[1], attn[...])
    outs[3] = dot_tn(pieces[3], attn[...])
    outs_sends = [
        send(outs.at[1], outs_two.at[0], sibling),
        send(outs.at[3], outs_two.at[1], sibling),
    ]
    outs[0] = dot_tn(pieces[0], attn[...])
    outs[2] = dot_tn(pieces[2], attn[...])
    near_send.wait_recv()
    store(near.at[2], near_out.at[1])
    for copy in outs_sends:
        copy.wait_recv()
    out_sum[...] = outs[0] + outs_two[0]
    out_far[...] = (outs[2] + outs_two[1]).astype(jnp.bfloat16)
    unit_send.wait_recv()
    for copy in sends:
        copy.wait_send()
    for copy in stores:
        copy.wait()


def middle(w_in, in_two, w_down, down_two, w_out, out_rest, branch, slope, normed, inverse, wide,
           pieces, vectors):
    share, width = normed.shape
    slab = w_in.shape[1]
    head_slab = w_out.shape[0]
    low_type, full_type = jnp.bfloat16, jnp.float32
    vmem = pl.BlockSpec(memory_space=pltpu.VMEM)
    anywhere = pl.BlockSpec(memory_space=pl.ANY)
    shapes = [
        jax.ShapeDtypeStruct((2, share, 2 * slab), low_type),
        jax.ShapeDtypeStruct((share, width), full_type),
        jax.ShapeDtypeStruct((share, width), low_type),
        jax.ShapeDtypeStruct((2, share, head_slab), low_type),
        jax.ShapeDtypeStruct((2, share, head_slab), low_type),
        jax.ShapeDtypeStruct((head_slab, width), full_type),
        jax.ShapeDtypeStruct((head_slab, width), low_type),
        jax.ShapeDtypeStruct((1, 2 * slab), full_type),
        jax.ShapeDtypeStruct((1, slab), full_type),
        jax.ShapeDtypeStruct((6, width), full_type),
    ]
    return pl.pallas_call(
        middle_kernel,
        in_specs=[anywhere] * 12 + [vmem],
        out_specs=[anywhere] * 2 + [anywhere] * 3 + [vmem] * 5,
        out_shape=shapes,
        scratch_shapes=[
            pltpu.VMEM((2,) + w_in.shape, low_type),
            pltpu.VMEM((2 * slab, width), low_type),
            pltpu.VMEM((4,) + w_out.shape, low_type),
            pltpu.VMEM((2, share, width), low_type),
            pltpu.VMEM((2, share, 2 * slab), full_type),
            pltpu.VMEM((share, width), full_type),
            pltpu.VMEM((share, 1), full_type),
            pltpu.VMEM((share, width), full_type),
            pltpu.VMEM((2, share, 2 * slab), low_type),
            pltpu.VMEM((share, width), full_type),
            pltpu.VMEM((share, width), full_type),
            pltpu.VMEM((share, width), full_type),
            pltpu.VMEM((share, width), low_type),
            pltpu.VMEM((3, share, head_slab), low_type),
            pltpu.VMEM((2, share, head_slab), low_type),
            pltpu.VMEM((4, share, head_slab), low_type),
            pltpu.VMEM((4, head_slab, width), full_type),
            pltpu.VMEM((2, head_slab, width), full_type),
            pltpu.SemaphoreType.DMA((13,)),
            pltpu.SemaphoreType.DMA((8,)),
            pltpu.SemaphoreType.DMA((6,)),
            pltpu.SemaphoreType.DMA((6,)),
        ],
        compiler_params=pltpu.CompilerParams(
            collective_id=4, has_side_effects=True, vmem_limit_bytes=VMEM_GRANT
        ),
        cost_estimate=pl.CostEstimate(
            flops=2 * share * width * (8 * slab + 8 * head_slab),
            bytes_accessed=60 * share * width, transcendentals=0,
        ),
        name="middle",
    )(w_in, in_two, w_down, down_two, w_out, out_rest, branch, slope, normed, inverse, wide,
      pieces, vectors)


def layer_general(tokens, segments, w_qkv, head_bias, w_out, w_in, unit_bias, w_down, vectors,
                  cotangent):
    token_count, model_width = tokens.shape
    seq_count, length = segments.shape
    head_slab = w_qkv.shape[2]
    head_count = head_slab // DH
    tensor_size = lax.axis_size("tensor")
    share_rows = token_count // tensor_size
    tensor_place = lax.axis_index("tensor")
    row_start = tensor_place * share_rows
    head_scale = 1.0 / math.sqrt(DH)

    def own_rows(values):
        return lax.dynamic_slice_in_dim(values, row_start, share_rows, 0)

    flat_qkv = w_qkv.reshape(model_width, 3 * head_slab)
    projected = jnp.dot(tokens, flat_qkv, preferred_element_type=jnp.float32).reshape(
        token_count, 3, head_slab
    )
    head_shape = (seq_count, length, head_count, DH)
    queries = (
        ((projected[:, 0] + head_bias[0]) * head_scale).astype(jnp.bfloat16).reshape(head_shape)
    )
    key_heads = projected[:, 1].astype(jnp.bfloat16).reshape(head_shape)
    value_heads = (projected[:, 2] + head_bias[1]).astype(jnp.bfloat16).reshape(head_shape)
    mixed_heads, log_total = lax.map(attend_forward, (queries, key_heads, value_heads, segments))
    mixed_flat = mixed_heads.reshape(token_count, head_slab)
    attn_out = (
        lax.psum(jnp.dot(mixed_flat, w_out, preferred_element_type=jnp.float32), "tensor")
        + vectors[0]
    )
    first_norm, first_normed, first_inverse = norm_forward(
        tokens.astype(jnp.float32) + attn_out, vectors[2], vectors[3]
    )
    first_low = first_norm.astype(jnp.bfloat16)
    hidden = jnp.dot(first_low, w_in, preferred_element_type=jnp.float32) + unit_bias
    active, gelu_back = jax.vjp(partial(jax.nn.gelu, approximate=False), hidden)
    active_low = active.astype(jnp.bfloat16)
    grad_out_share = own_rows(cotangent).astype(jnp.float32)
    summed_input = (
        first_norm
        + lax.psum(jnp.dot(active_low, w_down, preferred_element_type=jnp.float32), "tensor")
        + vectors[1]
    )
    second_norm, second_normed, second_inverse = norm_forward(summed_input, vectors[4], vectors[5])
    layer_out = own_rows(second_norm).astype(jnp.bfloat16)
    grad_sum = norm_backward(
        cotangent.astype(jnp.float32), second_normed, second_inverse, vectors[4]
    )
    grad_branch = grad_sum.astype(jnp.bfloat16)
    second_share = own_rows(second_normed)
    grad_w_down = trans_times(active_low, grad_branch)
    grad_active = times_trans(grad_branch, w_down)
    grad_hidden = gelu_back(grad_active)[0].astype(jnp.bfloat16)
    grad_w_in = trans_times(first_low, grad_hidden)
    grad_units = jnp.sum(grad_hidden.astype(jnp.float32), axis=0)
    grad_first = lax.psum(times_trans(grad_hidden, w_in), "tensor") + grad_sum
    grad_h1 = norm_backward(grad_first, first_normed, first_inverse, vectors[2])
    grad_attn = grad_h1.astype(jnp.bfloat16)
    grad_first_share = own_rows(grad_first)
    first_normed_share = own_rows(first_normed)
    grad_h1_share = own_rows(grad_h1)
    grad_w_out = trans_times(mixed_flat, grad_attn)
    grad_mixed = times_trans(grad_attn, w_out).astype(jnp.bfloat16).reshape(head_shape)
    grad_query, grad_key, grad_value = lax.map(
        attend_backward, (queries, key_heads, value_heads, segments, grad_mixed, log_total)
    )
    grad_query = (
        grad_query.reshape(token_count, head_slab).astype(jnp.float32) * head_scale
    ).astype(jnp.bfloat16)
    grad_key = grad_key.reshape(token_count, head_slab)
    grad_value = grad_value.reshape(token_count, head_slab)
    grad_projected = jnp.stack([grad_query, grad_key, grad_value], axis=1).reshape(
        token_count, 3 * head_slab
    )
    grad_w_qkv = trans_times(tokens, grad_projected)
    grad_heads = jnp.stack(
        [
            jnp.sum(grad_query.astype(jnp.float32), axis=0),
            jnp.sum(grad_value.astype(jnp.float32), axis=0),
        ]
    )
    grad_tokens = (
        lax.psum_scatter(
            times_trans(grad_projected, flat_qkv).astype(jnp.bfloat16),
            "tensor",
            scatter_dimension=0,
            tiled=True,
        ).astype(jnp.float32)
        + grad_h1_share
    )
    local_vectors = jnp.stack(
        [
            jnp.sum(own_rows(grad_attn).astype(jnp.float32), axis=0),
            jnp.sum(own_rows(grad_branch).astype(jnp.float32), axis=0),
            jnp.sum(grad_first_share * first_normed_share, axis=0),
            jnp.sum(grad_first_share, axis=0),
            jnp.sum(grad_out_share * second_share, axis=0),
            jnp.sum(grad_out_share, axis=0),
        ]
    )
    return (
        layer_out,
        grad_tokens,
        (
            grad_w_qkv.reshape(model_width, 3, head_slab).transpose(1, 0, 2),
            grad_w_out,
            grad_w_in,
            grad_w_down,
        ),
        local_vectors,
        grad_heads,
        grad_units,
    )


def layer_split(tokens, segments, w_qkv, head_bias, w_out, w_in, unit_bias, w_down, vectors,
                cotangent):
    token_count, model_width = tokens.shape
    seq_count, length = segments.shape
    unit_slab = w_in.shape[1]
    tensor_size = lax.axis_size("tensor")
    share = token_count // tensor_size
    tensor_place = lax.axis_index("tensor")
    core = lax.rem(tensor_place, 2)
    seq = tensor_place // 2

    def to(values, step):
        return lax.ppermute(
            values, "tensor", [(place, place ^ step) for place in range(tensor_size)]
        )

    def rows_at(values, number, size):
        return lax.dynamic_slice_in_dim(values, number * size, size, 0)

    planes = w_qkv.transpose(1, 0, 2)
    seg_keys = jnp.broadcast_to(segments[:, :, None], (seq_count, length, LANES))
    seg_queries = segments[:, None, :]
    (projected, logs, in_two, down_two, out_rest, _, pieces, layer_out, low, active, grad_branch,
     slope, normed, inverse, wide, sums_one) = front(
        tokens, cotangent, planes, w_out, w_in, w_down, head_bias, unit_bias[None], vectors,
        seg_keys, seg_queries,
    )
    active_rows = active.reshape(2 * share, 2 * unit_slab)
    branch_rows = grad_branch.reshape(2 * share, model_width)
    low_rows = low.reshape(2 * share, model_width)
    down_far = to(trans_times(active_rows[:, unit_slab:], branch_rows).astype(jnp.bfloat16), 2)
    (grad_hidden, grad_h1, _, grad_near, grad_far, out_sum, out_far, units, unit_two, sums_two
     ) = middle(
        w_in, in_two, w_down, down_two, w_out, out_rest, grad_branch, slope, normed, inverse, wide,
        pieces, vectors,
    )
    hidden_rows = grad_hidden.reshape(2 * share, 2 * unit_slab)
    far_own = to(grad_far[0:1], 2)
    far_other = to(grad_far[1:2], 3)
    in_far = to(trans_times(low_rows, hidden_rows[:, unit_slab:]).astype(jnp.bfloat16), 2)
    out_back = to(out_far, 2)

    grad_projected = jnp.zeros_like(projected)
    grad_projected, heads_near = attend_back(
        projected, seg_keys, seg_queries, (grad_near, 0), (grad_near, 1), logs, 1,
        grad_projected, seq, core,
    )
    grad_projected, heads_far = attend_back(
        projected, seg_keys, seg_queries, (far_own, 0), (far_other, 0), logs, 0,
        grad_projected, 1 - seq, core,
    )
    token_part = jnp.einsum(
        "gtn,gdn->td", grad_projected, planes, preferred_element_type=jnp.float32
    ).astype(jnp.bfloat16)
    other_one = to(
        jnp.stack([rows_at(token_part, 2 * at + 1 - core, share) for at in (seq, 1 - seq)]), 1
    ).astype(jnp.float32)
    across_part = rows_at(token_part, 2 * (1 - seq) + core, share).astype(jnp.float32)
    from_two = to((across_part + other_one[1]).astype(jnp.bfloat16), 2)
    grad_tokens = (
        rows_at(token_part, 2 * seq + core, share).astype(jnp.float32)
        + other_one[0]
        + from_two.astype(jnp.float32)
        + grad_h1
    )
    grad_w_qkv = jnp.einsum(
        "td,gtn->gdn", tokens, grad_projected, preferred_element_type=jnp.float32
    )
    grad_w_down = trans_times(active_rows[:, :unit_slab], branch_rows) + down_far.astype(
        jnp.float32
    )
    grad_w_in = trans_times(low_rows, hidden_rows[:, :unit_slab]) + in_far.astype(jnp.float32)
    grad_w_out = out_sum + out_back.astype(jnp.float32)
    return (
        layer_out,
        grad_tokens,
        (grad_w_qkv, grad_w_out, grad_w_in, grad_w_down),
        sums_one + sums_two,
        heads_near + heads_far,
        units[0, :unit_slab] + unit_two[0],
    )


def local(
    tokens,
    segments,
    w_qkv,
    head_bias,
    w_out,
    w_in,
    unit_bias,
    w_down,
    vectors,
    cotangent,
    err_qkv,
    err_out,
    err_in,
    err_down,
    basis_qkv,
    basis_out,
    basis_in,
    basis_down,
    mom_qkv,
    mom_head_bias,
    mom_out,
    mom_in,
    mom_unit_bias,
    mom_down,
    mom_vectors,
):
    token_count, model_width = tokens.shape
    head_slab = w_qkv.shape[2]
    unit_slab = w_in.shape[1]
    tensor_size = lax.axis_size("tensor")
    replicas = lax.axis_size("dp")
    one_sequence_per_chip = 2 * segments.shape[0] == tensor_size and replicas % 2 == 0
    layer = layer_split if one_sequence_per_chip else layer_general
    layer_out, grad_tokens, grads, local_vectors, grad_heads, grad_units = layer(
        tokens, segments, w_qkv, head_bias, w_out, w_in, unit_bias, w_down, vectors, cotangent
    )
    grad_w_qkv, grad_w_out, grad_w_in, grad_w_down = grads
    small = jnp.concatenate(
        [
            local_vectors,
            jnp.pad(grad_units, (0, model_width - unit_slab))[None],
            jnp.pad(grad_heads.reshape(1, 2 * head_slab), ((0, 0), (0, model_width - 2 * head_slab))),
        ],
        axis=0,
    )
    planes = (1, 0, 2)
    combined_qkv = grad_w_qkv + err_qkv[0].transpose(planes)
    combined_out = grad_w_out + err_out[0]
    combined_in = grad_w_in + err_in[0]
    combined_down = grad_w_down + err_down[0]
    matrices = (combined_qkv, combined_out, combined_in, combined_down)
    bases, rights, small_sum = compress(
        matrices,
        (basis_qkv.transpose(planes), basis_out, basis_in, basis_down),
        small,
        replicas,
        tensor_size,
    )
    step_rate = 0.3 * math.sqrt(replicas / token_count)
    grads, errors, moments, news = update(
        matrices,
        (mom_qkv.transpose(planes), mom_out, mom_in, mom_down),
        (w_qkv.transpose(planes), w_out, w_in, w_down),
        bases,
        rights,
        step_rate,
    )
    reduced_qkv, rank_out, rank_in, rank_down = (grads[0].transpose(planes),) + tuple(grads[1:])
    new_err_qkv, new_err_out, new_err_in, new_err_down = (
        errors[0].transpose(planes)[None],
        errors[1][None],
        errors[2][None],
        errors[3][None],
    )
    new_mom_qkv, new_mom_out, new_mom_in, new_mom_down = (moments[0].transpose(planes),) + tuple(
        moments[1:]
    )
    new_w_qkv, new_w_out, new_w_in, new_w_down = (news[0].transpose(planes),) + tuple(news[1:])
    right_qkv, right_out, right_in, right_down = rights
    new_basis_qkv = right_qkv.transpose(planes)
    grad_vectors = small_sum[:6]
    grad_unit_bias = small_sum[6, :unit_slab]
    grad_head_bias = small_sum[7, : 2 * head_slab].reshape(2, head_slab)
    new_mom_head_bias = 0.9 * mom_head_bias + grad_head_bias
    new_mom_unit_bias = 0.9 * mom_unit_bias + grad_unit_bias
    new_mom_vectors = 0.9 * mom_vectors + grad_vectors
    new_head_bias = head_bias - step_rate * new_mom_head_bias
    new_unit_bias = unit_bias - step_rate * new_mom_unit_bias
    new_vectors = vectors - step_rate * new_mom_vectors
    return (
        layer_out,
        grad_tokens,
        reduced_qkv,
        grad_head_bias,
        rank_out,
        rank_in,
        grad_unit_bias,
        rank_down,
        grad_vectors,
        new_err_qkv,
        new_err_out,
        new_err_in,
        new_err_down,
        new_basis_qkv,
        right_out,
        right_in,
        right_down,
        new_mom_qkv,
        new_mom_head_bias,
        new_mom_out,
        new_mom_in,
        new_mom_unit_bias,
        new_mom_down,
        new_mom_vectors,
        new_w_qkv,
        new_head_bias,
        new_w_out,
        new_w_in,
        new_unit_bias,
        new_w_down,
        new_vectors,
    )


def solution(mesh):
    in_specs = (
        P("dp", None),
        P("dp", None),
        P(None, None, "tensor"),
        P(None, "tensor"),
        P("tensor", None),
        P(None, "tensor"),
        P("tensor"),
        P("tensor", None),
        P(),
        P("dp", None),
        P("dp", None, None, "tensor"),
        P("dp", "tensor", None),
        P("dp", None, "tensor"),
        P("dp", "tensor", None),
        P(None, None, "tensor"),
        P("tensor", None),
        P(None, "tensor"),
        P("tensor", None),
        P(None, None, "tensor"),
        P(None, "tensor"),
        P("tensor", None),
        P(None, "tensor"),
        P("tensor"),
        P("tensor", None),
        P(),
    )
    out_specs = (
        P(("dp", "tensor"), None),
        P(("dp", "tensor"), None),
        P(None, None, "tensor"),
        P(None, "tensor"),
        P("tensor", None),
        P(None, "tensor"),
        P("tensor"),
        P("tensor", None),
        P(),
        P("dp", None, None, "tensor"),
        P("dp", "tensor", None),
        P("dp", None, "tensor"),
        P("dp", "tensor", None),
        P(None, None, "tensor"),
        P("tensor", None),
        P(None, "tensor"),
        P("tensor", None),
        P(None, None, "tensor"),
        P(None, "tensor"),
        P("tensor", None),
        P(None, "tensor"),
        P("tensor"),
        P("tensor", None),
        P(),
        P(None, None, "tensor"),
        P(None, "tensor"),
        P("tensor", None),
        P(None, "tensor"),
        P("tensor"),
        P("tensor", None),
        P(),
    )
    return jax.shard_map(local, mesh=mesh, in_specs=in_specs, out_specs=out_specs, check_vma=False)
```

```python
from functools import partial
import math

import jax
import jax.numpy as jnp
from jax import lax
from jax.experimental import pallas as pl
from jax.experimental.pallas import tpu as pltpu
from jax.sharding import PartitionSpec as P

DH = 64
LANES = 128
MESH = pl.DeviceIdType.MESH
VMEM_GRANT = 60 << 20


PRECISE = lax.Precision.HIGHEST
EPS_NORM = 1e-05
EPS_BASIS = 1e-08
MASKED = -1000000000.0


def norm_forward(values, gain, shift):
    row_mean = jnp.mean(values, axis=-1, keepdims=True)
    centred = values - row_mean
    variance = jnp.mean(centred * centred, axis=-1, keepdims=True)
    inverse = lax.rsqrt(variance + EPS_NORM)
    normed = centred * inverse
    return (normed * gain + shift, normed, inverse)


def norm_backward(grad_norm, normed, inverse, gain):
    scaled_grad = grad_norm * gain
    grad_mean = jnp.mean(scaled_grad, axis=-1, keepdims=True)
    along_norm = jnp.mean(scaled_grad * normed, axis=-1, keepdims=True)
    return inverse * (scaled_grad - grad_mean - normed * along_norm)


def times_trans(left_side, right_side):
    return lax.dot_general(
        left_side, right_side, (((1,), (1,)), ((), ())), preferred_element_type=jnp.float32
    )


def trans_times(left_side, right_side):
    return lax.dot_general(
        left_side, right_side, (((0,), (0,)), ((), ())), preferred_element_type=jnp.float32
    )


def split_bf16(values):
    high = values.astype(jnp.bfloat16)
    low = (values - high.astype(jnp.float32)).astype(jnp.bfloat16)
    return high, low


def dot_nt(left_side, right_side):
    return lax.dot_general(
        left_side, right_side, (((1,), (1,)), ((), ())), preferred_element_type=jnp.float32
    )


def dot_nn(left_side, right_side):
    return lax.dot_general(
        left_side, right_side, (((1,), (0,)), ((), ())), preferred_element_type=jnp.float32
    )


def dot_tn(left_side, right_side):
    return lax.dot_general(
        left_side, right_side, (((0,), (0,)), ((), ())), preferred_element_type=jnp.float32
    )


def left_factor(factor, matrix):
    rank_size = factor.shape[0]
    factor_high, factor_low = split_bf16(factor)
    matrix_high, matrix_low = split_bf16(matrix)
    both = dot_nt(jnp.concatenate([factor_high, factor_low], axis=0), matrix_high)
    return both[:rank_size] + both[rank_size:] + dot_nt(factor_high, matrix_low)


def right_factor(basis_rows, matrix):
    rank_size = basis_rows.shape[0]
    basis_high, basis_low = split_bf16(basis_rows)
    matrix_high, matrix_low = split_bf16(matrix)
    both = dot_nn(jnp.concatenate([basis_high, basis_low], axis=0), matrix_high)
    return both[:rank_size] + both[rank_size:] + dot_nn(basis_high, matrix_low)


def place_tiles(target, offset, values):
    per_chunk = target.shape[2] // LANES
    for tile in range(values.shape[1] // LANES):
        spot = offset + tile
        target[spot // per_chunk, :, pl.ds(spot % per_chunk * LANES, LANES)] = values[
            :, tile * LANES : (tile + 1) * LANES
        ]
    return offset + values.shape[1] // LANES


def take_tiles(source, offset, size):
    per_chunk = source.shape[2] // LANES
    pieces = []
    for tile in range(size // LANES):
        spot = offset + tile
        pieces.append(source[spot // per_chunk, :, pl.ds(spot % per_chunk * LANES, LANES)])
    return jnp.concatenate(pieces, axis=1) if len(pieces) > 1 else pieces[0]


def orthonormal_rows(rows):
    rank_size = rows.shape[0]
    row_number = lax.broadcasted_iota(jnp.int32, (rank_size, 1), 0)
    for position in range(rank_size):
        row = rows[position : position + 1]
        length = jnp.sqrt(jnp.sum(row * row, axis=1, keepdims=True)) + EPS_BASIS
        unit = row / length
        along = jnp.sum(rows * unit, axis=1, keepdims=True)
        later = jnp.where(row_number > position, along, 0.0)
        rows = jnp.where(row_number == position, unit, rows - later * unit)
    return rows


def dp_exchange(replicas, mine, wire, arrived, total, sems, meanwhile=None):
    send_one, recv_one, send_two, recv_two = sems
    dp_place = lax.axis_index("dp")
    tensor_place = lax.axis_index("tensor")

    def peer_of(step):
        return lax.rem(dp_place + step, replicas)

    def scatter(step, slot):
        return pltpu.make_async_remote_copy(
            src_ref=wire.at[peer_of(step)],
            dst_ref=arrived.at[slot],
            send_sem=send_one.at[step],
            recv_sem=recv_one.at[slot],
            device_id=(peer_of(step), tensor_place),
            device_id_type=MESH,
        )

    def gather(step, slot):
        return pltpu.make_async_remote_copy(
            src_ref=total.at[dp_place],
            dst_ref=total.at[slot],
            send_sem=send_two.at[step],
            recv_sem=recv_two.at[slot],
            device_id=(peer_of(step), tensor_place),
            device_id_type=MESH,
        )

    def start_scatter(step, carry):
        scatter(step, dp_place).start()
        return carry

    def add_arrived(step, carry):
        scatter(step, peer_of(step)).wait_recv()
        return carry + arrived[peer_of(step)].astype(jnp.float32)

    def start_gather(step, carry):
        gather(step, dp_place).start()
        return carry

    def finish(step, carry):
        gather(step, peer_of(step)).wait_recv()
        return carry

    wire[...] = mine[...].astype(wire.dtype)
    lax.fori_loop(1, replicas, start_scatter, 0)
    total[dp_place] = lax.fori_loop(1, replicas, add_arrived, mine[dp_place])
    lax.fori_loop(1, replicas, start_gather, 0)
    lax.fori_loop(1, replicas, finish, 0)

    def drain(step, carry):
        scatter(step, dp_place).wait_send()
        gather(step, dp_place).wait_send()
        return carry

    return lambda: lax.fori_loop(1, replicas, drain, 0)


def compress_kernel(replicas, tensor_size, qkv_ref, out_ref, in_ref, down_ref,
                    fq_ref, fo_ref, fi_ref, fd_ref, small_ref,
                    bq_ref, bo_ref, bi_ref, bd_ref, rq_ref, ro_ref, ri_ref, rd_ref, sum_ref,
                    qkv, out, inw, down, mine, wire, arrived, total,
                    mine_two, wire_two, arrived_two, total_two, small_slots,
                    load_sem, *sems):
    first_sems, second_sems, (send_small, recv_small) = sems[:4], sems[4:8], sems[8:]
    dp_place = lax.axis_index("dp")
    tensor_place = lax.axis_index("tensor")
    loads = [
        pltpu.make_async_copy(source, target, load_sem.at[number])
        for number, (source, target) in enumerate(
            [(qkv_ref, qkv), (out_ref, out), (down_ref, down), (in_ref, inw)]
        )
    ]
    for load in loads:
        load.start()
    barrier = pltpu.get_barrier_semaphore()

    def greet_dp(step, carry):
        pl.semaphore_signal(
            barrier,
            inc=1,
            device_id=(lax.rem(dp_place + step, replicas), tensor_place),
            device_id_type=MESH,
        )
        return carry

    def greet_tensor(step, carry):
        pl.semaphore_signal(
            barrier,
            inc=1,
            device_id=(dp_place, lax.rem(tensor_place + step, tensor_size)),
            device_id_type=MESH,
        )
        return carry

    lax.fori_loop(1, replicas, greet_dp, 0)
    lax.fori_loop(1, tensor_size, greet_tensor, 0)
    mine[...] = jnp.zeros_like(mine)
    mine_two[...] = jnp.zeros_like(mine_two)
    block = 2 * LANES
    offset = 0
    loads[0].wait()
    for start in range(0, qkv.shape[1], block):
        rows = slice(start, start + block)
        left = left_factor(fq_ref[0], qkv[0, rows])
        for part in range(1, 3):
            left += left_factor(fq_ref[part], qkv[part, rows])
        offset = place_tiles(mine, offset, left)
    for load, factor_ref, matrix in zip(loads[1:], (fo_ref, fd_ref, fi_ref), (out, down, inw)):
        load.wait()
        rows_of = min(block, matrix.shape[0])
        for start in range(0, matrix.shape[0], rows_of):
            left = left_factor(factor_ref[...], matrix[start : start + rows_of])
            offset = place_tiles(mine, offset, left)
    place_tiles(mine, offset, small_ref[...])
    pl.semaphore_wait(barrier, replicas - 1 + tensor_size - 1)
    drain_one = dp_exchange(replicas, mine, wire, arrived, total, first_sems)

    def slot_copy(step, slot):
        peer = lax.rem(tensor_place + step, tensor_size)
        return pltpu.make_async_remote_copy(
            src_ref=small_slots.at[tensor_place],
            dst_ref=small_slots.at[slot],
            send_sem=send_small.at[step],
            recv_sem=recv_small.at[slot],
            device_id=(dp_place, peer),
            device_id_type=MESH,
        )

    def start_small(step, carry):
        slot_copy(step, tensor_place).start()
        return carry

    own_small = take_tiles(total, offset, small_ref.shape[1])
    small_slots[tensor_place] = own_small
    lax.fori_loop(1, tensor_size, start_small, 0)
    offset = 0
    offset_two = 0
    for basis_ref in (bq_ref, bo_ref, bd_ref, bi_ref):
        rows = take_tiles(total, offset, basis_ref.shape[1]) * (1.0 / replicas)
        basis_ref[...] = orthonormal_rows(rows)
        offset += basis_ref.shape[1] // LANES
    drain_one()
    for part in range(3):
        right = right_factor(bq_ref[:, :block], qkv[part, :block])
        for start in range(block, qkv.shape[1], block):
            rows = slice(start, start + block)
            right += right_factor(bq_ref[:, rows], qkv[part, rows])
        offset_two = place_tiles(mine_two, offset_two, right)
    for basis_ref, matrix in zip((bo_ref, bd_ref, bi_ref), (out, down, inw)):
        rows_of = min(block, matrix.shape[0])
        right = right_factor(basis_ref[:, :rows_of], matrix[:rows_of])
        for start in range(rows_of, matrix.shape[0], rows_of):
            rows = slice(start, start + rows_of)
            right += right_factor(basis_ref[:, rows], matrix[rows])
        offset_two = place_tiles(mine_two, offset_two, right)
    drain_two = dp_exchange(
        replicas, mine_two, wire_two, arrived_two, total_two, second_sems
    )

    def collect(step, carry):
        peer = lax.rem(tensor_place + step, tensor_size)
        slot_copy(step, peer).wait_recv()
        slot_copy(step, tensor_place).wait_send()
        return carry + small_slots[peer]

    everyone = lax.fori_loop(1, tensor_size, collect, own_small)
    row_number = lax.broadcasted_iota(jnp.int32, everyone.shape, 0)
    sum_ref[...] = jnp.where(row_number < 6, everyone, own_small) * (1.0 / replicas)
    offset = 0
    for part in range(3):
        rq_ref[part] = take_tiles(total_two, offset, rq_ref.shape[2]) * (1.0 / replicas)
        offset += rq_ref.shape[2] // LANES
    for ref in (ro_ref, rd_ref, ri_ref):
        ref[...] = take_tiles(total_two, offset, ref.shape[1]) * (1.0 / replicas)
        offset += ref.shape[1] // LANES
    drain_two()


def compress(matrices, factors, small, replicas, tensor_size):
    qkv, out, inw, down = matrices
    rank_size = small.shape[0]
    sizes = (qkv.shape[1], out.shape[0], inw.shape[0], down.shape[0])
    right_shapes = [(3, rank_size, qkv.shape[2])] + [(rank_size, one.shape[1]) for one in matrices[1:]]
    lanes_one = sum(sizes) + small.shape[1]
    lanes_two = 3 * qkv.shape[2] + sum(one.shape[1] for one in matrices[1:])
    scratch = [pltpu.VMEM(one.shape, jnp.float32) for one in matrices]
    for lanes in (lanes_one, lanes_two):
        shape = (replicas, rank_size, -(-lanes // (LANES * replicas)) * LANES)
        scratch += [
            pltpu.VMEM(shape, jnp.float32),
            pltpu.VMEM(shape, jnp.bfloat16),
            pltpu.VMEM(shape, jnp.bfloat16),
            pltpu.VMEM(shape, jnp.float32),
        ]
    scratch += [pltpu.VMEM((tensor_size,) + small.shape, jnp.float32), pltpu.SemaphoreType.DMA((4,))]
    scratch += [pltpu.SemaphoreType.DMA((replicas,))] * 8
    scratch += [pltpu.SemaphoreType.DMA((tensor_size,))] * 2
    vmem = pl.BlockSpec(memory_space=pltpu.VMEM)
    shapes = [(rank_size, size) for size in sizes] + right_shapes + [small.shape]
    outputs = pl.pallas_call(
        partial(compress_kernel, replicas, tensor_size),
        in_specs=[pl.BlockSpec(memory_space=pl.ANY)] * 4 + [vmem] * 5,
        out_specs=[vmem] * 9,
        out_shape=[jax.ShapeDtypeStruct(shape, jnp.float32) for shape in shapes],
        scratch_shapes=scratch,
        compiler_params=pltpu.CompilerParams(
            collective_id=1, has_side_effects=True, vmem_limit_bytes=VMEM_GRANT
        ),
        name="compress",
    )(*matrices, *factors, small)
    return outputs[:4], outputs[4:8], outputs[8]


def outer_of(basis_rows, right):
    basis_high, basis_low = split_bf16(basis_rows)
    right_high, right_low = split_bf16(right)
    return dot_tn(
        jnp.concatenate([basis_high, basis_low, basis_high], axis=0),
        jnp.concatenate([right_high, right_high, right_low], axis=0),
    )


def update_kernel(step_rate, out_steps, *refs):
    (mq, mo, mi, md, oq, oo, oi, od, wq, wo, wi, wd, bq, bo, bi, bd, rq, ro, ri, rd,
     gq, go, gi, gd, eq, eo, ei, ed, nq, no, ni, nd, vq, vo, vi, vd) = refs
    step = pl.program_id(0)

    def one(matrix, old, weight, rank, grad_ref, err_ref, mom_ref, new_ref, place):
        moment = 0.9 * old + rank
        grad_ref[place] = rank
        err_ref[place] = matrix - rank
        mom_ref[place] = moment
        new_ref[place] = weight.astype(jnp.float32) - step_rate * moment

    def lanes_of(ref, rows):
        return ref[:, pl.ds(pl.multiple_of(step * rows, LANES), rows)]

    rows = mq.shape[1]
    for part in range(3):
        rank = outer_of(lanes_of(bq, rows), rq[part])
        one(mq[part], oq[part], wq[part], rank, gq, eq, nq, vq, part)
    rank = outer_of(lanes_of(bi, mi.shape[0]), ri[...])
    one(mi[...], oi[...], wi[...], rank, gi, ei, ni, vi, slice(None))
    rank = outer_of(lanes_of(bd, md.shape[0]), rd[...])
    one(md[...], od[...], wd[...], rank, gd, ed, nd, vd, slice(None))

    @pl.when(step < out_steps)
    def _():
        rank = outer_of(lanes_of(bo, mo.shape[0]), ro[...])
        one(mo[...], oo[...], wo[...], rank, go, eo, no, vo, slice(None))


def update(matrices, momenta, weights, bases, rights, step_rate):
    qkv, out, inw, down = matrices
    rows = LANES
    steps = inw.shape[0] // rows
    down_rows = down.shape[0] // steps
    if down_rows < LANES:
        steps = down.shape[0] // LANES
        rows, down_rows = inw.shape[0] // steps, LANES
    out_steps = out.shape[0] // LANES

    def whole(array):
        return pl.BlockSpec(array.shape, lambda i: (0,) * array.ndim)

    def specs():
        return [
            pl.BlockSpec((3, rows, qkv.shape[2]), lambda i: (0, i, 0)),
            pl.BlockSpec((LANES, out.shape[1]), lambda i: (jnp.minimum(i, out_steps - 1), 0)),
            pl.BlockSpec((rows, inw.shape[1]), lambda i: (i, 0)),
            pl.BlockSpec((down_rows, down.shape[1]), lambda i: (i, 0)),
        ]

    shapes = [jax.ShapeDtypeStruct(one.shape, jnp.float32) for one in matrices]
    outputs = pl.pallas_call(
        partial(update_kernel, step_rate, out_steps),
        grid=(steps,),
        in_specs=specs() * 3 + [whole(one) for one in bases] + [whole(one) for one in rights],
        out_specs=specs() * 4,
        out_shape=shapes * 4,
        compiler_params=pltpu.CompilerParams(vmem_limit_bytes=VMEM_GRANT),
        name="update",
    )(*matrices, *momenta, *weights, *bases, *rights)
    return outputs[0:4], outputs[4:8], outputs[8:12], outputs[12:16]


def masked_scores(queries, key_heads, seg_ids):
    scores = jnp.einsum("qhd,khd->hqk", queries, key_heads, preferred_element_type=jnp.float32)
    same_doc = seg_ids[:, None] == seg_ids[None, :]
    return jnp.where(same_doc[None], scores, MASKED)


def attend_forward(inputs_of):
    queries, key_heads, value_heads, seg_ids = inputs_of
    scores = masked_scores(queries, key_heads, seg_ids)
    highest = jnp.max(scores, axis=-1, keepdims=True)
    powers = jnp.exp(scores - highest)
    denominator = jnp.sum(powers, axis=-1, keepdims=True)
    weights = (powers / denominator).astype(jnp.bfloat16)
    mixed_heads = jnp.einsum(
        "hqk,khd->qhd", weights, value_heads, preferred_element_type=jnp.float32
    )
    return (mixed_heads.astype(jnp.bfloat16), highest[..., 0] + jnp.log(denominator[..., 0]))


def attend_backward(inputs_of):
    queries, key_heads, value_heads, seg_ids, grad_mixed, log_total = inputs_of
    scores = masked_scores(queries, key_heads, seg_ids)
    probability = jnp.exp(scores - log_total[..., None])
    grad_probs = jnp.einsum(
        "qhd,khd->hqk", grad_mixed, value_heads, preferred_element_type=jnp.float32
    )
    centre = jnp.sum(probability * grad_probs, axis=-1, keepdims=True)
    grad_scores = (probability * (grad_probs - centre)).astype(jnp.bfloat16)
    grad_query = jnp.einsum(
        "hqk,khd->qhd", grad_scores, key_heads, preferred_element_type=jnp.float32
    )
    grad_key = jnp.einsum("hqk,qhd->khd", grad_scores, queries, preferred_element_type=jnp.float32)
    grad_value = jnp.einsum(
        "hqk,qhd->khd",
        probability.astype(jnp.bfloat16),
        grad_mixed,
        preferred_element_type=jnp.float32,
    )
    return (
        grad_query.astype(jnp.bfloat16),
        grad_key.astype(jnp.bfloat16),
        grad_value.astype(jnp.bfloat16),
    )


def stacked_heads(pair, lane_is_low):
    zero = jnp.zeros_like(pair)
    return jnp.concatenate(
        [jnp.where(lane_is_low, pair, zero), jnp.where(lane_is_low, zero, pair)], axis=0
    )


def own_blocks(both):
    rows = both.shape[1] // 2
    return jnp.concatenate([both[:DH, :rows], both[DH:, rows:]], axis=0).T


def mask_bias(seg_key_ref, seg_query_ref):
    same = seg_key_ref[...] == seg_query_ref[...]
    bias = jnp.where(same, 0.0, MASKED)
    return jnp.concatenate([bias, bias], axis=1)


def attend_back_kernel(place_ref, q_ref, k_ref, v_ref, seg_key_ref, seg_query_ref, gm_own_ref,
                       gm_other_ref, log_ref, old_ref, grad_ref, sums_ref, key_t, grad_key, grad_value):
    del old_ref
    step = pl.program_id(0)

    @pl.when(step == 0)
    def _():
        key_t[...] = k_ref[...].T
        grad_key[...] = jnp.zeros_like(grad_key)
        grad_value[...] = jnp.zeros_like(grad_value)

    pairs = q_ref.shape[1] // LANES
    lane_is_low = lax.broadcasted_iota(jnp.int32, (1, LANES), 1) < DH
    bias = mask_bias(seg_key_ref, seg_query_ref)
    head_scale = 1.0 / math.sqrt(DH)
    here = pl.ds(pl.multiple_of(step * LANES, LANES), LANES)
    is_own = lax.rem(step // (pl.num_programs(0) // 2) + place_ref[1], 2) == 0
    gm = jnp.where(is_own, gm_own_ref[...], gm_other_ref[...])
    for pair in range(pairs):
        lanes = slice(pair * LANES, (pair + 1) * LANES)
        queries = stacked_heads(q_ref[:, lanes], lane_is_low)
        grads = stacked_heads(gm[:, lanes], lane_is_low)
        log_total = jnp.concatenate(
            [log_ref[2 * pair : 2 * pair + 1], log_ref[2 * pair + 1 : 2 * pair + 2]], axis=1
        )
        probs = jnp.exp(dot_nt(k_ref[:, lanes], queries) + (bias - log_total))
        grad_probs = dot_nt(v_ref[:, lanes], grads)
        centre = jnp.sum(probs * grad_probs, axis=0, keepdims=True)
        grad_scores = (probs * (grad_probs - centre)).astype(jnp.bfloat16)
        grad_value[:, lanes] += dot_nn(probs.astype(jnp.bfloat16), grads)
        grad_key[:, lanes] += dot_nn(grad_scores, queries)
        grad_query = own_blocks(dot_nn(key_t[lanes], grad_scores)).astype(jnp.bfloat16)
        grad_ref[0, here, lanes] = (grad_query.astype(jnp.float32) * head_scale).astype(
            jnp.bfloat16
        )

    @pl.when(step == pl.num_programs(0) - 1)
    def _():
        grad_ref[1] = grad_key[...].astype(jnp.bfloat16)
        low_value = grad_value[...].astype(jnp.bfloat16)
        grad_ref[2] = low_value
        sums_ref[0:1] = jnp.sum(grad_ref[0].astype(jnp.float32), axis=0, keepdims=True)
        sums_ref[1:2] = jnp.sum(low_value.astype(jnp.float32), axis=0, keepdims=True)


def attend_back(projected, seg_keys, seg_queries, grad_own, grad_other, logs, slot, old, place, core):
    length = seg_keys.shape[1]
    slab = projected.shape[2]
    blocks = length // LANES
    half = blocks // 2
    grid_spec = pltpu.PrefetchScalarGridSpec(
        num_scalar_prefetch=1,
        grid=(blocks,),
        in_specs=[
            pl.BlockSpec((None, LANES, slab), lambda i, at: (0, at[0] * blocks + i, 0)),
            pl.BlockSpec((None, length, slab), lambda i, at: (1, at[0], 0)),
            pl.BlockSpec((None, length, slab), lambda i, at: (2, at[0], 0)),
            pl.BlockSpec((None, length, LANES), lambda i, at: (at[0], 0, 0)),
            pl.BlockSpec((None, 1, LANES), lambda i, at: (at[0], 0, i)),
            pl.BlockSpec((None, LANES, slab), lambda i, at: (grad_own[1], lax.rem(i, half), 0)),
            pl.BlockSpec((None, LANES, slab), lambda i, at: (grad_other[1], lax.rem(i, half), 0)),
            pl.BlockSpec((None, slab // DH, LANES), lambda i, at: (slot, 0, i)),
            pl.BlockSpec(memory_space=pl.ANY),
        ],
        out_specs=[
            pl.BlockSpec((3, length, slab), lambda i, at: (0, at[0], 0)),
            pl.BlockSpec((2, slab), lambda i, at: (0, 0)),
        ],
        scratch_shapes=[
            pltpu.VMEM((slab, length), jnp.bfloat16),
            pltpu.VMEM((length, slab), jnp.float32),
            pltpu.VMEM((length, slab), jnp.float32),
        ],
    )
    return pl.pallas_call(
        attend_back_kernel,
        grid_spec=grid_spec,
        out_shape=[
            jax.ShapeDtypeStruct(projected.shape, jnp.bfloat16),
            jax.ShapeDtypeStruct((2, slab), jnp.float32),
        ],
        input_output_aliases={9: 0},
        compiler_params=pltpu.CompilerParams(vmem_limit_bytes=24 << 20),
        cost_estimate=pl.CostEstimate(
            flops=40 * length * length * slab, bytes_accessed=16 * length * slab,
            transcendentals=length * length * slab // DH,
        ),
        name="attend_back",
    )(jnp.stack([place, core]), projected, projected, projected, seg_keys, seg_queries, grad_own[0],
      grad_other[0], logs, old)


def row_mean(values):
    return jnp.mean(values, axis=-1, keepdims=True)


def front_kernel(tokens, cotangent, w_qkv_ref, out_ref, in_ref, down_ref,
                 head_ref, bias_ref, vec_ref, seg_keys, seg_queries,
                 projected_out, log_out, in_two, down_two, out_rest, bias_two, pieces_out,
                 result_out, low_out, active_out, branch_out, slope_out, normed_out, inverse_out,
                 wide_out, sums_ref,
                 rows_in, w_qkv, projected, value_t, log_total, mixed, pieces,
                 w_out, w_in, w_down, bias, tok, cot, first, normed, inverse, low, slope, active,
                 part, other, acc, wide, branch, result,
                 load_sem, store_sem, send_sem, recv_sem):
    dp_place = lax.axis_index("dp")
    tensor_place = lax.axis_index("tensor")
    core = lax.rem(tensor_place, 2)
    seq = tensor_place // 2
    far = 1 - seq
    side = lax.rem(dp_place, 2)
    depth = lax.rem(dp_place // 2, 2)
    here = 2 * depth + side
    sibling = (dp_place, tensor_place + 1 - 2 * core)
    opposite = (dp_place, core + 2 * far)
    diagonal = (dp_place, 1 - core + 2 * far)
    beside = (dp_place + 1 - 2 * side, tensor_place)
    behind = (dp_place + 2 - 4 * depth, tensor_place)
    share, width = tok.shape
    slab = in_ref.shape[1]
    length = rows_in.shape[1]
    head_slab = w_qkv.shape[2]
    head_count = head_slab // DH
    stores = []
    sends = []

    def load(number, source, target):
        copy = pltpu.make_async_copy(source, target, load_sem.at[number])
        copy.start()
        return copy

    def store(source, target):
        copy = pltpu.make_async_copy(source, target, store_sem.at[len(stores)])
        copy.start()
        stores.append(copy)

    def send(source, target, device):
        number = len(sends)
        copy = pltpu.make_async_remote_copy(
            src_ref=source,
            dst_ref=target,
            send_sem=send_sem.at[number],
            recv_sem=recv_sem.at[number],
            device_id=device,
            device_id_type=MESH,
        )
        copy.start()
        sends.append(copy)
        return copy

    def rows_of(number, size):
        return pl.ds(pl.multiple_of(number * size, LANES), size)

    load_qkv = load(0, w_qkv_ref, w_qkv)
    load_far = load(1, tokens.at[rows_of(far, length)], rows_in.at[0])
    load_near = load(2, tokens.at[rows_of(seq, length)], rows_in.at[1])
    load_out = load(3, out_ref, w_out.at[0])
    load_in = load(4, in_ref, w_in.at[0])
    load_down = load(5, down_ref, w_down.at[pl.ds(0, slab)])
    load_tok = load(6, tokens.at[rows_of(tensor_place, share)], tok)
    load_cot = load(7, cotangent.at[rows_of(tensor_place, share)], cot)

    barrier = pltpu.get_barrier_semaphore()
    for device in (sibling, opposite, diagonal, beside, behind):
        pl.semaphore_signal(barrier, inc=1, device_id=device, device_id_type=MESH)
    pl.semaphore_wait(barrier, 5)
    sums_ref[...] = jnp.zeros_like(sums_ref)

    def rows_part(whole, number, parts):
        size = whole.shape[0] // parts
        return whole.at[pl.ds(pl.multiple_of(number * size, size), size)]

    class Fetch:
        def __init__(self, source, whole):
            self.whole = whole
            self.over_y = send(
                rows_part(source, here, 4), rows_part(whole, here, 4), opposite
            )

        def pass_on(self):
            self.over_y.wait_recv()
            own = rows_part(self.whole, here, 4)
            self.over_x = send(own, own, beside)
            self.over_z = send(own, own, behind)

        def pass_halves(self):
            self.over_x.wait_recv()
            half = rows_part(self.whole, 2 * (here + 1 - 2 * side), 8)
            self.half_z = send(half, half, behind)
            self.over_z.wait_recv()
            half = rows_part(self.whole, 2 * (here + 2 - 4 * depth) + 1, 8)
            self.half_x = send(half, half, beside)

        def wait(self):
            self.half_z.wait_recv()
            self.half_x.wait_recv()

    bias_send = send(bias_ref, bias_two, opposite)
    fetch_out = Fetch(out_ref, out_rest.at[1])
    fetch_in = Fetch(in_ref, in_two)

    chunk = 256
    scale = 1.0 / math.sqrt(DH)

    def project(slot):
        def rows_step(step, carry):
            rows = rows_of(step, chunk)
            values = rows_in[slot, rows]
            projected[slot, 0, rows] = (
                (dot_nn(values, w_qkv[0]) + head_ref[0:1]) * scale
            ).astype(jnp.bfloat16)
            projected[slot, 1, rows] = dot_nn(values, w_qkv[1]).astype(jnp.bfloat16)
            projected[slot, 2, rows] = (dot_nn(values, w_qkv[2]) + head_ref[1:2]).astype(
                jnp.bfloat16
            )
            return carry

        lax.fori_loop(0, length // chunk, rows_step, 0)
        value_t[...] = projected[slot, 2].T

    lane_is_low = lax.broadcasted_iota(jnp.int32, (1, LANES), 1) < DH

    def attend_rows(slot, place, start, stop):
        def block(step, carry):
            rows = rows_of(step, LANES)
            same = seg_keys[place] == seg_queries[place, :, rows]
            mask = jnp.where(same, 0.0, MASKED)
            mask = jnp.concatenate([mask, mask], axis=1)
            for pair in range(head_count // 2):
                lanes = slice(pair * LANES, (pair + 1) * LANES)
                queries = stacked_heads(projected[slot, 0, rows, lanes], lane_is_low)
                scores = dot_nt(projected[slot, 1, :, lanes], queries) + mask
                highest = jnp.max(scores, axis=0, keepdims=True)
                powers = jnp.exp(scores - highest)
                denominator = jnp.sum(powers, axis=0, keepdims=True)
                weights = (powers * (1.0 / denominator)).astype(jnp.bfloat16)
                mixed[slot, rows, lanes] = own_blocks(dot_nn(value_t[lanes], weights)).astype(
                    jnp.bfloat16
                )
                total = highest + jnp.log(denominator)
                log_total[slot, 2 * pair : 2 * pair + 1, rows] = total[:, :LANES]
                log_total[slot, 2 * pair + 1 : 2 * pair + 2, rows] = total[:, LANES:]
            return carry

        lax.fori_loop(start, stop, block, 0)

    blocks = length // LANES
    load_qkv.wait()
    load_far.wait()
    project(0)
    attend_rows(0, far, 0, 5)
    fetch_out.pass_on()
    fetch_in.pass_on()
    fetch_down = Fetch(down_ref, down_two)
    attend_rows(0, far, 5, blocks)
    own_rows = rows_of(core, share)
    sibling_rows = rows_of(1 - core, share)
    piece_two = send(mixed.at[0, own_rows], pieces.at[1], opposite)
    piece_three = send(mixed.at[0, sibling_rows], pieces.at[2], diagonal)
    store(projected.at[0, 0], projected_out.at[0, rows_of(far, length)])
    store(projected.at[0, 1], projected_out.at[1, rows_of(far, length)])
    store(projected.at[0, 2], projected_out.at[2, rows_of(far, length)])
    load_near.wait()
    project(1)
    attend_rows(1, seq, 0, 3)
    fetch_out.pass_halves()
    fetch_in.pass_halves()
    attend_rows(1, seq, 3, 5)
    fetch_down.pass_on()
    fetch_out.wait()
    out_pass = [
        send(out_ref, out_rest.at[0], sibling),
        send(out_rest.at[1], out_rest.at[2], sibling),
    ]
    load_two = load(8, out_rest.at[1], w_out.at[2])
    attend_rows(1, seq, 5, blocks)
    piece_one = send(mixed.at[1, sibling_rows], pieces.at[0], sibling)
    store(projected.at[1, 0], projected_out.at[0, rows_of(seq, length)])
    store(projected.at[1, 1], projected_out.at[1, rows_of(seq, length)])
    store(projected.at[1, 2], projected_out.at[2, rows_of(seq, length)])
    store(log_total, log_out)
    for copy in out_pass:
        copy.wait_recv()
    load_one = load(9, out_rest.at[0], w_out.at[1])
    load_three = load(10, out_rest.at[2], w_out.at[3])
    store(mixed.at[1, own_rows], pieces_out.at[0])
    for copy in (load_out, load_tok, load_one, load_two, load_three):
        copy.wait()
    for copy in (piece_two, piece_three, piece_one):
        copy.wait_recv()
    for number in range(3):
        store(pieces.at[number], pieces_out.at[number + 1])
    small = 64

    def attn_rows(step, carry):
        rows = rows_of(step, chunk)
        total = dot_nn(mixed[1, pl.ds(pl.multiple_of(core * share + step * chunk, LANES), chunk)],
                       w_out[0])
        for piece in range(3):
            total += dot_nn(pieces[piece, rows], w_out[piece + 1])
        acc[rows] = total
        return carry

    def first_rows(step, carry):
        rows = pl.ds(pl.multiple_of(step * small, small), small)
        values = tok[rows].astype(jnp.float32) + (acc[rows] + vec_ref[0:1])
        centred = values - row_mean(values)
        spread = lax.rsqrt(row_mean(centred * centred) + EPS_NORM)
        unit = centred * spread
        normed[rows] = unit
        inverse[rows] = spread
        shifted = unit * vec_ref[2:3] + vec_ref[3:4]
        first[rows] = shifted
        low[0, rows] = shifted.astype(jnp.bfloat16)
        return carry

    lax.fori_loop(0, share // chunk, attn_rows, 0)
    lax.fori_loop(0, share // small, first_rows, 0)
    low_send = send(low.at[0], low.at[1], sibling)
    store(normed, normed_out)
    store(inverse, inverse_out)
    load_in.wait()

    def hidden_of(slot, owner):
        def units(step, carry):
            inner = rows_of(step, chunk)
            outer = pl.ds(pl.multiple_of(owner * slab + step * chunk, chunk), chunk)
            values = dot_nn(low[slot], w_in[owner, :, inner]) + bias[owner, :, inner]
            share_of = 0.5 * (1.0 + lax.erf(values * math.sqrt(0.5)))
            density = jnp.exp(-0.5 * values * values) * (1.0 / math.sqrt(2.0 * math.pi))
            active[slot, :, outer] = (values * share_of).astype(jnp.bfloat16)
            slope[slot, :, outer] = (share_of + values * density).astype(jnp.bfloat16)
            return carry

        lax.fori_loop(0, slab // chunk, units, 0)

    def branch_of(slot, owner, target, start, size):
        units = slice(owner * slab, (owner + 1) * slab)

        def columns(step, carry):
            at = pl.ds(pl.multiple_of(start + step * chunk, chunk), chunk)
            values = dot_nn(active[slot, :, units], w_down[units, at])
            target[:, at] = values if owner == 0 else target[:, at] + values
            return carry

        lax.fori_loop(0, size // chunk, columns, 0)

    bias_send.wait_recv()
    bias[0] = bias_ref[...]
    load_bias = load(11, bias_two, bias.at[1])
    hidden_of(0, 0)
    low_send.wait_recv()
    store(low, low_out)
    hidden_of(1, 0)
    fetch_in.wait()
    load_in_two = load(12, in_two, w_in.at[1])
    fetch_down.pass_halves()
    load_down.wait()
    branch_of(1, 0, part, 0, width)
    branch_of(0, 0, acc, 0, width)
    load_bias.wait()
    load_in_two.wait()
    hidden_of(1, 1)
    hidden_of(0, 1)
    store(active, active_out)
    store(slope, slope_out)
    fetch_down.wait()
    load_down_two = load(13, down_two, w_down.at[pl.ds(slab, slab)])
    load_down_two.wait()
    half = width // 2
    part_sends = []
    for number in range(2):
        branch_of(1, 1, part, number * half, half)
        columns = slice(number * half, (number + 1) * half)
        part_sends.append(send(part.at[:, columns], other.at[:, columns], sibling))
    branch_of(0, 1, acc, 0, width)
    load_cot.wait()
    for copy in part_sends:
        copy.wait_recv()

    def second_rows(step, carry):
        rows = pl.ds(pl.multiple_of(step * small, small), small)
        values = first[rows] + (acc[rows] + other[rows]) + vec_ref[1:2]
        centred = values - row_mean(values)
        spread = lax.rsqrt(row_mean(centred * centred) + EPS_NORM)
        unit = centred * spread
        result[rows] = (unit * vec_ref[4:5] + vec_ref[5:6]).astype(jnp.bfloat16)
        upper = cot[rows].astype(jnp.float32)
        scaled = upper * vec_ref[4:5]
        grad = spread * (scaled - row_mean(scaled) - unit * row_mean(scaled * unit))
        wide[rows] = grad
        grad_low = grad.astype(jnp.bfloat16)
        branch[0, rows] = grad_low
        sums_ref[1:2] += jnp.sum(grad_low.astype(jnp.float32), axis=0, keepdims=True)
        sums_ref[4:5] += jnp.sum(upper * unit, axis=0, keepdims=True)
        sums_ref[5:6] += jnp.sum(upper, axis=0, keepdims=True)
        return carry

    branch_sends = []
    for number in range(2):
        steps = share // small // 2
        lax.fori_loop(number * steps, (number + 1) * steps, second_rows, 0)
        rows = slice(number * steps * small, (number + 1) * steps * small)
        branch_sends.append(send(branch.at[0, rows], branch.at[1, rows], sibling))
    store(result, result_out)
    store(wide, wide_out)
    for copy in branch_sends:
        copy.wait_recv()
    store(branch, branch_out)
    for copy in sends:
        copy.wait_send()
    for copy in stores:
        copy.wait()


def front(tokens, cotangent, planes, w_out, w_in, w_down, head_bias, unit_bias, vectors, seg_keys,
          seg_queries):
    token_count, width = tokens.shape
    seq_count, length = seg_keys.shape[:2]
    share = token_count // (2 * seq_count)
    head_slab = planes.shape[2]
    slab = w_in.shape[1]
    low_type, full_type = jnp.bfloat16, jnp.float32
    vmem = pl.BlockSpec(memory_space=pltpu.VMEM)
    anywhere = pl.BlockSpec(memory_space=pl.ANY)
    shapes = [
        jax.ShapeDtypeStruct((3, token_count, head_slab), low_type),
        jax.ShapeDtypeStruct((2, head_slab // DH, length), full_type),
        jax.ShapeDtypeStruct(w_in.shape, low_type),
        jax.ShapeDtypeStruct(w_down.shape, low_type),
        jax.ShapeDtypeStruct((3,) + w_out.shape, low_type),
        jax.ShapeDtypeStruct((1, slab), full_type),
        jax.ShapeDtypeStruct((4, share, head_slab), low_type),
        jax.ShapeDtypeStruct((share, width), low_type),
        jax.ShapeDtypeStruct((2, share, width), low_type),
        jax.ShapeDtypeStruct((2, share, 2 * slab), low_type),
        jax.ShapeDtypeStruct((2, share, width), low_type),
        jax.ShapeDtypeStruct((2, share, 2 * slab), low_type),
        jax.ShapeDtypeStruct((share, width), full_type),
        jax.ShapeDtypeStruct((share, 1), full_type),
        jax.ShapeDtypeStruct((share, width), full_type),
        jax.ShapeDtypeStruct((6, width), full_type),
    ]
    return pl.pallas_call(
        front_kernel,
        in_specs=[anywhere] * 6 + [vmem] * 5,
        out_specs=[anywhere] * 15 + [vmem],
        out_shape=shapes,
        scratch_shapes=[
            pltpu.VMEM((2, length, width), low_type),
            pltpu.VMEM(planes.shape, low_type),
            pltpu.VMEM((2, 3, length, head_slab), low_type),
            pltpu.VMEM((head_slab, length), low_type),
            pltpu.VMEM((2, head_slab // DH, length), full_type),
            pltpu.VMEM((2, length, head_slab), low_type),
            pltpu.VMEM((3, share, head_slab), low_type),
            pltpu.VMEM((4,) + w_out.shape, low_type),
            pltpu.VMEM((2,) + w_in.shape, low_type),
            pltpu.VMEM((2 * slab, width), low_type),
            pltpu.VMEM((2, 1, slab), full_type),
            pltpu.VMEM((share, width), low_type),
            pltpu.VMEM((share, width), low_type),
            pltpu.VMEM((share, width), full_type),
            pltpu.VMEM((share, width), full_type),
            pltpu.VMEM((share, 1), full_type),
            pltpu.VMEM((2, share, width), low_type),
            pltpu.VMEM((2, share, 2 * slab), low_type),
            pltpu.VMEM((2, share, 2 * slab), low_type),
            pltpu.VMEM((share, width), full_type),
            pltpu.VMEM((share, width), full_type),
            pltpu.VMEM((share, width), full_type),
            pltpu.VMEM((share, width), full_type),
            pltpu.VMEM((2, share, width), low_type),
            pltpu.VMEM((share, width), low_type),
            pltpu.SemaphoreType.DMA((14,)),
            pltpu.SemaphoreType.DMA((20,)),
            pltpu.SemaphoreType.DMA((26,)),
            pltpu.SemaphoreType.DMA((26,)),
        ],
        compiler_params=pltpu.CompilerParams(
            collective_id=3, has_side_effects=True, vmem_limit_bytes=VMEM_GRANT
        ),
        name="front",
    )(tokens, cotangent, planes, w_out, w_in, w_down, head_bias, unit_bias, vectors, seg_keys,
      seg_queries)


def middle_kernel(in_ref, in_two, down_ref, down_two, out_ref, out_rest, branch_ref, slope_ref,
                  normed_ref, inverse_ref, wide_ref, pieces_ref, vec_ref,
                  hidden_out, norm_out, attn_out, near_out, far_out, out_sum, out_far,
                  unit_ref, unit_two, sums_ref,
                  w_in, w_down, w_out, branch, slope, normed, inverse, wide, hidden, part, other,
                  acc, attn, near, far_mixed, pieces, outs, outs_two,
                  load_sem, store_sem, send_sem, recv_sem):
    dp_place = lax.axis_index("dp")
    tensor_place = lax.axis_index("tensor")
    core = lax.rem(tensor_place, 2)
    far = 1 - tensor_place // 2
    sibling = (dp_place, tensor_place + 1 - 2 * core)
    opposite = (dp_place, core + 2 * far)
    share, width = normed.shape
    slab = in_ref.shape[1]
    loads = [
        pltpu.make_async_copy(source, target, load_sem.at[number])
        for number, (source, target) in enumerate(
            [
                (branch_ref, branch), (down_ref, w_down.at[pl.ds(0, slab)]),
                (slope_ref.at[0], slope.at[0]), (down_two, w_down.at[pl.ds(slab, slab)]),
                (slope_ref.at[1], slope.at[1]), (in_ref, w_in.at[0]), (in_two, w_in.at[1]),
                (wide_ref, wide), (normed_ref, normed), (inverse_ref, inverse),
                (out_ref, w_out.at[0]), (out_rest, w_out.at[pl.ds(1, 3)]), (pieces_ref, pieces),
            ]
        )
    ]
    for load in loads:
        load.start()
    barrier = pltpu.get_barrier_semaphore()
    for device in (sibling, opposite):
        pl.semaphore_signal(barrier, inc=1, device_id=device, device_id_type=MESH)
    pl.semaphore_wait(barrier, 2)
    sums_ref[...] = jnp.zeros_like(sums_ref)
    unit_ref[...] = jnp.zeros_like(unit_ref)
    stores = []
    sends = []

    def store(source, target):
        copy = pltpu.make_async_copy(source, target, store_sem.at[len(stores)])
        copy.start()
        stores.append(copy)

    def send(source, target, device):
        number = len(sends)
        copy = pltpu.make_async_remote_copy(
            src_ref=source,
            dst_ref=target,
            send_sem=send_sem.at[number],
            recv_sem=recv_sem.at[number],
            device_id=device,
            device_id_type=MESH,
        )
        copy.start()
        sends.append(copy)
        return copy

    chunk = 256
    small = 64

    def rows_of(number, size):
        return pl.ds(pl.multiple_of(number * size, size), size)

    def grad_hidden_of(slot, owner):
        def units(step, carry):
            outer = pl.ds(pl.multiple_of(owner * slab + step * chunk, chunk), chunk)
            grad = dot_nt(branch[slot], w_down[outer]) * slope[slot, :, outer].astype(jnp.float32)
            grad_low = grad.astype(jnp.bfloat16)
            hidden[slot, :, outer] = grad_low
            unit_ref[:, outer] += jnp.sum(grad_low.astype(jnp.float32), axis=0, keepdims=True)
            return carry

        lax.fori_loop(0, slab // chunk, units, 0)

    def grad_first_of(slot, target):
        def columns(step, carry):
            at = rows_of(step, chunk)
            target[:, at] = dot_nt(hidden[slot, :, :slab], w_in[0, at]) + dot_nt(
                hidden[slot, :, slab:], w_in[1, at]
            )
            return carry

        lax.fori_loop(0, width // chunk, columns, 0)

    for load in loads[:3]:
        load.wait()
    grad_hidden_of(0, 0)
    loads[3].wait()
    grad_hidden_of(0, 1)
    loads[4].wait()
    grad_hidden_of(1, 0)
    grad_hidden_of(1, 1)
    unit_send = send(unit_ref.at[:, pl.ds(slab, slab)], unit_two, opposite)
    store(hidden, hidden_out)
    loads[5].wait()
    loads[6].wait()
    grad_first_of(1, part)
    first_send = send(part, other, sibling)
    grad_first_of(0, acc)
    for load in loads[7:]:
        load.wait()
    first_send.wait_recv()

    def back_rows(step, carry):
        rows = rows_of(step, small)
        grad = acc[rows] + other[rows] + wide[rows]
        unit = normed[rows]
        scaled = grad * vec_ref[2:3]
        back = inverse[rows] * (scaled - row_mean(scaled) - unit * row_mean(scaled * unit))
        acc[rows] = back
        back_low = back.astype(jnp.bfloat16)
        attn[rows] = back_low
        sums_ref[0:1] += jnp.sum(back_low.astype(jnp.float32), axis=0, keepdims=True)
        sums_ref[2:3] += jnp.sum(grad * unit, axis=0, keepdims=True)
        sums_ref[3:4] += jnp.sum(grad, axis=0, keepdims=True)
        return carry

    lax.fori_loop(0, share // small, back_rows, 0)
    store(acc, norm_out)
    near[1] = dot_nt(attn[...], w_out[1]).astype(jnp.bfloat16)
    near_send = send(near.at[1], near.at[2], sibling)
    far_mixed[0] = dot_nt(attn[...], w_out[2]).astype(jnp.bfloat16)
    far_mixed[1] = dot_nt(attn[...], w_out[3]).astype(jnp.bfloat16)
    store(far_mixed, far_out)
    near[0] = dot_nt(attn[...], w_out[0]).astype(jnp.bfloat16)
    store(near.at[0], near_out.at[0])
    outs[1] = dot_tn(pieces[1], attn[...])
    outs[3] = dot_tn(pieces[3], attn[...])
    outs_sends = [
        send(outs.at[1], outs_two.at[0], sibling),
        send(outs.at[3], outs_two.at[1], sibling),
    ]
    outs[0] = dot_tn(pieces[0], attn[...])
    outs[2] = dot_tn(pieces[2], attn[...])
    near_send.wait_recv()
    store(near.at[2], near_out.at[1])
    for copy in outs_sends:
        copy.wait_recv()
    out_sum[...] = outs[0] + outs_two[0]
    out_far[...] = (outs[2] + outs_two[1]).astype(jnp.bfloat16)
    unit_send.wait_recv()
    for copy in sends:
        copy.wait_send()
    for copy in stores:
        copy.wait()


def middle(w_in, in_two, w_down, down_two, w_out, out_rest, branch, slope, normed, inverse, wide,
           pieces, vectors):
    share, width = normed.shape
    slab = w_in.shape[1]
    head_slab = w_out.shape[0]
    low_type, full_type = jnp.bfloat16, jnp.float32
    vmem = pl.BlockSpec(memory_space=pltpu.VMEM)
    anywhere = pl.BlockSpec(memory_space=pl.ANY)
    shapes = [
        jax.ShapeDtypeStruct((2, share, 2 * slab), low_type),
        jax.ShapeDtypeStruct((share, width), full_type),
        jax.ShapeDtypeStruct((share, width), low_type),
        jax.ShapeDtypeStruct((2, share, head_slab), low_type),
        jax.ShapeDtypeStruct((2, share, head_slab), low_type),
        jax.ShapeDtypeStruct((head_slab, width), full_type),
        jax.ShapeDtypeStruct((head_slab, width), low_type),
        jax.ShapeDtypeStruct((1, 2 * slab), full_type),
        jax.ShapeDtypeStruct((1, slab), full_type),
        jax.ShapeDtypeStruct((6, width), full_type),
    ]
    return pl.pallas_call(
        middle_kernel,
        in_specs=[anywhere] * 12 + [vmem],
        out_specs=[anywhere] * 2 + [anywhere] * 3 + [vmem] * 5,
        out_shape=shapes,
        scratch_shapes=[
            pltpu.VMEM((2,) + w_in.shape, low_type),
            pltpu.VMEM((2 * slab, width), low_type),
            pltpu.VMEM((4,) + w_out.shape, low_type),
            pltpu.VMEM((2, share, width), low_type),
            pltpu.VMEM((2, share, 2 * slab), low_type),
            pltpu.VMEM((share, width), full_type),
            pltpu.VMEM((share, 1), full_type),
            pltpu.VMEM((share, width), full_type),
            pltpu.VMEM((2, share, 2 * slab), low_type),
            pltpu.VMEM((share, width), full_type),
            pltpu.VMEM((share, width), full_type),
            pltpu.VMEM((share, width), full_type),
            pltpu.VMEM((share, width), low_type),
            pltpu.VMEM((3, share, head_slab), low_type),
            pltpu.VMEM((2, share, head_slab), low_type),
            pltpu.VMEM((4, share, head_slab), low_type),
            pltpu.VMEM((4, head_slab, width), full_type),
            pltpu.VMEM((2, head_slab, width), full_type),
            pltpu.SemaphoreType.DMA((13,)),
            pltpu.SemaphoreType.DMA((8,)),
            pltpu.SemaphoreType.DMA((6,)),
            pltpu.SemaphoreType.DMA((6,)),
        ],
        compiler_params=pltpu.CompilerParams(
            collective_id=4, has_side_effects=True, vmem_limit_bytes=VMEM_GRANT
        ),
        cost_estimate=pl.CostEstimate(
            flops=2 * share * width * (8 * slab + 8 * head_slab),
            bytes_accessed=60 * share * width, transcendentals=0,
        ),
        name="middle",
    )(w_in, in_two, w_down, down_two, w_out, out_rest, branch, slope, normed, inverse, wide,
      pieces, vectors)


def layer_general(tokens, segments, w_qkv, head_bias, w_out, w_in, unit_bias, w_down, vectors,
                  cotangent):
    token_count, model_width = tokens.shape
    seq_count, length = segments.shape
    head_slab = w_qkv.shape[2]
    head_count = head_slab // DH
    tensor_size = lax.axis_size("tensor")
    share_rows = token_count // tensor_size
    tensor_place = lax.axis_index("tensor")
    row_start = tensor_place * share_rows
    head_scale = 1.0 / math.sqrt(DH)

    def own_rows(values):
        return lax.dynamic_slice_in_dim(values, row_start, share_rows, 0)

    flat_qkv = w_qkv.reshape(model_width, 3 * head_slab)
    projected = jnp.dot(tokens, flat_qkv, preferred_element_type=jnp.float32).reshape(
        token_count, 3, head_slab
    )
    head_shape = (seq_count, length, head_count, DH)
    queries = (
        ((projected[:, 0] + head_bias[0]) * head_scale).astype(jnp.bfloat16).reshape(head_shape)
    )
    key_heads = projected[:, 1].astype(jnp.bfloat16).reshape(head_shape)
    value_heads = (projected[:, 2] + head_bias[1]).astype(jnp.bfloat16).reshape(head_shape)
    mixed_heads, log_total = lax.map(attend_forward, (queries, key_heads, value_heads, segments))
    mixed_flat = mixed_heads.reshape(token_count, head_slab)
    attn_out = (
        lax.psum(jnp.dot(mixed_flat, w_out, preferred_element_type=jnp.float32), "tensor")
        + vectors[0]
    )
    first_norm, first_normed, first_inverse = norm_forward(
        tokens.astype(jnp.float32) + attn_out, vectors[2], vectors[3]
    )
    first_low = first_norm.astype(jnp.bfloat16)
    hidden = jnp.dot(first_low, w_in, preferred_element_type=jnp.float32) + unit_bias
    active, gelu_back = jax.vjp(partial(jax.nn.gelu, approximate=False), hidden)
    active_low = active.astype(jnp.bfloat16)
    grad_out_share = own_rows(cotangent).astype(jnp.float32)
    summed_input = (
        first_norm
        + lax.psum(jnp.dot(active_low, w_down, preferred_element_type=jnp.float32), "tensor")
        + vectors[1]
    )
    second_norm, second_normed, second_inverse = norm_forward(summed_input, vectors[4], vectors[5])
    layer_out = own_rows(second_norm).astype(jnp.bfloat16)
    grad_sum = norm_backward(
        cotangent.astype(jnp.float32), second_normed, second_inverse, vectors[4]
    )
    grad_branch = grad_sum.astype(jnp.bfloat16)
    second_share = own_rows(second_normed)
    grad_w_down = trans_times(active_low, grad_branch)
    grad_active = times_trans(grad_branch, w_down)
    grad_hidden = gelu_back(grad_active)[0].astype(jnp.bfloat16)
    grad_w_in = trans_times(first_low, grad_hidden)
    grad_units = jnp.sum(grad_hidden.astype(jnp.float32), axis=0)
    grad_first = lax.psum(times_trans(grad_hidden, w_in), "tensor") + grad_sum
    grad_h1 = norm_backward(grad_first, first_normed, first_inverse, vectors[2])
    grad_attn = grad_h1.astype(jnp.bfloat16)
    grad_first_share = own_rows(grad_first)
    first_normed_share = own_rows(first_normed)
    grad_h1_share = own_rows(grad_h1)
    grad_w_out = trans_times(mixed_flat, grad_attn)
    grad_mixed = times_trans(grad_attn, w_out).astype(jnp.bfloat16).reshape(head_shape)
    grad_query, grad_key, grad_value = lax.map(
        attend_backward, (queries, key_heads, value_heads, segments, grad_mixed, log_total)
    )
    grad_query = (
        grad_query.reshape(token_count, head_slab).astype(jnp.float32) * head_scale
    ).astype(jnp.bfloat16)
    grad_key = grad_key.reshape(token_count, head_slab)
    grad_value = grad_value.reshape(token_count, head_slab)
    grad_projected = jnp.stack([grad_query, grad_key, grad_value], axis=1).reshape(
        token_count, 3 * head_slab
    )
    grad_w_qkv = trans_times(tokens, grad_projected)
    grad_heads = jnp.stack(
        [
            jnp.sum(grad_query.astype(jnp.float32), axis=0),
            jnp.sum(grad_value.astype(jnp.float32), axis=0),
        ]
    )
    grad_tokens = (
        lax.psum_scatter(
            times_trans(grad_projected, flat_qkv).astype(jnp.bfloat16),
            "tensor",
            scatter_dimension=0,
            tiled=True,
        ).astype(jnp.float32)
        + grad_h1_share
    )
    local_vectors = jnp.stack(
        [
            jnp.sum(own_rows(grad_attn).astype(jnp.float32), axis=0),
            jnp.sum(own_rows(grad_branch).astype(jnp.float32), axis=0),
            jnp.sum(grad_first_share * first_normed_share, axis=0),
            jnp.sum(grad_first_share, axis=0),
            jnp.sum(grad_out_share * second_share, axis=0),
            jnp.sum(grad_out_share, axis=0),
        ]
    )
    return (
        layer_out,
        grad_tokens,
        (
            grad_w_qkv.reshape(model_width, 3, head_slab).transpose(1, 0, 2),
            grad_w_out,
            grad_w_in,
            grad_w_down,
        ),
        local_vectors,
        grad_heads,
        grad_units,
    )


def layer_split(tokens, segments, w_qkv, head_bias, w_out, w_in, unit_bias, w_down, vectors,
                cotangent):
    token_count, model_width = tokens.shape
    seq_count, length = segments.shape
    unit_slab = w_in.shape[1]
    tensor_size = lax.axis_size("tensor")
    share = token_count // tensor_size
    tensor_place = lax.axis_index("tensor")
    core = lax.rem(tensor_place, 2)
    seq = tensor_place // 2

    def to(values, step):
        return lax.ppermute(
            values, "tensor", [(place, place ^ step) for place in range(tensor_size)]
        )

    def rows_at(values, number, size):
        return lax.dynamic_slice_in_dim(values, number * size, size, 0)

    planes = w_qkv.transpose(1, 0, 2)
    seg_keys = jnp.broadcast_to(segments[:, :, None], (seq_count, length, LANES))
    seg_queries = segments[:, None, :]
    (projected, logs, in_two, down_two, out_rest, _, pieces, layer_out, low, active, grad_branch,
     slope, normed, inverse, wide, sums_one) = front(
        tokens, cotangent, planes, w_out, w_in, w_down, head_bias, unit_bias[None], vectors,
        seg_keys, seg_queries,
    )
    active_rows = active.reshape(2 * share, 2 * unit_slab)
    branch_rows = grad_branch.reshape(2 * share, model_width)
    low_rows = low.reshape(2 * share, model_width)
    down_part, grad_branch = lax.optimization_barrier(
        (trans_times(active_rows[:, unit_slab:], branch_rows).astype(jnp.bfloat16), grad_branch)
    )
    down_far = to(down_part, 2)
    (grad_hidden, grad_h1, _, grad_near, grad_far, out_sum, out_far, units, unit_two, sums_two
     ) = middle(
        w_in, in_two, w_down, down_two, w_out, out_rest, grad_branch, slope, normed, inverse, wide,
        pieces, vectors,
    )
    hidden_rows = grad_hidden.reshape(2 * share, 2 * unit_slab)
    far_own = to(grad_far[0:1], 2)
    far_other = to(grad_far[1:2], 3)
    in_far = to(trans_times(low_rows, hidden_rows[:, unit_slab:]).astype(jnp.bfloat16), 2)
    out_back = to(out_far, 2)

    grad_projected = jnp.zeros_like(projected)
    grad_projected, heads_near = attend_back(
        projected, seg_keys, seg_queries, (grad_near, 0), (grad_near, 1), logs, 1,
        grad_projected, seq, core,
    )
    grad_projected, heads_far = attend_back(
        projected, seg_keys, seg_queries, (far_own, 0), (far_other, 0), logs, 0,
        grad_projected, 1 - seq, core,
    )
    token_part = jnp.einsum(
        "gtn,gdn->td", grad_projected, planes, preferred_element_type=jnp.float32
    ).astype(jnp.bfloat16)
    other_one = to(
        jnp.stack([rows_at(token_part, 2 * at + 1 - core, share) for at in (seq, 1 - seq)]), 1
    ).astype(jnp.float32)
    across_part = rows_at(token_part, 2 * (1 - seq) + core, share).astype(jnp.float32)
    from_two = to((across_part + other_one[1]).astype(jnp.bfloat16), 2)
    grad_tokens = (
        rows_at(token_part, 2 * seq + core, share).astype(jnp.float32)
        + other_one[0]
        + from_two.astype(jnp.float32)
        + grad_h1
    )
    grad_w_qkv = jnp.einsum(
        "td,gtn->gdn", tokens, grad_projected, preferred_element_type=jnp.float32
    )
    grad_w_down = trans_times(active_rows[:, :unit_slab], branch_rows) + down_far.astype(
        jnp.float32
    )
    grad_w_in = trans_times(low_rows, hidden_rows[:, :unit_slab]) + in_far.astype(jnp.float32)
    grad_w_out = out_sum + out_back.astype(jnp.float32)
    return (
        layer_out,
        grad_tokens,
        (grad_w_qkv, grad_w_out, grad_w_in, grad_w_down),
        sums_one + sums_two,
        heads_near + heads_far,
        units[0, :unit_slab] + unit_two[0],
    )


def local(
    tokens,
    segments,
    w_qkv,
    head_bias,
    w_out,
    w_in,
    unit_bias,
    w_down,
    vectors,
    cotangent,
    err_qkv,
    err_out,
    err_in,
    err_down,
    basis_qkv,
    basis_out,
    basis_in,
    basis_down,
    mom_qkv,
    mom_head_bias,
    mom_out,
    mom_in,
    mom_unit_bias,
    mom_down,
    mom_vectors,
):
    token_count, model_width = tokens.shape
    head_slab = w_qkv.shape[2]
    unit_slab = w_in.shape[1]
    tensor_size = lax.axis_size("tensor")
    replicas = lax.axis_size("dp")
    one_sequence_per_chip = 2 * segments.shape[0] == tensor_size and replicas % 4 == 0
    layer = layer_split if one_sequence_per_chip else layer_general
    layer_out, grad_tokens, grads, local_vectors, grad_heads, grad_units = layer(
        tokens, segments, w_qkv, head_bias, w_out, w_in, unit_bias, w_down, vectors, cotangent
    )
    grad_w_qkv, grad_w_out, grad_w_in, grad_w_down = grads
    small = jnp.concatenate(
        [
            local_vectors,
            jnp.pad(grad_units, (0, model_width - unit_slab))[None],
            jnp.pad(grad_heads.reshape(1, 2 * head_slab), ((0, 0), (0, model_width - 2 * head_slab))),
        ],
        axis=0,
    )
    planes = (1, 0, 2)
    combined_qkv = grad_w_qkv + err_qkv[0].transpose(planes)
    combined_out = grad_w_out + err_out[0]
    combined_in = grad_w_in + err_in[0]
    combined_down = grad_w_down + err_down[0]
    matrices = (combined_qkv, combined_out, combined_in, combined_down)
    bases, rights, small_sum = compress(
        matrices,
        (basis_qkv.transpose(planes), basis_out, basis_in, basis_down),
        small,
        replicas,
        tensor_size,
    )
    step_rate = 0.3 * math.sqrt(replicas / token_count)
    grads, errors, moments, news = update(
        matrices,
        (mom_qkv.transpose(planes), mom_out, mom_in, mom_down),
        (w_qkv.transpose(planes), w_out, w_in, w_down),
        bases,
        rights,
        step_rate,
    )
    reduced_qkv, rank_out, rank_in, rank_down = (grads[0].transpose(planes),) + tuple(grads[1:])
    new_err_qkv, new_err_out, new_err_in, new_err_down = (
        errors[0].transpose(planes)[None],
        errors[1][None],
        errors[2][None],
        errors[3][None],
    )
    new_mom_qkv, new_mom_out, new_mom_in, new_mom_down = (moments[0].transpose(planes),) + tuple(
        moments[1:]
    )
    new_w_qkv, new_w_out, new_w_in, new_w_down = (news[0].transpose(planes),) + tuple(news[1:])
    right_qkv, right_out, right_in, right_down = rights
    new_basis_qkv = right_qkv.transpose(planes)
    grad_vectors = small_sum[:6]
    grad_unit_bias = small_sum[6, :unit_slab]
    grad_head_bias = small_sum[7, : 2 * head_slab].reshape(2, head_slab)
    new_mom_head_bias = 0.9 * mom_head_bias + grad_head_bias
    new_mom_unit_bias = 0.9 * mom_unit_bias + grad_unit_bias
    new_mom_vectors = 0.9 * mom_vectors + grad_vectors
    new_head_bias = head_bias - step_rate * new_mom_head_bias
    new_unit_bias = unit_bias - step_rate * new_mom_unit_bias
    new_vectors = vectors - step_rate * new_mom_vectors
    return (
        layer_out,
        grad_tokens,
        reduced_qkv,
        grad_head_bias,
        rank_out,
        rank_in,
        grad_unit_bias,
        rank_down,
        grad_vectors,
        new_err_qkv,
        new_err_out,
        new_err_in,
        new_err_down,
        new_basis_qkv,
        right_out,
        right_in,
        right_down,
        new_mom_qkv,
        new_mom_head_bias,
        new_mom_out,
        new_mom_in,
        new_mom_unit_bias,
        new_mom_down,
        new_mom_vectors,
        new_w_qkv,
        new_head_bias,
        new_w_out,
        new_w_in,
        new_unit_bias,
        new_w_down,
        new_vectors,
    )


def solution(mesh):
    in_specs = (
        P("dp", None),
        P("dp", None),
        P(None, None, "tensor"),
        P(None, "tensor"),
        P("tensor", None),
        P(None, "tensor"),
        P("tensor"),
        P("tensor", None),
        P(),
        P("dp", None),
        P("dp", None, None, "tensor"),
        P("dp", "tensor", None),
        P("dp", None, "tensor"),
        P("dp", "tensor", None),
        P(None, None, "tensor"),
        P("tensor", None),
        P(None, "tensor"),
        P("tensor", None),
        P(None, None, "tensor"),
        P(None, "tensor"),
        P("tensor", None),
        P(None, "tensor"),
        P("tensor"),
        P("tensor", None),
        P(),
    )
    out_specs = (
        P(("dp", "tensor"), None),
        P(("dp", "tensor"), None),
        P(None, None, "tensor"),
        P(None, "tensor"),
        P("tensor", None),
        P(None, "tensor"),
        P("tensor"),
        P("tensor", None),
        P(),
        P("dp", None, None, "tensor"),
        P("dp", "tensor", None),
        P("dp", None, "tensor"),
        P("dp", "tensor", None),
        P(None, None, "tensor"),
        P("tensor", None),
        P(None, "tensor"),
        P("tensor", None),
        P(None, None, "tensor"),
        P(None, "tensor"),
        P("tensor", None),
        P(None, "tensor"),
        P("tensor"),
        P("tensor", None),
        P(),
        P(None, None, "tensor"),
        P(None, "tensor"),
        P("tensor", None),
        P(None, "tensor"),
        P("tensor"),
        P("tensor", None),
        P(),
    )
    return jax.shard_map(local, mesh=mesh, in_specs=in_specs, out_specs=out_specs, check_vma=False)
```

```python
from functools import partial
import math

import jax
import jax.numpy as jnp
from jax import lax
from jax.experimental import pallas as pl
from jax.experimental.pallas import tpu as pltpu
from jax.sharding import PartitionSpec as P

DH = 64
LANES = 128
MESH = pl.DeviceIdType.MESH
VMEM_GRANT = 60 << 20
BRIEF = pl.CostEstimate(flops=1, bytes_accessed=1, transcendentals=1)


PRECISE = lax.Precision.HIGHEST
EPS_NORM = 1e-05
EPS_BASIS = 1e-08
MASKED = -1000000000.0


def norm_forward(values, gain, shift):
    row_mean = jnp.mean(values, axis=-1, keepdims=True)
    centred = values - row_mean
    variance = jnp.mean(centred * centred, axis=-1, keepdims=True)
    inverse = lax.rsqrt(variance + EPS_NORM)
    normed = centred * inverse
    return (normed * gain + shift, normed, inverse)


def norm_backward(grad_norm, normed, inverse, gain):
    scaled_grad = grad_norm * gain
    grad_mean = jnp.mean(scaled_grad, axis=-1, keepdims=True)
    along_norm = jnp.mean(scaled_grad * normed, axis=-1, keepdims=True)
    return inverse * (scaled_grad - grad_mean - normed * along_norm)


def times_trans(left_side, right_side):
    return lax.dot_general(
        left_side, right_side, (((1,), (1,)), ((), ())), preferred_element_type=jnp.float32
    )


def trans_times(left_side, right_side):
    return lax.dot_general(
        left_side, right_side, (((0,), (0,)), ((), ())), preferred_element_type=jnp.float32
    )


def split_bf16(values):
    high = values.astype(jnp.bfloat16)
    low = (values - high.astype(jnp.float32)).astype(jnp.bfloat16)
    return high, low


def dot_nt(left_side, right_side):
    return lax.dot_general(
        left_side, right_side, (((1,), (1,)), ((), ())), preferred_element_type=jnp.float32
    )


def dot_nn(left_side, right_side):
    return lax.dot_general(
        left_side, right_side, (((1,), (0,)), ((), ())), preferred_element_type=jnp.float32
    )


def dot_tn(left_side, right_side):
    return lax.dot_general(
        left_side, right_side, (((0,), (0,)), ((), ())), preferred_element_type=jnp.float32
    )


def left_factor(factor, matrix):
    rank_size = factor.shape[0]
    factor_high, factor_low = split_bf16(factor)
    matrix_high, matrix_low = split_bf16(matrix)
    both = dot_nt(jnp.concatenate([factor_high, factor_low], axis=0), matrix_high)
    return both[:rank_size] + both[rank_size:] + dot_nt(factor_high, matrix_low)


def right_factor(basis_rows, matrix):
    rank_size = basis_rows.shape[0]
    basis_high, basis_low = split_bf16(basis_rows)
    matrix_high, matrix_low = split_bf16(matrix)
    both = dot_nn(jnp.concatenate([basis_high, basis_low], axis=0), matrix_high)
    return both[:rank_size] + both[rank_size:] + dot_nn(basis_high, matrix_low)


def place_tiles(target, offset, values):
    per_chunk = target.shape[2] // LANES
    for tile in range(values.shape[1] // LANES):
        spot = offset + tile
        target[spot // per_chunk, :, pl.ds(spot % per_chunk * LANES, LANES)] = values[
            :, tile * LANES : (tile + 1) * LANES
        ]
    return offset + values.shape[1] // LANES


def take_tiles(source, offset, size):
    per_chunk = source.shape[2] // LANES
    pieces = []
    for tile in range(size // LANES):
        spot = offset + tile
        pieces.append(source[spot // per_chunk, :, pl.ds(spot % per_chunk * LANES, LANES)])
    return jnp.concatenate(pieces, axis=1) if len(pieces) > 1 else pieces[0]


def orthonormal_rows(rows):
    rank_size = rows.shape[0]
    row_number = lax.broadcasted_iota(jnp.int32, (rank_size, 1), 0)
    for position in range(rank_size):
        row = rows[position : position + 1]
        length = jnp.sqrt(jnp.sum(row * row, axis=1, keepdims=True)) + EPS_BASIS
        unit = row / length
        along = jnp.sum(rows * unit, axis=1, keepdims=True)
        later = jnp.where(row_number > position, along, 0.0)
        rows = jnp.where(row_number == position, unit, rows - later * unit)
    return rows


def dp_exchange(replicas, mine, wire, arrived, total, sems, meanwhile=None):
    send_one, recv_one, send_two, recv_two = sems
    dp_place = lax.axis_index("dp")
    tensor_place = lax.axis_index("tensor")

    def peer_of(step):
        return lax.rem(dp_place + step, replicas)

    def scatter(step, slot):
        return pltpu.make_async_remote_copy(
            src_ref=wire.at[peer_of(step)],
            dst_ref=arrived.at[slot],
            send_sem=send_one.at[step],
            recv_sem=recv_one.at[slot],
            device_id=(peer_of(step), tensor_place),
            device_id_type=MESH,
        )

    def gather(step, slot):
        return pltpu.make_async_remote_copy(
            src_ref=total.at[dp_place],
            dst_ref=total.at[slot],
            send_sem=send_two.at[step],
            recv_sem=recv_two.at[slot],
            device_id=(peer_of(step), tensor_place),
            device_id_type=MESH,
        )

    def start_scatter(step, carry):
        scatter(step, dp_place).start()
        return carry

    def add_arrived(step, carry):
        scatter(step, peer_of(step)).wait_recv()
        return carry + arrived[peer_of(step)].astype(jnp.float32)

    def start_gather(step, carry):
        gather(step, dp_place).start()
        return carry

    def finish(step, carry):
        gather(step, peer_of(step)).wait_recv()
        return carry

    wire[...] = mine[...].astype(wire.dtype)
    lax.fori_loop(1, replicas, start_scatter, 0)
    total[dp_place] = lax.fori_loop(1, replicas, add_arrived, mine[dp_place])
    lax.fori_loop(1, replicas, start_gather, 0)
    lax.fori_loop(1, replicas, finish, 0)

    def drain(step, carry):
        scatter(step, dp_place).wait_send()
        gather(step, dp_place).wait_send()
        return carry

    return lambda: lax.fori_loop(1, replicas, drain, 0)


def compress_kernel(replicas, tensor_size, qkv_ref, out_ref, in_ref, down_ref,
                    fq_ref, fo_ref, fi_ref, fd_ref, small_ref,
                    bq_ref, bo_ref, bi_ref, bd_ref, rq_ref, ro_ref, ri_ref, rd_ref, sum_ref,
                    qkv, out, inw, down, mine, wire, arrived, total,
                    mine_two, wire_two, arrived_two, total_two, small_slots,
                    load_sem, *sems):
    first_sems, second_sems, (send_small, recv_small) = sems[:4], sems[4:8], sems[8:]
    dp_place = lax.axis_index("dp")
    tensor_place = lax.axis_index("tensor")
    loads = [
        pltpu.make_async_copy(source, target, load_sem.at[number])
        for number, (source, target) in enumerate(
            [(qkv_ref, qkv), (out_ref, out), (down_ref, down), (in_ref, inw)]
        )
    ]
    for load in loads:
        load.start()
    barrier = pltpu.get_barrier_semaphore()

    def greet_dp(step, carry):
        pl.semaphore_signal(
            barrier,
            inc=1,
            device_id=(lax.rem(dp_place + step, replicas), tensor_place),
            device_id_type=MESH,
        )
        return carry

    def greet_tensor(step, carry):
        pl.semaphore_signal(
            barrier,
            inc=1,
            device_id=(dp_place, lax.rem(tensor_place + step, tensor_size)),
            device_id_type=MESH,
        )
        return carry

    lax.fori_loop(1, replicas, greet_dp, 0)
    lax.fori_loop(1, tensor_size, greet_tensor, 0)
    mine[...] = jnp.zeros_like(mine)
    mine_two[...] = jnp.zeros_like(mine_two)
    block = 2 * LANES
    offset = 0
    loads[0].wait()
    for start in range(0, qkv.shape[1], block):
        rows = slice(start, start + block)
        left = left_factor(fq_ref[0], qkv[0, rows])
        for part in range(1, 3):
            left += left_factor(fq_ref[part], qkv[part, rows])
        offset = place_tiles(mine, offset, left)
    for load, factor_ref, matrix in zip(loads[1:], (fo_ref, fd_ref, fi_ref), (out, down, inw)):
        load.wait()
        rows_of = min(block, matrix.shape[0])
        for start in range(0, matrix.shape[0], rows_of):
            left = left_factor(factor_ref[...], matrix[start : start + rows_of])
            offset = place_tiles(mine, offset, left)
    place_tiles(mine, offset, small_ref[...])
    pl.semaphore_wait(barrier, replicas - 1 + tensor_size - 1)
    drain_one = dp_exchange(replicas, mine, wire, arrived, total, first_sems)

    def slot_copy(step, slot):
        peer = lax.rem(tensor_place + step, tensor_size)
        return pltpu.make_async_remote_copy(
            src_ref=small_slots.at[tensor_place],
            dst_ref=small_slots.at[slot],
            send_sem=send_small.at[step],
            recv_sem=recv_small.at[slot],
            device_id=(dp_place, peer),
            device_id_type=MESH,
        )

    def start_small(step, carry):
        slot_copy(step, tensor_place).start()
        return carry

    own_small = take_tiles(total, offset, small_ref.shape[1])
    small_slots[tensor_place] = own_small
    lax.fori_loop(1, tensor_size, start_small, 0)
    offset = 0
    offset_two = 0
    for basis_ref in (bq_ref, bo_ref, bd_ref, bi_ref):
        rows = take_tiles(total, offset, basis_ref.shape[1]) * (1.0 / replicas)
        basis_ref[...] = orthonormal_rows(rows)
        offset += basis_ref.shape[1] // LANES
    drain_one()
    for part in range(3):
        right = right_factor(bq_ref[:, :block], qkv[part, :block])
        for start in range(block, qkv.shape[1], block):
            rows = slice(start, start + block)
            right += right_factor(bq_ref[:, rows], qkv[part, rows])
        offset_two = place_tiles(mine_two, offset_two, right)
    for basis_ref, matrix in zip((bo_ref, bd_ref, bi_ref), (out, down, inw)):
        rows_of = min(block, matrix.shape[0])
        right = right_factor(basis_ref[:, :rows_of], matrix[:rows_of])
        for start in range(rows_of, matrix.shape[0], rows_of):
            rows = slice(start, start + rows_of)
            right += right_factor(basis_ref[:, rows], matrix[rows])
        offset_two = place_tiles(mine_two, offset_two, right)
    drain_two = dp_exchange(
        replicas, mine_two, wire_two, arrived_two, total_two, second_sems
    )

    def collect(step, carry):
        peer = lax.rem(tensor_place + step, tensor_size)
        slot_copy(step, peer).wait_recv()
        slot_copy(step, tensor_place).wait_send()
        return carry + small_slots[peer]

    everyone = lax.fori_loop(1, tensor_size, collect, own_small)
    row_number = lax.broadcasted_iota(jnp.int32, everyone.shape, 0)
    sum_ref[...] = jnp.where(row_number < 6, everyone, own_small) * (1.0 / replicas)
    offset = 0
    for part in range(3):
        rq_ref[part] = take_tiles(total_two, offset, rq_ref.shape[2]) * (1.0 / replicas)
        offset += rq_ref.shape[2] // LANES
    for ref in (ro_ref, rd_ref, ri_ref):
        ref[...] = take_tiles(total_two, offset, ref.shape[1]) * (1.0 / replicas)
        offset += ref.shape[1] // LANES
    drain_two()


def compress(matrices, factors, small, replicas, tensor_size):
    qkv, out, inw, down = matrices
    rank_size = small.shape[0]
    sizes = (qkv.shape[1], out.shape[0], inw.shape[0], down.shape[0])
    right_shapes = [(3, rank_size, qkv.shape[2])] + [(rank_size, one.shape[1]) for one in matrices[1:]]
    lanes_one = sum(sizes) + small.shape[1]
    lanes_two = 3 * qkv.shape[2] + sum(one.shape[1] for one in matrices[1:])
    scratch = [pltpu.VMEM(one.shape, jnp.float32) for one in matrices]
    for lanes in (lanes_one, lanes_two):
        shape = (replicas, rank_size, -(-lanes // (LANES * replicas)) * LANES)
        scratch += [
            pltpu.VMEM(shape, jnp.float32),
            pltpu.VMEM(shape, jnp.bfloat16),
            pltpu.VMEM(shape, jnp.bfloat16),
            pltpu.VMEM(shape, jnp.float32),
        ]
    scratch += [pltpu.VMEM((tensor_size,) + small.shape, jnp.float32), pltpu.SemaphoreType.DMA((4,))]
    scratch += [pltpu.SemaphoreType.DMA((replicas,))] * 8
    scratch += [pltpu.SemaphoreType.DMA((tensor_size,))] * 2
    vmem = pl.BlockSpec(memory_space=pltpu.VMEM)
    shapes = [(rank_size, size) for size in sizes] + right_shapes + [small.shape]
    outputs = pl.pallas_call(
        partial(compress_kernel, replicas, tensor_size),
        in_specs=[pl.BlockSpec(memory_space=pl.ANY)] * 4 + [vmem] * 5,
        out_specs=[vmem] * 9,
        out_shape=[jax.ShapeDtypeStruct(shape, jnp.float32) for shape in shapes],
        scratch_shapes=scratch,
        compiler_params=pltpu.CompilerParams(
            collective_id=1, has_side_effects=True, vmem_limit_bytes=VMEM_GRANT
        ),
        name="compress",
    )(*matrices, *factors, small)
    return outputs[:4], outputs[4:8], outputs[8]


def outer_of(basis_rows, right):
    basis_high, basis_low = split_bf16(basis_rows)
    right_high, right_low = split_bf16(right)
    return dot_tn(
        jnp.concatenate([basis_high, basis_low, basis_high], axis=0),
        jnp.concatenate([right_high, right_high, right_low], axis=0),
    )


def update_kernel(step_rate, out_steps, *refs):
    (mq, mo, mi, md, oq, oo, oi, od, wq, wo, wi, wd, bq, bo, bi, bd, rq, ro, ri, rd,
     gq, go, gi, gd, eq, eo, ei, ed, nq, no, ni, nd, vq, vo, vi, vd) = refs
    step = pl.program_id(0)

    def one(matrix, old, weight, rank, grad_ref, err_ref, mom_ref, new_ref, place):
        moment = 0.9 * old + rank
        grad_ref[place] = rank
        err_ref[place] = matrix - rank
        mom_ref[place] = moment
        new_ref[place] = weight.astype(jnp.float32) - step_rate * moment

    def lanes_of(ref, rows):
        return ref[:, pl.ds(pl.multiple_of(step * rows, LANES), rows)]

    rows = mq.shape[1]
    for part in range(3):
        rank = outer_of(lanes_of(bq, rows), rq[part])
        one(mq[part], oq[part], wq[part], rank, gq, eq, nq, vq, part)
    rank = outer_of(lanes_of(bi, mi.shape[0]), ri[...])
    one(mi[...], oi[...], wi[...], rank, gi, ei, ni, vi, slice(None))
    rank = outer_of(lanes_of(bd, md.shape[0]), rd[...])
    one(md[...], od[...], wd[...], rank, gd, ed, nd, vd, slice(None))

    @pl.when(step < out_steps)
    def _():
        rank = outer_of(lanes_of(bo, mo.shape[0]), ro[...])
        one(mo[...], oo[...], wo[...], rank, go, eo, no, vo, slice(None))


def update(matrices, momenta, weights, bases, rights, step_rate):
    qkv, out, inw, down = matrices
    rows = LANES
    steps = inw.shape[0] // rows
    down_rows = down.shape[0] // steps
    if down_rows < LANES:
        steps = down.shape[0] // LANES
        rows, down_rows = inw.shape[0] // steps, LANES
    out_steps = out.shape[0] // LANES

    def whole(array):
        return pl.BlockSpec(array.shape, lambda i: (0,) * array.ndim)

    def specs():
        return [
            pl.BlockSpec((3, rows, qkv.shape[2]), lambda i: (0, i, 0)),
            pl.BlockSpec((LANES, out.shape[1]), lambda i: (jnp.minimum(i, out_steps - 1), 0)),
            pl.BlockSpec((rows, inw.shape[1]), lambda i: (i, 0)),
            pl.BlockSpec((down_rows, down.shape[1]), lambda i: (i, 0)),
        ]

    shapes = [jax.ShapeDtypeStruct(one.shape, jnp.float32) for one in matrices]
    outputs = pl.pallas_call(
        partial(update_kernel, step_rate, out_steps),
        grid=(steps,),
        in_specs=specs() * 3 + [whole(one) for one in bases] + [whole(one) for one in rights],
        out_specs=specs() * 4,
        out_shape=shapes * 4,
        compiler_params=pltpu.CompilerParams(vmem_limit_bytes=VMEM_GRANT),
        name="update",
    )(*matrices, *momenta, *weights, *bases, *rights)
    return outputs[0:4], outputs[4:8], outputs[8:12], outputs[12:16]


def masked_scores(queries, key_heads, seg_ids):
    scores = jnp.einsum("qhd,khd->hqk", queries, key_heads, preferred_element_type=jnp.float32)
    same_doc = seg_ids[:, None] == seg_ids[None, :]
    return jnp.where(same_doc[None], scores, MASKED)


def attend_forward(inputs_of):
    queries, key_heads, value_heads, seg_ids = inputs_of
    scores = masked_scores(queries, key_heads, seg_ids)
    highest = jnp.max(scores, axis=-1, keepdims=True)
    powers = jnp.exp(scores - highest)
    denominator = jnp.sum(powers, axis=-1, keepdims=True)
    weights = (powers / denominator).astype(jnp.bfloat16)
    mixed_heads = jnp.einsum(
        "hqk,khd->qhd", weights, value_heads, preferred_element_type=jnp.float32
    )
    return (mixed_heads.astype(jnp.bfloat16), highest[..., 0] + jnp.log(denominator[..., 0]))


def attend_backward(inputs_of):
    queries, key_heads, value_heads, seg_ids, grad_mixed, log_total = inputs_of
    scores = masked_scores(queries, key_heads, seg_ids)
    probability = jnp.exp(scores - log_total[..., None])
    grad_probs = jnp.einsum(
        "qhd,khd->hqk", grad_mixed, value_heads, preferred_element_type=jnp.float32
    )
    centre = jnp.sum(probability * grad_probs, axis=-1, keepdims=True)
    grad_scores = (probability * (grad_probs - centre)).astype(jnp.bfloat16)
    grad_query = jnp.einsum(
        "hqk,khd->qhd", grad_scores, key_heads, preferred_element_type=jnp.float32
    )
    grad_key = jnp.einsum("hqk,qhd->khd", grad_scores, queries, preferred_element_type=jnp.float32)
    grad_value = jnp.einsum(
        "hqk,qhd->khd",
        probability.astype(jnp.bfloat16),
        grad_mixed,
        preferred_element_type=jnp.float32,
    )
    return (
        grad_query.astype(jnp.bfloat16),
        grad_key.astype(jnp.bfloat16),
        grad_value.astype(jnp.bfloat16),
    )


def stacked_heads(pair, lane_is_low):
    zero = jnp.zeros_like(pair)
    return jnp.concatenate(
        [jnp.where(lane_is_low, pair, zero), jnp.where(lane_is_low, zero, pair)], axis=0
    )


def own_blocks(both):
    rows = both.shape[1] // 2
    return jnp.concatenate([both[:DH, :rows], both[DH:, rows:]], axis=0).T


def attend_back_kernel(place_ref, q_ref, k_ref, v_ref, seg_key_ref, seg_query_ref, gm_own_ref,
                       gm_other_ref, mixed_ref, log_ref, old_ref, grad_ref, sums_ref, key_t, grad_key,
                       grad_value):
    del old_ref
    step = pl.program_id(0)

    @pl.when(step == 0)
    def _():
        key_t[...] = k_ref[...].T
        grad_key[...] = jnp.zeros_like(grad_key)
        grad_value[...] = jnp.zeros_like(grad_value)

    pairs = q_ref.shape[1] // LANES
    lane = lax.broadcasted_iota(jnp.int32, (1, LANES), 1)
    lane_is_low = lane < DH
    head_of_lane = (
        lax.broadcasted_iota(jnp.int32, (8, LANES), 0)
        == lax.broadcasted_iota(jnp.int32, (8, LANES), 1) // DH
    ).astype(jnp.bfloat16)
    head_scale = 1.0 / math.sqrt(DH)
    here = pl.ds(pl.multiple_of(step * LANES, LANES), LANES)
    is_own = lax.rem(step // (pl.num_programs(0) // 2) + place_ref[1], 2) == 0
    gm = jnp.where(is_own, gm_own_ref[...], gm_other_ref[...])
    seg_query = jnp.concatenate([seg_query_ref[...], seg_query_ref[...]], axis=1)
    seg_key = seg_key_ref[...]
    same = jnp.concatenate([seg_key, seg_key], axis=1) == seg_query
    all_lanes = [slice(pair * LANES, (pair + 1) * LANES) for pair in range(pairs)]
    queries, grads, centres, probs, grad_probs = [], [], [], [], []
    for pair, lanes in enumerate(all_lanes):
        queries.append(stacked_heads(q_ref[:, lanes], lane_is_low))
        grads.append(stacked_heads(gm[:, lanes], lane_is_low))
        high, low = split_bf16(
            gm[:, lanes].astype(jnp.float32) * mixed_ref[:, lanes].astype(jnp.float32)
        )
        sums = dot_nt(head_of_lane, high) + dot_nt(head_of_lane, low)
        centres.append(jnp.concatenate([sums[0:1], sums[1:2]], axis=1))
    for pair, lanes in enumerate(all_lanes):
        log_total = jnp.concatenate(
            [log_ref[2 * pair : 2 * pair + 1], log_ref[2 * pair + 1 : 2 * pair + 2]], axis=1
        )
        scores = dot_nt(k_ref[:, lanes], queries[pair])
        probs.append(jnp.exp(jnp.where(same, scores - log_total, MASKED)))
        grad_probs.append(dot_nt(v_ref[:, lanes], grads[pair]))
    for pair, lanes in enumerate(all_lanes):
        grad_scores = (probs[pair] * (grad_probs[pair] - centres[pair])).astype(jnp.bfloat16)
        grad_value[:, lanes] += dot_nn(probs[pair].astype(jnp.bfloat16), grads[pair])
        grad_key[:, lanes] += dot_nn(grad_scores, queries[pair])
        grad_query = own_blocks(dot_nn(key_t[lanes], grad_scores)).astype(jnp.bfloat16)
        grad_ref[0, here, lanes] = (grad_query.astype(jnp.float32) * head_scale).astype(
            jnp.bfloat16
        )

    @pl.when(step == pl.num_programs(0) - 1)
    def _():
        grad_ref[1] = grad_key[...].astype(jnp.bfloat16)
        low_value = grad_value[...].astype(jnp.bfloat16)
        grad_ref[2] = low_value
        sums_ref[0:1] = jnp.sum(grad_ref[0].astype(jnp.float32), axis=0, keepdims=True)
        sums_ref[1:2] = jnp.sum(low_value.astype(jnp.float32), axis=0, keepdims=True)


def attend_back(projected, seg_keys, seg_queries, grad_own, grad_other, mixed, logs, slot, old, place, core):
    length = seg_keys.shape[1]
    slab = projected.shape[2]
    blocks = length // LANES
    half = blocks // 2
    grid_spec = pltpu.PrefetchScalarGridSpec(
        num_scalar_prefetch=1,
        grid=(blocks,),
        in_specs=[
            pl.BlockSpec((None, LANES, slab), lambda i, at: (0, at[0] * blocks + i, 0)),
            pl.BlockSpec((None, length, slab), lambda i, at: (1, at[0], 0)),
            pl.BlockSpec((None, length, slab), lambda i, at: (2, at[0], 0)),
            pl.BlockSpec((None, length, LANES), lambda i, at: (at[0], 0, 0)),
            pl.BlockSpec((None, 1, LANES), lambda i, at: (at[0], 0, i)),
            pl.BlockSpec((None, LANES, slab), lambda i, at: (grad_own[1], lax.rem(i, half), 0)),
            pl.BlockSpec((None, LANES, slab), lambda i, at: (grad_other[1], lax.rem(i, half), 0)),
            pl.BlockSpec((None, LANES, slab), lambda i, at: (slot, i, 0)),
            pl.BlockSpec((None, slab // DH, LANES), lambda i, at: (slot, 0, i)),
            pl.BlockSpec(memory_space=pl.ANY),
        ],
        out_specs=[
            pl.BlockSpec((3, length, slab), lambda i, at: (0, at[0], 0)),
            pl.BlockSpec((2, slab), lambda i, at: (0, 0)),
        ],
        scratch_shapes=[
            pltpu.VMEM((slab, length), jnp.bfloat16),
            pltpu.VMEM((length, slab), jnp.float32),
            pltpu.VMEM((length, slab), jnp.float32),
        ],
    )
    return pl.pallas_call(
        attend_back_kernel,
        grid_spec=grid_spec,
        out_shape=[
            jax.ShapeDtypeStruct(projected.shape, jnp.bfloat16),
            jax.ShapeDtypeStruct((2, slab), jnp.float32),
        ],
        input_output_aliases={10: 0},
        compiler_params=pltpu.CompilerParams(vmem_limit_bytes=24 << 20),
        cost_estimate=BRIEF,
        name="attend_back",
    )(jnp.stack([place, core]), projected, projected, projected, seg_keys, seg_queries, grad_own[0],
      grad_other[0], mixed, logs, old)


def row_mean(values):
    return jnp.mean(values, axis=-1, keepdims=True)


def layer_kernel(tokens, cotangent, w_qkv_ref, out_ref, in_ref, down_ref,
                 head_ref, bias_ref, vec_ref, seg_keys, seg_queries,
                 projected_out, log_out, mixed_out, in_two, down_two, out_rest, bias_two,
                 result_out, low_out, active_out, branch_out, hidden_out, norm_out, near_out,
                 far_out, down_near, down_rest, in_part_out, out_sum, out_far, unit_ref, unit_two,
                 sums_ref,
                 rows_in, w_qkv, projected, value_t, log_total, mixed, pieces,
                 w_out, w_in, w_down, bias, tok, cot, first, normed, inverse, low, slope, active,
                 part, other, acc, wide, branch, result, down_part, near, far_mixed, outs_two,
                 load_sem, store_sem, send_sem, recv_sem):
    dp_place = lax.axis_index("dp")
    tensor_place = lax.axis_index("tensor")
    core = lax.rem(tensor_place, 2)
    seq = tensor_place // 2
    far = 1 - seq
    side = lax.rem(dp_place, 2)
    depth = lax.rem(dp_place // 2, 2)
    here = 2 * depth + side
    sibling = (dp_place, tensor_place + 1 - 2 * core)
    opposite = (dp_place, core + 2 * far)
    diagonal = (dp_place, 1 - core + 2 * far)
    beside = (dp_place + 1 - 2 * side, tensor_place)
    behind = (dp_place + 2 - 4 * depth, tensor_place)
    share, width = tok.shape
    slab = in_ref.shape[1]
    length = rows_in.shape[1]
    head_slab = w_qkv.shape[2]
    head_count = head_slab // DH
    stores = []
    sends = []
    numbers = iter(range(send_sem.shape[0]))

    def load(number, source, target):
        copy = pltpu.make_async_copy(source, target, load_sem.at[number])
        copy.start()
        return copy

    def store(source, target):
        copy = pltpu.make_async_copy(source, target, store_sem.at[len(stores)])
        copy.start()
        stores.append(copy)

    def send(source, target, device):
        number = next(numbers)
        copy = pltpu.make_async_remote_copy(
            src_ref=source,
            dst_ref=target,
            send_sem=send_sem.at[number],
            recv_sem=recv_sem.at[number],
            device_id=device,
            device_id_type=MESH,
        )
        copy.start()
        sends.append(copy)
        return copy

    def rows_of(number, size):
        return pl.ds(pl.multiple_of(number * size, LANES), size)

    load_qkv = load(0, w_qkv_ref, w_qkv)
    load_far = load(1, tokens.at[rows_of(far, length)], rows_in.at[0])
    load_near = load(2, tokens.at[rows_of(seq, length)], rows_in.at[1])
    load_out = load(3, out_ref, w_out.at[0])
    load_in = load(4, in_ref, w_in.at[0])
    load_down = load(5, down_ref, w_down.at[pl.ds(0, slab)])
    load_tok = load(6, tokens.at[rows_of(tensor_place, share)], tok)
    load_cot = load(7, cotangent.at[rows_of(tensor_place, share)], cot)

    barrier = pltpu.get_barrier_semaphore()
    for device in (sibling, opposite, diagonal, beside, behind):
        pl.semaphore_signal(barrier, inc=1, device_id=device, device_id_type=MESH)
    pl.semaphore_wait(barrier, 5)
    sums_ref[...] = jnp.zeros_like(sums_ref)
    unit_ref[...] = jnp.zeros_like(unit_ref)

    def rows_part(whole, number, parts):
        size = whole.shape[0] // parts
        return whole.at[pl.ds(pl.multiple_of(number * size, size), size)]

    class Fetch:
        def __init__(self, source, whole):
            self.whole = whole
            self.over_y = send(
                rows_part(source, here, 4), rows_part(whole, here, 4), opposite
            )

        def pass_on(self):
            self.over_y.wait_recv()
            own = rows_part(self.whole, here, 4)
            self.over_x = send(own, own, beside)
            self.over_z = send(own, own, behind)

        def pass_halves(self):
            self.over_x.wait_recv()
            half = rows_part(self.whole, 2 * (here + 1 - 2 * side), 8)
            self.half_z = send(half, half, behind)
            self.over_z.wait_recv()
            half = rows_part(self.whole, 2 * (here + 2 - 4 * depth) + 1, 8)
            self.half_x = send(half, half, beside)

        def wait(self):
            self.half_z.wait_recv()
            self.half_x.wait_recv()

    bias_send = send(bias_ref, bias_two, opposite)
    fetch_out = Fetch(out_ref, out_rest.at[1])
    fetch_in = Fetch(in_ref, in_two)

    chunk = 256
    scale = 1.0 / math.sqrt(DH)

    def project(slot):
        def rows_step(step, carry):
            rows = rows_of(step, chunk)
            values = rows_in[slot, rows]
            projected[slot, 0, rows] = (
                (dot_nn(values, w_qkv[0]) + head_ref[0:1]) * scale
            ).astype(jnp.bfloat16)
            projected[slot, 1, rows] = dot_nn(values, w_qkv[1]).astype(jnp.bfloat16)
            projected[slot, 2, rows] = (dot_nn(values, w_qkv[2]) + head_ref[1:2]).astype(
                jnp.bfloat16
            )
            return carry

        lax.fori_loop(0, length // chunk, rows_step, 0)
        value_t[...] = projected[slot, 2].T

    lane_is_low = lax.broadcasted_iota(jnp.int32, (1, LANES), 1) < DH

    def attend_rows(slot, place, start, stop):
        def block(step, carry):
            rows = rows_of(step, LANES)
            same = seg_keys[place] == seg_queries[place, :, rows]
            mask = jnp.where(same, 0.0, MASKED)
            mask = jnp.concatenate([mask, mask], axis=1)
            all_lanes = [slice(at, at + LANES) for at in range(0, head_slab, LANES)]
            all_scores = [
                dot_nt(
                    projected[slot, 1, :, lanes],
                    stacked_heads(projected[slot, 0, rows, lanes], lane_is_low),
                )
                + mask
                for lanes in all_lanes
            ]
            for pair, (lanes, scores) in enumerate(zip(all_lanes, all_scores)):
                highest = jnp.max(scores, axis=0, keepdims=True)
                powers = jnp.exp(scores - highest)
                denominator = jnp.sum(powers, axis=0, keepdims=True)
                blend = dot_nn(value_t[lanes], powers.astype(jnp.bfloat16))
                mixed[slot, rows, lanes] = own_blocks(blend * (1.0 / denominator)).astype(
                    jnp.bfloat16
                )
                total = highest + jnp.log(denominator)
                log_total[slot, 2 * pair : 2 * pair + 1, rows] = total[:, :LANES]
                log_total[slot, 2 * pair + 1 : 2 * pair + 2, rows] = total[:, LANES:]
            return carry

        lax.fori_loop(start, stop, block, 0, unroll=2)

    blocks = length // LANES
    load_qkv.wait()
    load_far.wait()
    project(0)
    attend_rows(0, far, 0, 4)
    fetch_out.pass_on()
    fetch_in.pass_on()
    fetch_down = Fetch(down_ref, down_two)
    attend_rows(0, far, 4, blocks)
    own_rows = rows_of(core, share)
    sibling_rows = rows_of(1 - core, share)
    piece_two = send(mixed.at[0, own_rows], pieces.at[1], opposite)
    piece_three = send(mixed.at[0, sibling_rows], pieces.at[2], diagonal)
    store(projected.at[0, 0], projected_out.at[0, rows_of(far, length)])
    store(projected.at[0, 1], projected_out.at[1, rows_of(far, length)])
    store(projected.at[0, 2], projected_out.at[2, rows_of(far, length)])
    load_near.wait()
    project(1)
    attend_rows(1, seq, 0, 4)
    fetch_out.pass_halves()
    fetch_in.pass_halves()
    attend_rows(1, seq, 4, 6)
    fetch_down.pass_on()
    fetch_out.wait()
    out_pass = [
        send(out_ref, out_rest.at[0], sibling),
        send(out_rest.at[1], out_rest.at[2], sibling),
    ]
    load_two = load(8, out_rest.at[1], w_out.at[2])
    attend_rows(1, seq, 6, blocks)
    piece_one = send(mixed.at[1, sibling_rows], pieces.at[0], sibling)
    store(projected.at[1, 0], projected_out.at[0, rows_of(seq, length)])
    store(projected.at[1, 1], projected_out.at[1, rows_of(seq, length)])
    store(projected.at[1, 2], projected_out.at[2, rows_of(seq, length)])
    store(log_total, log_out)
    for copy in out_pass:
        copy.wait_recv()
    load_one = load(9, out_rest.at[0], w_out.at[1])
    load_three = load(10, out_rest.at[2], w_out.at[3])
    store(mixed, mixed_out)
    for copy in (load_out, load_tok, load_one, load_two, load_three):
        copy.wait()
    for copy in (piece_two, piece_three, piece_one):
        copy.wait_recv()
    small = 64

    def attn_rows(step, carry):
        rows = rows_of(step, chunk)
        total = dot_nn(mixed[1, pl.ds(pl.multiple_of(core * share + step * chunk, LANES), chunk)],
                       w_out[0])
        for piece in range(3):
            total += dot_nn(pieces[piece, rows], w_out[piece + 1])
        acc[rows] = total
        return carry

    def first_rows(step, carry):
        rows = pl.ds(pl.multiple_of(step * small, small), small)
        values = tok[rows].astype(jnp.float32) + (acc[rows] + vec_ref[0:1])
        centred = values - row_mean(values)
        spread = lax.rsqrt(row_mean(centred * centred) + EPS_NORM)
        unit = centred * spread
        normed[rows] = unit
        inverse[rows] = spread
        shifted = unit * vec_ref[2:3] + vec_ref[3:4]
        first[rows] = shifted
        low[rows] = shifted.astype(jnp.bfloat16)
        return carry

    lax.fori_loop(0, share // chunk, attn_rows, 0)
    lax.fori_loop(0, share // small, first_rows, 0)
    slots = [slice(0, share), slice(share, 2 * share)]
    low_send = send(low.at[slots[0]], low.at[slots[1]], sibling)
    load_in.wait()

    def hidden_of(slot, owner):
        def units(step, carry):
            inner = rows_of(step, chunk)
            values = dot_nn(low[slots[slot]], w_in[owner, :, inner]) + bias[owner, :, inner]
            share_of = 0.5 * (1.0 + lax.erf(values * math.sqrt(0.5)))
            density = jnp.exp(-0.5 * values * values) * (1.0 / math.sqrt(2.0 * math.pi))
            active[owner, slots[slot], inner] = (values * share_of).astype(jnp.bfloat16)
            slope[owner, slots[slot], inner] = (share_of - 0.5 + values * density).astype(jnp.bfloat16)
            return carry

        lax.fori_loop(0, slab // chunk, units, 0)

    def branch_of(slot, owner, target, start, size):
        units = slice(owner * slab, (owner + 1) * slab)

        def columns(step, carry):
            at = pl.ds(pl.multiple_of(start + step * chunk, chunk), chunk)
            values = dot_nn(active[owner, slots[slot]], w_down[units, at])
            target[:, at] = values if owner == 0 else target[:, at] + values
            return carry

        lax.fori_loop(0, size // chunk, columns, 0)

    bias_send.wait_recv()
    bias[0] = bias_ref[...]
    load_bias = load(11, bias_two, bias.at[1])
    hidden_of(0, 0)
    low_send.wait_recv()
    store(low, low_out)
    hidden_of(1, 0)
    fetch_in.wait()
    load_in_two = load(12, in_two, w_in.at[1])
    fetch_down.pass_halves()
    load_down.wait()
    branch_of(1, 0, part, 0, width)
    branch_of(0, 0, acc, 0, width)
    load_bias.wait()
    load_in_two.wait()
    hidden_of(1, 1)
    hidden_of(0, 1)
    store(active.at[0], active_out)
    fetch_down.wait()
    load_down_two = load(13, down_two, w_down.at[pl.ds(slab, slab)])
    load_down_two.wait()
    half = width // 2
    part_sends = []
    for number in range(2):
        branch_of(1, 1, part, number * half, half)
        columns = slice(number * half, (number + 1) * half)
        part_sends.append(send(part.at[:, columns], other.at[:, columns], sibling))
    branch_of(0, 1, acc, 0, width)
    load_cot.wait()
    for copy in part_sends:
        copy.wait_recv()

    def second_rows(step, carry):
        rows = pl.ds(pl.multiple_of(step * small, small), small)
        values = first[rows] + (acc[rows] + other[rows]) + vec_ref[1:2]
        centred = values - row_mean(values)
        spread = lax.rsqrt(row_mean(centred * centred) + EPS_NORM)
        unit = centred * spread
        result[rows] = (unit * vec_ref[4:5] + vec_ref[5:6]).astype(jnp.bfloat16)
        upper = cot[rows].astype(jnp.float32)
        scaled = upper * vec_ref[4:5]
        grad = spread * (scaled - row_mean(scaled) - unit * row_mean(scaled * unit))
        wide[rows] = grad
        grad_low = grad.astype(jnp.bfloat16)
        branch[rows] = grad_low
        sums_ref[1:2] += jnp.sum(grad_low.astype(jnp.float32), axis=0, keepdims=True)
        sums_ref[4:5] += jnp.sum(upper * unit, axis=0, keepdims=True)
        sums_ref[5:6] += jnp.sum(upper, axis=0, keepdims=True)
        return carry

    branch_sends = []
    for number in range(2):
        steps = share // small // 2
        lax.fori_loop(number * steps, (number + 1) * steps, second_rows, 0)
        rows = slice(number * steps * small, (number + 1) * steps * small)
        there = slice(share + rows.start, share + rows.stop)
        branch_sends.append(send(branch.at[rows], branch.at[there], sibling))
    store(result, result_out)
    hidden = rows_in

    def grad_hidden_of(slot, owner):
        def units(step, carry):
            inner = rows_of(step, chunk)
            outer = pl.ds(pl.multiple_of(owner * slab + step * chunk, chunk), chunk)
            grad = dot_nt(branch[slots[slot]], w_down[outer]) * (
                0.5 + slope[owner, slots[slot], inner].astype(jnp.float32)
            )
            grad_low = grad.astype(jnp.bfloat16)
            hidden[owner, slots[slot], inner] = grad_low
            unit_ref[:, outer] += jnp.sum(grad_low.astype(jnp.float32), axis=0, keepdims=True)
            return carry

        lax.fori_loop(0, slab // chunk, units, 0)

    def grad_first_of(slot, target, start, size):
        def columns(step, carry):
            at = pl.ds(pl.multiple_of(start + step * chunk, chunk), chunk)
            target[:, at] = dot_nt(hidden[0, slots[slot]], w_in[0, at]) + dot_nt(
                hidden[1, slots[slot]], w_in[1, at]
            )
            return carry

        lax.fori_loop(0, size // chunk, columns, 0)

    def far_product(left_side, right_side, target, start, stop):
        def rows_step(step, carry):
            at = rows_of(step, LANES)
            target[at] = dot_tn(left_side[:, at], right_side[...]).astype(jnp.bfloat16)
            return carry

        lax.fori_loop(start // LANES, stop // LANES, rows_step, 0)

    grad_hidden_of(0, 0)
    grad_hidden_of(0, 1)
    for copy in branch_sends:
        copy.wait_recv()
    store(branch, branch_out)
    early = down_near.shape[0]
    far_product(active.at[1], branch, down_part, 0, early)
    down_send = send(down_part.at[pl.ds(0, early)], down_near, opposite)
    far_product(active.at[1], branch, down_part, early, slab)
    store(down_part.at[pl.ds(early, slab - early)], down_rest)
    grad_hidden_of(1, 0)
    grad_hidden_of(1, 1)
    unit_send = send(unit_ref.at[:, pl.ds(slab, slab)], unit_two, opposite)
    store(hidden.at[0], hidden_out)
    for copy in part_sends:
        copy.wait_send()
    sends[:] = [one for one in sends if all(one is not copy for copy in part_sends)]
    first_sends = []
    for number in range(2):
        grad_first_of(1, part, number * half, half)
        columns = slice(number * half, (number + 1) * half)
        first_sends.append(send(part.at[:, columns], other.at[:, columns], sibling))
    grad_first_of(0, acc, 0, width)
    for copy in first_sends:
        copy.wait_recv()

    def back_rows(step, carry):
        rows = pl.ds(pl.multiple_of(step * small, small), small)
        grad = acc[rows] + other[rows] + wide[rows]
        unit = normed[rows]
        scaled = grad * vec_ref[2:3]
        back = inverse[rows] * (scaled - row_mean(scaled) - unit * row_mean(scaled * unit))
        acc[rows] = back
        back_low = back.astype(jnp.bfloat16)
        tok[rows] = back_low
        sums_ref[0:1] += jnp.sum(back_low.astype(jnp.float32), axis=0, keepdims=True)
        sums_ref[2:3] += jnp.sum(grad * unit, axis=0, keepdims=True)
        sums_ref[3:4] += jnp.sum(grad, axis=0, keepdims=True)
        return carry

    lax.fori_loop(0, share // small, back_rows, 0)
    store(acc, norm_out)
    attn = tok[...]
    near[1] = dot_nt(attn, w_out[1]).astype(jnp.bfloat16)
    near_send = send(near.at[1], near.at[2], sibling)
    out_one = slice(0, head_slab)
    out_three = slice(head_slab, 2 * head_slab)
    first[out_one] = dot_tn(pieces[0], attn)
    first[out_three] = dot_tn(pieces[2], attn)
    outs_send = send(first.at[pl.ds(0, 2 * head_slab)], outs_two, sibling)
    far_mixed[0] = dot_nt(attn, w_out[2]).astype(jnp.bfloat16)
    far_mixed[1] = dot_nt(attn, w_out[3]).astype(jnp.bfloat16)
    store(far_mixed, far_out)
    near[0] = dot_nt(attn, w_out[0]).astype(jnp.bfloat16)
    store(near.at[0], near_out.at[0])
    far_product(low, hidden.at[1], active.at[1], 0, width)
    store(active.at[1], in_part_out)
    near_send.wait_recv()
    store(near.at[2], near_out.at[1])
    outs_send.wait_recv()
    out_sum[...] = dot_tn(mixed[1, own_rows], attn) + outs_two[out_one]
    out_far[...] = (dot_tn(pieces[1], attn) + outs_two[out_three]).astype(jnp.bfloat16)
    unit_send.wait_recv()
    down_send.wait_recv()
    for copy in sends:
        copy.wait_send()
    for copy in stores:
        copy.wait()


def layer_call(tokens, cotangent, planes, w_out, w_in, w_down, head_bias, unit_bias, vectors,
               seg_keys, seg_queries):
    token_count, width = tokens.shape
    seq_count, length = seg_keys.shape[:2]
    share = token_count // (2 * seq_count)
    head_slab = planes.shape[2]
    slab = w_in.shape[1]
    early = slab * 3 // 8
    low_type, full_type = jnp.bfloat16, jnp.float32
    vmem = pl.BlockSpec(memory_space=pltpu.VMEM)
    anywhere = pl.BlockSpec(memory_space=pl.ANY)
    shapes = [
        jax.ShapeDtypeStruct((3, token_count, head_slab), low_type),
        jax.ShapeDtypeStruct((2, head_slab // DH, length), full_type),
        jax.ShapeDtypeStruct((2, length, head_slab), low_type),
        jax.ShapeDtypeStruct(w_in.shape, low_type),
        jax.ShapeDtypeStruct(w_down.shape, low_type),
        jax.ShapeDtypeStruct((3,) + w_out.shape, low_type),
        jax.ShapeDtypeStruct((1, slab), full_type),
        jax.ShapeDtypeStruct((share, width), low_type),
        jax.ShapeDtypeStruct((2 * share, width), low_type),
        jax.ShapeDtypeStruct((2 * share, slab), low_type),
        jax.ShapeDtypeStruct((2 * share, width), low_type),
        jax.ShapeDtypeStruct((2 * share, slab), low_type),
        jax.ShapeDtypeStruct((share, width), full_type),
        jax.ShapeDtypeStruct((2, share, head_slab), low_type),
        jax.ShapeDtypeStruct((2, share, head_slab), low_type),
        jax.ShapeDtypeStruct((early, width), low_type),
        jax.ShapeDtypeStruct((slab - early, width), low_type),
        jax.ShapeDtypeStruct(w_in.shape, low_type),
        jax.ShapeDtypeStruct((head_slab, width), full_type),
        jax.ShapeDtypeStruct((head_slab, width), low_type),
        jax.ShapeDtypeStruct((1, 2 * slab), full_type),
        jax.ShapeDtypeStruct((1, slab), full_type),
        jax.ShapeDtypeStruct((6, width), full_type),
    ]
    return pl.pallas_call(
        layer_kernel,
        in_specs=[anywhere] * 6 + [vmem] * 5,
        out_specs=[anywhere] * 18 + [vmem] * 5,
        out_shape=shapes,
        scratch_shapes=[
            pltpu.VMEM((2, length, width), low_type),
            pltpu.VMEM(planes.shape, low_type),
            pltpu.VMEM((2, 3, length, head_slab), low_type),
            pltpu.VMEM((head_slab, length), low_type),
            pltpu.VMEM((2, head_slab // DH, length), full_type),
            pltpu.VMEM((2, length, head_slab), low_type),
            pltpu.VMEM((3, share, head_slab), low_type),
            pltpu.VMEM((4,) + w_out.shape, low_type),
            pltpu.VMEM((2,) + w_in.shape, low_type),
            pltpu.VMEM((2 * slab, width), low_type),
            pltpu.VMEM((2, 1, slab), full_type),
            pltpu.VMEM((share, width), low_type),
            pltpu.VMEM((share, width), low_type),
            pltpu.VMEM((share, width), full_type),
            pltpu.VMEM((share, width), full_type),
            pltpu.VMEM((share, 1), full_type),
            pltpu.VMEM((2 * share, width), low_type),
            pltpu.VMEM((2, 2 * share, slab), low_type),
            pltpu.VMEM((2, 2 * share, slab), low_type),
            pltpu.VMEM((share, width), full_type),
            pltpu.VMEM((share, width), full_type),
            pltpu.VMEM((share, width), full_type),
            pltpu.VMEM((share, width), full_type),
            pltpu.VMEM((2 * share, width), low_type),
            pltpu.VMEM((share, width), low_type),
            pltpu.VMEM((slab, width), low_type),
            pltpu.VMEM((3, share, head_slab), low_type),
            pltpu.VMEM((2, share, head_slab), low_type),
            pltpu.VMEM((2 * head_slab, width), full_type),
            pltpu.SemaphoreType.DMA((14,)),
            pltpu.SemaphoreType.DMA((24,)),
            pltpu.SemaphoreType.DMA((34,)),
            pltpu.SemaphoreType.DMA((34,)),
        ],
        compiler_params=pltpu.CompilerParams(
            collective_id=3, has_side_effects=True, vmem_limit_bytes=VMEM_GRANT
        ),
        name="layer",
    )(tokens, cotangent, planes, w_out, w_in, w_down, head_bias, unit_bias, vectors, seg_keys,
      seg_queries)


def layer_general(tokens, segments, w_qkv, head_bias, w_out, w_in, unit_bias, w_down, vectors,
                  cotangent):
    token_count, model_width = tokens.shape
    seq_count, length = segments.shape
    head_slab = w_qkv.shape[2]
    head_count = head_slab // DH
    tensor_size = lax.axis_size("tensor")
    share_rows = token_count // tensor_size
    tensor_place = lax.axis_index("tensor")
    row_start = tensor_place * share_rows
    head_scale = 1.0 / math.sqrt(DH)

    def own_rows(values):
        return lax.dynamic_slice_in_dim(values, row_start, share_rows, 0)

    flat_qkv = w_qkv.reshape(model_width, 3 * head_slab)
    projected = jnp.dot(tokens, flat_qkv, preferred_element_type=jnp.float32).reshape(
        token_count, 3, head_slab
    )
    head_shape = (seq_count, length, head_count, DH)
    queries = (
        ((projected[:, 0] + head_bias[0]) * head_scale).astype(jnp.bfloat16).reshape(head_shape)
    )
    key_heads = projected[:, 1].astype(jnp.bfloat16).reshape(head_shape)
    value_heads = (projected[:, 2] + head_bias[1]).astype(jnp.bfloat16).reshape(head_shape)
    mixed_heads, log_total = lax.map(attend_forward, (queries, key_heads, value_heads, segments))
    mixed_flat = mixed_heads.reshape(token_count, head_slab)
    attn_out = (
        lax.psum(jnp.dot(mixed_flat, w_out, preferred_element_type=jnp.float32), "tensor")
        + vectors[0]
    )
    first_norm, first_normed, first_inverse = norm_forward(
        tokens.astype(jnp.float32) + attn_out, vectors[2], vectors[3]
    )
    first_low = first_norm.astype(jnp.bfloat16)
    hidden = jnp.dot(first_low, w_in, preferred_element_type=jnp.float32) + unit_bias
    active, gelu_back = jax.vjp(partial(jax.nn.gelu, approximate=False), hidden)
    active_low = active.astype(jnp.bfloat16)
    grad_out_share = own_rows(cotangent).astype(jnp.float32)
    summed_input = (
        first_norm
        + lax.psum(jnp.dot(active_low, w_down, preferred_element_type=jnp.float32), "tensor")
        + vectors[1]
    )
    second_norm, second_normed, second_inverse = norm_forward(summed_input, vectors[4], vectors[5])
    layer_out = own_rows(second_norm).astype(jnp.bfloat16)
    grad_sum = norm_backward(
        cotangent.astype(jnp.float32), second_normed, second_inverse, vectors[4]
    )
    grad_branch = grad_sum.astype(jnp.bfloat16)
    second_share = own_rows(second_normed)
    grad_w_down = trans_times(active_low, grad_branch)
    grad_active = times_trans(grad_branch, w_down)
    grad_hidden = gelu_back(grad_active)[0].astype(jnp.bfloat16)
    grad_w_in = trans_times(first_low, grad_hidden)
    grad_units = jnp.sum(grad_hidden.astype(jnp.float32), axis=0)
    grad_first = lax.psum(times_trans(grad_hidden, w_in), "tensor") + grad_sum
    grad_h1 = norm_backward(grad_first, first_normed, first_inverse, vectors[2])
    grad_attn = grad_h1.astype(jnp.bfloat16)
    grad_first_share = own_rows(grad_first)
    first_normed_share = own_rows(first_normed)
    grad_h1_share = own_rows(grad_h1)
    grad_w_out = trans_times(mixed_flat, grad_attn)
    grad_mixed = times_trans(grad_attn, w_out).astype(jnp.bfloat16).reshape(head_shape)
    grad_query, grad_key, grad_value = lax.map(
        attend_backward, (queries, key_heads, value_heads, segments, grad_mixed, log_total)
    )
    grad_query = (
        grad_query.reshape(token_count, head_slab).astype(jnp.float32) * head_scale
    ).astype(jnp.bfloat16)
    grad_key = grad_key.reshape(token_count, head_slab)
    grad_value = grad_value.reshape(token_count, head_slab)
    grad_projected = jnp.stack([grad_query, grad_key, grad_value], axis=1).reshape(
        token_count, 3 * head_slab
    )
    grad_w_qkv = trans_times(tokens, grad_projected)
    grad_heads = jnp.stack(
        [
            jnp.sum(grad_query.astype(jnp.float32), axis=0),
            jnp.sum(grad_value.astype(jnp.float32), axis=0),
        ]
    )
    grad_tokens = (
        lax.psum_scatter(
            times_trans(grad_projected, flat_qkv).astype(jnp.bfloat16),
            "tensor",
            scatter_dimension=0,
            tiled=True,
        ).astype(jnp.float32)
        + grad_h1_share
    )
    local_vectors = jnp.stack(
        [
            jnp.sum(own_rows(grad_attn).astype(jnp.float32), axis=0),
            jnp.sum(own_rows(grad_branch).astype(jnp.float32), axis=0),
            jnp.sum(grad_first_share * first_normed_share, axis=0),
            jnp.sum(grad_first_share, axis=0),
            jnp.sum(grad_out_share * second_share, axis=0),
            jnp.sum(grad_out_share, axis=0),
        ]
    )
    return (
        layer_out,
        grad_tokens,
        (
            grad_w_qkv.reshape(model_width, 3, head_slab).transpose(1, 0, 2),
            grad_w_out,
            grad_w_in,
            grad_w_down,
        ),
        local_vectors,
        grad_heads,
        grad_units,
    )


def layer_split(tokens, segments, w_qkv, head_bias, w_out, w_in, unit_bias, w_down, vectors,
                cotangent):
    token_count, model_width = tokens.shape
    seq_count, length = segments.shape
    unit_slab = w_in.shape[1]
    tensor_size = lax.axis_size("tensor")
    share = token_count // tensor_size
    tensor_place = lax.axis_index("tensor")
    core = lax.rem(tensor_place, 2)
    seq = tensor_place // 2

    def to(values, step):
        return lax.ppermute(
            values, "tensor", [(place, place ^ step) for place in range(tensor_size)]
        )

    def rows_at(values, number, size):
        return lax.dynamic_slice_in_dim(values, number * size, size, 0)

    planes = w_qkv.transpose(1, 0, 2)
    seg_keys = jnp.broadcast_to(segments[:, :, None], (seq_count, length, LANES))
    seg_queries = segments[:, None, :]
    (projected, logs, mixed, _, _, _, _, layer_out, low, active, grad_branch, grad_hidden, grad_h1,
     grad_near, grad_far, down_near, down_rest, in_part, out_sum, out_far, units, unit_two, sums
     ) = layer_call(
        tokens, cotangent, planes, w_out, w_in, w_down, head_bias, unit_bias[None], vectors,
        seg_keys, seg_queries,
    )
    far_own = to(grad_far[0:1], 2)
    far_other = to(grad_far[1:2], 3)
    down_far = jnp.concatenate([down_near, to(down_rest, 2)], axis=0)
    in_far = to(in_part, 2)
    out_back = to(out_far, 2)

    grad_projected = jnp.zeros_like(projected)
    grad_projected, heads_near = attend_back(
        projected, seg_keys, seg_queries, (grad_near, 0), (grad_near, 1), mixed, logs, 1,
        grad_projected, seq, core,
    )
    grad_projected, heads_far = attend_back(
        projected, seg_keys, seg_queries, (far_own, 0), (far_other, 0), mixed, logs, 0,
        grad_projected, 1 - seq, core,
    )
    token_part = jnp.einsum(
        "gtn,gdn->td", grad_projected, planes, preferred_element_type=jnp.float32
    ).astype(jnp.bfloat16)
    other_one = to(
        jnp.stack([rows_at(token_part, 2 * at + 1 - core, share) for at in (seq, 1 - seq)]), 1
    ).astype(jnp.float32)
    across_part = rows_at(token_part, 2 * (1 - seq) + core, share).astype(jnp.float32)
    from_two = to((across_part + other_one[1]).astype(jnp.bfloat16), 2)
    grad_tokens = (
        rows_at(token_part, 2 * seq + core, share).astype(jnp.float32)
        + other_one[0]
        + from_two.astype(jnp.float32)
        + grad_h1
    )
    grad_w_qkv = jnp.einsum(
        "td,gtn->gdn", tokens, grad_projected, preferred_element_type=jnp.float32
    )
    grad_w_down = trans_times(active, grad_branch) + down_far.astype(jnp.float32)
    grad_w_in = trans_times(low, grad_hidden) + in_far.astype(jnp.float32)
    grad_w_out = out_sum + out_back.astype(jnp.float32)
    return (
        layer_out,
        grad_tokens,
        (grad_w_qkv, grad_w_out, grad_w_in, grad_w_down),
        sums,
        heads_near + heads_far,
        units[0, :unit_slab] + unit_two[0],
    )


def local(
    tokens,
    segments,
    w_qkv,
    head_bias,
    w_out,
    w_in,
    unit_bias,
    w_down,
    vectors,
    cotangent,
    err_qkv,
    err_out,
    err_in,
    err_down,
    basis_qkv,
    basis_out,
    basis_in,
    basis_down,
    mom_qkv,
    mom_head_bias,
    mom_out,
    mom_in,
    mom_unit_bias,
    mom_down,
    mom_vectors,
):
    token_count, model_width = tokens.shape
    head_slab = w_qkv.shape[2]
    unit_slab = w_in.shape[1]
    tensor_size = lax.axis_size("tensor")
    replicas = lax.axis_size("dp")
    one_sequence_per_chip = 2 * segments.shape[0] == tensor_size and replicas % 4 == 0
    layer = layer_split if one_sequence_per_chip else layer_general
    layer_out, grad_tokens, grads, local_vectors, grad_heads, grad_units = layer(
        tokens, segments, w_qkv, head_bias, w_out, w_in, unit_bias, w_down, vectors, cotangent
    )
    grad_w_qkv, grad_w_out, grad_w_in, grad_w_down = grads
    small = jnp.concatenate(
        [
            local_vectors,
            jnp.pad(grad_units, (0, model_width - unit_slab))[None],
            jnp.pad(grad_heads.reshape(1, 2 * head_slab), ((0, 0), (0, model_width - 2 * head_slab))),
        ],
        axis=0,
    )
    planes = (1, 0, 2)
    combined_qkv = grad_w_qkv + err_qkv[0].transpose(planes)
    combined_out = grad_w_out + err_out[0]
    combined_in = grad_w_in + err_in[0]
    combined_down = grad_w_down + err_down[0]
    matrices = (combined_qkv, combined_out, combined_in, combined_down)
    bases, rights, small_sum = compress(
        matrices,
        (basis_qkv.transpose(planes), basis_out, basis_in, basis_down),
        small,
        replicas,
        tensor_size,
    )
    step_rate = 0.3 * math.sqrt(replicas / token_count)
    grads, errors, moments, news = update(
        matrices,
        (mom_qkv.transpose(planes), mom_out, mom_in, mom_down),
        (w_qkv.transpose(planes), w_out, w_in, w_down),
        bases,
        rights,
        step_rate,
    )
    reduced_qkv, rank_out, rank_in, rank_down = (grads[0].transpose(planes),) + tuple(grads[1:])
    new_err_qkv, new_err_out, new_err_in, new_err_down = (
        errors[0].transpose(planes)[None],
        errors[1][None],
        errors[2][None],
        errors[3][None],
    )
    new_mom_qkv, new_mom_out, new_mom_in, new_mom_down = (moments[0].transpose(planes),) + tuple(
        moments[1:]
    )
    new_w_qkv, new_w_out, new_w_in, new_w_down = (news[0].transpose(planes),) + tuple(news[1:])
    right_qkv, right_out, right_in, right_down = rights
    new_basis_qkv = right_qkv.transpose(planes)
    grad_vectors = small_sum[:6]
    grad_unit_bias = small_sum[6, :unit_slab]
    grad_head_bias = small_sum[7, : 2 * head_slab].reshape(2, head_slab)
    new_mom_head_bias = 0.9 * mom_head_bias + grad_head_bias
    new_mom_unit_bias = 0.9 * mom_unit_bias + grad_unit_bias
    new_mom_vectors = 0.9 * mom_vectors + grad_vectors
    new_head_bias = head_bias - step_rate * new_mom_head_bias
    new_unit_bias = unit_bias - step_rate * new_mom_unit_bias
    new_vectors = vectors - step_rate * new_mom_vectors
    return (
        layer_out,
        grad_tokens,
        reduced_qkv,
        grad_head_bias,
        rank_out,
        rank_in,
        grad_unit_bias,
        rank_down,
        grad_vectors,
        new_err_qkv,
        new_err_out,
        new_err_in,
        new_err_down,
        new_basis_qkv,
        right_out,
        right_in,
        right_down,
        new_mom_qkv,
        new_mom_head_bias,
        new_mom_out,
        new_mom_in,
        new_mom_unit_bias,
        new_mom_down,
        new_mom_vectors,
        new_w_qkv,
        new_head_bias,
        new_w_out,
        new_w_in,
        new_unit_bias,
        new_w_down,
        new_vectors,
    )


def solution(mesh):
    in_specs = (
        P("dp", None),
        P("dp", None),
        P(None, None, "tensor"),
        P(None, "tensor"),
        P("tensor", None),
        P(None, "tensor"),
        P("tensor"),
        P("tensor", None),
        P(),
        P("dp", None),
        P("dp", None, None, "tensor"),
        P("dp", "tensor", None),
        P("dp", None, "tensor"),
        P("dp", "tensor", None),
        P(None, None, "tensor"),
        P("tensor", None),
        P(None, "tensor"),
        P("tensor", None),
        P(None, None, "tensor"),
        P(None, "tensor"),
        P("tensor", None),
        P(None, "tensor"),
        P("tensor"),
        P("tensor", None),
        P(),
    )
    out_specs = (
        P(("dp", "tensor"), None),
        P(("dp", "tensor"), None),
        P(None, None, "tensor"),
        P(None, "tensor"),
        P("tensor", None),
        P(None, "tensor"),
        P("tensor"),
        P("tensor", None),
        P(),
        P("dp", None, None, "tensor"),
        P("dp", "tensor", None),
        P("dp", None, "tensor"),
        P("dp", "tensor", None),
        P(None, None, "tensor"),
        P("tensor", None),
        P(None, "tensor"),
        P("tensor", None),
        P(None, None, "tensor"),
        P(None, "tensor"),
        P("tensor", None),
        P(None, "tensor"),
        P("tensor"),
        P("tensor", None),
        P(),
        P(None, None, "tensor"),
        P(None, "tensor"),
        P("tensor", None),
        P(None, "tensor"),
        P("tensor"),
        P("tensor", None),
        P(),
    )
    return jax.shard_map(local, mesh=mesh, in_specs=in_specs, out_specs=out_specs, check_vma=False)
```

```python
from functools import partial
import math

import jax
import jax.numpy as jnp
from jax import lax
from jax.experimental import pallas as pl
from jax.experimental.pallas import tpu as pltpu
from jax.sharding import PartitionSpec as P

DH = 64
LANES = 128
MESH = pl.DeviceIdType.MESH
VMEM_GRANT = 60 << 20
BRIEF = pl.CostEstimate(flops=1, bytes_accessed=1, transcendentals=1)


PRECISE = lax.Precision.HIGHEST
EPS_NORM = 1e-05
EPS_BASIS = 1e-08
MASKED = -1000000000.0


def norm_forward(values, gain, shift):
    row_mean = jnp.mean(values, axis=-1, keepdims=True)
    centred = values - row_mean
    variance = jnp.mean(centred * centred, axis=-1, keepdims=True)
    inverse = lax.rsqrt(variance + EPS_NORM)
    normed = centred * inverse
    return (normed * gain + shift, normed, inverse)


def norm_backward(grad_norm, normed, inverse, gain):
    scaled_grad = grad_norm * gain
    grad_mean = jnp.mean(scaled_grad, axis=-1, keepdims=True)
    along_norm = jnp.mean(scaled_grad * normed, axis=-1, keepdims=True)
    return inverse * (scaled_grad - grad_mean - normed * along_norm)


def times_trans(left_side, right_side):
    return lax.dot_general(
        left_side, right_side, (((1,), (1,)), ((), ())), preferred_element_type=jnp.float32
    )


def trans_times(left_side, right_side):
    return lax.dot_general(
        left_side, right_side, (((0,), (0,)), ((), ())), preferred_element_type=jnp.float32
    )


def split_bf16(values):
    high = values.astype(jnp.bfloat16)
    low = (values - high.astype(jnp.float32)).astype(jnp.bfloat16)
    return high, low


def dot_nt(left_side, right_side):
    return lax.dot_general(
        left_side, right_side, (((1,), (1,)), ((), ())), preferred_element_type=jnp.float32
    )


def dot_nn(left_side, right_side):
    return lax.dot_general(
        left_side, right_side, (((1,), (0,)), ((), ())), preferred_element_type=jnp.float32
    )


def dot_tn(left_side, right_side):
    return lax.dot_general(
        left_side, right_side, (((0,), (0,)), ((), ())), preferred_element_type=jnp.float32
    )


def low_left(factor, matrix):
    both = dot_nt(jnp.concatenate(split_bf16(factor), axis=0), matrix)
    return both[: factor.shape[0]] + both[factor.shape[0] :]


def low_right(basis_rows, matrix):
    both = dot_nn(jnp.concatenate(split_bf16(basis_rows), axis=0), matrix)
    return both[: basis_rows.shape[0]] + both[basis_rows.shape[0] :]


def left_factor(factor, matrix):
    rank_size = factor.shape[0]
    factor_high, factor_low = split_bf16(factor)
    matrix_high, matrix_low = split_bf16(matrix)
    both = dot_nt(jnp.concatenate([factor_high, factor_low], axis=0), matrix_high)
    return both[:rank_size] + both[rank_size:] + dot_nt(factor_high, matrix_low)


def right_factor(basis_rows, matrix):
    rank_size = basis_rows.shape[0]
    basis_high, basis_low = split_bf16(basis_rows)
    matrix_high, matrix_low = split_bf16(matrix)
    both = dot_nn(jnp.concatenate([basis_high, basis_low], axis=0), matrix_high)
    return both[:rank_size] + both[rank_size:] + dot_nn(basis_high, matrix_low)


def place_tiles(target, offset, values):
    per_chunk = target.shape[2] // LANES
    for tile in range(values.shape[1] // LANES):
        spot = offset + tile
        target[spot // per_chunk, :, pl.ds(spot % per_chunk * LANES, LANES)] = values[
            :, tile * LANES : (tile + 1) * LANES
        ]
    return offset + values.shape[1] // LANES


def add_tiles(target, offset, values):
    per_chunk = target.shape[2] // LANES
    for tile in range(values.shape[1] // LANES):
        spot = offset + tile
        target[spot // per_chunk, :, pl.ds(spot % per_chunk * LANES, LANES)] += values[
            :, tile * LANES : (tile + 1) * LANES
        ]


def take_tiles(source, offset, size):
    per_chunk = source.shape[2] // LANES
    pieces = []
    for tile in range(size // LANES):
        spot = offset + tile
        pieces.append(source[spot // per_chunk, :, pl.ds(spot % per_chunk * LANES, LANES)])
    return jnp.concatenate(pieces, axis=1) if len(pieces) > 1 else pieces[0]


def orthonormal_rows(rows):
    rank_size = rows.shape[0]
    row_number = lax.broadcasted_iota(jnp.int32, (rank_size, 1), 0)
    for position in range(rank_size):
        row = rows[position : position + 1]
        length = jnp.sqrt(jnp.sum(row * row, axis=1, keepdims=True)) + EPS_BASIS
        unit = row / length
        along = jnp.sum(rows * unit, axis=1, keepdims=True)
        later = jnp.where(row_number > position, along, 0.0)
        rows = jnp.where(row_number == position, unit, rows - later * unit)
    return rows


def dp_exchange(replicas, mine, wire, arrived, total, sems, meanwhile=None):
    send_one, recv_one, send_two, recv_two = sems
    dp_place = lax.axis_index("dp")
    tensor_place = lax.axis_index("tensor")

    def peer_of(step):
        return lax.rem(dp_place + step, replicas)

    def scatter(step, slot):
        return pltpu.make_async_remote_copy(
            src_ref=wire.at[peer_of(step)],
            dst_ref=arrived.at[slot],
            send_sem=send_one.at[step],
            recv_sem=recv_one.at[slot],
            device_id=(peer_of(step), tensor_place),
            device_id_type=MESH,
        )

    def gather(step, slot):
        return pltpu.make_async_remote_copy(
            src_ref=total.at[dp_place],
            dst_ref=total.at[slot],
            send_sem=send_two.at[step],
            recv_sem=recv_two.at[slot],
            device_id=(peer_of(step), tensor_place),
            device_id_type=MESH,
        )

    def start_scatter(step, carry):
        scatter(step, dp_place).start()
        return carry

    def add_arrived(step, carry):
        scatter(step, peer_of(step)).wait_recv()
        return carry + arrived[peer_of(step)].astype(jnp.float32)

    def start_gather(step, carry):
        gather(step, dp_place).start()
        return carry

    def finish(step, carry):
        gather(step, peer_of(step)).wait_recv()
        return carry

    wire[...] = mine[...].astype(wire.dtype)
    lax.fori_loop(1, replicas, start_scatter, 0)
    total[dp_place] = lax.fori_loop(1, replicas, add_arrived, mine[dp_place])
    lax.fori_loop(1, replicas, start_gather, 0)
    lax.fori_loop(1, replicas, finish, 0)

    def drain(step, carry):
        scatter(step, dp_place).wait_send()
        gather(step, dp_place).wait_send()
        return carry

    return lambda: lax.fori_loop(1, replicas, drain, 0)


def compress_kernel(replicas, tensor_size, has_far, *refs):
    if has_far:
        far_refs, refs = refs[:4], refs[4:]
    compress_body(replicas, tensor_size, far_refs if has_far else None, *refs)


def compress_body(replicas, tensor_size, far_refs, qkv_ref, out_ref, in_ref, down_ref,
                    fq_ref, fo_ref, fi_ref, fd_ref, small_ref,
                    bq_ref, bo_ref, bi_ref, bd_ref, rq_ref, ro_ref, ri_ref, rd_ref, sum_ref,
                    qkv, out, inw, down, mine, wire, arrived, total,
                    mine_two, wire_two, arrived_two, total_two, small_slots,
                    load_sem, *sems):
    first_sems, second_sems, (send_small, recv_small) = sems[:4], sems[4:8], sems[8:10]
    dp_place = lax.axis_index("dp")
    tensor_place = lax.axis_index("tensor")
    loads = [
        pltpu.make_async_copy(source, target, load_sem.at[number])
        for number, (source, target) in enumerate(
            [(qkv_ref, qkv), (out_ref, out), (down_ref, down), (in_ref, inw)]
        )
    ]
    if far_refs:
        far_in_ref, far_down_ref, far_factor_in, far_factor_down = far_refs
        far_in, far_down, sent, got, far_send, far_recv = sems[10:]
        far_loads = [
            pltpu.make_async_copy(far_in_ref, far_in, load_sem.at[4]),
            pltpu.make_async_copy(far_down_ref, far_down, load_sem.at[5]),
        ]
        for load in far_loads:
            load.start()

        def far_copy(number):
            return pltpu.make_async_remote_copy(
                src_ref=sent.at[number],
                dst_ref=got.at[number],
                send_sem=far_send.at[number],
                recv_sem=far_recv.at[number],
                device_id=(dp_place, tensor_place + 2 - 4 * (tensor_place // 2)),
                device_id_type=MESH,
            )

    for load in loads:
        load.start()
    barrier = pltpu.get_barrier_semaphore()

    def greet_dp(step, carry):
        pl.semaphore_signal(
            barrier,
            inc=1,
            device_id=(lax.rem(dp_place + step, replicas), tensor_place),
            device_id_type=MESH,
        )
        return carry

    def greet_tensor(step, carry):
        pl.semaphore_signal(
            barrier,
            inc=1,
            device_id=(dp_place, lax.rem(tensor_place + step, tensor_size)),
            device_id_type=MESH,
        )
        return carry

    lax.fori_loop(1, replicas, greet_dp, 0)
    lax.fori_loop(1, tensor_size, greet_tensor, 0)
    mine[...] = jnp.zeros_like(mine)
    mine_two[...] = jnp.zeros_like(mine_two)
    block = 2 * LANES
    if far_refs:
        for number, (factor_ref, matrix) in enumerate(
            ((far_factor_down, far_down), (far_factor_in, far_in))
        ):
            far_loads[1 - number].wait()
            for start in range(0, matrix.shape[0], block):
                rows = slice(start, start + block)
                sent[0, number, :, rows] = low_left(factor_ref[...], matrix[rows])
        pl.semaphore_wait(barrier, replicas - 1 + tensor_size - 1)
        far_copy(0).start()
    offset = 0
    loads[0].wait()
    for start in range(0, qkv.shape[1], block):
        rows = slice(start, start + block)
        left = left_factor(fq_ref[0], qkv[0, rows])
        for part in range(1, 3):
            left += left_factor(fq_ref[part], qkv[part, rows])
        offset = place_tiles(mine, offset, left)
    for load, factor_ref, matrix in zip(loads[1:], (fo_ref, fd_ref, fi_ref), (out, down, inw)):
        load.wait()
        rows_of = min(block, matrix.shape[0])
        for start in range(0, matrix.shape[0], rows_of):
            left = left_factor(factor_ref[...], matrix[start : start + rows_of])
            offset = place_tiles(mine, offset, left)
    place_tiles(mine, offset, small_ref[...])
    if far_refs:
        far_copy(0).wait_recv()
        add_tiles(mine, offset - 2 * down.shape[0] // LANES, got[0, 0])
        add_tiles(mine, offset - inw.shape[0] // LANES, got[0, 1])
    else:
        pl.semaphore_wait(barrier, replicas - 1 + tensor_size - 1)
    drain_one = dp_exchange(replicas, mine, wire, arrived, total, first_sems)

    def slot_copy(step, slot):
        peer = lax.rem(tensor_place + step, tensor_size)
        return pltpu.make_async_remote_copy(
            src_ref=small_slots.at[tensor_place],
            dst_ref=small_slots.at[slot],
            send_sem=send_small.at[step],
            recv_sem=recv_small.at[slot],
            device_id=(dp_place, peer),
            device_id_type=MESH,
        )

    def start_small(step, carry):
        slot_copy(step, tensor_place).start()
        return carry

    own_small = take_tiles(total, offset, small_ref.shape[1])
    small_slots[tensor_place] = own_small
    lax.fori_loop(1, tensor_size, start_small, 0)
    offset = 0
    offset_two = 0
    offsets = []
    for basis_ref in (bq_ref, bo_ref, bd_ref, bi_ref):
        offsets.append(offset)
        offset += basis_ref.shape[1] // LANES
    for number in (2, 3, 0, 1):
        basis_ref = (bq_ref, bo_ref, bd_ref, bi_ref)[number]
        rows = take_tiles(total, offsets[number], basis_ref.shape[1]) * (1.0 / replicas)
        basis_ref[...] = orthonormal_rows(rows)
        if far_refs and number >= 2:
            sent[1, number - 2] = basis_ref[...]
        if far_refs and number == 3:
            far_copy(1).start()
    drain_one()
    for part in range(3):
        right = right_factor(bq_ref[:, :block], qkv[part, :block])
        for start in range(block, qkv.shape[1], block):
            rows = slice(start, start + block)
            right += right_factor(bq_ref[:, rows], qkv[part, rows])
        offset_two = place_tiles(mine_two, offset_two, right)
    for basis_ref, matrix in zip((bo_ref, bd_ref, bi_ref), (out, down, inw)):
        rows_of = min(block, matrix.shape[0])
        right = right_factor(basis_ref[:, :rows_of], matrix[:rows_of])
        for start in range(rows_of, matrix.shape[0], rows_of):
            rows = slice(start, start + rows_of)
            right += right_factor(basis_ref[:, rows], matrix[rows])
        offset_two = place_tiles(mine_two, offset_two, right)
    if far_refs:
        far_copy(1).wait_recv()
        sent[2, 0] = low_right(got[1, 0], far_down[...])
        sent[2, 1] = low_right(got[1, 1], far_in[...])
        far_copy(2).start()
        far_copy(2).wait_recv()
        add_tiles(mine_two, offset_two - (down.shape[1] + inw.shape[1]) // LANES, got[2, 0])
        add_tiles(mine_two, offset_two - inw.shape[1] // LANES, got[2, 1])
    drain_two = dp_exchange(
        replicas, mine_two, wire_two, arrived_two, total_two, second_sems
    )

    def collect(step, carry):
        peer = lax.rem(tensor_place + step, tensor_size)
        slot_copy(step, peer).wait_recv()
        slot_copy(step, tensor_place).wait_send()
        return carry + small_slots[peer]

    everyone = lax.fori_loop(1, tensor_size, collect, own_small)
    row_number = lax.broadcasted_iota(jnp.int32, everyone.shape, 0)
    sum_ref[...] = jnp.where(row_number < 6, everyone, own_small) * (1.0 / replicas)
    offset = 0
    for part in range(3):
        rq_ref[part] = take_tiles(total_two, offset, rq_ref.shape[2]) * (1.0 / replicas)
        offset += rq_ref.shape[2] // LANES
    for ref in (ro_ref, rd_ref, ri_ref):
        ref[...] = take_tiles(total_two, offset, ref.shape[1]) * (1.0 / replicas)
        offset += ref.shape[1] // LANES
    drain_two()
    if far_refs:
        for number in range(3):
            far_copy(number).wait_send()


def compress(matrices, factors, small, replicas, tensor_size, far):
    qkv, out, inw, down = matrices
    rank_size = small.shape[0]
    sizes = (qkv.shape[1], out.shape[0], inw.shape[0], down.shape[0])
    right_shapes = [(3, rank_size, qkv.shape[2])] + [(rank_size, one.shape[1]) for one in matrices[1:]]
    lanes_one = sum(sizes) + small.shape[1]
    lanes_two = 3 * qkv.shape[2] + sum(one.shape[1] for one in matrices[1:])
    scratch = [pltpu.VMEM(one.shape, jnp.float32) for one in matrices]
    for lanes in (lanes_one, lanes_two):
        shape = (replicas, rank_size, -(-lanes // (LANES * replicas)) * LANES)
        scratch += [
            pltpu.VMEM(shape, jnp.float32),
            pltpu.VMEM(shape, jnp.bfloat16),
            pltpu.VMEM(shape, jnp.bfloat16),
            pltpu.VMEM(shape, jnp.float32),
        ]
    scratch += [pltpu.VMEM((tensor_size,) + small.shape, jnp.float32), pltpu.SemaphoreType.DMA((6,))]
    scratch += [pltpu.SemaphoreType.DMA((replicas,))] * 8
    scratch += [pltpu.SemaphoreType.DMA((tensor_size,))] * 2
    if far:
        scratch += [pltpu.VMEM(one.shape, one.dtype) for one in far[:2]]
        scratch += [pltpu.VMEM((3, 2, rank_size, inw.shape[0]), jnp.float32)] * 2
        scratch += [pltpu.SemaphoreType.DMA((3,))] * 2
    vmem = pl.BlockSpec(memory_space=pltpu.VMEM)
    shapes = [(rank_size, size) for size in sizes] + right_shapes + [small.shape]
    outputs = pl.pallas_call(
        partial(compress_kernel, replicas, tensor_size, bool(far)),
        in_specs=([pl.BlockSpec(memory_space=pl.ANY)] * 2 + [vmem] * 2 if far else [])
        + [pl.BlockSpec(memory_space=pl.ANY)] * 4
        + [vmem] * 5,
        out_specs=[vmem] * 9,
        out_shape=[jax.ShapeDtypeStruct(shape, jnp.float32) for shape in shapes],
        scratch_shapes=scratch,
        compiler_params=pltpu.CompilerParams(
            collective_id=1, has_side_effects=True, vmem_limit_bytes=VMEM_GRANT
        ),
        name="compress",
    )(*far, *matrices, *factors, small)
    return outputs[:4], outputs[4:8], outputs[8]


def outer_of(basis_rows, right):
    basis_high, basis_low = split_bf16(basis_rows)
    right_high, right_low = split_bf16(right)
    return dot_tn(
        jnp.concatenate([basis_high, basis_low, basis_high], axis=0),
        jnp.concatenate([right_high, right_high, right_low], axis=0),
    )


def update_kernel(step_rate, out_steps, near_steps, *refs):
    (mq, mo, mi, md, oq, oo, oi, od, wq, wo, wi, wd, bq, bo, bi, bd, rq, ro, ri, rd,
     gq, go, gi, gd, eq, eo, ei, ed, nq, no, ni, nd, vq, vo, vi, vd) = refs[:20] + refs[-16:]
    step = pl.program_id(0)
    whole_in, whole_down = mi[...], md[...]
    if len(refs) > 36:
        late_in, near_down, rest_down = refs[20:23]
        whole_in += late_in[...].astype(jnp.float32)
        whole_down += jnp.where(step < near_steps, near_down[...], rest_down[...]).astype(
            jnp.float32
        )

    def one(matrix, old, weight, rank, grad_ref, err_ref, mom_ref, new_ref, place):
        moment = 0.9 * old + rank
        grad_ref[place] = rank
        err_ref[place] = matrix - rank
        mom_ref[place] = moment
        new_ref[place] = weight.astype(jnp.float32) - step_rate * moment

    def lanes_of(ref, rows):
        return ref[:, pl.ds(pl.multiple_of(step * rows, LANES), rows)]

    rows = mq.shape[1]
    for part in range(3):
        rank = outer_of(lanes_of(bq, rows), rq[part])
        one(mq[part], oq[part], wq[part], rank, gq, eq, nq, vq, part)
    rank = outer_of(lanes_of(bi, mi.shape[0]), ri[...])
    one(whole_in, oi[...], wi[...], rank, gi, ei, ni, vi, slice(None))
    rank = outer_of(lanes_of(bd, md.shape[0]), rd[...])
    one(whole_down, od[...], wd[...], rank, gd, ed, nd, vd, slice(None))

    @pl.when(step < out_steps)
    def _():
        rank = outer_of(lanes_of(bo, mo.shape[0]), ro[...])
        one(mo[...], oo[...], wo[...], rank, go, eo, no, vo, slice(None))


def update(matrices, momenta, weights, bases, rights, late, step_rate):
    qkv, out, inw, down = matrices
    rows = LANES
    steps = inw.shape[0] // rows
    down_rows = down.shape[0] // steps
    if down_rows < LANES:
        steps = down.shape[0] // LANES
        rows, down_rows = inw.shape[0] // steps, LANES
    out_steps = out.shape[0] // LANES
    near_steps = late[1].shape[0] // down_rows if late else 0
    late_specs = [
        pl.BlockSpec((rows, inw.shape[1]), lambda i: (i, 0)),
        pl.BlockSpec((down_rows, down.shape[1]), lambda i: (jnp.minimum(i, near_steps - 1), 0)),
        pl.BlockSpec((down_rows, down.shape[1]), lambda i: (jnp.maximum(i - near_steps, 0), 0)),
    ]

    def whole(array):
        return pl.BlockSpec(array.shape, lambda i: (0,) * array.ndim)

    def specs():
        return [
            pl.BlockSpec((3, rows, qkv.shape[2]), lambda i: (0, i, 0)),
            pl.BlockSpec((LANES, out.shape[1]), lambda i: (jnp.minimum(i, out_steps - 1), 0)),
            pl.BlockSpec((rows, inw.shape[1]), lambda i: (i, 0)),
            pl.BlockSpec((down_rows, down.shape[1]), lambda i: (i, 0)),
        ]

    shapes = [jax.ShapeDtypeStruct(one.shape, jnp.float32) for one in matrices]
    outputs = pl.pallas_call(
        partial(update_kernel, step_rate, out_steps, near_steps),
        grid=(steps,),
        in_specs=specs() * 3
        + [whole(one) for one in bases]
        + [whole(one) for one in rights]
        + late_specs[: len(late)],
        out_specs=specs() * 4,
        out_shape=shapes * 4,
        compiler_params=pltpu.CompilerParams(vmem_limit_bytes=VMEM_GRANT),
        name="update",
    )(*matrices, *momenta, *weights, *bases, *rights, *late)
    return outputs[0:4], outputs[4:8], outputs[8:12], outputs[12:16]


def masked_scores(queries, key_heads, seg_ids):
    scores = jnp.einsum("qhd,khd->hqk", queries, key_heads, preferred_element_type=jnp.float32)
    same_doc = seg_ids[:, None] == seg_ids[None, :]
    return jnp.where(same_doc[None], scores, MASKED)


def attend_forward(inputs_of):
    queries, key_heads, value_heads, seg_ids = inputs_of
    scores = masked_scores(queries, key_heads, seg_ids)
    highest = jnp.max(scores, axis=-1, keepdims=True)
    powers = jnp.exp(scores - highest)
    denominator = jnp.sum(powers, axis=-1, keepdims=True)
    weights = (powers / denominator).astype(jnp.bfloat16)
    mixed_heads = jnp.einsum(
        "hqk,khd->qhd", weights, value_heads, preferred_element_type=jnp.float32
    )
    return (mixed_heads.astype(jnp.bfloat16), highest[..., 0] + jnp.log(denominator[..., 0]))


def attend_backward(inputs_of):
    queries, key_heads, value_heads, seg_ids, grad_mixed, log_total = inputs_of
    scores = masked_scores(queries, key_heads, seg_ids)
    probability = jnp.exp(scores - log_total[..., None])
    grad_probs = jnp.einsum(
        "qhd,khd->hqk", grad_mixed, value_heads, preferred_element_type=jnp.float32
    )
    centre = jnp.sum(probability * grad_probs, axis=-1, keepdims=True)
    grad_scores = (probability * (grad_probs - centre)).astype(jnp.bfloat16)
    grad_query = jnp.einsum(
        "hqk,khd->qhd", grad_scores, key_heads, preferred_element_type=jnp.float32
    )
    grad_key = jnp.einsum("hqk,qhd->khd", grad_scores, queries, preferred_element_type=jnp.float32)
    grad_value = jnp.einsum(
        "hqk,qhd->khd",
        probability.astype(jnp.bfloat16),
        grad_mixed,
        preferred_element_type=jnp.float32,
    )
    return (
        grad_query.astype(jnp.bfloat16),
        grad_key.astype(jnp.bfloat16),
        grad_value.astype(jnp.bfloat16),
    )


def stacked_heads(pair, lane_is_low):
    zero = jnp.zeros_like(pair)
    return jnp.concatenate(
        [jnp.where(lane_is_low, pair, zero), jnp.where(lane_is_low, zero, pair)], axis=0
    )


def own_blocks(both):
    rows = both.shape[1] // 2
    return jnp.concatenate([both[:DH, :rows], both[DH:, rows:]], axis=0).T


def window_sizes(length):
    return (length * 3 // 8, length * 5 // 8, length)


def windows_of(bounds, length):
    first = bounds[0] // LANES * LANES
    need = bounds[1] - first
    small, large, whole = window_sizes(length)
    number = jnp.where(need <= small, 0, jnp.where(need <= large, 1, 2))
    room = jnp.where(need <= small, length - small, jnp.where(need <= large, length - large, 0))
    return jnp.concatenate([jnp.minimum(first, room), number])


def attend_back_kernel(place_ref, q_ref, k_ref, v_ref, seg_key_ref, seg_query_ref, gm_own_ref,
                       gm_other_ref, mixed_ref, log_ref, old_ref, grad_ref, sums_ref, key_t, grad_key,
                       grad_value):
    del old_ref
    step = pl.program_id(0)

    @pl.when(step == 0)
    def _():
        key_t[...] = k_ref[...].T
        grad_key[...] = jnp.zeros_like(grad_key)
        grad_value[...] = jnp.zeros_like(grad_value)

    pairs = q_ref.shape[1] // LANES
    lane = lax.broadcasted_iota(jnp.int32, (1, LANES), 1)
    lane_is_low = lane < DH
    head_of_lane = (
        lax.broadcasted_iota(jnp.int32, (8, LANES), 0)
        == lax.broadcasted_iota(jnp.int32, (8, LANES), 1) // DH
    ).astype(jnp.bfloat16)
    head_scale = 1.0 / math.sqrt(DH)
    here = pl.ds(pl.multiple_of(step * LANES, LANES), LANES)
    is_own = lax.rem(step // (pl.num_programs(0) // 2) + place_ref[1], 2) == 0
    gm = jnp.where(is_own, gm_own_ref[...], gm_other_ref[...])
    seg_query = jnp.concatenate([seg_query_ref[...], seg_query_ref[...]], axis=1)
    all_lanes = [slice(pair * LANES, (pair + 1) * LANES) for pair in range(pairs)]
    length = k_ref.shape[0]

    def window(size):
        start = 0 if size == length else pl.multiple_of(place_ref[2 + step], LANES)
        keys = pl.ds(start, size)
        seg_key = seg_key_ref[keys]
        same = jnp.concatenate([seg_key, seg_key], axis=1) == seg_query
        queries, grads, centres, probs, grad_probs = [], [], [], [], []
        for lanes in all_lanes:
            queries.append(stacked_heads(q_ref[:, lanes], lane_is_low))
            grads.append(stacked_heads(gm[:, lanes], lane_is_low))
            high, low = split_bf16(
                gm[:, lanes].astype(jnp.float32) * mixed_ref[:, lanes].astype(jnp.float32)
            )
            sums = dot_nt(head_of_lane, high) + dot_nt(head_of_lane, low)
            centres.append(jnp.concatenate([sums[0:1], sums[1:2]], axis=1))
        for pair, lanes in enumerate(all_lanes):
            log_total = jnp.concatenate(
                [log_ref[2 * pair : 2 * pair + 1], log_ref[2 * pair + 1 : 2 * pair + 2]], axis=1
            )
            scores = dot_nt(k_ref[keys, lanes], queries[pair])
            probs.append(jnp.exp(jnp.where(same, scores - log_total, MASKED)))
            grad_probs.append(dot_nt(v_ref[keys, lanes], grads[pair]))
        for pair, lanes in enumerate(all_lanes):
            grad_scores = (probs[pair] * (grad_probs[pair] - centres[pair])).astype(jnp.bfloat16)
            grad_value[keys, lanes] += dot_nn(probs[pair].astype(jnp.bfloat16), grads[pair])
            grad_key[keys, lanes] += dot_nn(grad_scores, queries[pair])
            grad_query = own_blocks(dot_nn(key_t[lanes, keys], grad_scores)).astype(jnp.bfloat16)
            grad_ref[0, here, lanes] = (grad_query.astype(jnp.float32) * head_scale).astype(
                jnp.bfloat16
            )

    for number, size in enumerate(window_sizes(length)):
        pl.when(place_ref[2 + pl.num_programs(0) + step] == number)(partial(window, size))

    @pl.when(step == pl.num_programs(0) - 1)
    def _():
        grad_ref[1] = grad_key[...].astype(jnp.bfloat16)
        low_value = grad_value[...].astype(jnp.bfloat16)
        grad_ref[2] = low_value
        sums_ref[0:1] = jnp.sum(grad_ref[0].astype(jnp.float32), axis=0, keepdims=True)
        sums_ref[1:2] = jnp.sum(low_value.astype(jnp.float32), axis=0, keepdims=True)


def attend_back(projected, seg_keys, seg_queries, grad_own, grad_other, mixed, logs, slot, bounds,
                old, place, core):
    length = seg_keys.shape[1]
    slab = projected.shape[2]
    blocks = length // LANES
    half = blocks // 2
    at = jnp.concatenate(
        [
            jnp.stack([place, core]),
            windows_of(bounds[2 * slot : 2 * slot + 2, :blocks], length),
        ]
    )
    grid_spec = pltpu.PrefetchScalarGridSpec(
        num_scalar_prefetch=1,
        grid=(blocks,),
        in_specs=[
            pl.BlockSpec((None, LANES, slab), lambda i, at: (0, at[0] * blocks + i, 0)),
            pl.BlockSpec((None, length, slab), lambda i, at: (1, at[0], 0)),
            pl.BlockSpec((None, length, slab), lambda i, at: (2, at[0], 0)),
            pl.BlockSpec((None, length, LANES), lambda i, at: (at[0], 0, 0)),
            pl.BlockSpec((None, 1, LANES), lambda i, at: (at[0], 0, i)),
            pl.BlockSpec((None, LANES, slab), lambda i, at: (grad_own[1], lax.rem(i, half), 0)),
            pl.BlockSpec((None, LANES, slab), lambda i, at: (grad_other[1], lax.rem(i, half), 0)),
            pl.BlockSpec((None, LANES, slab), lambda i, at: (slot, i, 0)),
            pl.BlockSpec((None, slab // DH, LANES), lambda i, at: (slot, 0, i)),
            pl.BlockSpec(memory_space=pl.ANY),
        ],
        out_specs=[
            pl.BlockSpec((3, length, slab), lambda i, at: (0, at[0], 0)),
            pl.BlockSpec((2, slab), lambda i, at: (0, 0)),
        ],
        scratch_shapes=[
            pltpu.VMEM((slab, length), jnp.bfloat16),
            pltpu.VMEM((length, slab), jnp.float32),
            pltpu.VMEM((length, slab), jnp.float32),
        ],
    )
    return pl.pallas_call(
        attend_back_kernel,
        grid_spec=grid_spec,
        out_shape=[
            jax.ShapeDtypeStruct(projected.shape, jnp.bfloat16),
            jax.ShapeDtypeStruct((2, slab), jnp.float32),
        ],
        input_output_aliases={} if old is None else {10: 0},
        compiler_params=pltpu.CompilerParams(vmem_limit_bytes=24 << 20),
        cost_estimate=BRIEF,
        name="attend_back",
    )(at, projected, projected, projected, seg_keys, seg_queries, grad_own[0],
      grad_other[0], mixed, logs, seg_keys if old is None else old)


def row_mean(values):
    return jnp.mean(values, axis=-1, keepdims=True)


def layer_kernel(tokens, cotangent, w_qkv_ref, out_ref, in_ref, down_ref,
                 factor_in_ref, factor_down_ref, head_ref, bias_ref, vec_ref, seg_keys, seg_queries,
                 projected_out, log_out, mixed_out, in_two, down_two, out_rest, bias_two,
                 result_out, low_out, active_out, branch_out, hidden_out, norm_out, near_out,
                 far_out, down_near, down_part_out, in_part_out, far_in_out, far_down_out, out_sum,
                 out_far, unit_ref, unit_two, sums_ref, bounds_ref,
                 rows_in, w_qkv, projected, value_t, log_total, mixed, pieces,
                 w_out, w_in, w_down, bias, tok, cot, first, normed, inverse, low, slope, active,
                 part, other, acc, wide, branch, result, down_part, near, far_mixed, outs_two,
                 load_sem, store_sem, send_sem, recv_sem):
    dp_place = lax.axis_index("dp")
    tensor_place = lax.axis_index("tensor")
    core = lax.rem(tensor_place, 2)
    seq = tensor_place // 2
    far = 1 - seq
    side = lax.rem(dp_place, 2)
    depth = lax.rem(dp_place // 2, 2)
    here = 2 * depth + side
    sibling = (dp_place, tensor_place + 1 - 2 * core)
    opposite = (dp_place, core + 2 * far)
    diagonal = (dp_place, 1 - core + 2 * far)
    beside = (dp_place + 1 - 2 * side, tensor_place)
    behind = (dp_place + 2 - 4 * depth, tensor_place)
    share, width = tok.shape
    slab = in_ref.shape[1]
    length = rows_in.shape[1]
    head_slab = w_qkv.shape[2]
    head_count = head_slab // DH
    stores = []
    sends = []
    numbers = iter(range(send_sem.shape[0]))

    def load(number, source, target):
        copy = pltpu.make_async_copy(source, target, load_sem.at[number])
        copy.start()
        return copy

    def store(source, target):
        copy = pltpu.make_async_copy(source, target, store_sem.at[len(stores)])
        copy.start()
        stores.append(copy)

    def send(source, target, device):
        number = next(numbers)
        copy = pltpu.make_async_remote_copy(
            src_ref=source,
            dst_ref=target,
            send_sem=send_sem.at[number],
            recv_sem=recv_sem.at[number],
            device_id=device,
            device_id_type=MESH,
        )
        copy.start()
        sends.append(copy)
        return copy

    def rows_of(number, size):
        return pl.ds(pl.multiple_of(number * size, LANES), size)

    load_qkv = load(0, w_qkv_ref, w_qkv)
    load_far = load(1, tokens.at[rows_of(far, length)], rows_in.at[0])
    load_near = load(2, tokens.at[rows_of(seq, length)], rows_in.at[1])
    load_out = load(3, out_ref, w_out.at[0])
    load_in = load(4, in_ref, w_in.at[0])
    load_down = load(5, down_ref, w_down.at[pl.ds(0, slab)])
    load_tok = load(6, tokens.at[rows_of(tensor_place, share)], tok)
    load_cot = load(7, cotangent.at[rows_of(tensor_place, share)], cot)

    barrier = pltpu.get_barrier_semaphore()
    for device in (sibling, opposite, diagonal, beside, behind):
        pl.semaphore_signal(barrier, inc=1, device_id=device, device_id_type=MESH)
    pl.semaphore_wait(barrier, 5)
    sums_ref[...] = jnp.zeros_like(sums_ref)
    unit_ref[...] = jnp.zeros_like(unit_ref)

    def rows_part(whole, number, parts):
        size = whole.shape[0] // parts
        return whole.at[pl.ds(pl.multiple_of(number * size, size), size)]

    class Fetch:
        def __init__(self, source, whole):
            self.whole = whole
            self.over_y = send(
                rows_part(source, here, 4), rows_part(whole, here, 4), opposite
            )

        def pass_on(self):
            self.over_y.wait_recv()
            own = rows_part(self.whole, here, 4)
            self.over_x = send(own, own, beside)
            self.over_z = send(own, own, behind)

        def pass_halves(self):
            self.over_x.wait_recv()
            half = rows_part(self.whole, 2 * (here + 1 - 2 * side), 8)
            self.half_z = send(half, half, behind)
            self.over_z.wait_recv()
            half = rows_part(self.whole, 2 * (here + 2 - 4 * depth) + 1, 8)
            self.half_x = send(half, half, beside)

        def wait(self):
            self.half_z.wait_recv()
            self.half_x.wait_recv()

    bias_send = send(bias_ref, bias_two, opposite)
    factor_sends = [
        send(factor_in_ref, far_in_out, opposite), send(factor_down_ref, far_down_out, opposite)
    ]
    fetch_out = Fetch(out_ref, out_rest.at[1])
    fetch_in = Fetch(in_ref, in_two)

    chunk = 256
    scale = 1.0 / math.sqrt(DH)

    def project(slot):
        def rows_step(step, carry):
            rows = rows_of(step, chunk)
            values = rows_in[slot, rows]
            projected[slot, 0, rows] = (
                (dot_nn(values, w_qkv[0]) + head_ref[0:1]) * scale
            ).astype(jnp.bfloat16)
            projected[slot, 1, rows] = dot_nn(values, w_qkv[1]).astype(jnp.bfloat16)
            projected[slot, 2, rows] = (dot_nn(values, w_qkv[2]) + head_ref[1:2]).astype(
                jnp.bfloat16
            )
            return carry

        lax.fori_loop(0, length // chunk, rows_step, 0)
        value_t[...] = projected[slot, 2].T

    lane_is_low = lax.broadcasted_iota(jnp.int32, (1, LANES), 1) < DH

    def attend_rows(slot, place, start, stop):
        def block(step, carry):
            rows = rows_of(step, LANES)
            same = seg_keys[place] == seg_queries[place, :, rows]
            mask = jnp.where(same, 0.0, MASKED)
            mask = jnp.concatenate([mask, mask], axis=1)
            all_lanes = [slice(at, at + LANES) for at in range(0, head_slab, LANES)]
            all_scores = [
                dot_nt(
                    projected[slot, 1, :, lanes],
                    stacked_heads(projected[slot, 0, rows, lanes], lane_is_low),
                )
                + mask
                for lanes in all_lanes
            ]
            for pair, (lanes, scores) in enumerate(zip(all_lanes, all_scores)):
                highest = jnp.max(scores, axis=0, keepdims=True)
                powers = jnp.exp(scores - highest)
                denominator = jnp.sum(powers, axis=0, keepdims=True)
                blend = dot_nn(value_t[lanes], powers.astype(jnp.bfloat16))
                mixed[slot, rows, lanes] = own_blocks(blend * (1.0 / denominator)).astype(
                    jnp.bfloat16
                )
                total = highest + jnp.log(denominator)
                log_total[slot, 2 * pair : 2 * pair + 1, rows] = total[:, :LANES]
                log_total[slot, 2 * pair + 1 : 2 * pair + 2, rows] = total[:, LANES:]
            return carry

        lax.fori_loop(start, stop, block, 0, unroll=2)

    blocks = length // LANES
    load_qkv.wait()
    load_far.wait()
    project(0)
    attend_rows(0, far, 0, 4)
    fetch_out.pass_on()
    fetch_in.pass_on()
    fetch_down = Fetch(down_ref, down_two)
    attend_rows(0, far, 4, blocks)
    own_rows = rows_of(core, share)
    sibling_rows = rows_of(1 - core, share)
    piece_two = send(mixed.at[0, own_rows], pieces.at[1], opposite)
    piece_three = send(mixed.at[0, sibling_rows], pieces.at[2], diagonal)
    store(projected.at[0, 0], projected_out.at[0, rows_of(far, length)])
    store(projected.at[0, 1], projected_out.at[1, rows_of(far, length)])
    store(projected.at[0, 2], projected_out.at[2, rows_of(far, length)])
    load_near.wait()
    project(1)
    attend_rows(1, seq, 0, 4)
    fetch_out.pass_halves()
    fetch_in.pass_halves()
    attend_rows(1, seq, 4, 6)
    fetch_down.pass_on()
    fetch_out.wait()
    out_pass = [
        send(out_ref, out_rest.at[0], sibling),
        send(out_rest.at[1], out_rest.at[2], sibling),
    ]
    load_two = load(8, out_rest.at[1], w_out.at[2])
    attend_rows(1, seq, 6, blocks)
    piece_one = send(mixed.at[1, sibling_rows], pieces.at[0], sibling)
    store(projected.at[1, 0], projected_out.at[0, rows_of(seq, length)])
    store(projected.at[1, 1], projected_out.at[1, rows_of(seq, length)])
    store(projected.at[1, 2], projected_out.at[2, rows_of(seq, length)])
    store(log_total, log_out)
    for copy in out_pass:
        copy.wait_recv()
    load_one = load(9, out_rest.at[0], w_out.at[1])
    load_three = load(10, out_rest.at[2], w_out.at[3])
    store(mixed, mixed_out)
    for copy in (load_out, load_tok, load_one, load_two, load_three):
        copy.wait()
    for copy in (piece_two, piece_three, piece_one):
        copy.wait_recv()
    small = 64

    def attn_rows(step, carry):
        rows = rows_of(step, chunk)
        total = dot_nn(mixed[1, pl.ds(pl.multiple_of(core * share + step * chunk, LANES), chunk)],
                       w_out[0])
        for piece in range(3):
            total += dot_nn(pieces[piece, rows], w_out[piece + 1])
        acc[rows] = total
        return carry

    def first_rows(step, carry):
        rows = pl.ds(pl.multiple_of(step * small, small), small)
        values = tok[rows].astype(jnp.float32) + (acc[rows] + vec_ref[0:1])
        centred = values - row_mean(values)
        spread = lax.rsqrt(row_mean(centred * centred) + EPS_NORM)
        unit = centred * spread
        normed[rows] = unit
        inverse[rows] = spread
        shifted = unit * vec_ref[2:3] + vec_ref[3:4]
        first[rows] = shifted
        low[rows] = shifted.astype(jnp.bfloat16)
        return carry

    lax.fori_loop(0, share // chunk, attn_rows, 0)
    lax.fori_loop(0, share // small, first_rows, 0)
    slots = [slice(0, share), slice(share, 2 * share)]
    low_send = send(low.at[slots[0]], low.at[slots[1]], sibling)
    load_in.wait()

    def hidden_of(slot, owner):
        def units(step, carry):
            inner = rows_of(step, chunk)
            values = dot_nn(low[slots[slot]], w_in[owner, :, inner]) + bias[owner, :, inner]
            share_of = 0.5 * (1.0 + lax.erf(values * math.sqrt(0.5)))
            density = jnp.exp(-0.5 * values * values) * (1.0 / math.sqrt(2.0 * math.pi))
            active[owner, slots[slot], inner] = (values * share_of).astype(jnp.bfloat16)
            slope[owner, slots[slot], inner] = (share_of - 0.5 + values * density).astype(jnp.bfloat16)
            return carry

        lax.fori_loop(0, slab // chunk, units, 0)

    def branch_of(slot, owner, target, start, size):
        units = slice(owner * slab, (owner + 1) * slab)

        def columns(step, carry):
            at = pl.ds(pl.multiple_of(start + step * chunk, chunk), chunk)
            values = dot_nn(active[owner, slots[slot]], w_down[units, at])
            target[:, at] = values if owner == 0 else target[:, at] + values
            return carry

        lax.fori_loop(0, size // chunk, columns, 0)

    bias_send.wait_recv()
    bias[0] = bias_ref[...]
    load_bias = load(11, bias_two, bias.at[1])
    hidden_of(0, 0)
    low_send.wait_recv()
    store(low, low_out)
    hidden_of(1, 0)
    fetch_in.wait()
    load_in_two = load(12, in_two, w_in.at[1])
    fetch_down.pass_halves()
    load_down.wait()
    branch_of(1, 0, part, 0, width)
    branch_of(0, 0, acc, 0, width)
    load_bias.wait()
    load_in_two.wait()
    hidden_of(1, 1)
    hidden_of(0, 1)
    store(active.at[0], active_out)
    lane = lax.broadcasted_iota(jnp.int32, (1, LANES), 1)
    for slot, place in ((0, far), (1, seq)):
        firsts = jnp.zeros((1, LANES), jnp.int32)
        lasts = jnp.zeros((1, LANES), jnp.int32)
        for block in range(blocks):
            start = block * LANES
            firsts = jnp.where(lane == block, seg_keys[place, start : start + 1], firsts)
            lasts = jnp.where(
                lane == block, seg_keys[place, start + LANES - 1 : start + LANES], lasts
            )
        documents = seg_keys[place]
        bounds_ref[2 * slot : 2 * slot + 1] = jnp.sum(
            jnp.where(documents < firsts, 1.0, 0.0), axis=0, keepdims=True
        ).astype(jnp.int32)
        bounds_ref[2 * slot + 1 : 2 * slot + 2] = jnp.sum(
            jnp.where(documents <= lasts, 1.0, 0.0), axis=0, keepdims=True
        ).astype(jnp.int32)
    fetch_down.wait()
    load_down_two = load(13, down_two, w_down.at[pl.ds(slab, slab)])
    load_down_two.wait()
    half = width // 2
    part_sends = []
    for number in range(2):
        branch_of(1, 1, part, number * half, half)
        columns = slice(number * half, (number + 1) * half)
        part_sends.append(send(part.at[:, columns], other.at[:, columns], sibling))
    branch_of(0, 1, acc, 0, width)
    load_cot.wait()
    for copy in part_sends:
        copy.wait_recv()

    def second_rows(step, carry):
        rows = pl.ds(pl.multiple_of(step * small, small), small)
        values = first[rows] + (acc[rows] + other[rows]) + vec_ref[1:2]
        centred = values - row_mean(values)
        spread = lax.rsqrt(row_mean(centred * centred) + EPS_NORM)
        unit = centred * spread
        result[rows] = (unit * vec_ref[4:5] + vec_ref[5:6]).astype(jnp.bfloat16)
        upper = cot[rows].astype(jnp.float32)
        scaled = upper * vec_ref[4:5]
        grad = spread * (scaled - row_mean(scaled) - unit * row_mean(scaled * unit))
        wide[rows] = grad
        grad_low = grad.astype(jnp.bfloat16)
        branch[rows] = grad_low
        sums_ref[1:2] += jnp.sum(grad_low.astype(jnp.float32), axis=0, keepdims=True)
        sums_ref[4:5] += jnp.sum(upper * unit, axis=0, keepdims=True)
        sums_ref[5:6] += jnp.sum(upper, axis=0, keepdims=True)
        return carry

    branch_sends = []
    for number in range(2):
        steps = share // small // 2
        lax.fori_loop(number * steps, (number + 1) * steps, second_rows, 0)
        rows = slice(number * steps * small, (number + 1) * steps * small)
        there = slice(share + rows.start, share + rows.stop)
        branch_sends.append(send(branch.at[rows], branch.at[there], sibling))
    store(result, result_out)
    hidden = rows_in

    def grad_hidden_of(slot, owner):
        def units(step, carry):
            inner = rows_of(step, chunk)
            outer = pl.ds(pl.multiple_of(owner * slab + step * chunk, chunk), chunk)
            grad = dot_nt(branch[slots[slot]], w_down[outer]) * (
                0.5 + slope[owner, slots[slot], inner].astype(jnp.float32)
            )
            grad_low = grad.astype(jnp.bfloat16)
            hidden[owner, slots[slot], inner] = grad_low
            unit_ref[:, outer] += jnp.sum(grad_low.astype(jnp.float32), axis=0, keepdims=True)
            return carry

        lax.fori_loop(0, slab // chunk, units, 0)

    def grad_first_of(slot, target, start, size):
        def columns(step, carry):
            at = pl.ds(pl.multiple_of(start + step * chunk, chunk), chunk)
            target[:, at] = dot_nt(hidden[0, slots[slot]], w_in[0, at]) + dot_nt(
                hidden[1, slots[slot]], w_in[1, at]
            )
            return carry

        lax.fori_loop(0, size // chunk, columns, 0)

    def far_product(left_side, right_side, target, start, stop):
        def rows_step(step, carry):
            at = rows_of(step, LANES)
            target[at] = dot_tn(left_side[:, at], right_side[...]).astype(jnp.bfloat16)
            return carry

        lax.fori_loop(start // LANES, stop // LANES, rows_step, 0)

    grad_hidden_of(0, 0)
    grad_hidden_of(0, 1)
    for copy in branch_sends:
        copy.wait_recv()
    store(branch, branch_out)
    early = down_near.shape[0]
    far_product(active.at[1], branch, down_part, 0, early)
    down_send = send(down_part.at[pl.ds(0, early)], down_near, opposite)
    far_product(active.at[1], branch, down_part, early, slab)
    store(down_part, down_part_out)
    grad_hidden_of(1, 0)
    grad_hidden_of(1, 1)
    unit_send = send(unit_ref.at[:, pl.ds(slab, slab)], unit_two, opposite)
    store(hidden.at[0], hidden_out)
    for copy in part_sends:
        copy.wait_send()
    sends[:] = [one for one in sends if all(one is not copy for copy in part_sends)]
    first_sends = []
    for number in range(2):
        grad_first_of(1, part, number * half, half)
        columns = slice(number * half, (number + 1) * half)
        first_sends.append(send(part.at[:, columns], other.at[:, columns], sibling))
    grad_first_of(0, acc, 0, width)
    for copy in first_sends:
        copy.wait_recv()

    def back_rows(step, carry):
        rows = pl.ds(pl.multiple_of(step * small, small), small)
        grad = acc[rows] + other[rows] + wide[rows]
        unit = normed[rows]
        scaled = grad * vec_ref[2:3]
        back = inverse[rows] * (scaled - row_mean(scaled) - unit * row_mean(scaled * unit))
        acc[rows] = back
        back_low = back.astype(jnp.bfloat16)
        tok[rows] = back_low
        sums_ref[0:1] += jnp.sum(back_low.astype(jnp.float32), axis=0, keepdims=True)
        sums_ref[2:3] += jnp.sum(grad * unit, axis=0, keepdims=True)
        sums_ref[3:4] += jnp.sum(grad, axis=0, keepdims=True)
        return carry

    lax.fori_loop(0, share // small, back_rows, 0)
    store(acc, norm_out)
    attn = tok[...]
    near[1] = dot_nt(attn, w_out[1]).astype(jnp.bfloat16)
    near_send = send(near.at[1], near.at[2], sibling)
    out_one = slice(0, head_slab)
    out_three = slice(head_slab, 2 * head_slab)
    first[out_one] = dot_tn(pieces[0], attn)
    first[out_three] = dot_tn(pieces[2], attn)
    outs_send = send(first.at[pl.ds(0, 2 * head_slab)], outs_two, sibling)
    far_mixed[0] = dot_nt(attn, w_out[2]).astype(jnp.bfloat16)
    far_mixed[1] = dot_nt(attn, w_out[3]).astype(jnp.bfloat16)
    store(far_mixed, far_out)
    near[0] = dot_nt(attn, w_out[0]).astype(jnp.bfloat16)
    store(near.at[0], near_out.at[0])
    far_product(low, hidden.at[1], active.at[1], 0, width)
    store(active.at[1], in_part_out)
    near_send.wait_recv()
    store(near.at[2], near_out.at[1])
    outs_send.wait_recv()
    out_sum[...] = dot_tn(mixed[1, own_rows], attn) + outs_two[out_one]
    out_far[...] = (dot_tn(pieces[1], attn) + outs_two[out_three]).astype(jnp.bfloat16)
    unit_send.wait_recv()
    down_send.wait_recv()
    for copy in factor_sends:
        copy.wait_recv()
    for copy in sends:
        copy.wait_send()
    for copy in stores:
        copy.wait()


def layer_call(tokens, cotangent, planes, w_out, w_in, w_down, factor_in, factor_down, head_bias,
               unit_bias, vectors, seg_keys, seg_queries):
    token_count, width = tokens.shape
    seq_count, length = seg_keys.shape[:2]
    share = token_count // (2 * seq_count)
    head_slab = planes.shape[2]
    slab = w_in.shape[1]
    early = slab * 3 // 8
    low_type, full_type = jnp.bfloat16, jnp.float32
    vmem = pl.BlockSpec(memory_space=pltpu.VMEM)
    anywhere = pl.BlockSpec(memory_space=pl.ANY)
    shapes = [
        jax.ShapeDtypeStruct((3, token_count, head_slab), low_type),
        jax.ShapeDtypeStruct((2, head_slab // DH, length), full_type),
        jax.ShapeDtypeStruct((2, length, head_slab), low_type),
        jax.ShapeDtypeStruct(w_in.shape, low_type),
        jax.ShapeDtypeStruct(w_down.shape, low_type),
        jax.ShapeDtypeStruct((3,) + w_out.shape, low_type),
        jax.ShapeDtypeStruct((1, slab), full_type),
        jax.ShapeDtypeStruct((share, width), low_type),
        jax.ShapeDtypeStruct((2 * share, width), low_type),
        jax.ShapeDtypeStruct((2 * share, slab), low_type),
        jax.ShapeDtypeStruct((2 * share, width), low_type),
        jax.ShapeDtypeStruct((2 * share, slab), low_type),
        jax.ShapeDtypeStruct((share, width), full_type),
        jax.ShapeDtypeStruct((2, share, head_slab), low_type),
        jax.ShapeDtypeStruct((2, share, head_slab), low_type),
        jax.ShapeDtypeStruct((early, width), low_type),
        jax.ShapeDtypeStruct((slab, width), low_type),
        jax.ShapeDtypeStruct(w_in.shape, low_type),
        jax.ShapeDtypeStruct(factor_in.shape, full_type),
        jax.ShapeDtypeStruct(factor_down.shape, full_type),
        jax.ShapeDtypeStruct((head_slab, width), full_type),
        jax.ShapeDtypeStruct((head_slab, width), low_type),
        jax.ShapeDtypeStruct((1, 2 * slab), full_type),
        jax.ShapeDtypeStruct((1, slab), full_type),
        jax.ShapeDtypeStruct((6, width), full_type),
        jax.ShapeDtypeStruct((4, LANES), jnp.int32),
    ]
    return pl.pallas_call(
        layer_kernel,
        in_specs=[anywhere] * 8 + [vmem] * 5,
        out_specs=[anywhere] * 20 + [vmem] * 6,
        out_shape=shapes,
        scratch_shapes=[
            pltpu.VMEM((2, length, width), low_type),
            pltpu.VMEM(planes.shape, low_type),
            pltpu.VMEM((2, 3, length, head_slab), low_type),
            pltpu.VMEM((head_slab, length), low_type),
            pltpu.VMEM((2, head_slab // DH, length), full_type),
            pltpu.VMEM((2, length, head_slab), low_type),
            pltpu.VMEM((3, share, head_slab), low_type),
            pltpu.VMEM((4,) + w_out.shape, low_type),
            pltpu.VMEM((2,) + w_in.shape, low_type),
            pltpu.VMEM((2 * slab, width), low_type),
            pltpu.VMEM((2, 1, slab), full_type),
            pltpu.VMEM((share, width), low_type),
            pltpu.VMEM((share, width), low_type),
            pltpu.VMEM((share, width), full_type),
            pltpu.VMEM((share, width), full_type),
            pltpu.VMEM((share, 1), full_type),
            pltpu.VMEM((2 * share, width), low_type),
            pltpu.VMEM((2, 2 * share, slab), low_type),
            pltpu.VMEM((2, 2 * share, slab), low_type),
            pltpu.VMEM((share, width), full_type),
            pltpu.VMEM((share, width), full_type),
            pltpu.VMEM((share, width), full_type),
            pltpu.VMEM((share, width), full_type),
            pltpu.VMEM((2 * share, width), low_type),
            pltpu.VMEM((share, width), low_type),
            pltpu.VMEM((slab, width), low_type),
            pltpu.VMEM((3, share, head_slab), low_type),
            pltpu.VMEM((2, share, head_slab), low_type),
            pltpu.VMEM((2 * head_slab, width), full_type),
            pltpu.SemaphoreType.DMA((14,)),
            pltpu.SemaphoreType.DMA((24,)),
            pltpu.SemaphoreType.DMA((36,)),
            pltpu.SemaphoreType.DMA((36,)),
        ],
        compiler_params=pltpu.CompilerParams(
            collective_id=3, has_side_effects=True, vmem_limit_bytes=VMEM_GRANT
        ),
        name="layer",
    )(tokens, cotangent, planes, w_out, w_in, w_down, factor_in, factor_down, head_bias, unit_bias,
      vectors, seg_keys, seg_queries)


def layer_general(tokens, segments, w_qkv, head_bias, w_out, w_in, unit_bias, w_down, vectors,
                  cotangent, basis_in, basis_down):
    token_count, model_width = tokens.shape
    seq_count, length = segments.shape
    head_slab = w_qkv.shape[2]
    head_count = head_slab // DH
    tensor_size = lax.axis_size("tensor")
    share_rows = token_count // tensor_size
    tensor_place = lax.axis_index("tensor")
    row_start = tensor_place * share_rows
    head_scale = 1.0 / math.sqrt(DH)

    def own_rows(values):
        return lax.dynamic_slice_in_dim(values, row_start, share_rows, 0)

    flat_qkv = w_qkv.reshape(model_width, 3 * head_slab)
    projected = jnp.dot(tokens, flat_qkv, preferred_element_type=jnp.float32).reshape(
        token_count, 3, head_slab
    )
    head_shape = (seq_count, length, head_count, DH)
    queries = (
        ((projected[:, 0] + head_bias[0]) * head_scale).astype(jnp.bfloat16).reshape(head_shape)
    )
    key_heads = projected[:, 1].astype(jnp.bfloat16).reshape(head_shape)
    value_heads = (projected[:, 2] + head_bias[1]).astype(jnp.bfloat16).reshape(head_shape)
    mixed_heads, log_total = lax.map(attend_forward, (queries, key_heads, value_heads, segments))
    mixed_flat = mixed_heads.reshape(token_count, head_slab)
    attn_out = (
        lax.psum(jnp.dot(mixed_flat, w_out, preferred_element_type=jnp.float32), "tensor")
        + vectors[0]
    )
    first_norm, first_normed, first_inverse = norm_forward(
        tokens.astype(jnp.float32) + attn_out, vectors[2], vectors[3]
    )
    first_low = first_norm.astype(jnp.bfloat16)
    hidden = jnp.dot(first_low, w_in, preferred_element_type=jnp.float32) + unit_bias
    active, gelu_back = jax.vjp(partial(jax.nn.gelu, approximate=False), hidden)
    active_low = active.astype(jnp.bfloat16)
    grad_out_share = own_rows(cotangent).astype(jnp.float32)
    summed_input = (
        first_norm
        + lax.psum(jnp.dot(active_low, w_down, preferred_element_type=jnp.float32), "tensor")
        + vectors[1]
    )
    second_norm, second_normed, second_inverse = norm_forward(summed_input, vectors[4], vectors[5])
    layer_out = own_rows(second_norm).astype(jnp.bfloat16)
    grad_sum = norm_backward(
        cotangent.astype(jnp.float32), second_normed, second_inverse, vectors[4]
    )
    grad_branch = grad_sum.astype(jnp.bfloat16)
    second_share = own_rows(second_normed)
    grad_w_down = trans_times(active_low, grad_branch)
    grad_active = times_trans(grad_branch, w_down)
    grad_hidden = gelu_back(grad_active)[0].astype(jnp.bfloat16)
    grad_w_in = trans_times(first_low, grad_hidden)
    grad_units = jnp.sum(grad_hidden.astype(jnp.float32), axis=0)
    grad_first = lax.psum(times_trans(grad_hidden, w_in), "tensor") + grad_sum
    grad_h1 = norm_backward(grad_first, first_normed, first_inverse, vectors[2])
    grad_attn = grad_h1.astype(jnp.bfloat16)
    grad_first_share = own_rows(grad_first)
    first_normed_share = own_rows(first_normed)
    grad_h1_share = own_rows(grad_h1)
    grad_w_out = trans_times(mixed_flat, grad_attn)
    grad_mixed = times_trans(grad_attn, w_out).astype(jnp.bfloat16).reshape(head_shape)
    grad_query, grad_key, grad_value = lax.map(
        attend_backward, (queries, key_heads, value_heads, segments, grad_mixed, log_total)
    )
    grad_query = (
        grad_query.reshape(token_count, head_slab).astype(jnp.float32) * head_scale
    ).astype(jnp.bfloat16)
    grad_key = grad_key.reshape(token_count, head_slab)
    grad_value = grad_value.reshape(token_count, head_slab)
    grad_projected = jnp.stack([grad_query, grad_key, grad_value], axis=1).reshape(
        token_count, 3 * head_slab
    )
    grad_w_qkv = trans_times(tokens, grad_projected)
    grad_heads = jnp.stack(
        [
            jnp.sum(grad_query.astype(jnp.float32), axis=0),
            jnp.sum(grad_value.astype(jnp.float32), axis=0),
        ]
    )
    grad_tokens = (
        lax.psum_scatter(
            times_trans(grad_projected, flat_qkv).astype(jnp.bfloat16),
            "tensor",
            scatter_dimension=0,
            tiled=True,
        ).astype(jnp.float32)
        + grad_h1_share
    )
    local_vectors = jnp.stack(
        [
            jnp.sum(own_rows(grad_attn).astype(jnp.float32), axis=0),
            jnp.sum(own_rows(grad_branch).astype(jnp.float32), axis=0),
            jnp.sum(grad_first_share * first_normed_share, axis=0),
            jnp.sum(grad_first_share, axis=0),
            jnp.sum(grad_out_share * second_share, axis=0),
            jnp.sum(grad_out_share, axis=0),
        ]
    )
    return (
        layer_out,
        grad_tokens,
        (
            grad_w_qkv.reshape(model_width, 3, head_slab).transpose(1, 0, 2),
            grad_w_out,
            grad_w_in,
            grad_w_down,
        ),
        local_vectors,
        grad_heads,
        grad_units,
        (),
        (),
    )


def layer_split(tokens, segments, w_qkv, head_bias, w_out, w_in, unit_bias, w_down, vectors,
                cotangent, basis_in, basis_down):
    token_count, model_width = tokens.shape
    seq_count, length = segments.shape
    unit_slab = w_in.shape[1]
    tensor_size = lax.axis_size("tensor")
    share = token_count // tensor_size
    tensor_place = lax.axis_index("tensor")
    core = lax.rem(tensor_place, 2)
    seq = tensor_place // 2

    def to(values, step):
        return lax.ppermute(
            values, "tensor", [(place, place ^ step) for place in range(tensor_size)]
        )

    def rows_at(values, number, size):
        return lax.dynamic_slice_in_dim(values, number * size, size, 0)

    planes = w_qkv.transpose(1, 0, 2)
    seg_keys = jnp.broadcast_to(segments[:, :, None], (seq_count, length, LANES))
    seg_queries = segments[:, None, :]
    (projected, logs, mixed, _, _, _, _, layer_out, low, active, grad_branch, grad_hidden, grad_h1,
     grad_near, grad_far, down_near, down_part, in_part, far_in, far_down, out_sum, out_far, units,
     unit_two, sums, bounds) = layer_call(
        tokens, cotangent, planes, w_out, w_in, w_down, basis_in, basis_down, head_bias,
        unit_bias[None], vectors, seg_keys, seg_queries,
    )
    far_own = to(grad_far[0:1], 2)
    far_other = to(grad_far[1:2], 3)
    down_rest = to(down_part[down_near.shape[0] :], 2)
    in_far = to(in_part, 2)
    out_back = to(out_far, 2)

    grad_projected, heads_near = attend_back(
        projected, seg_keys, seg_queries, (grad_near, 0), (grad_near, 1), mixed, logs, 1,
        bounds, None, seq, core,
    )
    grad_projected, heads_far = attend_back(
        projected, seg_keys, seg_queries, (far_own, 0), (far_other, 0), mixed, logs, 0,
        bounds, grad_projected, 1 - seq, core,
    )
    token_part = jnp.einsum(
        "gtn,gdn->td", grad_projected, planes, preferred_element_type=jnp.float32
    ).astype(jnp.bfloat16)
    other_one = to(
        jnp.stack([rows_at(token_part, 2 * at + 1 - core, share) for at in (seq, 1 - seq)]), 1
    ).astype(jnp.float32)
    across_part = rows_at(token_part, 2 * (1 - seq) + core, share).astype(jnp.float32)
    from_two = to((across_part + other_one[1]).astype(jnp.bfloat16), 2)
    grad_tokens = (
        rows_at(token_part, 2 * seq + core, share).astype(jnp.float32)
        + other_one[0]
        + from_two.astype(jnp.float32)
        + grad_h1
    )
    grad_w_qkv = jnp.einsum(
        "td,gtn->gdn", tokens, grad_projected, preferred_element_type=jnp.float32
    )
    grad_w_down = trans_times(active, grad_branch)
    grad_w_in = trans_times(low, grad_hidden)
    grad_w_out = out_sum + out_back.astype(jnp.float32)
    return (
        layer_out,
        grad_tokens,
        (grad_w_qkv, grad_w_out, grad_w_in, grad_w_down),
        sums,
        heads_near + heads_far,
        units[0, :unit_slab] + unit_two[0],
        (in_part, down_part, far_in, far_down),
        (in_far, down_near, down_rest),
    )


def local(
    tokens,
    segments,
    w_qkv,
    head_bias,
    w_out,
    w_in,
    unit_bias,
    w_down,
    vectors,
    cotangent,
    err_qkv,
    err_out,
    err_in,
    err_down,
    basis_qkv,
    basis_out,
    basis_in,
    basis_down,
    mom_qkv,
    mom_head_bias,
    mom_out,
    mom_in,
    mom_unit_bias,
    mom_down,
    mom_vectors,
):
    token_count, model_width = tokens.shape
    head_slab = w_qkv.shape[2]
    unit_slab = w_in.shape[1]
    tensor_size = lax.axis_size("tensor")
    replicas = lax.axis_size("dp")
    one_sequence_per_chip = 2 * segments.shape[0] == tensor_size and replicas % 4 == 0
    layer = layer_split if one_sequence_per_chip else layer_general
    layer_out, grad_tokens, grads, local_vectors, grad_heads, grad_units, far, late = layer(
        tokens, segments, w_qkv, head_bias, w_out, w_in, unit_bias, w_down, vectors, cotangent,
        basis_in, basis_down,
    )
    grad_w_qkv, grad_w_out, grad_w_in, grad_w_down = grads
    small = jnp.concatenate(
        [
            local_vectors,
            jnp.pad(grad_units, (0, model_width - unit_slab))[None],
            jnp.pad(grad_heads.reshape(1, 2 * head_slab), ((0, 0), (0, model_width - 2 * head_slab))),
        ],
        axis=0,
    )
    planes = (1, 0, 2)
    combined_qkv = grad_w_qkv + err_qkv[0].transpose(planes)
    combined_out = grad_w_out + err_out[0]
    combined_in = grad_w_in + err_in[0]
    combined_down = grad_w_down + err_down[0]
    matrices = (combined_qkv, combined_out, combined_in, combined_down)
    bases, rights, small_sum = compress(
        matrices,
        (basis_qkv.transpose(planes), basis_out, basis_in, basis_down),
        small,
        replicas,
        tensor_size,
        far,
    )
    step_rate = 0.3 * math.sqrt(replicas / token_count)
    grads, errors, moments, news = update(
        matrices,
        (mom_qkv.transpose(planes), mom_out, mom_in, mom_down),
        (w_qkv.transpose(planes), w_out, w_in, w_down),
        bases,
        rights,
        late,
        step_rate,
    )
    reduced_qkv, rank_out, rank_in, rank_down = (grads[0].transpose(planes),) + tuple(grads[1:])
    new_err_qkv, new_err_out, new_err_in, new_err_down = (
        errors[0].transpose(planes)[None],
        errors[1][None],
        errors[2][None],
        errors[3][None],
    )
    new_mom_qkv, new_mom_out, new_mom_in, new_mom_down = (moments[0].transpose(planes),) + tuple(
        moments[1:]
    )
    new_w_qkv, new_w_out, new_w_in, new_w_down = (news[0].transpose(planes),) + tuple(news[1:])
    right_qkv, right_out, right_in, right_down = rights
    new_basis_qkv = right_qkv.transpose(planes)
    grad_vectors = small_sum[:6]
    grad_unit_bias = small_sum[6, :unit_slab]
    grad_head_bias = small_sum[7, : 2 * head_slab].reshape(2, head_slab)
    new_mom_head_bias = 0.9 * mom_head_bias + grad_head_bias
    new_mom_unit_bias = 0.9 * mom_unit_bias + grad_unit_bias
    new_mom_vectors = 0.9 * mom_vectors + grad_vectors
    new_head_bias = head_bias - step_rate * new_mom_head_bias
    new_unit_bias = unit_bias - step_rate * new_mom_unit_bias
    new_vectors = vectors - step_rate * new_mom_vectors
    return (
        layer_out,
        grad_tokens,
        reduced_qkv,
        grad_head_bias,
        rank_out,
        rank_in,
        grad_unit_bias,
        rank_down,
        grad_vectors,
        new_err_qkv,
        new_err_out,
        new_err_in,
        new_err_down,
        new_basis_qkv,
        right_out,
        right_in,
        right_down,
        new_mom_qkv,
        new_mom_head_bias,
        new_mom_out,
        new_mom_in,
        new_mom_unit_bias,
        new_mom_down,
        new_mom_vectors,
        new_w_qkv,
        new_head_bias,
        new_w_out,
        new_w_in,
        new_unit_bias,
        new_w_down,
        new_vectors,
    )


def solution(mesh):
    in_specs = (
        P("dp", None),
        P("dp", None),
        P(None, None, "tensor"),
        P(None, "tensor"),
        P("tensor", None),
        P(None, "tensor"),
        P("tensor"),
        P("tensor", None),
        P(),
        P("dp", None),
        P("dp", None, None, "tensor"),
        P("dp", "tensor", None),
        P("dp", None, "tensor"),
        P("dp", "tensor", None),
        P(None, None, "tensor"),
        P("tensor", None),
        P(None, "tensor"),
        P("tensor", None),
        P(None, None, "tensor"),
        P(None, "tensor"),
        P("tensor", None),
        P(None, "tensor"),
        P("tensor"),
        P("tensor", None),
        P(),
    )
    out_specs = (
        P(("dp", "tensor"), None),
        P(("dp", "tensor"), None),
        P(None, None, "tensor"),
        P(None, "tensor"),
        P("tensor", None),
        P(None, "tensor"),
        P("tensor"),
        P("tensor", None),
        P(),
        P("dp", None, None, "tensor"),
        P("dp", "tensor", None),
        P("dp", None, "tensor"),
        P("dp", "tensor", None),
        P(None, None, "tensor"),
        P("tensor", None),
        P(None, "tensor"),
        P("tensor", None),
        P(None, None, "tensor"),
        P(None, "tensor"),
        P("tensor", None),
        P(None, "tensor"),
        P("tensor"),
        P("tensor", None),
        P(),
        P(None, None, "tensor"),
        P(None, "tensor"),
        P("tensor", None),
        P(None, "tensor"),
        P("tensor"),
        P("tensor", None),
        P(),
    )
    return jax.shard_map(local, mesh=mesh, in_specs=in_specs, out_specs=out_specs, check_vma=False)
```

```python
from functools import partial
import math

import jax
import jax.numpy as jnp
from jax import lax
from jax.experimental import pallas as pl
from jax.experimental.pallas import tpu as pltpu
from jax.sharding import PartitionSpec as P

DH = 64
LANES = 128
MESH = pl.DeviceIdType.MESH
VMEM_GRANT = 60 << 20
BRIEF = pl.CostEstimate(flops=1, bytes_accessed=1, transcendentals=1)


PRECISE = lax.Precision.HIGHEST
EPS_NORM = 1e-05
EPS_BASIS = 1e-08
MASKED = -1000000000.0


def norm_forward(values, gain, shift):
    row_mean = jnp.mean(values, axis=-1, keepdims=True)
    centred = values - row_mean
    variance = jnp.mean(centred * centred, axis=-1, keepdims=True)
    inverse = lax.rsqrt(variance + EPS_NORM)
    normed = centred * inverse
    return (normed * gain + shift, normed, inverse)


def norm_backward(grad_norm, normed, inverse, gain):
    scaled_grad = grad_norm * gain
    grad_mean = jnp.mean(scaled_grad, axis=-1, keepdims=True)
    along_norm = jnp.mean(scaled_grad * normed, axis=-1, keepdims=True)
    return inverse * (scaled_grad - grad_mean - normed * along_norm)


def times_trans(left_side, right_side):
    return lax.dot_general(
        left_side, right_side, (((1,), (1,)), ((), ())), preferred_element_type=jnp.float32
    )


def trans_times(left_side, right_side):
    return lax.dot_general(
        left_side, right_side, (((0,), (0,)), ((), ())), preferred_element_type=jnp.float32
    )


def split_bf16(values):
    high = values.astype(jnp.bfloat16)
    low = (values - high.astype(jnp.float32)).astype(jnp.bfloat16)
    return high, low


def dot_nt(left_side, right_side):
    return lax.dot_general(
        left_side, right_side, (((1,), (1,)), ((), ())), preferred_element_type=jnp.float32
    )


def dot_nn(left_side, right_side):
    return lax.dot_general(
        left_side, right_side, (((1,), (0,)), ((), ())), preferred_element_type=jnp.float32
    )


def dot_tn(left_side, right_side):
    return lax.dot_general(
        left_side, right_side, (((0,), (0,)), ((), ())), preferred_element_type=jnp.float32
    )


def low_left(factor, matrix):
    both = dot_nt(jnp.concatenate(split_bf16(factor), axis=0), matrix)
    return both[: factor.shape[0]] + both[factor.shape[0] :]


def low_right(basis_rows, matrix):
    both = dot_nn(jnp.concatenate(split_bf16(basis_rows), axis=0), matrix)
    return both[: basis_rows.shape[0]] + both[basis_rows.shape[0] :]


def left_factor(factor, matrix):
    rank_size = factor.shape[0]
    factor_high, factor_low = split_bf16(factor)
    matrix_high, matrix_low = split_bf16(matrix)
    both = dot_nt(jnp.concatenate([factor_high, factor_low], axis=0), matrix_high)
    return both[:rank_size] + both[rank_size:] + dot_nt(factor_high, matrix_low)


def right_factor(basis_rows, matrix):
    rank_size = basis_rows.shape[0]
    basis_high, basis_low = split_bf16(basis_rows)
    matrix_high, matrix_low = split_bf16(matrix)
    both = dot_nn(jnp.concatenate([basis_high, basis_low], axis=0), matrix_high)
    return both[:rank_size] + both[rank_size:] + dot_nn(basis_high, matrix_low)


def place_tiles(target, offset, values):
    per_chunk = target.shape[2] // LANES
    for tile in range(values.shape[1] // LANES):
        spot = offset + tile
        target[spot // per_chunk, :, pl.ds(spot % per_chunk * LANES, LANES)] = values[
            :, tile * LANES : (tile + 1) * LANES
        ]
    return offset + values.shape[1] // LANES


def add_tiles(target, offset, values):
    per_chunk = target.shape[2] // LANES
    for tile in range(values.shape[1] // LANES):
        spot = offset + tile
        target[spot // per_chunk, :, pl.ds(spot % per_chunk * LANES, LANES)] += values[
            :, tile * LANES : (tile + 1) * LANES
        ]


def take_tiles(source, offset, size):
    per_chunk = source.shape[2] // LANES
    pieces = []
    for tile in range(size // LANES):
        spot = offset + tile
        pieces.append(source[spot // per_chunk, :, pl.ds(spot % per_chunk * LANES, LANES)])
    return jnp.concatenate(pieces, axis=1) if len(pieces) > 1 else pieces[0]


def orthonormal_rows(rows):
    rank_size = rows.shape[0]
    row_number = lax.broadcasted_iota(jnp.int32, (rank_size, 1), 0)
    for position in range(rank_size):
        row = rows[position : position + 1]
        length = jnp.sqrt(jnp.sum(row * row, axis=1, keepdims=True)) + EPS_BASIS
        unit = row / length
        along = jnp.sum(rows * unit, axis=1, keepdims=True)
        later = jnp.where(row_number > position, along, 0.0)
        rows = jnp.where(row_number == position, unit, rows - later * unit)
    return rows


def dp_exchange(replicas, mine, wire, arrived, total, sems, meanwhile=None):
    send_one, recv_one, send_two, recv_two = sems
    dp_place = lax.axis_index("dp")
    tensor_place = lax.axis_index("tensor")

    def peer_of(step):
        return lax.rem(dp_place + step, replicas)

    def scatter(step, slot):
        return pltpu.make_async_remote_copy(
            src_ref=wire.at[peer_of(step)],
            dst_ref=arrived.at[slot],
            send_sem=send_one.at[step],
            recv_sem=recv_one.at[slot],
            device_id=(peer_of(step), tensor_place),
            device_id_type=MESH,
        )

    def gather(step, slot):
        return pltpu.make_async_remote_copy(
            src_ref=total.at[dp_place],
            dst_ref=total.at[slot],
            send_sem=send_two.at[step],
            recv_sem=recv_two.at[slot],
            device_id=(peer_of(step), tensor_place),
            device_id_type=MESH,
        )

    def start_scatter(step, carry):
        scatter(step, dp_place).start()
        return carry

    def add_arrived(step, carry):
        scatter(step, peer_of(step)).wait_recv()
        return carry + arrived[peer_of(step)].astype(jnp.float32)

    def start_gather(step, carry):
        gather(step, dp_place).start()
        return carry

    def finish(step, carry):
        gather(step, peer_of(step)).wait_recv()
        return carry

    wire[...] = mine[...].astype(wire.dtype)
    lax.fori_loop(1, replicas, start_scatter, 0)
    total[dp_place] = lax.fori_loop(1, replicas, add_arrived, mine[dp_place])
    lax.fori_loop(1, replicas, start_gather, 0)
    lax.fori_loop(1, replicas, finish, 0)

    def drain(step, carry):
        scatter(step, dp_place).wait_send()
        gather(step, dp_place).wait_send()
        return carry

    return lambda: lax.fori_loop(1, replicas, drain, 0)


def compress_kernel(replicas, tensor_size, has_far, *refs):
    if has_far:
        far_refs, refs, late_ref = refs[:4], refs[4:13] + refs[14:], refs[13]
        compress_body(replicas, tensor_size, far_refs, late_ref, *refs)
    else:
        compress_body(replicas, tensor_size, None, None, *refs)


def compress_body(replicas, tensor_size, far_refs, late_ref, qkv_ref, out_ref, in_ref, down_ref,
                    fq_ref, fo_ref, fi_ref, fd_ref, small_ref,
                    bq_ref, bo_ref, bi_ref, bd_ref, rq_ref, ro_ref, ri_ref, rd_ref, sum_ref,
                    qkv, out, inw, down, mine, wire, arrived, total,
                    mine_two, wire_two, arrived_two, total_two, small_slots,
                    load_sem, *sems):
    first_sems, second_sems, (send_small, recv_small) = sems[:4], sems[4:8], sems[8:10]
    dp_place = lax.axis_index("dp")
    tensor_place = lax.axis_index("tensor")
    loads = [
        pltpu.make_async_copy(source, target, load_sem.at[number])
        for number, (source, target) in enumerate(
            [(qkv_ref, qkv), (out_ref, out), (down_ref, down), (in_ref, inw)]
        )
    ]
    if far_refs:
        far_in_ref, far_down_ref, far_factor_in, far_factor_down = far_refs
        far_in, far_down, sent, got, far_send, far_recv = sems[10:]
        opposite = (dp_place, tensor_place + 2 - 4 * (tensor_place // 2))
        head = far_in_ref.shape[0] - late_ref.shape[0]
        cut = head + 2 * LANES

        def bulk(number, start, stop):
            return pltpu.make_async_remote_copy(
                src_ref=far_in_ref.at[pl.ds(start, stop - start)],
                dst_ref=late_ref.at[pl.ds(start - head, stop - start)],
                send_sem=far_send.at[number],
                recv_sem=far_recv.at[number],
                device_id=opposite,
                device_id_type=MESH,
            )

        bulks = [bulk(3, head, cut), bulk(4, cut, far_in_ref.shape[0])]
        far_loads = [
            pltpu.make_async_copy(far_in_ref, far_in, load_sem.at[4]),
            pltpu.make_async_copy(far_down_ref, far_down, load_sem.at[5]),
        ]
        for load in far_loads:
            load.start()

        def far_copy(number):
            return pltpu.make_async_remote_copy(
                src_ref=sent.at[number],
                dst_ref=got.at[number],
                send_sem=far_send.at[number],
                recv_sem=far_recv.at[number],
                device_id=opposite,
                device_id_type=MESH,
            )

    for load in loads:
        load.start()
    barrier = pltpu.get_barrier_semaphore()

    def greet_dp(step, carry):
        pl.semaphore_signal(
            barrier,
            inc=1,
            device_id=(lax.rem(dp_place + step, replicas), tensor_place),
            device_id_type=MESH,
        )
        return carry

    def greet_tensor(step, carry):
        pl.semaphore_signal(
            barrier,
            inc=1,
            device_id=(dp_place, lax.rem(tensor_place + step, tensor_size)),
            device_id_type=MESH,
        )
        return carry

    lax.fori_loop(1, replicas, greet_dp, 0)
    lax.fori_loop(1, tensor_size, greet_tensor, 0)
    mine[...] = jnp.zeros_like(mine)
    mine_two[...] = jnp.zeros_like(mine_two)
    block = 2 * LANES
    if far_refs:
        for number, (factor_ref, matrix) in enumerate(
            ((far_factor_down, far_down), (far_factor_in, far_in))
        ):
            far_loads[1 - number].wait()
            for start in range(0, matrix.shape[0], block):
                rows = slice(start, start + block)
                sent[0, number, :, rows] = low_left(factor_ref[...], matrix[rows])
        pl.semaphore_wait(barrier, replicas - 1 + tensor_size - 1)
        far_copy(0).start()
        bulks[0].start()
    offset = 0
    loads[0].wait()
    for start in range(0, qkv.shape[1], block):
        rows = slice(start, start + block)
        left = left_factor(fq_ref[0], qkv[0, rows])
        for part in range(1, 3):
            left += left_factor(fq_ref[part], qkv[part, rows])
        offset = place_tiles(mine, offset, left)
    for load, factor_ref, matrix in zip(loads[1:], (fo_ref, fd_ref, fi_ref), (out, down, inw)):
        load.wait()
        rows_of = min(block, matrix.shape[0])
        for start in range(0, matrix.shape[0], rows_of):
            left = left_factor(factor_ref[...], matrix[start : start + rows_of])
            offset = place_tiles(mine, offset, left)
    place_tiles(mine, offset, small_ref[...])
    if far_refs:
        far_copy(0).wait_recv()
        add_tiles(mine, offset - 2 * down.shape[0] // LANES, got[0, 0])
        add_tiles(mine, offset - inw.shape[0] // LANES, got[0, 1])
    else:
        pl.semaphore_wait(barrier, replicas - 1 + tensor_size - 1)
    drain_one = dp_exchange(replicas, mine, wire, arrived, total, first_sems)

    def slot_copy(step, slot):
        peer = lax.rem(tensor_place + step, tensor_size)
        return pltpu.make_async_remote_copy(
            src_ref=small_slots.at[tensor_place],
            dst_ref=small_slots.at[slot],
            send_sem=send_small.at[step],
            recv_sem=recv_small.at[slot],
            device_id=(dp_place, peer),
            device_id_type=MESH,
        )

    def start_small(step, carry):
        slot_copy(step, tensor_place).start()
        return carry

    own_small = take_tiles(total, offset, small_ref.shape[1])
    small_slots[tensor_place] = own_small
    lax.fori_loop(1, tensor_size, start_small, 0)
    offset = 0
    offset_two = 0
    offsets = []
    for basis_ref in (bq_ref, bo_ref, bd_ref, bi_ref):
        offsets.append(offset)
        offset += basis_ref.shape[1] // LANES
    for number in (2, 3, 0, 1):
        basis_ref = (bq_ref, bo_ref, bd_ref, bi_ref)[number]
        rows = take_tiles(total, offsets[number], basis_ref.shape[1]) * (1.0 / replicas)
        basis_ref[...] = orthonormal_rows(rows)
        if far_refs and number >= 2:
            sent[1, number - 2] = basis_ref[...]
        if far_refs and number == 3:
            far_copy(1).start()
    drain_one()
    for part in range(3):
        right = right_factor(bq_ref[:, :block], qkv[part, :block])
        for start in range(block, qkv.shape[1], block):
            rows = slice(start, start + block)
            right += right_factor(bq_ref[:, rows], qkv[part, rows])
        offset_two = place_tiles(mine_two, offset_two, right)
    for basis_ref, matrix in zip((bo_ref, bd_ref, bi_ref), (out, down, inw)):
        rows_of = min(block, matrix.shape[0])
        right = right_factor(basis_ref[:, :rows_of], matrix[:rows_of])
        for start in range(rows_of, matrix.shape[0], rows_of):
            rows = slice(start, start + rows_of)
            right += right_factor(basis_ref[:, rows], matrix[rows])
        offset_two = place_tiles(mine_two, offset_two, right)
    if far_refs:
        far_copy(1).wait_recv()
        sent[2, 0] = low_right(got[1, 0], far_down[...])
        sent[2, 1] = low_right(got[1, 1], far_in[...])
        far_copy(2).start()
        bulks[1].start()
        far_copy(2).wait_recv()
        add_tiles(mine_two, offset_two - (down.shape[1] + inw.shape[1]) // LANES, got[2, 0])
        add_tiles(mine_two, offset_two - inw.shape[1] // LANES, got[2, 1])
    drain_two = dp_exchange(
        replicas, mine_two, wire_two, arrived_two, total_two, second_sems
    )

    def collect(step, carry):
        peer = lax.rem(tensor_place + step, tensor_size)
        slot_copy(step, peer).wait_recv()
        slot_copy(step, tensor_place).wait_send()
        return carry + small_slots[peer]

    everyone = lax.fori_loop(1, tensor_size, collect, own_small)
    row_number = lax.broadcasted_iota(jnp.int32, everyone.shape, 0)
    sum_ref[...] = jnp.where(row_number < 6, everyone, own_small) * (1.0 / replicas)
    offset = 0
    for part in range(3):
        rq_ref[part] = take_tiles(total_two, offset, rq_ref.shape[2]) * (1.0 / replicas)
        offset += rq_ref.shape[2] // LANES
    for ref in (ro_ref, rd_ref, ri_ref):
        ref[...] = take_tiles(total_two, offset, ref.shape[1]) * (1.0 / replicas)
        offset += ref.shape[1] // LANES
    drain_two()
    if far_refs:
        for number in range(3):
            far_copy(number).wait_send()
        for copy in bulks:
            copy.wait()


def compress(matrices, factors, small, replicas, tensor_size, far):
    qkv, out, inw, down = matrices
    rank_size = small.shape[0]
    sizes = (qkv.shape[1], out.shape[0], inw.shape[0], down.shape[0])
    right_shapes = [(3, rank_size, qkv.shape[2])] + [(rank_size, one.shape[1]) for one in matrices[1:]]
    lanes_one = sum(sizes) + small.shape[1]
    lanes_two = 3 * qkv.shape[2] + sum(one.shape[1] for one in matrices[1:])
    scratch = [pltpu.VMEM(one.shape, jnp.float32) for one in matrices]
    for lanes in (lanes_one, lanes_two):
        shape = (replicas, rank_size, -(-lanes // (LANES * replicas)) * LANES)
        scratch += [
            pltpu.VMEM(shape, jnp.float32),
            pltpu.VMEM(shape, jnp.bfloat16),
            pltpu.VMEM(shape, jnp.bfloat16),
            pltpu.VMEM(shape, jnp.float32),
        ]
    scratch += [pltpu.VMEM((tensor_size,) + small.shape, jnp.float32), pltpu.SemaphoreType.DMA((6,))]
    scratch += [pltpu.SemaphoreType.DMA((replicas,))] * 8
    scratch += [pltpu.SemaphoreType.DMA((tensor_size,))] * 2
    if far:
        scratch += [pltpu.VMEM(one.shape, one.dtype) for one in far[:2]]
        scratch += [pltpu.VMEM((3, 2, rank_size, inw.shape[0]), jnp.float32)] * 2
        scratch += [pltpu.SemaphoreType.DMA((5,))] * 2
    vmem = pl.BlockSpec(memory_space=pltpu.VMEM)
    shapes = [(rank_size, size) for size in sizes] + right_shapes + [small.shape]
    shapes = [jax.ShapeDtypeStruct(shape, jnp.float32) for shape in shapes]
    late_shape = []
    if far:
        late_shape = [jax.ShapeDtypeStruct((inw.shape[0] * 5 // 8, inw.shape[1]), far[0].dtype)]
    outputs = pl.pallas_call(
        partial(compress_kernel, replicas, tensor_size, bool(far)),
        in_specs=([pl.BlockSpec(memory_space=pl.ANY)] * 2 + [vmem] * 2 if far else [])
        + [pl.BlockSpec(memory_space=pl.ANY)] * 4
        + [vmem] * 5,
        out_specs=[pl.BlockSpec(memory_space=pl.ANY)] * len(late_shape) + [vmem] * 9,
        out_shape=late_shape + shapes,
        scratch_shapes=scratch,
        compiler_params=pltpu.CompilerParams(
            collective_id=1, has_side_effects=True, vmem_limit_bytes=VMEM_GRANT
        ),
        name="compress",
    )(*far, *matrices, *factors, small)
    late, outputs = outputs[:-9], outputs[-9:]
    return outputs[:4], outputs[4:8], outputs[8], late


def outer_of(basis_rows, right):
    basis_high, basis_low = split_bf16(basis_rows)
    right_high, right_low = split_bf16(right)
    return dot_tn(
        jnp.concatenate([basis_high, basis_low, basis_high], axis=0),
        jnp.concatenate([right_high, right_high, right_low], axis=0),
    )


def update_kernel(step_rate, out_steps, near_steps, *refs):
    (mq, mo, mi, md, oq, oo, oi, od, wq, wo, wi, wd, bq, bo, bi, bd, rq, ro, ri, rd,
     gq, go, gi, gd, eq, eo, ei, ed, nq, no, ni, nd, vq, vo, vi, vd) = refs[:20] + refs[-16:]
    step = pl.program_id(0)
    whole_in, whole_down = mi[...], md[...]
    if len(refs) > 36:
        near_in, rest_in, near_down, rest_down = refs[20:24]
        whole_in += jnp.where(step < near_steps, near_in[...], rest_in[...]).astype(jnp.float32)
        whole_down += jnp.where(step < near_steps, near_down[...], rest_down[...]).astype(
            jnp.float32
        )

    def one(matrix, old, weight, rank, grad_ref, err_ref, mom_ref, new_ref, place):
        moment = 0.9 * old + rank
        grad_ref[place] = rank
        err_ref[place] = matrix - rank
        mom_ref[place] = moment
        new_ref[place] = weight.astype(jnp.float32) - step_rate * moment

    def lanes_of(ref, rows):
        return ref[:, pl.ds(pl.multiple_of(step * rows, LANES), rows)]

    rows = mq.shape[1]
    for part in range(3):
        rank = outer_of(lanes_of(bq, rows), rq[part])
        one(mq[part], oq[part], wq[part], rank, gq, eq, nq, vq, part)
    rank = outer_of(lanes_of(bi, mi.shape[0]), ri[...])
    one(whole_in, oi[...], wi[...], rank, gi, ei, ni, vi, slice(None))
    rank = outer_of(lanes_of(bd, md.shape[0]), rd[...])
    one(whole_down, od[...], wd[...], rank, gd, ed, nd, vd, slice(None))

    @pl.when(step < out_steps)
    def _():
        rank = outer_of(lanes_of(bo, mo.shape[0]), ro[...])
        one(mo[...], oo[...], wo[...], rank, go, eo, no, vo, slice(None))


def update(matrices, momenta, weights, bases, rights, late, step_rate):
    qkv, out, inw, down = matrices
    rows = LANES
    steps = inw.shape[0] // rows
    down_rows = down.shape[0] // steps
    if down_rows < LANES:
        steps = down.shape[0] // LANES
        rows, down_rows = inw.shape[0] // steps, LANES
    out_steps = out.shape[0] // LANES
    near_steps = late[0].shape[0] // rows if late else 0
    late_specs = [
        pl.BlockSpec((rows, inw.shape[1]), lambda i: (jnp.minimum(i, near_steps - 1), 0)),
        pl.BlockSpec((rows, inw.shape[1]), lambda i: (jnp.maximum(i - near_steps, 0), 0)),
        pl.BlockSpec((down_rows, down.shape[1]), lambda i: (jnp.minimum(i, near_steps - 1), 0)),
        pl.BlockSpec((down_rows, down.shape[1]), lambda i: (jnp.maximum(i - near_steps, 0), 0)),
    ]

    def whole(array):
        return pl.BlockSpec(array.shape, lambda i: (0,) * array.ndim)

    def specs():
        return [
            pl.BlockSpec((3, rows, qkv.shape[2]), lambda i: (0, i, 0)),
            pl.BlockSpec((LANES, out.shape[1]), lambda i: (jnp.minimum(i, out_steps - 1), 0)),
            pl.BlockSpec((rows, inw.shape[1]), lambda i: (i, 0)),
            pl.BlockSpec((down_rows, down.shape[1]), lambda i: (i, 0)),
        ]

    shapes = [jax.ShapeDtypeStruct(one.shape, jnp.float32) for one in matrices]
    outputs = pl.pallas_call(
        partial(update_kernel, step_rate, out_steps, near_steps),
        grid=(steps,),
        in_specs=specs() * 3
        + [whole(one) for one in bases]
        + [whole(one) for one in rights]
        + late_specs[: len(late)],
        out_specs=specs() * 4,
        out_shape=shapes * 4,
        compiler_params=pltpu.CompilerParams(vmem_limit_bytes=VMEM_GRANT),
        name="update",
    )(*matrices, *momenta, *weights, *bases, *rights, *late)
    return outputs[0:4], outputs[4:8], outputs[8:12], outputs[12:16]


def masked_scores(queries, key_heads, seg_ids):
    scores = jnp.einsum("qhd,khd->hqk", queries, key_heads, preferred_element_type=jnp.float32)
    same_doc = seg_ids[:, None] == seg_ids[None, :]
    return jnp.where(same_doc[None], scores, MASKED)


def attend_forward(inputs_of):
    queries, key_heads, value_heads, seg_ids = inputs_of
    scores = masked_scores(queries, key_heads, seg_ids)
    highest = jnp.max(scores, axis=-1, keepdims=True)
    powers = jnp.exp(scores - highest)
    denominator = jnp.sum(powers, axis=-1, keepdims=True)
    weights = (powers / denominator).astype(jnp.bfloat16)
    mixed_heads = jnp.einsum(
        "hqk,khd->qhd", weights, value_heads, preferred_element_type=jnp.float32
    )
    return (mixed_heads.astype(jnp.bfloat16), highest[..., 0] + jnp.log(denominator[..., 0]))


def attend_backward(inputs_of):
    queries, key_heads, value_heads, seg_ids, grad_mixed, log_total = inputs_of
    scores = masked_scores(queries, key_heads, seg_ids)
    probability = jnp.exp(scores - log_total[..., None])
    grad_probs = jnp.einsum(
        "qhd,khd->hqk", grad_mixed, value_heads, preferred_element_type=jnp.float32
    )
    centre = jnp.sum(probability * grad_probs, axis=-1, keepdims=True)
    grad_scores = (probability * (grad_probs - centre)).astype(jnp.bfloat16)
    grad_query = jnp.einsum(
        "hqk,khd->qhd", grad_scores, key_heads, preferred_element_type=jnp.float32
    )
    grad_key = jnp.einsum("hqk,qhd->khd", grad_scores, queries, preferred_element_type=jnp.float32)
    grad_value = jnp.einsum(
        "hqk,qhd->khd",
        probability.astype(jnp.bfloat16),
        grad_mixed,
        preferred_element_type=jnp.float32,
    )
    return (
        grad_query.astype(jnp.bfloat16),
        grad_key.astype(jnp.bfloat16),
        grad_value.astype(jnp.bfloat16),
    )


def stacked_heads(pair, lane_is_low):
    zero = jnp.zeros_like(pair)
    return jnp.concatenate(
        [jnp.where(lane_is_low, pair, zero), jnp.where(lane_is_low, zero, pair)], axis=0
    )


def own_blocks(both):
    rows = both.shape[1] // 2
    return jnp.concatenate([both[:DH, :rows], both[DH:, rows:]], axis=0).T


def window_sizes(length):
    return (length * 3 // 8, length * 5 // 8, length)


def windows_of(bounds, length):
    first = bounds[0] // LANES * LANES
    need = bounds[1] - first
    small, large, whole = window_sizes(length)
    number = jnp.where(need <= small, 0, jnp.where(need <= large, 1, 2))
    room = jnp.where(need <= small, length - small, jnp.where(need <= large, length - large, 0))
    return jnp.concatenate([jnp.minimum(first, room), number])


def attend_back_kernel(place_ref, q_ref, k_ref, v_ref, seg_key_ref, seg_query_ref, gm_own_ref,
                       gm_other_ref, mixed_ref, log_ref, old_ref, grad_ref, sums_ref, key_t, grad_key,
                       grad_value):
    del old_ref
    step = pl.program_id(0)

    @pl.when(step == 0)
    def _():
        key_t[...] = k_ref[...].T
        grad_key[...] = jnp.zeros_like(grad_key)
        grad_value[...] = jnp.zeros_like(grad_value)

    pairs = q_ref.shape[1] // LANES
    lane = lax.broadcasted_iota(jnp.int32, (1, LANES), 1)
    lane_is_low = lane < DH
    head_of_lane = (
        lax.broadcasted_iota(jnp.int32, (8, LANES), 0)
        == lax.broadcasted_iota(jnp.int32, (8, LANES), 1) // DH
    ).astype(jnp.bfloat16)
    head_scale = 1.0 / math.sqrt(DH)
    here = pl.ds(pl.multiple_of(step * LANES, LANES), LANES)
    is_own = lax.rem(step // (pl.num_programs(0) // 2) + place_ref[1], 2) == 0
    gm = jnp.where(is_own, gm_own_ref[...], gm_other_ref[...])
    seg_query = jnp.concatenate([seg_query_ref[...], seg_query_ref[...]], axis=1)
    all_lanes = [slice(pair * LANES, (pair + 1) * LANES) for pair in range(pairs)]
    length = k_ref.shape[0]

    def window(size):
        start = 0 if size == length else pl.multiple_of(place_ref[2 + step], LANES)
        keys = pl.ds(start, size)
        seg_key = seg_key_ref[keys]
        same = jnp.concatenate([seg_key, seg_key], axis=1) == seg_query
        queries, grads, centres, probs, grad_probs = [], [], [], [], []
        for lanes in all_lanes:
            queries.append(stacked_heads(q_ref[:, lanes], lane_is_low))
            grads.append(stacked_heads(gm[:, lanes], lane_is_low))
            high, low = split_bf16(
                gm[:, lanes].astype(jnp.float32) * mixed_ref[:, lanes].astype(jnp.float32)
            )
            sums = dot_nt(head_of_lane, high) + dot_nt(head_of_lane, low)
            centres.append(jnp.concatenate([sums[0:1], sums[1:2]], axis=1))
        for pair, lanes in enumerate(all_lanes):
            log_total = jnp.concatenate(
                [log_ref[2 * pair : 2 * pair + 1], log_ref[2 * pair + 1 : 2 * pair + 2]], axis=1
            )
            scores = dot_nt(k_ref[keys, lanes], queries[pair])
            probs.append(jnp.exp(jnp.where(same, scores - log_total, MASKED)))
            grad_probs.append(dot_nt(v_ref[keys, lanes], grads[pair]))
        for pair, lanes in enumerate(all_lanes):
            grad_scores = (probs[pair] * (grad_probs[pair] - centres[pair])).astype(jnp.bfloat16)
            grad_value[keys, lanes] += dot_nn(probs[pair].astype(jnp.bfloat16), grads[pair])
            grad_key[keys, lanes] += dot_nn(grad_scores, queries[pair])
            grad_query = own_blocks(dot_nn(key_t[lanes, keys], grad_scores)).astype(jnp.bfloat16)
            grad_ref[0, here, lanes] = (grad_query.astype(jnp.float32) * head_scale).astype(
                jnp.bfloat16
            )

    for number, size in enumerate(window_sizes(length)):
        pl.when(place_ref[2 + pl.num_programs(0) + step] == number)(partial(window, size))

    @pl.when(step == pl.num_programs(0) - 1)
    def _():
        grad_ref[1] = grad_key[...].astype(jnp.bfloat16)
        low_value = grad_value[...].astype(jnp.bfloat16)
        grad_ref[2] = low_value
        sums_ref[0:1] = jnp.sum(grad_ref[0].astype(jnp.float32), axis=0, keepdims=True)
        sums_ref[1:2] = jnp.sum(low_value.astype(jnp.float32), axis=0, keepdims=True)


def attend_back(projected, seg_keys, seg_queries, grad_own, grad_other, mixed, logs, slot, bounds,
                old, place, core):
    length = seg_keys.shape[1]
    slab = projected.shape[2]
    blocks = length // LANES
    half = blocks // 2
    at = jnp.concatenate(
        [
            jnp.stack([place, core]),
            windows_of(bounds[2 * slot : 2 * slot + 2, :blocks], length),
        ]
    )
    grid_spec = pltpu.PrefetchScalarGridSpec(
        num_scalar_prefetch=1,
        grid=(blocks,),
        in_specs=[
            pl.BlockSpec((None, LANES, slab), lambda i, at: (0, at[0] * blocks + i, 0)),
            pl.BlockSpec((None, length, slab), lambda i, at: (1, at[0], 0)),
            pl.BlockSpec((None, length, slab), lambda i, at: (2, at[0], 0)),
            pl.BlockSpec((None, length, LANES), lambda i, at: (at[0], 0, 0)),
            pl.BlockSpec((None, 1, LANES), lambda i, at: (at[0], 0, i)),
            pl.BlockSpec((None, LANES, slab), lambda i, at: (grad_own[1], lax.rem(i, half), 0)),
            pl.BlockSpec((None, LANES, slab), lambda i, at: (grad_other[1], lax.rem(i, half), 0)),
            pl.BlockSpec((None, LANES, slab), lambda i, at: (slot, i, 0)),
            pl.BlockSpec((None, slab // DH, LANES), lambda i, at: (slot, 0, i)),
            pl.BlockSpec(memory_space=pl.ANY),
        ],
        out_specs=[
            pl.BlockSpec((3, length, slab), lambda i, at: (0, at[0], 0)),
            pl.BlockSpec((2, slab), lambda i, at: (0, 0)),
        ],
        scratch_shapes=[
            pltpu.VMEM((slab, length), jnp.bfloat16),
            pltpu.VMEM((length, slab), jnp.float32),
            pltpu.VMEM((length, slab), jnp.float32),
        ],
    )
    return pl.pallas_call(
        attend_back_kernel,
        grid_spec=grid_spec,
        out_shape=[
            jax.ShapeDtypeStruct(projected.shape, jnp.bfloat16),
            jax.ShapeDtypeStruct((2, slab), jnp.float32),
        ],
        input_output_aliases={} if old is None else {10: 0},
        compiler_params=pltpu.CompilerParams(vmem_limit_bytes=24 << 20),
        cost_estimate=BRIEF,
        name="attend_back",
    )(at, projected, projected, projected, seg_keys, seg_queries, grad_own[0],
      grad_other[0], mixed, logs, seg_keys if old is None else old)


def row_mean(values):
    return jnp.mean(values, axis=-1, keepdims=True)


def layer_kernel(tokens, cotangent, w_qkv_ref, out_ref, in_ref, down_ref,
                 factor_in_ref, factor_down_ref, head_ref, bias_ref, vec_ref, seg_keys, seg_queries,
                 projected_out, log_out, mixed_out, in_two, down_two, out_rest, bias_two,
                 result_out, low_out, active_out, branch_out, hidden_out, norm_out, near_out,
                 far_out, down_near, down_part_out, down_rest, in_part_out, in_head,
                 far_in_out, far_down_out, out_sum,
                 out_far, unit_ref, unit_two, sums_ref, bounds_ref,
                 rows_in, w_qkv, projected, value_t, log_total, mixed, pieces,
                 w_out, w_in, w_down, bias, tok, cot, first, normed, inverse, low, slope, active,
                 part, other, acc, wide, branch, result, down_part, near, far_mixed, outs_two,
                 load_sem, store_sem, send_sem, recv_sem):
    dp_place = lax.axis_index("dp")
    tensor_place = lax.axis_index("tensor")
    core = lax.rem(tensor_place, 2)
    seq = tensor_place // 2
    far = 1 - seq
    side = lax.rem(dp_place, 2)
    depth = lax.rem(dp_place // 2, 2)
    here = 2 * depth + side
    sibling = (dp_place, tensor_place + 1 - 2 * core)
    opposite = (dp_place, core + 2 * far)
    diagonal = (dp_place, 1 - core + 2 * far)
    beside = (dp_place + 1 - 2 * side, tensor_place)
    behind = (dp_place + 2 - 4 * depth, tensor_place)
    share, width = tok.shape
    slab = in_ref.shape[1]
    length = rows_in.shape[1]
    head_slab = w_qkv.shape[2]
    head_count = head_slab // DH
    stores = []
    sends = []
    numbers = iter(range(send_sem.shape[0]))

    def load_later(number, source, target):
        return pltpu.make_async_copy(source, target, load_sem.at[number])

    def load(number, source, target):
        copy = load_later(number, source, target)
        copy.start()
        return copy

    def store(source, target):
        copy = pltpu.make_async_copy(source, target, store_sem.at[len(stores)])
        copy.start()
        stores.append(copy)

    def send_later(source, target, device):
        number = next(numbers)
        copy = pltpu.make_async_remote_copy(
            src_ref=source,
            dst_ref=target,
            send_sem=send_sem.at[number],
            recv_sem=recv_sem.at[number],
            device_id=device,
            device_id_type=MESH,
        )
        sends.append(copy)
        return copy

    def send(source, target, device):
        copy = send_later(source, target, device)
        copy.start()
        return copy

    def rows_of(number, size):
        return pl.ds(pl.multiple_of(number * size, LANES), size)

    load_qkv = load(0, w_qkv_ref, w_qkv)
    load_far = load(1, tokens.at[rows_of(far, length)], rows_in.at[0])
    load_near = load(2, tokens.at[rows_of(seq, length)], rows_in.at[1])
    load_out = load(3, out_ref, w_out.at[0])
    load_in = load(4, in_ref, w_in.at[0])
    load_down = load(5, down_ref, w_down.at[pl.ds(0, slab)])
    load_tok = load(6, tokens.at[rows_of(tensor_place, share)], tok)
    load_cot = load(7, cotangent.at[rows_of(tensor_place, share)], cot)

    barrier = pltpu.get_barrier_semaphore()
    for device in (sibling, opposite, diagonal, beside, behind):
        pl.semaphore_signal(barrier, inc=1, device_id=device, device_id_type=MESH)
    pl.semaphore_wait(barrier, 5)
    sums_ref[...] = jnp.zeros_like(sums_ref)
    unit_ref[...] = jnp.zeros_like(unit_ref)

    def rows_part(whole, number, parts):
        size = whole.shape[0] // parts
        return whole.at[pl.ds(pl.multiple_of(number * size, size), size)]

    class Fetch:
        def __init__(self, source, whole):
            own = rows_part(whole, here, 4)
            half_one = rows_part(whole, 2 * (here + 1 - 2 * side), 8)
            half_two = rows_part(whole, 2 * (here + 2 - 4 * depth) + 1, 8)
            self.over_y = send_later(rows_part(source, here, 4), own, opposite)
            self.over_x = send_later(own, own, beside)
            self.over_z = send_later(own, own, behind)
            self.half_z = send_later(half_one, half_one, behind)
            self.half_x = send_later(half_two, half_two, beside)

        def start(self):
            self.over_y.start()

        def pass_on(self):
            self.over_y.wait_recv()
            self.over_x.start()
            self.over_z.start()

        def pass_halves(self):
            self.over_x.wait_recv()
            self.half_z.start()
            self.over_z.wait_recv()
            self.half_x.start()

        def wait(self):
            self.half_z.wait_recv()
            self.half_x.wait_recv()

    bias_send = send(bias_ref, bias_two, opposite)
    factor_sends = [
        send(factor_in_ref, far_in_out, opposite), send(factor_down_ref, far_down_out, opposite)
    ]
    fetch_out = Fetch(out_ref, out_rest.at[1])
    upper, lower = pl.ds(0, width // 2), pl.ds(width // 2, width // 2)
    fetch_in = [Fetch(in_ref.at[rows], in_two.at[rows]) for rows in (upper, lower)]
    upper, lower = pl.ds(0, slab // 2), pl.ds(slab // 2, slab // 2)
    fetch_down = [Fetch(down_ref.at[rows], down_two.at[rows]) for rows in (upper, lower)]
    fetch_out.start()
    fetch_in[0].start()
    fetch_in[1].start()
    fetch_down[0].start()

    chunk = 256
    scale = 1.0 / math.sqrt(DH)

    def project(slot):
        def rows_step(step, carry):
            rows = rows_of(step, chunk)
            values = rows_in[slot, rows]
            projected[slot, 0, rows] = (
                (dot_nn(values, w_qkv[0]) + head_ref[0:1]) * scale
            ).astype(jnp.bfloat16)
            projected[slot, 1, rows] = dot_nn(values, w_qkv[1]).astype(jnp.bfloat16)
            projected[slot, 2, rows] = (dot_nn(values, w_qkv[2]) + head_ref[1:2]).astype(
                jnp.bfloat16
            )
            return carry

        lax.fori_loop(0, length // chunk, rows_step, 0)
        value_t[...] = projected[slot, 2].T

    lane_is_low = lax.broadcasted_iota(jnp.int32, (1, LANES), 1) < DH

    def attend_rows(slot, place, tasks):
        def block(step):
            rows = rows_of(step, LANES)
            same = seg_keys[place] == seg_queries[place, :, rows]
            mask = jnp.where(same, 0.0, MASKED)
            mask = jnp.concatenate([mask, mask], axis=1)
            all_lanes = [slice(at, at + LANES) for at in range(0, head_slab, LANES)]
            all_scores = [
                dot_nt(
                    projected[slot, 1, :, lanes],
                    stacked_heads(projected[slot, 0, rows, lanes], lane_is_low),
                )
                + mask
                for lanes in all_lanes
            ]
            for pair, (lanes, scores) in enumerate(zip(all_lanes, all_scores)):
                highest = jnp.max(scores, axis=0, keepdims=True)
                powers = jnp.exp(scores - highest)
                denominator = jnp.sum(powers, axis=0, keepdims=True)
                blend = dot_nn(value_t[lanes], powers.astype(jnp.bfloat16))
                mixed[slot, rows, lanes] = own_blocks(blend * (1.0 / denominator)).astype(
                    jnp.bfloat16
                )
                total = highest + jnp.log(denominator)
                log_total[slot, 2 * pair : 2 * pair + 1, rows] = total[:, :LANES]
                log_total[slot, 2 * pair + 1 : 2 * pair + 2, rows] = total[:, LANES:]

        def two_blocks(step, carry):
            for number, task in tasks:
                pl.when(step == number)(task)
            block(2 * step)
            block(2 * step + 1)
            return carry

        lax.fori_loop(0, length // LANES // 2, two_blocks, 0)

    load_qkv.wait()
    load_far.wait()
    project(0)
    attend_rows(0, far, [(2, fetch_out.pass_on)])
    fetch_in[0].pass_on()
    own_rows = rows_of(core, share)
    sibling_rows = rows_of(1 - core, share)
    piece_two = send(mixed.at[0, own_rows], pieces.at[1], opposite)
    piece_three = send(mixed.at[0, sibling_rows], pieces.at[2], diagonal)
    fetch_down[1].start()
    store(projected.at[0, 0], projected_out.at[0, rows_of(far, length)])
    store(projected.at[0, 1], projected_out.at[1, rows_of(far, length)])
    store(projected.at[0, 2], projected_out.at[2, rows_of(far, length)])
    load_near.wait()
    project(1)
    out_pass = [
        send_later(out_ref, out_rest.at[0], sibling),
        send_later(out_rest.at[1], out_rest.at[2], sibling),
    ]
    load_two = load_later(8, out_rest.at[1], w_out.at[2])

    def pass_in():
        fetch_in[1].pass_on()
        fetch_in[0].pass_halves()

    def pass_out():
        fetch_out.wait()
        for copy in out_pass:
            copy.start()
        load_two.start()

    attend_rows(1, seq, [(0, fetch_out.pass_halves), (2, pass_in), (3, pass_out)])
    piece_one = send(mixed.at[1, sibling_rows], pieces.at[0], sibling)
    store(projected.at[1, 0], projected_out.at[0, rows_of(seq, length)])
    store(projected.at[1, 1], projected_out.at[1, rows_of(seq, length)])
    store(projected.at[1, 2], projected_out.at[2, rows_of(seq, length)])
    store(log_total, log_out)
    for copy in out_pass:
        copy.wait_recv()
    load_one = load(9, out_rest.at[0], w_out.at[1])
    load_three = load(10, out_rest.at[2], w_out.at[3])
    store(mixed, mixed_out)
    fetch_down[0].pass_on()
    fetch_in[1].pass_halves()
    for copy in (load_out, load_tok, load_one, load_two, load_three):
        copy.wait()
    for copy in (piece_two, piece_three, piece_one):
        copy.wait_recv()
    small = 64

    def attn_rows(step, carry):
        rows = rows_of(step, chunk)
        total = dot_nn(mixed[1, pl.ds(pl.multiple_of(core * share + step * chunk, LANES), chunk)],
                       w_out[0])
        for piece in range(3):
            total += dot_nn(pieces[piece, rows], w_out[piece + 1])
        acc[rows] = total
        return carry

    def first_rows(step, carry):
        rows = pl.ds(pl.multiple_of(step * small, small), small)
        values = tok[rows].astype(jnp.float32) + (acc[rows] + vec_ref[0:1])
        centred = values - row_mean(values)
        spread = lax.rsqrt(row_mean(centred * centred) + EPS_NORM)
        unit = centred * spread
        normed[rows] = unit
        inverse[rows] = spread
        shifted = unit * vec_ref[2:3] + vec_ref[3:4]
        first[rows] = shifted
        low[rows] = shifted.astype(jnp.bfloat16)
        return carry

    lax.fori_loop(0, share // chunk, attn_rows, 0)
    lax.fori_loop(0, share // small, first_rows, 0)
    slots = [slice(0, share), slice(share, 2 * share)]
    low_send = send(low.at[slots[0]], low.at[slots[1]], sibling)
    fetch_down[0].pass_halves()
    load_in.wait()

    def hidden_of(slot, owner):
        def units(step, carry):
            inner = rows_of(step, chunk)
            values = dot_nn(low[slots[slot]], w_in[owner, :, inner]) + bias[owner, :, inner]
            share_of = 0.5 * (1.0 + lax.erf(values * math.sqrt(0.5)))
            density = jnp.exp(-0.5 * values * values) * (1.0 / math.sqrt(2.0 * math.pi))
            active[owner, slots[slot], inner] = (values * share_of).astype(jnp.bfloat16)
            slope[owner, slots[slot], inner] = (share_of - 0.5 + values * density).astype(jnp.bfloat16)
            return carry

        lax.fori_loop(0, slab // chunk, units, 0)

    def branch_of(slot, owner, target, start, size):
        units = slice(owner * slab, (owner + 1) * slab)

        def columns(step, carry):
            at = pl.ds(pl.multiple_of(start + step * chunk, chunk), chunk)
            values = dot_nn(active[owner, slots[slot]], w_down[units, at])
            target[:, at] = values if owner == 0 else target[:, at] + values
            return carry

        lax.fori_loop(0, size // chunk, columns, 0)

    bias_send.wait_recv()
    bias[0] = bias_ref[...]
    load_bias = load(11, bias_two, bias.at[1])
    hidden_of(0, 0)
    low_send.wait_recv()
    store(low, low_out)
    fetch_down[1].pass_on()
    hidden_of(1, 0)
    for fetch in fetch_in:
        fetch.wait()
    load_in_two = load(12, in_two, w_in.at[1])
    load_down.wait()
    branch_of(1, 0, part, 0, width)
    branch_of(0, 0, acc, 0, width)
    load_bias.wait()
    load_in_two.wait()
    fetch_down[1].pass_halves()
    hidden_of(1, 1)
    hidden_of(0, 1)
    store(active.at[0], active_out)
    lane = lax.broadcasted_iota(jnp.int32, (1, LANES), 1)
    for slot, place in ((0, far), (1, seq)):
        firsts = jnp.zeros((1, LANES), jnp.int32)
        lasts = jnp.zeros((1, LANES), jnp.int32)
        for block in range(length // LANES):
            start = block * LANES
            firsts = jnp.where(lane == block, seg_keys[place, start : start + 1], firsts)
            lasts = jnp.where(
                lane == block, seg_keys[place, start + LANES - 1 : start + LANES], lasts
            )
        documents = seg_keys[place]
        bounds_ref[2 * slot : 2 * slot + 1] = jnp.sum(
            jnp.where(documents < firsts, 1.0, 0.0), axis=0, keepdims=True
        ).astype(jnp.int32)
        bounds_ref[2 * slot + 1 : 2 * slot + 2] = jnp.sum(
            jnp.where(documents <= lasts, 1.0, 0.0), axis=0, keepdims=True
        ).astype(jnp.int32)
    for fetch in fetch_down:
        fetch.wait()
    load_down_two = load(13, down_two, w_down.at[pl.ds(slab, slab)])
    load_down_two.wait()
    half = width // 2
    part_sends = []
    for number in range(2):
        branch_of(1, 1, part, number * half, half)
        columns = slice(number * half, (number + 1) * half)
        part_sends.append(send(part.at[:, columns], other.at[:, columns], sibling))
    branch_of(0, 1, acc, 0, width)
    load_cot.wait()
    for copy in part_sends:
        copy.wait_recv()

    def second_rows(step, carry):
        rows = pl.ds(pl.multiple_of(step * small, small), small)
        values = first[rows] + (acc[rows] + other[rows]) + vec_ref[1:2]
        centred = values - row_mean(values)
        spread = lax.rsqrt(row_mean(centred * centred) + EPS_NORM)
        unit = centred * spread
        result[rows] = (unit * vec_ref[4:5] + vec_ref[5:6]).astype(jnp.bfloat16)
        upper = cot[rows].astype(jnp.float32)
        scaled = upper * vec_ref[4:5]
        grad = spread * (scaled - row_mean(scaled) - unit * row_mean(scaled * unit))
        wide[rows] = grad
        grad_low = grad.astype(jnp.bfloat16)
        branch[rows] = grad_low
        sums_ref[1:2] += jnp.sum(grad_low.astype(jnp.float32), axis=0, keepdims=True)
        sums_ref[4:5] += jnp.sum(upper * unit, axis=0, keepdims=True)
        sums_ref[5:6] += jnp.sum(upper, axis=0, keepdims=True)
        return carry

    branch_sends = []
    for number in range(2):
        steps = share // small // 2
        lax.fori_loop(number * steps, (number + 1) * steps, second_rows, 0)
        rows = slice(number * steps * small, (number + 1) * steps * small)
        there = slice(share + rows.start, share + rows.stop)
        branch_sends.append(send(branch.at[rows], branch.at[there], sibling))
    store(result, result_out)
    hidden = rows_in

    def grad_hidden_of(slot, owner):
        def units(step, carry):
            inner = rows_of(step, chunk)
            outer = pl.ds(pl.multiple_of(owner * slab + step * chunk, chunk), chunk)
            grad = dot_nt(branch[slots[slot]], w_down[outer]) * (
                0.5 + slope[owner, slots[slot], inner].astype(jnp.float32)
            )
            grad_low = grad.astype(jnp.bfloat16)
            hidden[owner, slots[slot], inner] = grad_low
            unit_ref[:, outer] += jnp.sum(grad_low.astype(jnp.float32), axis=0, keepdims=True)
            return carry

        lax.fori_loop(0, slab // chunk, units, 0)

    def grad_first_of(slot, target, start, size):
        def columns(step, carry):
            at = pl.ds(pl.multiple_of(start + step * chunk, chunk), chunk)
            target[:, at] = dot_nt(hidden[0, slots[slot]], w_in[0, at]) + dot_nt(
                hidden[1, slots[slot]], w_in[1, at]
            )
            return carry

        lax.fori_loop(0, size // chunk, columns, 0)

    def far_product(left_side, right_side, target, start, stop):
        def rows_step(step, carry):
            at = rows_of(step, LANES)
            target[at] = dot_tn(left_side[:, at], right_side[...]).astype(jnp.bfloat16)
            return carry

        lax.fori_loop(start // LANES, stop // LANES, rows_step, 0)

    grad_hidden_of(0, 0)
    grad_hidden_of(0, 1)
    for copy in branch_sends:
        copy.wait_recv()
    store(branch, branch_out)
    early = down_near.shape[0]
    far_product(active.at[1], branch, down_part, 0, early)
    down_send = send(down_part.at[pl.ds(0, early)], down_near, opposite)
    far_product(active.at[1], branch, down_part, early, slab)
    store(down_part, down_part_out)
    store(down_part.at[pl.ds(early, slab - early)], down_rest)
    grad_hidden_of(1, 0)
    grad_hidden_of(1, 1)
    unit_send = send(unit_ref.at[:, pl.ds(slab, slab)], unit_two, opposite)
    store(hidden.at[0], hidden_out)
    for copy in part_sends:
        copy.wait_send()
    sends[:] = [one for one in sends if all(one is not copy for copy in part_sends)]
    first_sends = []
    for number in range(2):
        grad_first_of(1, part, number * half, half)
        columns = slice(number * half, (number + 1) * half)
        first_sends.append(send(part.at[:, columns], other.at[:, columns], sibling))
    grad_first_of(0, acc, 0, width)
    for copy in first_sends:
        copy.wait_recv()

    def back_rows(step, carry):
        rows = pl.ds(pl.multiple_of(step * small, small), small)
        grad = acc[rows] + other[rows] + wide[rows]
        unit = normed[rows]
        scaled = grad * vec_ref[2:3]
        back = inverse[rows] * (scaled - row_mean(scaled) - unit * row_mean(scaled * unit))
        acc[rows] = back
        back_low = back.astype(jnp.bfloat16)
        tok[rows] = back_low
        sums_ref[0:1] += jnp.sum(back_low.astype(jnp.float32), axis=0, keepdims=True)
        sums_ref[2:3] += jnp.sum(grad * unit, axis=0, keepdims=True)
        sums_ref[3:4] += jnp.sum(grad, axis=0, keepdims=True)
        return carry

    lax.fori_loop(0, share // small, back_rows, 0)
    store(acc, norm_out)
    attn = tok[...]
    near[1] = dot_nt(attn, w_out[1]).astype(jnp.bfloat16)
    near_send = send(near.at[1], near.at[2], sibling)
    out_one = slice(0, head_slab)
    out_three = slice(head_slab, 2 * head_slab)
    first[out_one] = dot_tn(pieces[0], attn)
    first[out_three] = dot_tn(pieces[2], attn)
    outs_send = send(first.at[pl.ds(0, 2 * head_slab)], outs_two, sibling)
    far_mixed[0] = dot_nt(attn, w_out[2]).astype(jnp.bfloat16)
    far_mixed[1] = dot_nt(attn, w_out[3]).astype(jnp.bfloat16)
    store(far_mixed, far_out)
    near[0] = dot_nt(attn, w_out[0]).astype(jnp.bfloat16)
    store(near.at[0], near_out.at[0])
    far_product(low, hidden.at[1], active.at[1], 0, width)
    store(active.at[1], in_part_out)
    store(active.at[1, pl.ds(0, in_head.shape[0])], in_head)
    near_send.wait_recv()
    store(near.at[2], near_out.at[1])
    outs_send.wait_recv()
    out_sum[...] = dot_tn(mixed[1, own_rows], attn) + outs_two[out_one]
    out_far[...] = (dot_tn(pieces[1], attn) + outs_two[out_three]).astype(jnp.bfloat16)
    unit_send.wait_recv()
    down_send.wait_recv()
    for copy in factor_sends:
        copy.wait_recv()
    for copy in sends:
        copy.wait_send()
    for copy in stores:
        copy.wait()


def layer_call(tokens, cotangent, planes, w_out, w_in, w_down, factor_in, factor_down, head_bias,
               unit_bias, vectors, seg_keys, seg_queries):
    token_count, width = tokens.shape
    seq_count, length = seg_keys.shape[:2]
    share = token_count // (2 * seq_count)
    head_slab = planes.shape[2]
    slab = w_in.shape[1]
    early = slab * 3 // 8
    low_type, full_type = jnp.bfloat16, jnp.float32
    vmem = pl.BlockSpec(memory_space=pltpu.VMEM)
    anywhere = pl.BlockSpec(memory_space=pl.ANY)
    shapes = [
        jax.ShapeDtypeStruct((3, token_count, head_slab), low_type),
        jax.ShapeDtypeStruct((2, head_slab // DH, length), full_type),
        jax.ShapeDtypeStruct((2, length, head_slab), low_type),
        jax.ShapeDtypeStruct(w_in.shape, low_type),
        jax.ShapeDtypeStruct(w_down.shape, low_type),
        jax.ShapeDtypeStruct((3,) + w_out.shape, low_type),
        jax.ShapeDtypeStruct((1, slab), full_type),
        jax.ShapeDtypeStruct((share, width), low_type),
        jax.ShapeDtypeStruct((2 * share, width), low_type),
        jax.ShapeDtypeStruct((2 * share, slab), low_type),
        jax.ShapeDtypeStruct((2 * share, width), low_type),
        jax.ShapeDtypeStruct((2 * share, slab), low_type),
        jax.ShapeDtypeStruct((share, width), full_type),
        jax.ShapeDtypeStruct((2, share, head_slab), low_type),
        jax.ShapeDtypeStruct((2, share, head_slab), low_type),
        jax.ShapeDtypeStruct((early, width), low_type),
        jax.ShapeDtypeStruct((slab, width), low_type),
        jax.ShapeDtypeStruct((slab - early, width), low_type),
        jax.ShapeDtypeStruct(w_in.shape, low_type),
        jax.ShapeDtypeStruct((early, slab), low_type),
        jax.ShapeDtypeStruct(factor_in.shape, full_type),
        jax.ShapeDtypeStruct(factor_down.shape, full_type),
        jax.ShapeDtypeStruct((head_slab, width), full_type),
        jax.ShapeDtypeStruct((head_slab, width), low_type),
        jax.ShapeDtypeStruct((1, 2 * slab), full_type),
        jax.ShapeDtypeStruct((1, slab), full_type),
        jax.ShapeDtypeStruct((6, width), full_type),
        jax.ShapeDtypeStruct((4, LANES), jnp.int32),
    ]
    return pl.pallas_call(
        layer_kernel,
        in_specs=[anywhere] * 8 + [vmem] * 5,
        out_specs=[anywhere] * 22 + [vmem] * 6,
        out_shape=shapes,
        scratch_shapes=[
            pltpu.VMEM((2, length, width), low_type),
            pltpu.VMEM(planes.shape, low_type),
            pltpu.VMEM((2, 3, length, head_slab), low_type),
            pltpu.VMEM((head_slab, length), low_type),
            pltpu.VMEM((2, head_slab // DH, length), full_type),
            pltpu.VMEM((2, length, head_slab), low_type),
            pltpu.VMEM((3, share, head_slab), low_type),
            pltpu.VMEM((4,) + w_out.shape, low_type),
            pltpu.VMEM((2,) + w_in.shape, low_type),
            pltpu.VMEM((2 * slab, width), low_type),
            pltpu.VMEM((2, 1, slab), full_type),
            pltpu.VMEM((share, width), low_type),
            pltpu.VMEM((share, width), low_type),
            pltpu.VMEM((share, width), full_type),
            pltpu.VMEM((share, width), full_type),
            pltpu.VMEM((share, 1), full_type),
            pltpu.VMEM((2 * share, width), low_type),
            pltpu.VMEM((2, 2 * share, slab), low_type),
            pltpu.VMEM((2, 2 * share, slab), low_type),
            pltpu.VMEM((share, width), full_type),
            pltpu.VMEM((share, width), full_type),
            pltpu.VMEM((share, width), full_type),
            pltpu.VMEM((share, width), full_type),
            pltpu.VMEM((2 * share, width), low_type),
            pltpu.VMEM((share, width), low_type),
            pltpu.VMEM((slab, width), low_type),
            pltpu.VMEM((3, share, head_slab), low_type),
            pltpu.VMEM((2, share, head_slab), low_type),
            pltpu.VMEM((2 * head_slab, width), full_type),
            pltpu.SemaphoreType.DMA((14,)),
            pltpu.SemaphoreType.DMA((24,)),
            pltpu.SemaphoreType.DMA((46,)),
            pltpu.SemaphoreType.DMA((46,)),
        ],
        compiler_params=pltpu.CompilerParams(
            collective_id=3, has_side_effects=True, vmem_limit_bytes=VMEM_GRANT
        ),
        name="layer",
    )(tokens, cotangent, planes, w_out, w_in, w_down, factor_in, factor_down, head_bias, unit_bias,
      vectors, seg_keys, seg_queries)


def layer_general(tokens, segments, w_qkv, head_bias, w_out, w_in, unit_bias, w_down, vectors,
                  cotangent, basis_in, basis_down):
    token_count, model_width = tokens.shape
    seq_count, length = segments.shape
    head_slab = w_qkv.shape[2]
    head_count = head_slab // DH
    tensor_size = lax.axis_size("tensor")
    share_rows = token_count // tensor_size
    tensor_place = lax.axis_index("tensor")
    row_start = tensor_place * share_rows
    head_scale = 1.0 / math.sqrt(DH)

    def own_rows(values):
        return lax.dynamic_slice_in_dim(values, row_start, share_rows, 0)

    flat_qkv = w_qkv.reshape(model_width, 3 * head_slab)
    projected = jnp.dot(tokens, flat_qkv, preferred_element_type=jnp.float32).reshape(
        token_count, 3, head_slab
    )
    head_shape = (seq_count, length, head_count, DH)
    queries = (
        ((projected[:, 0] + head_bias[0]) * head_scale).astype(jnp.bfloat16).reshape(head_shape)
    )
    key_heads = projected[:, 1].astype(jnp.bfloat16).reshape(head_shape)
    value_heads = (projected[:, 2] + head_bias[1]).astype(jnp.bfloat16).reshape(head_shape)
    mixed_heads, log_total = lax.map(attend_forward, (queries, key_heads, value_heads, segments))
    mixed_flat = mixed_heads.reshape(token_count, head_slab)
    attn_out = (
        lax.psum(jnp.dot(mixed_flat, w_out, preferred_element_type=jnp.float32), "tensor")
        + vectors[0]
    )
    first_norm, first_normed, first_inverse = norm_forward(
        tokens.astype(jnp.float32) + attn_out, vectors[2], vectors[3]
    )
    first_low = first_norm.astype(jnp.bfloat16)
    hidden = jnp.dot(first_low, w_in, preferred_element_type=jnp.float32) + unit_bias
    active, gelu_back = jax.vjp(partial(jax.nn.gelu, approximate=False), hidden)
    active_low = active.astype(jnp.bfloat16)
    grad_out_share = own_rows(cotangent).astype(jnp.float32)
    summed_input = (
        first_norm
        + lax.psum(jnp.dot(active_low, w_down, preferred_element_type=jnp.float32), "tensor")
        + vectors[1]
    )
    second_norm, second_normed, second_inverse = norm_forward(summed_input, vectors[4], vectors[5])
    layer_out = own_rows(second_norm).astype(jnp.bfloat16)
    grad_sum = norm_backward(
        cotangent.astype(jnp.float32), second_normed, second_inverse, vectors[4]
    )
    grad_branch = grad_sum.astype(jnp.bfloat16)
    second_share = own_rows(second_normed)
    grad_w_down = trans_times(active_low, grad_branch)
    grad_active = times_trans(grad_branch, w_down)
    grad_hidden = gelu_back(grad_active)[0].astype(jnp.bfloat16)
    grad_w_in = trans_times(first_low, grad_hidden)
    grad_units = jnp.sum(grad_hidden.astype(jnp.float32), axis=0)
    grad_first = lax.psum(times_trans(grad_hidden, w_in), "tensor") + grad_sum
    grad_h1 = norm_backward(grad_first, first_normed, first_inverse, vectors[2])
    grad_attn = grad_h1.astype(jnp.bfloat16)
    grad_first_share = own_rows(grad_first)
    first_normed_share = own_rows(first_normed)
    grad_h1_share = own_rows(grad_h1)
    grad_w_out = trans_times(mixed_flat, grad_attn)
    grad_mixed = times_trans(grad_attn, w_out).astype(jnp.bfloat16).reshape(head_shape)
    grad_query, grad_key, grad_value = lax.map(
        attend_backward, (queries, key_heads, value_heads, segments, grad_mixed, log_total)
    )
    grad_query = (
        grad_query.reshape(token_count, head_slab).astype(jnp.float32) * head_scale
    ).astype(jnp.bfloat16)
    grad_key = grad_key.reshape(token_count, head_slab)
    grad_value = grad_value.reshape(token_count, head_slab)
    grad_projected = jnp.stack([grad_query, grad_key, grad_value], axis=1).reshape(
        token_count, 3 * head_slab
    )
    grad_w_qkv = trans_times(tokens, grad_projected)
    grad_heads = jnp.stack(
        [
            jnp.sum(grad_query.astype(jnp.float32), axis=0),
            jnp.sum(grad_value.astype(jnp.float32), axis=0),
        ]
    )
    grad_tokens = (
        lax.psum_scatter(
            times_trans(grad_projected, flat_qkv).astype(jnp.bfloat16),
            "tensor",
            scatter_dimension=0,
            tiled=True,
        ).astype(jnp.float32)
        + grad_h1_share
    )
    local_vectors = jnp.stack(
        [
            jnp.sum(own_rows(grad_attn).astype(jnp.float32), axis=0),
            jnp.sum(own_rows(grad_branch).astype(jnp.float32), axis=0),
            jnp.sum(grad_first_share * first_normed_share, axis=0),
            jnp.sum(grad_first_share, axis=0),
            jnp.sum(grad_out_share * second_share, axis=0),
            jnp.sum(grad_out_share, axis=0),
        ]
    )
    return (
        layer_out,
        lambda after: grad_tokens,
        (
            grad_w_qkv.reshape(model_width, 3, head_slab).transpose(1, 0, 2),
            grad_w_out,
            grad_w_in,
            grad_w_down,
        ),
        local_vectors,
        grad_heads,
        grad_units,
        (),
        (),
    )


def layer_split(tokens, segments, w_qkv, head_bias, w_out, w_in, unit_bias, w_down, vectors,
                cotangent, basis_in, basis_down):
    token_count, model_width = tokens.shape
    seq_count, length = segments.shape
    unit_slab = w_in.shape[1]
    tensor_size = lax.axis_size("tensor")
    share = token_count // tensor_size
    tensor_place = lax.axis_index("tensor")
    core = lax.rem(tensor_place, 2)
    seq = tensor_place // 2

    def to(values, step):
        return lax.ppermute(
            values, "tensor", [(place, place ^ step) for place in range(tensor_size)]
        )

    def rows_at(values, number, size):
        return lax.dynamic_slice_in_dim(values, number * size, size, 0)

    planes = w_qkv.transpose(1, 0, 2)
    seg_keys = jnp.broadcast_to(segments[:, :, None], (seq_count, length, LANES))
    seg_queries = segments[:, None, :]
    (projected, logs, mixed, _, _, _, _, layer_out, low, active, grad_branch, grad_hidden, grad_h1,
     grad_near, grad_far, down_near, down_part, down_rest, in_part, in_head, far_in, far_down,
     out_sum, out_far, units, unit_two, sums, bounds) = layer_call(
        tokens, cotangent, planes, w_out, w_in, w_down, basis_in, basis_down, head_bias,
        unit_bias[None], vectors, seg_keys, seg_queries,
    )
    far_own = to(grad_far[0:1], 2)
    far_other = to(grad_far[1:2], 3)
    down_rest = to(down_rest, 2)
    in_near = to(in_head, 2)
    out_back = to(out_far, 2)

    grad_projected, heads_near = attend_back(
        projected, seg_keys, seg_queries, (grad_near, 0), (grad_near, 1), mixed, logs, 1,
        bounds, None, seq, core,
    )
    grad_projected, heads_far = attend_back(
        projected, seg_keys, seg_queries, (far_own, 0), (far_other, 0), mixed, logs, 0,
        bounds, grad_projected, 1 - seq, core,
    )
    token_part = jnp.einsum(
        "gtn,gdn->td", grad_projected, planes, preferred_element_type=jnp.float32
    ).astype(jnp.bfloat16)
    other_one = to(
        jnp.stack([rows_at(token_part, 2 * at + 1 - core, share) for at in (seq, 1 - seq)]), 1
    )
    across_part = rows_at(token_part, 2 * (1 - seq) + core, share).astype(jnp.float32)
    across_part = (across_part + other_one[1].astype(jnp.float32)).astype(jnp.bfloat16)
    own_part = rows_at(token_part, 2 * seq + core, share)

    def finish_tokens(after):
        from_two = to(lax.optimization_barrier((across_part, after))[0], 2)
        return (
            own_part.astype(jnp.float32)
            + other_one[0].astype(jnp.float32)
            + from_two.astype(jnp.float32)
            + grad_h1
        )

    grad_w_qkv = jnp.einsum(
        "td,gtn->gdn", tokens, grad_projected, preferred_element_type=jnp.float32
    )
    grad_w_down = trans_times(active, grad_branch)
    grad_w_in = trans_times(low, grad_hidden)
    grad_w_out = out_sum + out_back.astype(jnp.float32)
    return (
        layer_out,
        finish_tokens,
        (grad_w_qkv, grad_w_out, grad_w_in, grad_w_down),
        sums,
        heads_near + heads_far,
        units[0, :unit_slab] + unit_two[0],
        (in_part, down_part, far_in, far_down),
        (in_near, down_near, down_rest),
    )


def local(
    tokens,
    segments,
    w_qkv,
    head_bias,
    w_out,
    w_in,
    unit_bias,
    w_down,
    vectors,
    cotangent,
    err_qkv,
    err_out,
    err_in,
    err_down,
    basis_qkv,
    basis_out,
    basis_in,
    basis_down,
    mom_qkv,
    mom_head_bias,
    mom_out,
    mom_in,
    mom_unit_bias,
    mom_down,
    mom_vectors,
):
    token_count, model_width = tokens.shape
    head_slab = w_qkv.shape[2]
    unit_slab = w_in.shape[1]
    tensor_size = lax.axis_size("tensor")
    replicas = lax.axis_size("dp")
    one_sequence_per_chip = 2 * segments.shape[0] == tensor_size and replicas % 4 == 0
    layer = layer_split if one_sequence_per_chip else layer_general
    layer_out, finish_tokens, grads, local_vectors, grad_heads, grad_units, far, late = layer(
        tokens, segments, w_qkv, head_bias, w_out, w_in, unit_bias, w_down, vectors, cotangent,
        basis_in, basis_down,
    )
    grad_w_qkv, grad_w_out, grad_w_in, grad_w_down = grads
    small = jnp.concatenate(
        [
            local_vectors,
            jnp.pad(grad_units, (0, model_width - unit_slab))[None],
            jnp.pad(grad_heads.reshape(1, 2 * head_slab), ((0, 0), (0, model_width - 2 * head_slab))),
        ],
        axis=0,
    )
    planes = (1, 0, 2)
    combined_qkv = grad_w_qkv + err_qkv[0].transpose(planes)
    combined_out = grad_w_out + err_out[0]
    combined_in = grad_w_in + err_in[0]
    combined_down = grad_w_down + err_down[0]
    matrices = (combined_qkv, combined_out, combined_in, combined_down)
    bases, rights, small_sum, late_rest = compress(
        matrices,
        (basis_qkv.transpose(planes), basis_out, basis_in, basis_down),
        small,
        replicas,
        tensor_size,
        far,
    )
    grad_tokens = finish_tokens(small_sum)
    if late:
        late = (late[0], late_rest[0]) + late[1:]
    step_rate = 0.3 * math.sqrt(replicas / token_count)
    grads, errors, moments, news = update(
        matrices,
        (mom_qkv.transpose(planes), mom_out, mom_in, mom_down),
        (w_qkv.transpose(planes), w_out, w_in, w_down),
        bases,
        rights,
        late,
        step_rate,
    )
    reduced_qkv, rank_out, rank_in, rank_down = (grads[0].transpose(planes),) + tuple(grads[1:])
    new_err_qkv, new_err_out, new_err_in, new_err_down = (
        errors[0].transpose(planes)[None],
        errors[1][None],
        errors[2][None],
        errors[3][None],
    )
    new_mom_qkv, new_mom_out, new_mom_in, new_mom_down = (moments[0].transpose(planes),) + tuple(
        moments[1:]
    )
    new_w_qkv, new_w_out, new_w_in, new_w_down = (news[0].transpose(planes),) + tuple(news[1:])
    right_qkv, right_out, right_in, right_down = rights
    new_basis_qkv = right_qkv.transpose(planes)
    grad_vectors = small_sum[:6]
    grad_unit_bias = small_sum[6, :unit_slab]
    grad_head_bias = small_sum[7, : 2 * head_slab].reshape(2, head_slab)
    new_mom_head_bias = 0.9 * mom_head_bias + grad_head_bias
    new_mom_unit_bias = 0.9 * mom_unit_bias + grad_unit_bias
    new_mom_vectors = 0.9 * mom_vectors + grad_vectors
    new_head_bias = head_bias - step_rate * new_mom_head_bias
    new_unit_bias = unit_bias - step_rate * new_mom_unit_bias
    new_vectors = vectors - step_rate * new_mom_vectors
    return (
        layer_out,
        grad_tokens,
        reduced_qkv,
        grad_head_bias,
        rank_out,
        rank_in,
        grad_unit_bias,
        rank_down,
        grad_vectors,
        new_err_qkv,
        new_err_out,
        new_err_in,
        new_err_down,
        new_basis_qkv,
        right_out,
        right_in,
        right_down,
        new_mom_qkv,
        new_mom_head_bias,
        new_mom_out,
        new_mom_in,
        new_mom_unit_bias,
        new_mom_down,
        new_mom_vectors,
        new_w_qkv,
        new_head_bias,
        new_w_out,
        new_w_in,
        new_unit_bias,
        new_w_down,
        new_vectors,
    )


def solution(mesh):
    in_specs = (
        P("dp", None),
        P("dp", None),
        P(None, None, "tensor"),
        P(None, "tensor"),
        P("tensor", None),
        P(None, "tensor"),
        P("tensor"),
        P("tensor", None),
        P(),
        P("dp", None),
        P("dp", None, None, "tensor"),
        P("dp", "tensor", None),
        P("dp", None, "tensor"),
        P("dp", "tensor", None),
        P(None, None, "tensor"),
        P("tensor", None),
        P(None, "tensor"),
        P("tensor", None),
        P(None, None, "tensor"),
        P(None, "tensor"),
        P("tensor", None),
        P(None, "tensor"),
        P("tensor"),
        P("tensor", None),
        P(),
    )
    out_specs = (
        P(("dp", "tensor"), None),
        P(("dp", "tensor"), None),
        P(None, None, "tensor"),
        P(None, "tensor"),
        P("tensor", None),
        P(None, "tensor"),
        P("tensor"),
        P("tensor", None),
        P(),
        P("dp", None, None, "tensor"),
        P("dp", "tensor", None),
        P("dp", None, "tensor"),
        P("dp", "tensor", None),
        P(None, None, "tensor"),
        P("tensor", None),
        P(None, "tensor"),
        P("tensor", None),
        P(None, None, "tensor"),
        P(None, "tensor"),
        P("tensor", None),
        P(None, "tensor"),
        P("tensor"),
        P("tensor", None),
        P(),
        P(None, None, "tensor"),
        P(None, "tensor"),
        P("tensor", None),
        P(None, "tensor"),
        P("tensor"),
        P("tensor", None),
        P(),
    )
    return jax.shard_map(local, mesh=mesh, in_specs=in_specs, out_specs=out_specs, check_vma=False)
```

```python
from functools import partial
import math

import jax
import jax.numpy as jnp
from jax import lax
from jax.experimental import pallas as pl
from jax.experimental.pallas import tpu as pltpu
from jax.sharding import PartitionSpec as P

DH = 64
LANES = 128
MESH = pl.DeviceIdType.MESH
VMEM_GRANT = 60 << 20
BRIEF = pl.CostEstimate(flops=1, bytes_accessed=1, transcendentals=1)


PRECISE = lax.Precision.HIGHEST
EPS_NORM = 1e-05
EPS_BASIS = 1e-08
MASKED = -1000000000.0


def norm_forward(values, gain, shift):
    row_mean = jnp.mean(values, axis=-1, keepdims=True)
    centred = values - row_mean
    variance = jnp.mean(centred * centred, axis=-1, keepdims=True)
    inverse = lax.rsqrt(variance + EPS_NORM)
    normed = centred * inverse
    return (normed * gain + shift, normed, inverse)


def norm_backward(grad_norm, normed, inverse, gain):
    scaled_grad = grad_norm * gain
    grad_mean = jnp.mean(scaled_grad, axis=-1, keepdims=True)
    along_norm = jnp.mean(scaled_grad * normed, axis=-1, keepdims=True)
    return inverse * (scaled_grad - grad_mean - normed * along_norm)


def times_trans(left_side, right_side):
    return lax.dot_general(
        left_side, right_side, (((1,), (1,)), ((), ())), preferred_element_type=jnp.float32
    )


def trans_times(left_side, right_side):
    return lax.dot_general(
        left_side, right_side, (((0,), (0,)), ((), ())), preferred_element_type=jnp.float32
    )


def split_bf16(values):
    high = values.astype(jnp.bfloat16)
    low = (values - high.astype(jnp.float32)).astype(jnp.bfloat16)
    return high, low


def dot_nt(left_side, right_side):
    return lax.dot_general(
        left_side, right_side, (((1,), (1,)), ((), ())), preferred_element_type=jnp.float32
    )


def dot_nn(left_side, right_side):
    return lax.dot_general(
        left_side, right_side, (((1,), (0,)), ((), ())), preferred_element_type=jnp.float32
    )


def dot_tn(left_side, right_side):
    return lax.dot_general(
        left_side, right_side, (((0,), (0,)), ((), ())), preferred_element_type=jnp.float32
    )


def low_left(factor, matrix):
    both = dot_nt(jnp.concatenate(split_bf16(factor), axis=0), matrix)
    return both[: factor.shape[0]] + both[factor.shape[0] :]


def low_right(basis_rows, matrix):
    both = dot_nn(jnp.concatenate(split_bf16(basis_rows), axis=0), matrix)
    return both[: basis_rows.shape[0]] + both[basis_rows.shape[0] :]


def left_factor(factor, matrix):
    rank_size = factor.shape[0]
    factor_high, factor_low = split_bf16(factor)
    matrix_high, matrix_low = split_bf16(matrix)
    both = dot_nt(jnp.concatenate([factor_high, factor_low], axis=0), matrix_high)
    return both[:rank_size] + both[rank_size:] + dot_nt(factor_high, matrix_low)


def right_factor(basis_rows, matrix):
    rank_size = basis_rows.shape[0]
    basis_high, basis_low = split_bf16(basis_rows)
    matrix_high, matrix_low = split_bf16(matrix)
    both = dot_nn(jnp.concatenate([basis_high, basis_low], axis=0), matrix_high)
    return both[:rank_size] + both[rank_size:] + dot_nn(basis_high, matrix_low)


def place_tiles(target, offset, values):
    per_chunk = target.shape[2] // LANES
    for tile in range(values.shape[1] // LANES):
        spot = offset + tile
        target[spot // per_chunk, :, pl.ds(spot % per_chunk * LANES, LANES)] = values[
            :, tile * LANES : (tile + 1) * LANES
        ]
    return offset + values.shape[1] // LANES


def add_tiles(target, offset, values):
    per_chunk = target.shape[2] // LANES
    for tile in range(values.shape[1] // LANES):
        spot = offset + tile
        target[spot // per_chunk, :, pl.ds(spot % per_chunk * LANES, LANES)] += values[
            :, tile * LANES : (tile + 1) * LANES
        ]


def take_tiles(source, offset, size):
    per_chunk = source.shape[2] // LANES
    pieces = []
    for tile in range(size // LANES):
        spot = offset + tile
        pieces.append(source[spot // per_chunk, :, pl.ds(spot % per_chunk * LANES, LANES)])
    return jnp.concatenate(pieces, axis=1) if len(pieces) > 1 else pieces[0]


def orthonormal_rows(rows):
    rank_size = rows.shape[0]
    row_number = lax.broadcasted_iota(jnp.int32, (rank_size, 1), 0)
    for position in range(rank_size):
        row = rows[position : position + 1]
        length = jnp.sqrt(jnp.sum(row * row, axis=1, keepdims=True)) + EPS_BASIS
        unit = row / length
        along = jnp.sum(rows * unit, axis=1, keepdims=True)
        later = jnp.where(row_number > position, along, 0.0)
        rows = jnp.where(row_number == position, unit, rows - later * unit)
    return rows


def dp_exchange(replicas, mine, wire, arrived, total, sems, meanwhile=None):
    send_one, recv_one, send_two, recv_two = sems
    dp_place = lax.axis_index("dp")
    tensor_place = lax.axis_index("tensor")

    def peer_of(step):
        return lax.rem(dp_place + step, replicas)

    def scatter(step, slot):
        return pltpu.make_async_remote_copy(
            src_ref=wire.at[peer_of(step)],
            dst_ref=arrived.at[slot],
            send_sem=send_one.at[step],
            recv_sem=recv_one.at[slot],
            device_id=(peer_of(step), tensor_place),
            device_id_type=MESH,
        )

    def gather(step, slot):
        return pltpu.make_async_remote_copy(
            src_ref=total.at[dp_place],
            dst_ref=total.at[slot],
            send_sem=send_two.at[step],
            recv_sem=recv_two.at[slot],
            device_id=(peer_of(step), tensor_place),
            device_id_type=MESH,
        )

    def start_scatter(step, carry):
        scatter(step, dp_place).start()
        return carry

    def add_arrived(step, carry):
        scatter(step, peer_of(step)).wait_recv()
        return carry + arrived[peer_of(step)].astype(jnp.float32)

    def start_gather(step, carry):
        gather(step, dp_place).start()
        return carry

    def finish(step, carry):
        gather(step, peer_of(step)).wait_recv()
        return carry

    wire[...] = mine[...].astype(wire.dtype)
    lax.fori_loop(1, replicas, start_scatter, 0)
    total[dp_place] = lax.fori_loop(1, replicas, add_arrived, mine[dp_place])
    lax.fori_loop(1, replicas, start_gather, 0)
    lax.fori_loop(1, replicas, finish, 0)

    def drain(step, carry):
        scatter(step, dp_place).wait_send()
        gather(step, dp_place).wait_send()
        return carry

    return lambda: lax.fori_loop(1, replicas, drain, 0)


def compress_kernel(replicas, tensor_size, has_far, *refs):
    if has_far:
        far_refs, refs, late_ref = refs[:4], refs[4:13] + refs[14:], refs[13]
        compress_body(replicas, tensor_size, far_refs, late_ref, *refs)
    else:
        compress_body(replicas, tensor_size, None, None, *refs)


def compress_body(replicas, tensor_size, far_refs, late_ref, qkv_ref, out_ref, in_ref, down_ref,
                    fq_ref, fo_ref, fi_ref, fd_ref, small_ref,
                    bq_ref, bo_ref, bi_ref, bd_ref, rq_ref, ro_ref, ri_ref, rd_ref, sum_ref,
                    qkv, out, inw, down, mine, wire, arrived, total,
                    mine_two, wire_two, arrived_two, total_two, small_slots,
                    load_sem, *sems):
    first_sems, second_sems, (send_small, recv_small) = sems[:4], sems[4:8], sems[8:10]
    dp_place = lax.axis_index("dp")
    tensor_place = lax.axis_index("tensor")
    loads = [
        pltpu.make_async_copy(source, target, load_sem.at[number])
        for number, (source, target) in enumerate(
            [(qkv_ref, qkv), (out_ref, out), (down_ref, down), (in_ref, inw)]
        )
    ]
    if far_refs:
        far_in_ref, far_down_ref, far_factor_in, far_factor_down = far_refs
        far_in, far_down, sent, got, far_send, far_recv = sems[10:]
        opposite = (dp_place, tensor_place + 2 - 4 * (tensor_place // 2))
        head = far_in_ref.shape[0] - late_ref.shape[0]
        cut = head + 2 * LANES

        def bulk(number, start, stop):
            return pltpu.make_async_remote_copy(
                src_ref=far_in_ref.at[pl.ds(start, stop - start)],
                dst_ref=late_ref.at[pl.ds(start - head, stop - start)],
                send_sem=far_send.at[number],
                recv_sem=far_recv.at[number],
                device_id=opposite,
                device_id_type=MESH,
            )

        bulks = [bulk(3, head, cut), bulk(4, cut, far_in_ref.shape[0])]
        far_loads = [
            pltpu.make_async_copy(far_in_ref, far_in, load_sem.at[4]),
            pltpu.make_async_copy(far_down_ref, far_down, load_sem.at[5]),
        ]
        for load in far_loads:
            load.start()

        def far_copy(number):
            return pltpu.make_async_remote_copy(
                src_ref=sent.at[number],
                dst_ref=got.at[number],
                send_sem=far_send.at[number],
                recv_sem=far_recv.at[number],
                device_id=opposite,
                device_id_type=MESH,
            )

    for load in loads:
        load.start()
    barrier = pltpu.get_barrier_semaphore()

    def greet_dp(step, carry):
        pl.semaphore_signal(
            barrier,
            inc=1,
            device_id=(lax.rem(dp_place + step, replicas), tensor_place),
            device_id_type=MESH,
        )
        return carry

    def greet_tensor(step, carry):
        pl.semaphore_signal(
            barrier,
            inc=1,
            device_id=(dp_place, lax.rem(tensor_place + step, tensor_size)),
            device_id_type=MESH,
        )
        return carry

    lax.fori_loop(1, replicas, greet_dp, 0)
    lax.fori_loop(1, tensor_size, greet_tensor, 0)
    mine[...] = jnp.zeros_like(mine)
    mine_two[...] = jnp.zeros_like(mine_two)
    block = 2 * LANES
    if far_refs:
        for number, (factor_ref, matrix) in enumerate(
            ((far_factor_down, far_down), (far_factor_in, far_in))
        ):
            far_loads[1 - number].wait()
            for start in range(0, matrix.shape[0], block):
                rows = slice(start, start + block)
                sent[0, number, :, rows] = low_left(factor_ref[...], matrix[rows])
        pl.semaphore_wait(barrier, replicas - 1 + tensor_size - 1)
        far_copy(0).start()
        bulks[0].start()
    offset = 0
    loads[0].wait()
    for start in range(0, qkv.shape[1], block):
        rows = slice(start, start + block)
        left = left_factor(fq_ref[0], qkv[0, rows])
        for part in range(1, 3):
            left += left_factor(fq_ref[part], qkv[part, rows])
        offset = place_tiles(mine, offset, left)
    for load, factor_ref, matrix in zip(loads[1:], (fo_ref, fd_ref, fi_ref), (out, down, inw)):
        load.wait()
        rows_of = min(block, matrix.shape[0])
        for start in range(0, matrix.shape[0], rows_of):
            left = left_factor(factor_ref[...], matrix[start : start + rows_of])
            offset = place_tiles(mine, offset, left)
    place_tiles(mine, offset, small_ref[...])
    if far_refs:
        far_copy(0).wait_recv()
        add_tiles(mine, offset - 2 * down.shape[0] // LANES, got[0, 0])
        add_tiles(mine, offset - inw.shape[0] // LANES, got[0, 1])
    else:
        pl.semaphore_wait(barrier, replicas - 1 + tensor_size - 1)
    drain_one = dp_exchange(replicas, mine, wire, arrived, total, first_sems)

    def slot_copy(step, slot):
        peer = lax.rem(tensor_place + step, tensor_size)
        return pltpu.make_async_remote_copy(
            src_ref=small_slots.at[tensor_place],
            dst_ref=small_slots.at[slot],
            send_sem=send_small.at[step],
            recv_sem=recv_small.at[slot],
            device_id=(dp_place, peer),
            device_id_type=MESH,
        )

    def start_small(step, carry):
        slot_copy(step, tensor_place).start()
        return carry

    own_small = take_tiles(total, offset, small_ref.shape[1])
    small_slots[tensor_place] = own_small
    lax.fori_loop(1, tensor_size, start_small, 0)
    offset = 0
    offset_two = 0
    offsets = []
    for basis_ref in (bq_ref, bo_ref, bd_ref, bi_ref):
        offsets.append(offset)
        offset += basis_ref.shape[1] // LANES
    for number in (2, 3, 0, 1):
        basis_ref = (bq_ref, bo_ref, bd_ref, bi_ref)[number]
        rows = take_tiles(total, offsets[number], basis_ref.shape[1]) * (1.0 / replicas)
        basis_ref[...] = orthonormal_rows(rows)
        if far_refs and number >= 2:
            sent[1, number - 2] = basis_ref[...]
        if far_refs and number == 3:
            far_copy(1).start()
    drain_one()
    for part in range(3):
        right = right_factor(bq_ref[:, :block], qkv[part, :block])
        for start in range(block, qkv.shape[1], block):
            rows = slice(start, start + block)
            right += right_factor(bq_ref[:, rows], qkv[part, rows])
        offset_two = place_tiles(mine_two, offset_two, right)
    for basis_ref, matrix in zip((bo_ref, bd_ref, bi_ref), (out, down, inw)):
        rows_of = min(block, matrix.shape[0])
        right = right_factor(basis_ref[:, :rows_of], matrix[:rows_of])
        for start in range(rows_of, matrix.shape[0], rows_of):
            rows = slice(start, start + rows_of)
            right += right_factor(basis_ref[:, rows], matrix[rows])
        offset_two = place_tiles(mine_two, offset_two, right)
    if far_refs:
        far_copy(1).wait_recv()
        sent[2, 0] = low_right(got[1, 0], far_down[...])
        sent[2, 1] = low_right(got[1, 1], far_in[...])
        far_copy(2).start()
        bulks[1].start()
        far_copy(2).wait_recv()
        add_tiles(mine_two, offset_two - (down.shape[1] + inw.shape[1]) // LANES, got[2, 0])
        add_tiles(mine_two, offset_two - inw.shape[1] // LANES, got[2, 1])
    drain_two = dp_exchange(
        replicas, mine_two, wire_two, arrived_two, total_two, second_sems
    )

    def collect(step, carry):
        peer = lax.rem(tensor_place + step, tensor_size)
        slot_copy(step, peer).wait_recv()
        slot_copy(step, tensor_place).wait_send()
        return carry + small_slots[peer]

    everyone = lax.fori_loop(1, tensor_size, collect, own_small)
    row_number = lax.broadcasted_iota(jnp.int32, everyone.shape, 0)
    sum_ref[...] = jnp.where(row_number < 6, everyone, own_small) * (1.0 / replicas)
    offset = 0
    for part in range(3):
        rq_ref[part] = take_tiles(total_two, offset, rq_ref.shape[2]) * (1.0 / replicas)
        offset += rq_ref.shape[2] // LANES
    for ref in (ro_ref, rd_ref, ri_ref):
        ref[...] = take_tiles(total_two, offset, ref.shape[1]) * (1.0 / replicas)
        offset += ref.shape[1] // LANES
    drain_two()
    if far_refs:
        for number in range(3):
            far_copy(number).wait_send()
        for copy in bulks:
            copy.wait()


def compress(matrices, factors, small, replicas, tensor_size, far):
    qkv, out, inw, down = matrices
    rank_size = small.shape[0]
    sizes = (qkv.shape[1], out.shape[0], inw.shape[0], down.shape[0])
    right_shapes = [(3, rank_size, qkv.shape[2])] + [(rank_size, one.shape[1]) for one in matrices[1:]]
    lanes_one = sum(sizes) + small.shape[1]
    lanes_two = 3 * qkv.shape[2] + sum(one.shape[1] for one in matrices[1:])
    scratch = [pltpu.VMEM(one.shape, jnp.float32) for one in matrices]
    for lanes in (lanes_one, lanes_two):
        shape = (replicas, rank_size, -(-lanes // (LANES * replicas)) * LANES)
        scratch += [
            pltpu.VMEM(shape, jnp.float32),
            pltpu.VMEM(shape, jnp.bfloat16),
            pltpu.VMEM(shape, jnp.bfloat16),
            pltpu.VMEM(shape, jnp.float32),
        ]
    scratch += [pltpu.VMEM((tensor_size,) + small.shape, jnp.float32), pltpu.SemaphoreType.DMA((6,))]
    scratch += [pltpu.SemaphoreType.DMA((replicas,))] * 8
    scratch += [pltpu.SemaphoreType.DMA((tensor_size,))] * 2
    if far:
        scratch += [pltpu.VMEM(one.shape, one.dtype) for one in far[:2]]
        scratch += [pltpu.VMEM((3, 2, rank_size, inw.shape[0]), jnp.float32)] * 2
        scratch += [pltpu.SemaphoreType.DMA((5,))] * 2
    vmem = pl.BlockSpec(memory_space=pltpu.VMEM)
    shapes = [(rank_size, size) for size in sizes] + right_shapes + [small.shape]
    shapes = [jax.ShapeDtypeStruct(shape, jnp.float32) for shape in shapes]
    late_shape = []
    if far:
        late_shape = [jax.ShapeDtypeStruct((inw.shape[0] * 5 // 8, inw.shape[1]), far[0].dtype)]
    outputs = pl.pallas_call(
        partial(compress_kernel, replicas, tensor_size, bool(far)),
        in_specs=([pl.BlockSpec(memory_space=pl.ANY)] * 2 + [vmem] * 2 if far else [])
        + [pl.BlockSpec(memory_space=pl.ANY)] * 4
        + [vmem] * 5,
        out_specs=[pl.BlockSpec(memory_space=pl.ANY)] * len(late_shape) + [vmem] * 9,
        out_shape=late_shape + shapes,
        scratch_shapes=scratch,
        compiler_params=pltpu.CompilerParams(
            collective_id=1, has_side_effects=True, vmem_limit_bytes=VMEM_GRANT
        ),
        name="compress",
    )(*far, *matrices, *factors, small)
    late, outputs = outputs[:-9], outputs[-9:]
    return outputs[:4], outputs[4:8], outputs[8], late


def outer_of(basis_rows, right):
    basis_high, basis_low = split_bf16(basis_rows)
    right_high, right_low = split_bf16(right)
    return dot_tn(
        jnp.concatenate([basis_high, basis_low, basis_high], axis=0),
        jnp.concatenate([right_high, right_high, right_low], axis=0),
    )


def update_kernel(step_rate, out_steps, near_steps, *refs):
    (mq, mo, mi, md, oq, oo, oi, od, wq, wo, wi, wd, bq, bo, bi, bd, rq, ro, ri, rd,
     gq, go, gi, gd, eq, eo, ei, ed, nq, no, ni, nd, vq, vo, vi, vd) = refs[:20] + refs[-16:]
    step = pl.program_id(0)
    whole_in, whole_down = mi[...], md[...]
    if len(refs) > 36:
        near_in, rest_in, near_down, rest_down = refs[20:24]
        whole_in += jnp.where(step < near_steps, near_in[...], rest_in[...]).astype(jnp.float32)
        whole_down += jnp.where(step < near_steps, near_down[...], rest_down[...]).astype(
            jnp.float32
        )

    def one(matrix, old, weight, rank, grad_ref, err_ref, mom_ref, new_ref, place):
        moment = 0.9 * old + rank
        grad_ref[place] = rank
        err_ref[place] = matrix - rank
        mom_ref[place] = moment
        new_ref[place] = weight.astype(jnp.float32) - step_rate * moment

    def lanes_of(ref, rows):
        return ref[:, pl.ds(pl.multiple_of(step * rows, LANES), rows)]

    rows = mq.shape[1]
    for part in range(3):
        rank = outer_of(lanes_of(bq, rows), rq[part])
        one(mq[part], oq[part], wq[part], rank, gq, eq, nq, vq, part)
    rank = outer_of(lanes_of(bi, mi.shape[0]), ri[...])
    one(whole_in, oi[...], wi[...], rank, gi, ei, ni, vi, slice(None))
    rank = outer_of(lanes_of(bd, md.shape[0]), rd[...])
    one(whole_down, od[...], wd[...], rank, gd, ed, nd, vd, slice(None))

    @pl.when(step < out_steps)
    def _():
        rank = outer_of(lanes_of(bo, mo.shape[0]), ro[...])
        one(mo[...], oo[...], wo[...], rank, go, eo, no, vo, slice(None))


def update(matrices, momenta, weights, bases, rights, late, step_rate):
    qkv, out, inw, down = matrices
    rows = LANES
    steps = inw.shape[0] // rows
    down_rows = down.shape[0] // steps
    if down_rows < LANES:
        steps = down.shape[0] // LANES
        rows, down_rows = inw.shape[0] // steps, LANES
    out_steps = out.shape[0] // LANES
    near_steps = late[0].shape[0] // rows if late else 0
    late_specs = [
        pl.BlockSpec((rows, inw.shape[1]), lambda i: (jnp.minimum(i, near_steps - 1), 0)),
        pl.BlockSpec((rows, inw.shape[1]), lambda i: (jnp.maximum(i - near_steps, 0), 0)),
        pl.BlockSpec((down_rows, down.shape[1]), lambda i: (jnp.minimum(i, near_steps - 1), 0)),
        pl.BlockSpec((down_rows, down.shape[1]), lambda i: (jnp.maximum(i - near_steps, 0), 0)),
    ]

    def whole(array):
        return pl.BlockSpec(array.shape, lambda i: (0,) * array.ndim)

    def specs():
        return [
            pl.BlockSpec((3, rows, qkv.shape[2]), lambda i: (0, i, 0)),
            pl.BlockSpec((LANES, out.shape[1]), lambda i: (jnp.minimum(i, out_steps - 1), 0)),
            pl.BlockSpec((rows, inw.shape[1]), lambda i: (i, 0)),
            pl.BlockSpec((down_rows, down.shape[1]), lambda i: (i, 0)),
        ]

    shapes = [jax.ShapeDtypeStruct(one.shape, jnp.float32) for one in matrices]
    outputs = pl.pallas_call(
        partial(update_kernel, step_rate, out_steps, near_steps),
        grid=(steps,),
        in_specs=specs() * 3
        + [whole(one) for one in bases]
        + [whole(one) for one in rights]
        + late_specs[: len(late)],
        out_specs=specs() * 4,
        out_shape=shapes * 4,
        compiler_params=pltpu.CompilerParams(vmem_limit_bytes=VMEM_GRANT),
        name="update",
    )(*matrices, *momenta, *weights, *bases, *rights, *late)
    return outputs[0:4], outputs[4:8], outputs[8:12], outputs[12:16]


def masked_scores(queries, key_heads, seg_ids):
    scores = jnp.einsum("qhd,khd->hqk", queries, key_heads, preferred_element_type=jnp.float32)
    same_doc = seg_ids[:, None] == seg_ids[None, :]
    return jnp.where(same_doc[None], scores, MASKED)


def attend_forward(inputs_of):
    queries, key_heads, value_heads, seg_ids = inputs_of
    scores = masked_scores(queries, key_heads, seg_ids)
    highest = jnp.max(scores, axis=-1, keepdims=True)
    powers = jnp.exp(scores - highest)
    denominator = jnp.sum(powers, axis=-1, keepdims=True)
    weights = (powers / denominator).astype(jnp.bfloat16)
    mixed_heads = jnp.einsum(
        "hqk,khd->qhd", weights, value_heads, preferred_element_type=jnp.float32
    )
    return (mixed_heads.astype(jnp.bfloat16), highest[..., 0] + jnp.log(denominator[..., 0]))


def attend_backward(inputs_of):
    queries, key_heads, value_heads, seg_ids, grad_mixed, log_total = inputs_of
    scores = masked_scores(queries, key_heads, seg_ids)
    probability = jnp.exp(scores - log_total[..., None])
    grad_probs = jnp.einsum(
        "qhd,khd->hqk", grad_mixed, value_heads, preferred_element_type=jnp.float32
    )
    centre = jnp.sum(probability * grad_probs, axis=-1, keepdims=True)
    grad_scores = (probability * (grad_probs - centre)).astype(jnp.bfloat16)
    grad_query = jnp.einsum(
        "hqk,khd->qhd", grad_scores, key_heads, preferred_element_type=jnp.float32
    )
    grad_key = jnp.einsum("hqk,qhd->khd", grad_scores, queries, preferred_element_type=jnp.float32)
    grad_value = jnp.einsum(
        "hqk,qhd->khd",
        probability.astype(jnp.bfloat16),
        grad_mixed,
        preferred_element_type=jnp.float32,
    )
    return (
        grad_query.astype(jnp.bfloat16),
        grad_key.astype(jnp.bfloat16),
        grad_value.astype(jnp.bfloat16),
    )


def stacked_heads(pair, lane_is_low):
    zero = jnp.zeros_like(pair)
    return jnp.concatenate(
        [jnp.where(lane_is_low, pair, zero), jnp.where(lane_is_low, zero, pair)], axis=0
    )


def own_blocks(both):
    rows = both.shape[1] // 2
    return jnp.concatenate([both[:DH, :rows], both[DH:, rows:]], axis=0).T


def window_sizes(length):
    return (length * 3 // 8, length * 5 // 8, length)


def windows_of(bounds, length):
    first = bounds[0] // LANES * LANES
    need = bounds[1] - first
    small, large, whole = window_sizes(length)
    number = jnp.where(need <= small, 0, jnp.where(need <= large, 1, 2))
    room = jnp.where(need <= small, length - small, jnp.where(need <= large, length - large, 0))
    return jnp.concatenate([jnp.minimum(first, room), number])


def attend_back_kernel(place_ref, q_ref, k_ref, v_ref, seg_key_ref, seg_query_ref, gm_own_ref,
                       gm_other_ref, mixed_ref, log_ref, old_ref, grad_ref, sums_ref, key_t, grad_key,
                       grad_value):
    del old_ref
    step = pl.program_id(0)

    @pl.when(step == 0)
    def _():
        key_t[...] = k_ref[...].T
        grad_key[...] = jnp.zeros_like(grad_key)
        grad_value[...] = jnp.zeros_like(grad_value)

    pairs = q_ref.shape[1] // LANES
    lane = lax.broadcasted_iota(jnp.int32, (1, LANES), 1)
    lane_is_low = lane < DH
    head_of_lane = (
        lax.broadcasted_iota(jnp.int32, (8, LANES), 0)
        == lax.broadcasted_iota(jnp.int32, (8, LANES), 1) // DH
    ).astype(jnp.bfloat16)
    head_scale = 1.0 / math.sqrt(DH)
    here = pl.ds(pl.multiple_of(step * LANES, LANES), LANES)
    is_own = lax.rem(step // (pl.num_programs(0) // 2) + place_ref[1], 2) == 0
    gm = jnp.where(is_own, gm_own_ref[...], gm_other_ref[...])
    seg_query = jnp.concatenate([seg_query_ref[...], seg_query_ref[...]], axis=1)
    all_lanes = [slice(pair * LANES, (pair + 1) * LANES) for pair in range(pairs)]
    length = k_ref.shape[0]

    def window(size):
        start = 0 if size == length else pl.multiple_of(place_ref[2 + step], LANES)
        keys = pl.ds(start, size)
        seg_key = seg_key_ref[keys]
        same = jnp.concatenate([seg_key, seg_key], axis=1) == seg_query
        queries, grads, centres, probs, grad_probs = [], [], [], [], []
        for lanes in all_lanes:
            queries.append(stacked_heads(q_ref[:, lanes], lane_is_low))
            grads.append(stacked_heads(gm[:, lanes], lane_is_low))
            high, low = split_bf16(
                gm[:, lanes].astype(jnp.float32) * mixed_ref[:, lanes].astype(jnp.float32)
            )
            sums = dot_nt(head_of_lane, high) + dot_nt(head_of_lane, low)
            centres.append(jnp.concatenate([sums[0:1], sums[1:2]], axis=1))
        for pair, lanes in enumerate(all_lanes):
            log_total = jnp.concatenate(
                [log_ref[2 * pair : 2 * pair + 1], log_ref[2 * pair + 1 : 2 * pair + 2]], axis=1
            )
            scores = dot_nt(k_ref[keys, lanes], queries[pair])
            probs.append(jnp.exp(jnp.where(same, scores - log_total, MASKED)))
            grad_probs.append(dot_nt(v_ref[keys, lanes], grads[pair]))
        for pair, lanes in enumerate(all_lanes):
            grad_scores = (probs[pair] * (grad_probs[pair] - centres[pair])).astype(jnp.bfloat16)
            grad_value[keys, lanes] += dot_nn(probs[pair].astype(jnp.bfloat16), grads[pair])
            grad_key[keys, lanes] += dot_nn(grad_scores, queries[pair])
            grad_query = own_blocks(dot_nn(key_t[lanes, keys], grad_scores)).astype(jnp.bfloat16)
            grad_ref[0, here, lanes] = (grad_query.astype(jnp.float32) * head_scale).astype(
                jnp.bfloat16
            )

    for number, size in enumerate(window_sizes(length)):
        pl.when(place_ref[2 + pl.num_programs(0) + step] == number)(partial(window, size))

    @pl.when(step == pl.num_programs(0) - 1)
    def _():
        grad_ref[1] = grad_key[...].astype(jnp.bfloat16)
        low_value = grad_value[...].astype(jnp.bfloat16)
        grad_ref[2] = low_value
        sums_ref[0:1] = jnp.sum(grad_ref[0].astype(jnp.float32), axis=0, keepdims=True)
        sums_ref[1:2] = jnp.sum(low_value.astype(jnp.float32), axis=0, keepdims=True)


def attend_back(projected, seg_keys, seg_queries, grad_own, grad_other, mixed, logs, slot, bounds,
                old, place, core):
    length = seg_keys.shape[1]
    slab = projected.shape[2]
    blocks = length // LANES
    half = blocks // 2
    at = jnp.concatenate(
        [
            jnp.stack([place, core]),
            windows_of(bounds[2 * slot : 2 * slot + 2, :blocks], length),
        ]
    )
    grid_spec = pltpu.PrefetchScalarGridSpec(
        num_scalar_prefetch=1,
        grid=(blocks,),
        in_specs=[
            pl.BlockSpec((None, LANES, slab), lambda i, at: (0, at[0] * blocks + i, 0)),
            pl.BlockSpec((None, length, slab), lambda i, at: (1, at[0], 0)),
            pl.BlockSpec((None, length, slab), lambda i, at: (2, at[0], 0)),
            pl.BlockSpec((None, length, LANES), lambda i, at: (at[0], 0, 0)),
            pl.BlockSpec((None, 1, LANES), lambda i, at: (at[0], 0, i)),
            pl.BlockSpec((None, LANES, slab), lambda i, at: (grad_own[1], lax.rem(i, half), 0)),
            pl.BlockSpec((None, LANES, slab), lambda i, at: (grad_other[1], lax.rem(i, half), 0)),
            pl.BlockSpec((None, LANES, slab), lambda i, at: (slot, i, 0)),
            pl.BlockSpec((None, slab // DH, LANES), lambda i, at: (slot, 0, i)),
            pl.BlockSpec(memory_space=pl.ANY),
        ],
        out_specs=[
            pl.BlockSpec((3, length, slab), lambda i, at: (0, at[0], 0)),
            pl.BlockSpec((2, slab), lambda i, at: (0, 0)),
        ],
        scratch_shapes=[
            pltpu.VMEM((slab, length), jnp.bfloat16),
            pltpu.VMEM((length, slab), jnp.float32),
            pltpu.VMEM((length, slab), jnp.float32),
        ],
    )
    return pl.pallas_call(
        attend_back_kernel,
        grid_spec=grid_spec,
        out_shape=[
            jax.ShapeDtypeStruct(projected.shape, jnp.bfloat16),
            jax.ShapeDtypeStruct((2, slab), jnp.float32),
        ],
        input_output_aliases={} if old is None else {10: 0},
        compiler_params=pltpu.CompilerParams(vmem_limit_bytes=24 << 20),
        cost_estimate=BRIEF,
        name="attend_back",
    )(at, projected, projected, projected, seg_keys, seg_queries, grad_own[0],
      grad_other[0], mixed, logs, seg_keys if old is None else old)


def row_mean(values):
    return jnp.mean(values, axis=-1, keepdims=True)


def layer_kernel(tokens, cotangent, w_qkv_ref, out_ref, in_ref, down_ref,
                 factor_in_ref, factor_down_ref, head_ref, bias_ref, vec_ref, segments,
                 projected_out, log_out, mixed_out, in_two, down_two, out_rest, bias_two,
                 result_out, low_out, active_out, branch_out, hidden_out, norm_out, near_out,
                 far_one_out, far_two_out, keys_out, rows_out, down_near, down_part_out, down_rest, in_part_out, in_head,
                 far_in_out, far_down_out, out_sum,
                 out_far, unit_ref, unit_two, sums_ref, bounds_ref,
                 rows_in, w_qkv, projected, value_t, log_total, mixed, pieces,
                 w_out, w_in, w_down, bias, tok, cot, first, normed, inverse, low, slope, active,
                 part, other, acc, wide, branch, result, down_part, near, far_mixed, outs_two,
                 seg_keys, seg_queries, load_sem, store_sem, send_sem, recv_sem):
    dp_place = lax.axis_index("dp")
    tensor_place = lax.axis_index("tensor")
    core = lax.rem(tensor_place, 2)
    seq = tensor_place // 2
    far = 1 - seq
    side = lax.rem(dp_place, 2)
    depth = lax.rem(dp_place // 2, 2)
    here = 2 * depth + side
    sibling = (dp_place, tensor_place + 1 - 2 * core)
    opposite = (dp_place, core + 2 * far)
    diagonal = (dp_place, 1 - core + 2 * far)
    beside = (dp_place + 1 - 2 * side, tensor_place)
    behind = (dp_place + 2 - 4 * depth, tensor_place)
    share, width = tok.shape
    slab = in_ref.shape[1]
    length = rows_in.shape[1]
    head_slab = w_qkv.shape[2]
    head_count = head_slab // DH
    stores = []
    sends = []
    numbers = iter(range(send_sem.shape[0]))

    def load_later(number, source, target):
        return pltpu.make_async_copy(source, target, load_sem.at[number])

    def load(number, source, target):
        copy = load_later(number, source, target)
        copy.start()
        return copy

    def store(source, target):
        copy = pltpu.make_async_copy(source, target, store_sem.at[len(stores)])
        copy.start()
        stores.append(copy)

    def send_later(source, target, device):
        number = next(numbers)
        copy = pltpu.make_async_remote_copy(
            src_ref=source,
            dst_ref=target,
            send_sem=send_sem.at[number],
            recv_sem=recv_sem.at[number],
            device_id=device,
            device_id_type=MESH,
        )
        sends.append(copy)
        return copy

    def send(source, target, device):
        copy = send_later(source, target, device)
        copy.start()
        return copy

    def rows_of(number, size):
        return pl.ds(pl.multiple_of(number * size, LANES), size)

    load_qkv = load(0, w_qkv_ref, w_qkv)
    load_far = load(1, tokens.at[rows_of(far, length)], rows_in.at[0])
    load_near = load(2, tokens.at[rows_of(seq, length)], rows_in.at[1])
    load_out = load(3, out_ref, w_out.at[0])
    load_in = load(4, in_ref, w_in.at[0])
    load_down = load(5, down_ref, w_down.at[pl.ds(0, slab)])
    load_tok = load(6, tokens.at[rows_of(tensor_place, share)], tok)
    load_cot = load(7, cotangent.at[rows_of(tensor_place, share)], cot)

    barrier = pltpu.get_barrier_semaphore()
    for device in (sibling, opposite, diagonal, beside, behind):
        pl.semaphore_signal(barrier, inc=1, device_id=device, device_id_type=MESH)
    pl.semaphore_wait(barrier, 5)
    sums_ref[...] = jnp.zeros_like(sums_ref)
    unit_ref[...] = jnp.zeros_like(unit_ref)

    def rows_part(whole, number, parts):
        size = whole.shape[0] // parts
        return whole.at[pl.ds(pl.multiple_of(number * size, size), size)]

    class Fetch:
        def __init__(self, source, whole):
            own = rows_part(whole, here, 4)
            half_one = rows_part(whole, 2 * (here + 1 - 2 * side), 8)
            half_two = rows_part(whole, 2 * (here + 2 - 4 * depth) + 1, 8)
            self.over_y = send_later(rows_part(source, here, 4), own, opposite)
            self.over_x = send_later(own, own, beside)
            self.over_z = send_later(own, own, behind)
            self.half_z = send_later(half_one, half_one, behind)
            self.half_x = send_later(half_two, half_two, beside)

        def start(self):
            self.over_y.start()

        def pass_on(self):
            self.over_y.wait_recv()
            self.over_x.start()
            self.over_z.start()

        def pass_halves(self):
            self.over_x.wait_recv()
            self.half_z.start()
            self.over_z.wait_recv()
            self.half_x.start()

        def wait(self):
            self.half_z.wait_recv()
            self.half_x.wait_recv()

    bias_send = send(bias_ref, bias_two, opposite)
    factor_sends = [
        send(factor_in_ref, far_in_out, opposite), send(factor_down_ref, far_down_out, opposite)
    ]
    fetch_out = Fetch(out_ref, out_rest.at[1])
    upper, lower = pl.ds(0, width // 2), pl.ds(width // 2, width // 2)
    fetch_in = [Fetch(in_ref.at[rows], in_two.at[rows]) for rows in (upper, lower)]
    upper, lower = pl.ds(0, slab // 2), pl.ds(slab // 2, slab // 2)
    fetch_down = [Fetch(down_ref.at[rows], down_two.at[rows]) for rows in (upper, lower)]
    fetch_out.start()
    fetch_in[0].start()
    fetch_in[1].start()
    fetch_down[0].start()

    chunk = 256
    scale = 1.0 / math.sqrt(DH)

    def project(slot):
        def rows_step(step, carry):
            rows = rows_of(step, chunk)
            values = rows_in[slot, rows]
            projected[slot, 0, rows] = (
                (dot_nn(values, w_qkv[0]) + head_ref[0:1]) * scale
            ).astype(jnp.bfloat16)
            projected[slot, 1, rows] = dot_nn(values, w_qkv[1]).astype(jnp.bfloat16)
            projected[slot, 2, rows] = (dot_nn(values, w_qkv[2]) + head_ref[1:2]).astype(
                jnp.bfloat16
            )
            return carry

        lax.fori_loop(0, length // chunk, rows_step, 0)
        value_t[...] = projected[slot, 2].T

    lane_is_low = lax.broadcasted_iota(jnp.int32, (1, LANES), 1) < DH

    def attend_rows(slot, place, tasks):
        def block(step):
            rows = rows_of(step, LANES)
            same = seg_keys[place] == seg_queries[place, :, rows]
            mask = jnp.where(same, 0.0, MASKED)
            mask = jnp.concatenate([mask, mask], axis=1)
            all_lanes = [slice(at, at + LANES) for at in range(0, head_slab, LANES)]
            all_scores = [
                dot_nt(
                    projected[slot, 1, :, lanes],
                    stacked_heads(projected[slot, 0, rows, lanes], lane_is_low),
                )
                + mask
                for lanes in all_lanes
            ]
            for pair, (lanes, scores) in enumerate(zip(all_lanes, all_scores)):
                highest = jnp.max(scores, axis=0, keepdims=True)
                powers = jnp.exp(scores - highest)
                denominator = jnp.sum(powers, axis=0, keepdims=True)
                blend = dot_nn(value_t[lanes], powers.astype(jnp.bfloat16))
                mixed[slot, rows, lanes] = own_blocks(blend * (1.0 / denominator)).astype(
                    jnp.bfloat16
                )
                total = highest + jnp.log(denominator)
                log_total[slot, 2 * pair : 2 * pair + 1, rows] = total[:, :LANES]
                log_total[slot, 2 * pair + 1 : 2 * pair + 2, rows] = total[:, LANES:]

        def two_blocks(step, carry):
            for number, task in tasks:
                pl.when(step == number)(task)
            block(2 * step)
            block(2 * step + 1)
            return carry

        lax.fori_loop(0, length // LANES // 2, two_blocks, 0)

    for number in range(segments.shape[0]):
        documents = segments[number : number + 1].astype(jnp.float32)
        seg_queries[number] = documents
        seg_keys[number] = jnp.broadcast_to(documents, (LANES, length)).T
    store(seg_keys, keys_out)
    store(seg_queries, rows_out)
    load_qkv.wait()
    load_far.wait()
    project(0)
    attend_rows(0, far, [(2, fetch_out.pass_on)])
    fetch_in[0].pass_on()
    own_rows = rows_of(core, share)
    sibling_rows = rows_of(1 - core, share)
    piece_two = send(mixed.at[0, own_rows], pieces.at[1], opposite)
    piece_three = send(mixed.at[0, sibling_rows], pieces.at[2], diagonal)
    fetch_down[1].start()
    store(projected.at[0, 0], projected_out.at[0, rows_of(far, length)])
    store(projected.at[0, 1], projected_out.at[1, rows_of(far, length)])
    store(projected.at[0, 2], projected_out.at[2, rows_of(far, length)])
    load_near.wait()
    project(1)
    out_pass = [
        send_later(out_ref, out_rest.at[0], sibling),
        send_later(out_rest.at[1], out_rest.at[2], sibling),
    ]
    load_two = load_later(8, out_rest.at[1], w_out.at[2])

    def pass_in():
        fetch_in[1].pass_on()
        fetch_in[0].pass_halves()

    def pass_out():
        fetch_out.wait()
        for copy in out_pass:
            copy.start()
        load_two.start()

    attend_rows(1, seq, [(0, fetch_out.pass_halves), (2, pass_in), (3, pass_out)])
    piece_one = send(mixed.at[1, sibling_rows], pieces.at[0], sibling)
    store(projected.at[1, 0], projected_out.at[0, rows_of(seq, length)])
    store(projected.at[1, 1], projected_out.at[1, rows_of(seq, length)])
    store(projected.at[1, 2], projected_out.at[2, rows_of(seq, length)])
    store(log_total, log_out)
    for copy in out_pass:
        copy.wait_recv()
    load_one = load(9, out_rest.at[0], w_out.at[1])
    load_three = load(10, out_rest.at[2], w_out.at[3])
    store(mixed, mixed_out)
    fetch_down[0].pass_on()
    fetch_in[1].pass_halves()
    for copy in (load_out, load_tok, load_one, load_two, load_three):
        copy.wait()
    for copy in (piece_two, piece_three, piece_one):
        copy.wait_recv()
    small = 64

    def attn_rows(step, carry):
        rows = rows_of(step, chunk)
        total = dot_nn(mixed[1, pl.ds(pl.multiple_of(core * share + step * chunk, LANES), chunk)],
                       w_out[0])
        for piece in range(3):
            total += dot_nn(pieces[piece, rows], w_out[piece + 1])
        acc[rows] = total
        return carry

    def first_rows(step, carry):
        rows = pl.ds(pl.multiple_of(step * small, small), small)
        values = tok[rows].astype(jnp.float32) + (acc[rows] + vec_ref[0:1])
        centred = values - row_mean(values)
        spread = lax.rsqrt(row_mean(centred * centred) + EPS_NORM)
        unit = centred * spread
        normed[rows] = unit
        inverse[rows] = spread
        shifted = unit * vec_ref[2:3] + vec_ref[3:4]
        first[rows] = shifted
        low[rows] = shifted.astype(jnp.bfloat16)
        return carry

    lax.fori_loop(0, share // chunk, attn_rows, 0)
    lax.fori_loop(0, share // small, first_rows, 0)
    slots = [slice(0, share), slice(share, 2 * share)]
    low_send = send(low.at[slots[0]], low.at[slots[1]], sibling)
    fetch_down[0].pass_halves()
    load_in.wait()

    def hidden_of(slot, owner):
        def units(step, carry):
            inner = rows_of(step, chunk)
            values = dot_nn(low[slots[slot]], w_in[owner, :, inner]) + bias[owner, :, inner]
            share_of = 0.5 * (1.0 + lax.erf(values * math.sqrt(0.5)))
            density = jnp.exp(-0.5 * values * values) * (1.0 / math.sqrt(2.0 * math.pi))
            active[owner, slots[slot], inner] = (values * share_of).astype(jnp.bfloat16)
            slope[owner, slots[slot], inner] = (share_of - 0.5 + values * density).astype(jnp.bfloat16)
            return carry

        lax.fori_loop(0, slab // chunk, units, 0)

    def branch_of(slot, owner, target, start, size):
        units = slice(owner * slab, (owner + 1) * slab)

        def columns(step, carry):
            at = pl.ds(pl.multiple_of(start + step * chunk, chunk), chunk)
            values = dot_nn(active[owner, slots[slot]], w_down[units, at])
            target[:, at] = values if owner == 0 else target[:, at] + values
            return carry

        lax.fori_loop(0, size // chunk, columns, 0)

    bias_send.wait_recv()
    bias[0] = bias_ref[...]
    load_bias = load(11, bias_two, bias.at[1])
    hidden_of(0, 0)
    low_send.wait_recv()
    store(low, low_out)
    fetch_down[1].pass_on()
    hidden_of(1, 0)
    for fetch in fetch_in:
        fetch.wait()
    load_in_two = load(12, in_two, w_in.at[1])
    load_down.wait()
    branch_of(1, 0, part, 0, width)
    branch_of(0, 0, acc, 0, width)
    load_bias.wait()
    load_in_two.wait()
    fetch_down[1].pass_halves()
    hidden_of(1, 1)
    hidden_of(0, 1)
    store(active.at[0], active_out)
    lane = lax.broadcasted_iota(jnp.int32, (1, LANES), 1)
    for slot, place in ((0, far), (1, seq)):
        firsts = jnp.zeros((1, LANES), jnp.float32)
        lasts = jnp.zeros((1, LANES), jnp.float32)
        for block in range(length // LANES):
            start = block * LANES
            firsts = jnp.where(lane == block, seg_keys[place, start : start + 1], firsts)
            lasts = jnp.where(
                lane == block, seg_keys[place, start + LANES - 1 : start + LANES], lasts
            )
        documents = seg_keys[place]
        bounds_ref[2 * slot : 2 * slot + 1] = jnp.sum(
            jnp.where(documents < firsts, 1.0, 0.0), axis=0, keepdims=True
        ).astype(jnp.int32)
        bounds_ref[2 * slot + 1 : 2 * slot + 2] = jnp.sum(
            jnp.where(documents <= lasts, 1.0, 0.0), axis=0, keepdims=True
        ).astype(jnp.int32)
    for fetch in fetch_down:
        fetch.wait()
    load_down_two = load(13, down_two, w_down.at[pl.ds(slab, slab)])
    load_down_two.wait()
    half = width // 2
    part_sends = []
    for number in range(2):
        branch_of(1, 1, part, number * half, half)
        columns = slice(number * half, (number + 1) * half)
        part_sends.append(send(part.at[:, columns], other.at[:, columns], sibling))
    branch_of(0, 1, acc, 0, width)
    load_cot.wait()
    for copy in part_sends:
        copy.wait_recv()

    def second_rows(step, carry):
        rows = pl.ds(pl.multiple_of(step * small, small), small)
        values = first[rows] + (acc[rows] + other[rows]) + vec_ref[1:2]
        centred = values - row_mean(values)
        spread = lax.rsqrt(row_mean(centred * centred) + EPS_NORM)
        unit = centred * spread
        result[rows] = (unit * vec_ref[4:5] + vec_ref[5:6]).astype(jnp.bfloat16)
        upper = cot[rows].astype(jnp.float32)
        scaled = upper * vec_ref[4:5]
        grad = spread * (scaled - row_mean(scaled) - unit * row_mean(scaled * unit))
        wide[rows] = grad
        grad_low = grad.astype(jnp.bfloat16)
        branch[rows] = grad_low
        sums_ref[1:2] += jnp.sum(grad_low.astype(jnp.float32), axis=0, keepdims=True)
        sums_ref[4:5] += jnp.sum(upper * unit, axis=0, keepdims=True)
        sums_ref[5:6] += jnp.sum(upper, axis=0, keepdims=True)
        return carry

    branch_sends = []
    for number in range(2):
        steps = share // small // 2
        lax.fori_loop(number * steps, (number + 1) * steps, second_rows, 0)
        rows = slice(number * steps * small, (number + 1) * steps * small)
        there = slice(share + rows.start, share + rows.stop)
        branch_sends.append(send(branch.at[rows], branch.at[there], sibling))
    store(result, result_out)
    hidden = rows_in

    def grad_hidden_of(slot, owner):
        def units(step, carry):
            inner = rows_of(step, chunk)
            outer = pl.ds(pl.multiple_of(owner * slab + step * chunk, chunk), chunk)
            grad = dot_nt(branch[slots[slot]], w_down[outer]) * (
                0.5 + slope[owner, slots[slot], inner].astype(jnp.float32)
            )
            grad_low = grad.astype(jnp.bfloat16)
            hidden[owner, slots[slot], inner] = grad_low
            unit_ref[:, outer] += jnp.sum(grad_low.astype(jnp.float32), axis=0, keepdims=True)
            return carry

        lax.fori_loop(0, slab // chunk, units, 0)

    def grad_first_of(slot, target, start, size):
        def columns(step, carry):
            at = pl.ds(pl.multiple_of(start + step * chunk, chunk), chunk)
            target[:, at] = dot_nt(hidden[0, slots[slot]], w_in[0, at]) + dot_nt(
                hidden[1, slots[slot]], w_in[1, at]
            )
            return carry

        lax.fori_loop(0, size // chunk, columns, 0)

    def far_product(left_side, right_side, target, start, stop):
        def rows_step(step, carry):
            at = rows_of(step, LANES)
            target[at] = dot_tn(left_side[:, at], right_side[...]).astype(jnp.bfloat16)
            return carry

        lax.fori_loop(start // LANES, stop // LANES, rows_step, 0)

    grad_hidden_of(0, 0)
    grad_hidden_of(0, 1)
    for copy in branch_sends:
        copy.wait_recv()
    store(branch, branch_out)
    early = down_near.shape[0]
    far_product(active.at[1], branch, down_part, 0, early)
    down_send = send(down_part.at[pl.ds(0, early)], down_near, opposite)
    far_product(active.at[1], branch, down_part, early, slab)
    store(down_part, down_part_out)
    store(down_part.at[pl.ds(early, slab - early)], down_rest)
    grad_hidden_of(1, 0)
    grad_hidden_of(1, 1)
    unit_send = send(unit_ref.at[:, pl.ds(slab, slab)], unit_two, opposite)
    store(hidden.at[0], hidden_out)
    for copy in part_sends:
        copy.wait_send()
    sends[:] = [one for one in sends if all(one is not copy for copy in part_sends)]
    first_sends = []
    for number in range(2):
        grad_first_of(1, part, number * half, half)
        columns = slice(number * half, (number + 1) * half)
        first_sends.append(send(part.at[:, columns], other.at[:, columns], sibling))
    grad_first_of(0, acc, 0, width)
    for copy in first_sends:
        copy.wait_recv()

    def back_rows(step, carry):
        rows = pl.ds(pl.multiple_of(step * small, small), small)
        grad = acc[rows] + other[rows] + wide[rows]
        unit = normed[rows]
        scaled = grad * vec_ref[2:3]
        back = inverse[rows] * (scaled - row_mean(scaled) - unit * row_mean(scaled * unit))
        acc[rows] = back
        back_low = back.astype(jnp.bfloat16)
        tok[rows] = back_low
        sums_ref[0:1] += jnp.sum(back_low.astype(jnp.float32), axis=0, keepdims=True)
        sums_ref[2:3] += jnp.sum(grad * unit, axis=0, keepdims=True)
        sums_ref[3:4] += jnp.sum(grad, axis=0, keepdims=True)
        return carry

    lax.fori_loop(0, share // small, back_rows, 0)
    store(acc, norm_out)
    attn = tok[...]
    near[1] = dot_nt(attn, w_out[1]).astype(jnp.bfloat16)
    near_send = send(near.at[1], near.at[2], sibling)
    out_one = slice(0, head_slab)
    out_three = slice(head_slab, 2 * head_slab)
    first[out_one] = dot_tn(pieces[0], attn)
    first[out_three] = dot_tn(pieces[2], attn)
    outs_send = send(first.at[pl.ds(0, 2 * head_slab)], outs_two, sibling)
    far_mixed[0] = dot_nt(attn, w_out[2]).astype(jnp.bfloat16)
    far_mixed[1] = dot_nt(attn, w_out[3]).astype(jnp.bfloat16)
    store(far_mixed.at[0], far_one_out.at[0])
    store(far_mixed.at[1], far_two_out.at[0])
    near[0] = dot_nt(attn, w_out[0]).astype(jnp.bfloat16)
    store(near.at[0], near_out.at[0])
    far_product(low, hidden.at[1], active.at[1], 0, width)
    store(active.at[1], in_part_out)
    store(active.at[1, pl.ds(0, in_head.shape[0])], in_head)
    near_send.wait_recv()
    store(near.at[2], near_out.at[1])
    outs_send.wait_recv()
    out_sum[...] = dot_tn(mixed[1, own_rows], attn) + outs_two[out_one]
    out_far[...] = (dot_tn(pieces[1], attn) + outs_two[out_three]).astype(jnp.bfloat16)
    unit_send.wait_recv()
    down_send.wait_recv()
    for copy in factor_sends:
        copy.wait_recv()
    for copy in sends:
        copy.wait_send()
    for copy in stores:
        copy.wait()


def layer_call(tokens, cotangent, planes, w_out, w_in, w_down, factor_in, factor_down, head_bias,
               unit_bias, vectors, segments):
    token_count, width = tokens.shape
    seq_count, length = segments.shape
    share = token_count // (2 * seq_count)
    head_slab = planes.shape[2]
    slab = w_in.shape[1]
    early = slab * 3 // 8
    low_type, full_type = jnp.bfloat16, jnp.float32
    vmem = pl.BlockSpec(memory_space=pltpu.VMEM)
    anywhere = pl.BlockSpec(memory_space=pl.ANY)
    shapes = [
        jax.ShapeDtypeStruct((3, token_count, head_slab), low_type),
        jax.ShapeDtypeStruct((2, head_slab // DH, length), full_type),
        jax.ShapeDtypeStruct((2, length, head_slab), low_type),
        jax.ShapeDtypeStruct(w_in.shape, low_type),
        jax.ShapeDtypeStruct(w_down.shape, low_type),
        jax.ShapeDtypeStruct((3,) + w_out.shape, low_type),
        jax.ShapeDtypeStruct((1, slab), full_type),
        jax.ShapeDtypeStruct((share, width), low_type),
        jax.ShapeDtypeStruct((2 * share, width), low_type),
        jax.ShapeDtypeStruct((2 * share, slab), low_type),
        jax.ShapeDtypeStruct((2 * share, width), low_type),
        jax.ShapeDtypeStruct((2 * share, slab), low_type),
        jax.ShapeDtypeStruct((share, width), full_type),
        jax.ShapeDtypeStruct((2, share, head_slab), low_type),
        jax.ShapeDtypeStruct((1, share, head_slab), low_type),
        jax.ShapeDtypeStruct((1, share, head_slab), low_type),
        jax.ShapeDtypeStruct((seq_count, length, LANES), full_type),
        jax.ShapeDtypeStruct((seq_count, 1, length), full_type),
        jax.ShapeDtypeStruct((early, width), low_type),
        jax.ShapeDtypeStruct((slab, width), low_type),
        jax.ShapeDtypeStruct((slab - early, width), low_type),
        jax.ShapeDtypeStruct(w_in.shape, low_type),
        jax.ShapeDtypeStruct((early, slab), low_type),
        jax.ShapeDtypeStruct(factor_in.shape, full_type),
        jax.ShapeDtypeStruct(factor_down.shape, full_type),
        jax.ShapeDtypeStruct((head_slab, width), full_type),
        jax.ShapeDtypeStruct((head_slab, width), low_type),
        jax.ShapeDtypeStruct((1, 2 * slab), full_type),
        jax.ShapeDtypeStruct((1, slab), full_type),
        jax.ShapeDtypeStruct((6, width), full_type),
        jax.ShapeDtypeStruct((4, LANES), jnp.int32),
    ]
    return pl.pallas_call(
        layer_kernel,
        in_specs=[anywhere] * 8 + [vmem] * 4,
        out_specs=[anywhere] * 25 + [vmem] * 6,
        out_shape=shapes,
        scratch_shapes=[
            pltpu.VMEM((2, length, width), low_type),
            pltpu.VMEM(planes.shape, low_type),
            pltpu.VMEM((2, 3, length, head_slab), low_type),
            pltpu.VMEM((head_slab, length), low_type),
            pltpu.VMEM((2, head_slab // DH, length), full_type),
            pltpu.VMEM((2, length, head_slab), low_type),
            pltpu.VMEM((3, share, head_slab), low_type),
            pltpu.VMEM((4,) + w_out.shape, low_type),
            pltpu.VMEM((2,) + w_in.shape, low_type),
            pltpu.VMEM((2 * slab, width), low_type),
            pltpu.VMEM((2, 1, slab), full_type),
            pltpu.VMEM((share, width), low_type),
            pltpu.VMEM((share, width), low_type),
            pltpu.VMEM((share, width), full_type),
            pltpu.VMEM((share, width), full_type),
            pltpu.VMEM((share, 1), full_type),
            pltpu.VMEM((2 * share, width), low_type),
            pltpu.VMEM((2, 2 * share, slab), low_type),
            pltpu.VMEM((2, 2 * share, slab), low_type),
            pltpu.VMEM((share, width), full_type),
            pltpu.VMEM((share, width), full_type),
            pltpu.VMEM((share, width), full_type),
            pltpu.VMEM((share, width), full_type),
            pltpu.VMEM((2 * share, width), low_type),
            pltpu.VMEM((share, width), low_type),
            pltpu.VMEM((slab, width), low_type),
            pltpu.VMEM((3, share, head_slab), low_type),
            pltpu.VMEM((2, share, head_slab), low_type),
            pltpu.VMEM((2 * head_slab, width), full_type),
            pltpu.VMEM((seq_count, length, LANES), full_type),
            pltpu.VMEM((seq_count, 1, length), full_type),
            pltpu.SemaphoreType.DMA((14,)),
            pltpu.SemaphoreType.DMA((28,)),
            pltpu.SemaphoreType.DMA((46,)),
            pltpu.SemaphoreType.DMA((46,)),
        ],
        compiler_params=pltpu.CompilerParams(
            collective_id=3, has_side_effects=True, vmem_limit_bytes=VMEM_GRANT
        ),
        name="layer",
    )(tokens, cotangent, planes, w_out, w_in, w_down, factor_in, factor_down, head_bias, unit_bias,
      vectors, segments)


def layer_general(tokens, segments, w_qkv, head_bias, w_out, w_in, unit_bias, w_down, vectors,
                  cotangent, basis_in, basis_down):
    token_count, model_width = tokens.shape
    seq_count, length = segments.shape
    head_slab = w_qkv.shape[2]
    head_count = head_slab // DH
    tensor_size = lax.axis_size("tensor")
    share_rows = token_count // tensor_size
    tensor_place = lax.axis_index("tensor")
    row_start = tensor_place * share_rows
    head_scale = 1.0 / math.sqrt(DH)

    def own_rows(values):
        return lax.dynamic_slice_in_dim(values, row_start, share_rows, 0)

    flat_qkv = w_qkv.reshape(model_width, 3 * head_slab)
    projected = jnp.dot(tokens, flat_qkv, preferred_element_type=jnp.float32).reshape(
        token_count, 3, head_slab
    )
    head_shape = (seq_count, length, head_count, DH)
    queries = (
        ((projected[:, 0] + head_bias[0]) * head_scale).astype(jnp.bfloat16).reshape(head_shape)
    )
    key_heads = projected[:, 1].astype(jnp.bfloat16).reshape(head_shape)
    value_heads = (projected[:, 2] + head_bias[1]).astype(jnp.bfloat16).reshape(head_shape)
    mixed_heads, log_total = lax.map(attend_forward, (queries, key_heads, value_heads, segments))
    mixed_flat = mixed_heads.reshape(token_count, head_slab)
    attn_out = (
        lax.psum(jnp.dot(mixed_flat, w_out, preferred_element_type=jnp.float32), "tensor")
        + vectors[0]
    )
    first_norm, first_normed, first_inverse = norm_forward(
        tokens.astype(jnp.float32) + attn_out, vectors[2], vectors[3]
    )
    first_low = first_norm.astype(jnp.bfloat16)
    hidden = jnp.dot(first_low, w_in, preferred_element_type=jnp.float32) + unit_bias
    active, gelu_back = jax.vjp(partial(jax.nn.gelu, approximate=False), hidden)
    active_low = active.astype(jnp.bfloat16)
    grad_out_share = own_rows(cotangent).astype(jnp.float32)
    summed_input = (
        first_norm
        + lax.psum(jnp.dot(active_low, w_down, preferred_element_type=jnp.float32), "tensor")
        + vectors[1]
    )
    second_norm, second_normed, second_inverse = norm_forward(summed_input, vectors[4], vectors[5])
    layer_out = own_rows(second_norm).astype(jnp.bfloat16)
    grad_sum = norm_backward(
        cotangent.astype(jnp.float32), second_normed, second_inverse, vectors[4]
    )
    grad_branch = grad_sum.astype(jnp.bfloat16)
    second_share = own_rows(second_normed)
    grad_w_down = trans_times(active_low, grad_branch)
    grad_active = times_trans(grad_branch, w_down)
    grad_hidden = gelu_back(grad_active)[0].astype(jnp.bfloat16)
    grad_w_in = trans_times(first_low, grad_hidden)
    grad_units = jnp.sum(grad_hidden.astype(jnp.float32), axis=0)
    grad_first = lax.psum(times_trans(grad_hidden, w_in), "tensor") + grad_sum
    grad_h1 = norm_backward(grad_first, first_normed, first_inverse, vectors[2])
    grad_attn = grad_h1.astype(jnp.bfloat16)
    grad_first_share = own_rows(grad_first)
    first_normed_share = own_rows(first_normed)
    grad_h1_share = own_rows(grad_h1)
    grad_w_out = trans_times(mixed_flat, grad_attn)
    grad_mixed = times_trans(grad_attn, w_out).astype(jnp.bfloat16).reshape(head_shape)
    grad_query, grad_key, grad_value = lax.map(
        attend_backward, (queries, key_heads, value_heads, segments, grad_mixed, log_total)
    )
    grad_query = (
        grad_query.reshape(token_count, head_slab).astype(jnp.float32) * head_scale
    ).astype(jnp.bfloat16)
    grad_key = grad_key.reshape(token_count, head_slab)
    grad_value = grad_value.reshape(token_count, head_slab)
    grad_projected = jnp.stack([grad_query, grad_key, grad_value], axis=1).reshape(
        token_count, 3 * head_slab
    )
    grad_w_qkv = trans_times(tokens, grad_projected)
    grad_heads = jnp.stack(
        [
            jnp.sum(grad_query.astype(jnp.float32), axis=0),
            jnp.sum(grad_value.astype(jnp.float32), axis=0),
        ]
    )
    grad_tokens = (
        lax.psum_scatter(
            times_trans(grad_projected, flat_qkv).astype(jnp.bfloat16),
            "tensor",
            scatter_dimension=0,
            tiled=True,
        ).astype(jnp.float32)
        + grad_h1_share
    )
    local_vectors = jnp.stack(
        [
            jnp.sum(own_rows(grad_attn).astype(jnp.float32), axis=0),
            jnp.sum(own_rows(grad_branch).astype(jnp.float32), axis=0),
            jnp.sum(grad_first_share * first_normed_share, axis=0),
            jnp.sum(grad_first_share, axis=0),
            jnp.sum(grad_out_share * second_share, axis=0),
            jnp.sum(grad_out_share, axis=0),
        ]
    )
    return (
        layer_out,
        lambda after: grad_tokens,
        (
            grad_w_qkv.reshape(model_width, 3, head_slab).transpose(1, 0, 2),
            grad_w_out,
            grad_w_in,
            grad_w_down,
        ),
        local_vectors,
        grad_heads,
        grad_units,
        (),
        (),
    )


def layer_split(tokens, segments, w_qkv, head_bias, w_out, w_in, unit_bias, w_down, vectors,
                cotangent, basis_in, basis_down):
    token_count, model_width = tokens.shape
    unit_slab = w_in.shape[1]
    tensor_size = lax.axis_size("tensor")
    share = token_count // tensor_size
    tensor_place = lax.axis_index("tensor")
    core = lax.rem(tensor_place, 2)
    seq = tensor_place // 2

    def to(values, step):
        return lax.ppermute(
            values, "tensor", [(place, place ^ step) for place in range(tensor_size)]
        )

    def rows_at(values, number, size):
        return lax.dynamic_slice_in_dim(values, number * size, size, 0)

    planes = w_qkv.transpose(1, 0, 2)
    (projected, logs, mixed, _, _, _, _, layer_out, low, active, grad_branch, grad_hidden, grad_h1,
     grad_near, far_one, far_two, seg_keys, seg_queries, down_near, down_part, down_rest, in_part, in_head, far_in, far_down,
     out_sum, out_far, units, unit_two, sums, bounds) = layer_call(
        tokens, cotangent, planes, w_out, w_in, w_down, basis_in, basis_down, head_bias,
        unit_bias[None], vectors, segments,
    )
    far_own = to(far_one, 2)
    far_other = to(far_two, 3)
    down_rest = to(down_rest, 2)
    in_near = to(in_head, 2)
    out_back = to(out_far, 2)

    grad_projected, heads_near = attend_back(
        projected, seg_keys, seg_queries, (grad_near, 0), (grad_near, 1), mixed, logs, 1,
        bounds, None, seq, core,
    )
    grad_projected, heads_far = attend_back(
        projected, seg_keys, seg_queries, (far_own, 0), (far_other, 0), mixed, logs, 0,
        bounds, grad_projected, 1 - seq, core,
    )
    token_part = jnp.einsum(
        "gtn,gdn->td", grad_projected, planes, preferred_element_type=jnp.float32
    ).astype(jnp.bfloat16)
    other_one = to(
        jnp.stack([rows_at(token_part, 2 * at + 1 - core, share) for at in (seq, 1 - seq)]), 1
    )
    across_part = rows_at(token_part, 2 * (1 - seq) + core, share).astype(jnp.float32)
    across_part = (across_part + other_one[1].astype(jnp.float32)).astype(jnp.bfloat16)
    own_part = rows_at(token_part, 2 * seq + core, share)

    def finish_tokens(after):
        from_two = to(lax.optimization_barrier((across_part, after))[0], 2)
        return (
            own_part.astype(jnp.float32)
            + other_one[0].astype(jnp.float32)
            + from_two.astype(jnp.float32)
            + grad_h1
        )

    grad_w_qkv = jnp.einsum(
        "td,gtn->gdn", tokens, grad_projected, preferred_element_type=jnp.float32
    )
    grad_w_down = trans_times(active, grad_branch)
    grad_w_in = trans_times(low, grad_hidden)
    out_sum, in_near = lax.optimization_barrier((out_sum, in_near))
    grad_w_out = out_sum + out_back.astype(jnp.float32)
    return (
        layer_out,
        finish_tokens,
        (grad_w_qkv, grad_w_out, grad_w_in, grad_w_down),
        sums,
        heads_near + heads_far,
        units[0, :unit_slab] + unit_two[0],
        (in_part, down_part, far_in, far_down),
        (in_near, down_near, down_rest),
    )


def local(
    tokens,
    segments,
    w_qkv,
    head_bias,
    w_out,
    w_in,
    unit_bias,
    w_down,
    vectors,
    cotangent,
    err_qkv,
    err_out,
    err_in,
    err_down,
    basis_qkv,
    basis_out,
    basis_in,
    basis_down,
    mom_qkv,
    mom_head_bias,
    mom_out,
    mom_in,
    mom_unit_bias,
    mom_down,
    mom_vectors,
):
    token_count, model_width = tokens.shape
    head_slab = w_qkv.shape[2]
    unit_slab = w_in.shape[1]
    tensor_size = lax.axis_size("tensor")
    replicas = lax.axis_size("dp")
    one_sequence_per_chip = 2 * segments.shape[0] == tensor_size and replicas % 4 == 0
    layer = layer_split if one_sequence_per_chip else layer_general
    layer_out, finish_tokens, grads, local_vectors, grad_heads, grad_units, far, late = layer(
        tokens, segments, w_qkv, head_bias, w_out, w_in, unit_bias, w_down, vectors, cotangent,
        basis_in, basis_down,
    )
    grad_w_qkv, grad_w_out, grad_w_in, grad_w_down = grads
    small = jnp.concatenate(
        [
            local_vectors,
            jnp.pad(grad_units, (0, model_width - unit_slab))[None],
            jnp.pad(grad_heads.reshape(1, 2 * head_slab), ((0, 0), (0, model_width - 2 * head_slab))),
        ],
        axis=0,
    )
    planes = (1, 0, 2)
    combined_qkv = grad_w_qkv + err_qkv[0].transpose(planes)
    combined_out = grad_w_out + err_out[0]
    combined_in = grad_w_in + err_in[0]
    combined_down = grad_w_down + err_down[0]
    matrices = (combined_qkv, combined_out, combined_in, combined_down)
    bases, rights, small_sum, late_rest = compress(
        matrices,
        (basis_qkv.transpose(planes), basis_out, basis_in, basis_down),
        small,
        replicas,
        tensor_size,
        far,
    )
    grad_tokens = finish_tokens(small_sum)
    if late:
        late = (late[0], late_rest[0]) + late[1:]
    step_rate = 0.3 * math.sqrt(replicas / token_count)
    grads, errors, moments, news = update(
        matrices,
        (mom_qkv.transpose(planes), mom_out, mom_in, mom_down),
        (w_qkv.transpose(planes), w_out, w_in, w_down),
        bases,
        rights,
        late,
        step_rate,
    )
    reduced_qkv, rank_out, rank_in, rank_down = (grads[0].transpose(planes),) + tuple(grads[1:])
    new_err_qkv, new_err_out, new_err_in, new_err_down = (
        errors[0].transpose(planes)[None],
        errors[1][None],
        errors[2][None],
        errors[3][None],
    )
    new_mom_qkv, new_mom_out, new_mom_in, new_mom_down = (moments[0].transpose(planes),) + tuple(
        moments[1:]
    )
    new_w_qkv, new_w_out, new_w_in, new_w_down = (news[0].transpose(planes),) + tuple(news[1:])
    right_qkv, right_out, right_in, right_down = rights
    new_basis_qkv = right_qkv.transpose(planes)
    grad_vectors = small_sum[:6]
    grad_unit_bias = small_sum[6, :unit_slab]
    grad_head_bias = small_sum[7, : 2 * head_slab].reshape(2, head_slab)
    new_mom_head_bias = 0.9 * mom_head_bias + grad_head_bias
    new_mom_unit_bias = 0.9 * mom_unit_bias + grad_unit_bias
    new_mom_vectors = 0.9 * mom_vectors + grad_vectors
    new_head_bias = head_bias - step_rate * new_mom_head_bias
    new_unit_bias = unit_bias - step_rate * new_mom_unit_bias
    new_vectors = vectors - step_rate * new_mom_vectors
    return (
        layer_out,
        grad_tokens,
        reduced_qkv,
        grad_head_bias,
        rank_out,
        rank_in,
        grad_unit_bias,
        rank_down,
        grad_vectors,
        new_err_qkv,
        new_err_out,
        new_err_in,
        new_err_down,
        new_basis_qkv,
        right_out,
        right_in,
        right_down,
        new_mom_qkv,
        new_mom_head_bias,
        new_mom_out,
        new_mom_in,
        new_mom_unit_bias,
        new_mom_down,
        new_mom_vectors,
        new_w_qkv,
        new_head_bias,
        new_w_out,
        new_w_in,
        new_unit_bias,
        new_w_down,
        new_vectors,
    )


def solution(mesh):
    in_specs = (
        P("dp", None),
        P("dp", None),
        P(None, None, "tensor"),
        P(None, "tensor"),
        P("tensor", None),
        P(None, "tensor"),
        P("tensor"),
        P("tensor", None),
        P(),
        P("dp", None),
        P("dp", None, None, "tensor"),
        P("dp", "tensor", None),
        P("dp", None, "tensor"),
        P("dp", "tensor", None),
        P(None, None, "tensor"),
        P("tensor", None),
        P(None, "tensor"),
        P("tensor", None),
        P(None, None, "tensor"),
        P(None, "tensor"),
        P("tensor", None),
        P(None, "tensor"),
        P("tensor"),
        P("tensor", None),
        P(),
    )
    out_specs = (
        P(("dp", "tensor"), None),
        P(("dp", "tensor"), None),
        P(None, None, "tensor"),
        P(None, "tensor"),
        P("tensor", None),
        P(None, "tensor"),
        P("tensor"),
        P("tensor", None),
        P(),
        P("dp", None, None, "tensor"),
        P("dp", "tensor", None),
        P("dp", None, "tensor"),
        P("dp", "tensor", None),
        P(None, None, "tensor"),
        P("tensor", None),
        P(None, "tensor"),
        P("tensor", None),
        P(None, None, "tensor"),
        P(None, "tensor"),
        P("tensor", None),
        P(None, "tensor"),
        P("tensor"),
        P("tensor", None),
        P(),
        P(None, None, "tensor"),
        P(None, "tensor"),
        P("tensor", None),
        P(None, "tensor"),
        P("tensor"),
        P("tensor", None),
        P(),
    )
    return jax.shard_map(local, mesh=mesh, in_specs=in_specs, out_specs=out_specs, check_vma=False)
```

```python
from functools import partial
import math

import jax
import jax.numpy as jnp
from jax import lax
from jax.experimental import pallas as pl
from jax.experimental.pallas import tpu as pltpu
from jax.sharding import PartitionSpec as P

DH = 64
LANES = 128
MESH = pl.DeviceIdType.MESH
VMEM_GRANT = 60 << 20
BRIEF = pl.CostEstimate(flops=1, bytes_accessed=1, transcendentals=1)


PRECISE = lax.Precision.HIGHEST
EPS_NORM = 1e-05
EPS_BASIS = 1e-08
MASKED = -1000000000.0


def norm_forward(values, gain, shift):
    row_mean = jnp.mean(values, axis=-1, keepdims=True)
    centred = values - row_mean
    variance = jnp.mean(centred * centred, axis=-1, keepdims=True)
    inverse = lax.rsqrt(variance + EPS_NORM)
    normed = centred * inverse
    return (normed * gain + shift, normed, inverse)


def norm_backward(grad_norm, normed, inverse, gain):
    scaled_grad = grad_norm * gain
    grad_mean = jnp.mean(scaled_grad, axis=-1, keepdims=True)
    along_norm = jnp.mean(scaled_grad * normed, axis=-1, keepdims=True)
    return inverse * (scaled_grad - grad_mean - normed * along_norm)


def times_trans(left_side, right_side):
    return lax.dot_general(
        left_side, right_side, (((1,), (1,)), ((), ())), preferred_element_type=jnp.float32
    )


def trans_times(left_side, right_side):
    return lax.dot_general(
        left_side, right_side, (((0,), (0,)), ((), ())), preferred_element_type=jnp.float32
    )


def split_bf16(values):
    high = values.astype(jnp.bfloat16)
    low = (values - high.astype(jnp.float32)).astype(jnp.bfloat16)
    return high, low


def dot_nt(left_side, right_side):
    return lax.dot_general(
        left_side, right_side, (((1,), (1,)), ((), ())), preferred_element_type=jnp.float32
    )


def dot_nn(left_side, right_side):
    return lax.dot_general(
        left_side, right_side, (((1,), (0,)), ((), ())), preferred_element_type=jnp.float32
    )


def dot_tn(left_side, right_side):
    return lax.dot_general(
        left_side, right_side, (((0,), (0,)), ((), ())), preferred_element_type=jnp.float32
    )


def low_left(factor, matrix):
    both = dot_nt(jnp.concatenate(split_bf16(factor), axis=0), matrix)
    return both[: factor.shape[0]] + both[factor.shape[0] :]


def low_right(basis_rows, matrix):
    both = dot_nn(jnp.concatenate(split_bf16(basis_rows), axis=0), matrix)
    return both[: basis_rows.shape[0]] + both[basis_rows.shape[0] :]


def left_factor(factor, matrix):
    rank_size = factor.shape[0]
    factor_high, factor_low = split_bf16(factor)
    matrix_high, matrix_low = split_bf16(matrix)
    both = dot_nt(jnp.concatenate([factor_high, factor_low], axis=0), matrix_high)
    return both[:rank_size] + both[rank_size:] + dot_nt(factor_high, matrix_low)


def right_factor(basis_rows, matrix):
    rank_size = basis_rows.shape[0]
    basis_high, basis_low = split_bf16(basis_rows)
    matrix_high, matrix_low = split_bf16(matrix)
    both = dot_nn(jnp.concatenate([basis_high, basis_low], axis=0), matrix_high)
    return both[:rank_size] + both[rank_size:] + dot_nn(basis_high, matrix_low)


def place_tiles(target, offset, values):
    per_chunk = target.shape[2] // LANES
    for tile in range(values.shape[1] // LANES):
        spot = offset + tile
        target[spot // per_chunk, :, pl.ds(spot % per_chunk * LANES, LANES)] = values[
            :, tile * LANES : (tile + 1) * LANES
        ]
    return offset + values.shape[1] // LANES


def add_tiles(target, offset, values):
    per_chunk = target.shape[2] // LANES
    for tile in range(values.shape[1] // LANES):
        spot = offset + tile
        target[spot // per_chunk, :, pl.ds(spot % per_chunk * LANES, LANES)] += values[
            :, tile * LANES : (tile + 1) * LANES
        ]


def take_tiles(source, offset, size):
    per_chunk = source.shape[2] // LANES
    pieces = []
    for tile in range(size // LANES):
        spot = offset + tile
        piece = source[spot // per_chunk, :, pl.ds(spot % per_chunk * LANES, LANES)]
        pieces.append(piece.astype(jnp.float32))
    return jnp.concatenate(pieces, axis=1) if len(pieces) > 1 else pieces[0]


def orthonormal_rows(rows):
    rank_size = rows.shape[0]
    row_number = lax.broadcasted_iota(jnp.int32, (rank_size, 1), 0)
    for position in range(rank_size):
        row = rows[position : position + 1]
        length = jnp.sqrt(jnp.sum(row * row, axis=1, keepdims=True)) + EPS_BASIS
        unit = row / length
        along = jnp.sum(rows * unit, axis=1, keepdims=True)
        later = jnp.where(row_number > position, along, 0.0)
        rows = jnp.where(row_number == position, unit, rows - later * unit)
    return rows


def dp_exchange(replicas, mine, wire, arrived, total, sems, meanwhile=None):
    send_one, recv_one, send_two, recv_two = sems
    dp_place = lax.axis_index("dp")
    tensor_place = lax.axis_index("tensor")

    def peer_of(step):
        return lax.rem(dp_place + step, replicas)

    def scatter(step, slot):
        return pltpu.make_async_remote_copy(
            src_ref=wire.at[peer_of(step)],
            dst_ref=arrived.at[slot],
            send_sem=send_one.at[step],
            recv_sem=recv_one.at[slot],
            device_id=(peer_of(step), tensor_place),
            device_id_type=MESH,
        )

    def gather(step, slot):
        return pltpu.make_async_remote_copy(
            src_ref=total.at[dp_place],
            dst_ref=total.at[slot],
            send_sem=send_two.at[step],
            recv_sem=recv_two.at[slot],
            device_id=(peer_of(step), tensor_place),
            device_id_type=MESH,
        )

    def start_scatter(step, carry):
        scatter(step, dp_place).start()
        return carry

    def add_arrived(step, carry):
        scatter(step, peer_of(step)).wait_recv()
        return carry + arrived[peer_of(step)].astype(jnp.float32)

    def start_gather(step, carry):
        gather(step, dp_place).start()
        return carry

    def finish(step, carry):
        gather(step, peer_of(step)).wait_recv()
        return carry

    wire[...] = mine[...].astype(wire.dtype)
    lax.fori_loop(1, replicas, start_scatter, 0)
    total[dp_place] = lax.fori_loop(1, replicas, add_arrived, mine[dp_place]).astype(total.dtype)
    lax.fori_loop(1, replicas, start_gather, 0)
    lax.fori_loop(1, replicas, finish, 0)

    def drain(step, carry):
        scatter(step, dp_place).wait_send()
        gather(step, dp_place).wait_send()
        return carry

    return lambda: lax.fori_loop(1, replicas, drain, 0)


def product_kernel(left_ref, right_ref, err_ref, factor_ref, matrix_ref, factor_out):
    if len(matrix_ref.shape) == 2:
        matrix = dot_tn(left_ref[...], right_ref[...]) + err_ref[...]
        matrix_ref[...] = matrix
        factor_out[...] = left_factor(factor_ref[...], matrix)
    else:
        total = None
        for part in range(matrix_ref.shape[0]):
            matrix = dot_tn(left_ref[...], right_ref[part]) + err_ref[part]
            matrix_ref[part] = matrix
            piece = left_factor(factor_ref[part], matrix)
            total = piece if total is None else total + piece
        factor_out[...] = total


def product(left_side, right_side, err, factor):
    block = 2 * LANES
    length, rows = left_side.shape
    lead = err.shape[:-2]
    zeros = (0,) * len(lead)

    def whole(array):
        return pl.BlockSpec(array.shape, lambda i: (0,) * array.ndim)

    by_rows = pl.BlockSpec(lead + (block, err.shape[-1]), lambda i: zeros + (i, 0))
    return pl.pallas_call(
        product_kernel,
        grid=(rows // block,),
        in_specs=[
            pl.BlockSpec((length, block), lambda i: (0, i)),
            whole(right_side),
            by_rows,
            whole(factor),
        ],
        out_specs=[by_rows, pl.BlockSpec((factor.shape[-2], block), lambda i: (0, i))],
        out_shape=[
            jax.ShapeDtypeStruct(err.shape, jnp.float32),
            jax.ShapeDtypeStruct((factor.shape[-2], rows), jnp.float32),
        ],
        compiler_params=pltpu.CompilerParams(vmem_limit_bytes=24 << 20),
        cost_estimate=pl.CostEstimate(flops=10**10, bytes_accessed=10**8, transcendentals=1),
        name="product",
    )(left_side, right_side, err, factor)


def compress_kernel(replicas, tensor_size, has_far, *refs):
    if has_far:
        far_refs, refs, late_ref = refs[:4], refs[4:13] + refs[14:], refs[13]
        compress_body(replicas, tensor_size, far_refs, late_ref, *refs)
    else:
        compress_body(replicas, tensor_size, None, None, *refs)


def compress_body(replicas, tensor_size, far_refs, late_ref, qkv_ref, out_ref, in_ref, down_ref,
                    lq_ref, fo_ref, li_ref, ld_ref, small_ref,
                    bq_ref, bo_ref, bi_ref, bd_ref, rq_ref, ro_ref, ri_ref, rd_ref, sum_ref,
                    qkv, out, inw, down, mine, wire, arrived, total,
                    mine_two, wire_two, arrived_two, total_two, small_slots,
                    load_sem, *sems):
    first_sems, second_sems, (send_small, recv_small) = sems[:4], sems[4:8], sems[8:10]
    dp_place = lax.axis_index("dp")
    tensor_place = lax.axis_index("tensor")
    loads = [
        pltpu.make_async_copy(source, target, load_sem.at[number])
        for number, (source, target) in enumerate(
            [(out_ref, out), (qkv_ref, qkv), (down_ref, down), (in_ref, inw)]
        )
    ]
    if far_refs:
        far_in_ref, far_down_ref, far_factor_in, far_factor_down = far_refs
        far_in, far_down, sent, got, far_send, far_recv = sems[10:]
        opposite = (dp_place, tensor_place + 2 - 4 * (tensor_place // 2))
        head = far_in_ref.shape[0] - late_ref.shape[0]
        cut = head + 2 * LANES

        def bulk(number, start, stop):
            return pltpu.make_async_remote_copy(
                src_ref=far_in_ref.at[pl.ds(start, stop - start)],
                dst_ref=late_ref.at[pl.ds(start - head, stop - start)],
                send_sem=far_send.at[number],
                recv_sem=far_recv.at[number],
                device_id=opposite,
                device_id_type=MESH,
            )

        bulks = [bulk(3, head, cut), bulk(4, cut, far_in_ref.shape[0])]
        far_loads = [
            pltpu.make_async_copy(far_in_ref, far_in, load_sem.at[4]),
            pltpu.make_async_copy(far_down_ref, far_down, load_sem.at[5]),
        ]
        for load in far_loads:
            load.start()

        def far_copy(number):
            return pltpu.make_async_remote_copy(
                src_ref=sent.at[number],
                dst_ref=got.at[number],
                send_sem=far_send.at[number],
                recv_sem=far_recv.at[number],
                device_id=opposite,
                device_id_type=MESH,
            )

    for load in loads:
        load.start()
    barrier = pltpu.get_barrier_semaphore()

    def greet_dp(step, carry):
        pl.semaphore_signal(
            barrier,
            inc=1,
            device_id=(lax.rem(dp_place + step, replicas), tensor_place),
            device_id_type=MESH,
        )
        return carry

    def greet_tensor(step, carry):
        pl.semaphore_signal(
            barrier,
            inc=1,
            device_id=(dp_place, lax.rem(tensor_place + step, tensor_size)),
            device_id_type=MESH,
        )
        return carry

    lax.fori_loop(1, replicas, greet_dp, 0)
    lax.fori_loop(1, tensor_size, greet_tensor, 0)
    mine[...] = jnp.zeros_like(mine)
    mine_two[...] = jnp.zeros_like(mine_two)
    block = 2 * LANES
    if far_refs:
        for number, (factor_ref, matrix) in enumerate(
            ((far_factor_down, far_down), (far_factor_in, far_in))
        ):
            far_loads[1 - number].wait()
            for start in range(0, matrix.shape[0], block):
                rows = slice(start, start + block)
                sent[0, number, :, rows] = low_left(factor_ref[...], matrix[rows])
        pl.semaphore_wait(barrier, replicas - 1 + tensor_size - 1)
        far_copy(0).start()
        bulks[0].start()
    offset = place_tiles(mine, 0, lq_ref[...])
    loads[0].wait()
    offset = place_tiles(mine, offset, left_factor(fo_ref[...], out[...]))
    offset = place_tiles(mine, offset, ld_ref[...])
    offset = place_tiles(mine, offset, li_ref[...])
    place_tiles(mine, offset, small_ref[...])
    if far_refs:
        far_copy(0).wait_recv()
        add_tiles(mine, offset - 2 * down.shape[0] // LANES, got[0, 0])
        add_tiles(mine, offset - inw.shape[0] // LANES, got[0, 1])
    else:
        pl.semaphore_wait(barrier, replicas - 1 + tensor_size - 1)
    drain_one = dp_exchange(replicas, mine, wire, arrived, total, first_sems)

    def slot_copy(step, slot):
        peer = lax.rem(tensor_place + step, tensor_size)
        return pltpu.make_async_remote_copy(
            src_ref=small_slots.at[tensor_place],
            dst_ref=small_slots.at[slot],
            send_sem=send_small.at[step],
            recv_sem=recv_small.at[slot],
            device_id=(dp_place, peer),
            device_id_type=MESH,
        )

    def start_small(step, carry):
        slot_copy(step, tensor_place).start()
        return carry

    own_small = take_tiles(total, offset, small_ref.shape[1])
    small_slots[tensor_place] = own_small
    lax.fori_loop(1, tensor_size, start_small, 0)
    offset = 0
    offset_two = 0
    offsets = []
    for basis_ref in (bq_ref, bo_ref, bd_ref, bi_ref):
        offsets.append(offset)
        offset += basis_ref.shape[1] // LANES
    for number in (2, 3, 0, 1):
        basis_ref = (bq_ref, bo_ref, bd_ref, bi_ref)[number]
        rows = take_tiles(total, offsets[number], basis_ref.shape[1]) * (1.0 / replicas)
        basis_ref[...] = orthonormal_rows(rows)
        if far_refs and number >= 2:
            sent[1, number - 2] = basis_ref[...]
        if far_refs and number == 3:
            far_copy(1).start()
    drain_one()
    for load in loads[1:]:
        load.wait()
    for part in range(3):
        right = right_factor(bq_ref[:, :block], qkv[part, :block])
        for start in range(block, qkv.shape[1], block):
            rows = slice(start, start + block)
            right += right_factor(bq_ref[:, rows], qkv[part, rows])
        offset_two = place_tiles(mine_two, offset_two, right)
    for basis_ref, matrix in zip((bo_ref, bd_ref, bi_ref), (out, down, inw)):
        rows_of = min(block, matrix.shape[0])
        right = right_factor(basis_ref[:, :rows_of], matrix[:rows_of])
        for start in range(rows_of, matrix.shape[0], rows_of):
            rows = slice(start, start + rows_of)
            right += right_factor(basis_ref[:, rows], matrix[rows])
        offset_two = place_tiles(mine_two, offset_two, right)
    if far_refs:
        far_copy(1).wait_recv()
        sent[2, 0] = low_right(got[1, 0], far_down[...])
        sent[2, 1] = low_right(got[1, 1], far_in[...])
        far_copy(2).start()
        bulks[1].start()
        far_copy(2).wait_recv()
        add_tiles(mine_two, offset_two - (down.shape[1] + inw.shape[1]) // LANES, got[2, 0])
        add_tiles(mine_two, offset_two - inw.shape[1] // LANES, got[2, 1])
    drain_two = dp_exchange(
        replicas, mine_two, wire_two, arrived_two, total_two, second_sems
    )

    def collect(step, carry):
        peer = lax.rem(tensor_place + step, tensor_size)
        slot_copy(step, peer).wait_recv()
        slot_copy(step, tensor_place).wait_send()
        return carry + small_slots[peer]

    everyone = lax.fori_loop(1, tensor_size, collect, own_small)
    row_number = lax.broadcasted_iota(jnp.int32, everyone.shape, 0)
    sum_ref[...] = jnp.where(row_number < 6, everyone, own_small) * (1.0 / replicas)
    offset = 0
    for part in range(3):
        rq_ref[part] = take_tiles(total_two, offset, rq_ref.shape[2]) * (1.0 / replicas)
        offset += rq_ref.shape[2] // LANES
    for ref in (ro_ref, rd_ref, ri_ref):
        ref[...] = take_tiles(total_two, offset, ref.shape[1]) * (1.0 / replicas)
        offset += ref.shape[1] // LANES
    drain_two()
    if far_refs:
        for number in range(3):
            far_copy(number).wait_send()
        for copy in bulks:
            copy.wait()


def compress(matrices, lefts, small, replicas, tensor_size, far):
    qkv, out, inw, down = matrices
    rank_size = small.shape[0]
    sizes = (qkv.shape[1], out.shape[0], inw.shape[0], down.shape[0])
    right_shapes = [(3, rank_size, qkv.shape[2])] + [(rank_size, one.shape[1]) for one in matrices[1:]]
    lanes_one = sum(sizes) + small.shape[1]
    lanes_two = 3 * qkv.shape[2] + sum(one.shape[1] for one in matrices[1:])
    scratch = [pltpu.VMEM(one.shape, jnp.float32) for one in matrices]
    for lanes in (lanes_one, lanes_two):
        shape = (replicas, rank_size, -(-lanes // (LANES * replicas)) * LANES)
        scratch += [
            pltpu.VMEM(shape, jnp.float32),
            pltpu.VMEM(shape, jnp.bfloat16),
            pltpu.VMEM(shape, jnp.bfloat16),
            pltpu.VMEM(shape, jnp.bfloat16),
        ]
    scratch += [pltpu.VMEM((tensor_size,) + small.shape, jnp.float32), pltpu.SemaphoreType.DMA((6,))]
    scratch += [pltpu.SemaphoreType.DMA((replicas,))] * 8
    scratch += [pltpu.SemaphoreType.DMA((tensor_size,))] * 2
    if far:
        scratch += [pltpu.VMEM(one.shape, one.dtype) for one in far[:2]]
        scratch += [pltpu.VMEM((3, 2, rank_size, inw.shape[0]), jnp.float32)] * 2
        scratch += [pltpu.SemaphoreType.DMA((5,))] * 2
    vmem = pl.BlockSpec(memory_space=pltpu.VMEM)
    shapes = [(rank_size, size) for size in sizes] + right_shapes + [small.shape]
    shapes = [jax.ShapeDtypeStruct(shape, jnp.float32) for shape in shapes]
    late_shape = []
    if far:
        late_shape = [jax.ShapeDtypeStruct((inw.shape[0] // 2, inw.shape[1]), far[0].dtype)]
    outputs = pl.pallas_call(
        partial(compress_kernel, replicas, tensor_size, bool(far)),
        in_specs=([pl.BlockSpec(memory_space=pl.ANY)] * 2 + [vmem] * 2 if far else [])
        + [pl.BlockSpec(memory_space=pl.ANY)] * 4
        + [vmem] * 5,
        out_specs=[pl.BlockSpec(memory_space=pl.ANY)] * len(late_shape) + [vmem] * 9,
        out_shape=late_shape + shapes,
        scratch_shapes=scratch,
        compiler_params=pltpu.CompilerParams(
            collective_id=1, has_side_effects=True, vmem_limit_bytes=VMEM_GRANT
        ),
        name="compress",
    )(*far, *matrices, *lefts, small)
    late, outputs = outputs[:-9], outputs[-9:]
    return outputs[:4], outputs[4:8], outputs[8], late


def outer_of(basis_rows, right):
    basis_high, basis_low = split_bf16(basis_rows)
    right_high, right_low = split_bf16(right)
    return dot_tn(
        jnp.concatenate([basis_high, basis_low, basis_high], axis=0),
        jnp.concatenate([right_high, right_high, right_low], axis=0),
    )


def update_kernel(step_rate, out_steps, near_steps, *refs):
    (mq, mo, mi, md, oq, oo, oi, od, wq, wo, wi, wd, bq, bo, bi, bd, rq, ro, ri, rd,
     gq, go, gi, gd, eq, eo, ei, ed, nq, no, ni, nd, vq, vo, vi, vd) = refs[:20] + refs[-16:]
    step = pl.program_id(0)
    whole_in, whole_down = mi[...], md[...]
    if len(refs) > 36:
        near_in, rest_in, near_down, rest_down = refs[20:24]
        whole_in += jnp.where(step < near_steps, near_in[...], rest_in[...]).astype(jnp.float32)
        whole_down += jnp.where(step < near_steps, near_down[...], rest_down[...]).astype(
            jnp.float32
        )

    def one(matrix, old, weight, rank, grad_ref, err_ref, mom_ref, new_ref, place):
        moment = 0.9 * old + rank
        grad_ref[place] = rank
        err_ref[place] = matrix - rank
        mom_ref[place] = moment
        new_ref[place] = weight.astype(jnp.float32) - step_rate * moment

    def lanes_of(ref, rows):
        return ref[:, pl.ds(pl.multiple_of(step * rows, LANES), rows)]

    rows = mq.shape[1]
    for part in range(3):
        rank = outer_of(lanes_of(bq, rows), rq[part])
        one(mq[part], oq[part], wq[part], rank, gq, eq, nq, vq, part)
    rank = outer_of(lanes_of(bi, mi.shape[0]), ri[...])
    one(whole_in, oi[...], wi[...], rank, gi, ei, ni, vi, slice(None))
    rank = outer_of(lanes_of(bd, md.shape[0]), rd[...])
    one(whole_down, od[...], wd[...], rank, gd, ed, nd, vd, slice(None))

    @pl.when(step < out_steps)
    def _():
        rank = outer_of(lanes_of(bo, mo.shape[0]), ro[...])
        one(mo[...], oo[...], wo[...], rank, go, eo, no, vo, slice(None))


def update(matrices, momenta, weights, bases, rights, late, step_rate):
    qkv, out, inw, down = matrices
    rows = LANES
    steps = inw.shape[0] // rows
    down_rows = down.shape[0] // steps
    if down_rows < LANES:
        steps = down.shape[0] // LANES
        rows, down_rows = inw.shape[0] // steps, LANES
    out_steps = out.shape[0] // LANES
    near_steps = late[0].shape[0] // rows if late else 0
    late_specs = [
        pl.BlockSpec((rows, inw.shape[1]), lambda i: (jnp.minimum(i, near_steps - 1), 0)),
        pl.BlockSpec((rows, inw.shape[1]), lambda i: (jnp.maximum(i - near_steps, 0), 0)),
        pl.BlockSpec((down_rows, down.shape[1]), lambda i: (jnp.minimum(i, near_steps - 1), 0)),
        pl.BlockSpec((down_rows, down.shape[1]), lambda i: (jnp.maximum(i - near_steps, 0), 0)),
    ]

    def whole(array):
        return pl.BlockSpec(array.shape, lambda i: (0,) * array.ndim)

    def specs():
        return [
            pl.BlockSpec((3, rows, qkv.shape[2]), lambda i: (0, i, 0)),
            pl.BlockSpec((LANES, out.shape[1]), lambda i: (jnp.minimum(i, out_steps - 1), 0)),
            pl.BlockSpec((rows, inw.shape[1]), lambda i: (i, 0)),
            pl.BlockSpec((down_rows, down.shape[1]), lambda i: (i, 0)),
        ]

    shapes = [jax.ShapeDtypeStruct(one.shape, jnp.float32) for one in matrices]
    outputs = pl.pallas_call(
        partial(update_kernel, step_rate, out_steps, near_steps),
        grid=(steps,),
        in_specs=specs() * 3
        + [whole(one) for one in bases]
        + [whole(one) for one in rights]
        + late_specs[: len(late)],
        out_specs=specs() * 4,
        out_shape=shapes * 4,
        compiler_params=pltpu.CompilerParams(vmem_limit_bytes=VMEM_GRANT),
        name="update",
    )(*matrices, *momenta, *weights, *bases, *rights, *late)
    return outputs[0:4], outputs[4:8], outputs[8:12], outputs[12:16]


def masked_scores(queries, key_heads, seg_ids):
    scores = jnp.einsum("qhd,khd->hqk", queries, key_heads, preferred_element_type=jnp.float32)
    same_doc = seg_ids[:, None] == seg_ids[None, :]
    return jnp.where(same_doc[None], scores, MASKED)


def attend_forward(inputs_of):
    queries, key_heads, value_heads, seg_ids = inputs_of
    scores = masked_scores(queries, key_heads, seg_ids)
    highest = jnp.max(scores, axis=-1, keepdims=True)
    powers = jnp.exp(scores - highest)
    denominator = jnp.sum(powers, axis=-1, keepdims=True)
    weights = (powers / denominator).astype(jnp.bfloat16)
    mixed_heads = jnp.einsum(
        "hqk,khd->qhd", weights, value_heads, preferred_element_type=jnp.float32
    )
    return (mixed_heads.astype(jnp.bfloat16), highest[..., 0] + jnp.log(denominator[..., 0]))


def attend_backward(inputs_of):
    queries, key_heads, value_heads, seg_ids, grad_mixed, log_total = inputs_of
    scores = masked_scores(queries, key_heads, seg_ids)
    probability = jnp.exp(scores - log_total[..., None])
    grad_probs = jnp.einsum(
        "qhd,khd->hqk", grad_mixed, value_heads, preferred_element_type=jnp.float32
    )
    centre = jnp.sum(probability * grad_probs, axis=-1, keepdims=True)
    grad_scores = (probability * (grad_probs - centre)).astype(jnp.bfloat16)
    grad_query = jnp.einsum(
        "hqk,khd->qhd", grad_scores, key_heads, preferred_element_type=jnp.float32
    )
    grad_key = jnp.einsum("hqk,qhd->khd", grad_scores, queries, preferred_element_type=jnp.float32)
    grad_value = jnp.einsum(
        "hqk,qhd->khd",
        probability.astype(jnp.bfloat16),
        grad_mixed,
        preferred_element_type=jnp.float32,
    )
    return (
        grad_query.astype(jnp.bfloat16),
        grad_key.astype(jnp.bfloat16),
        grad_value.astype(jnp.bfloat16),
    )


def stacked_heads(pair, lane_is_low):
    zero = jnp.zeros_like(pair)
    return jnp.concatenate(
        [jnp.where(lane_is_low, pair, zero), jnp.where(lane_is_low, zero, pair)], axis=0
    )


def own_blocks(both):
    rows = both.shape[1] // 2
    return jnp.concatenate([both[:DH, :rows], both[DH:, rows:]], axis=0).T


def window_sizes(length):
    return (length * 3 // 8, length * 5 // 8, length)


def windows_of(bounds, length):
    first = bounds[0] // LANES * LANES
    need = bounds[1] - first
    small, large, whole = window_sizes(length)
    number = jnp.where(need <= small, 0, jnp.where(need <= large, 1, 2))
    room = jnp.where(need <= small, length - small, jnp.where(need <= large, length - large, 0))
    return jnp.concatenate([jnp.minimum(first, room), number])


def attend_back_kernel(place_ref, q_ref, k_ref, v_ref, seg_key_ref, seg_query_ref, gm_own_ref,
                       gm_other_ref, mixed_ref, log_ref, old_ref, grad_ref, sums_ref, key_t, grad_key,
                       grad_value):
    del old_ref
    step = pl.program_id(0)

    @pl.when(step == 0)
    def _():
        key_t[...] = k_ref[...].T
        grad_key[...] = jnp.zeros_like(grad_key)
        grad_value[...] = jnp.zeros_like(grad_value)

    pairs = q_ref.shape[1] // LANES
    lane = lax.broadcasted_iota(jnp.int32, (1, LANES), 1)
    lane_is_low = lane < DH
    head_of_lane = (
        lax.broadcasted_iota(jnp.int32, (8, LANES), 0)
        == lax.broadcasted_iota(jnp.int32, (8, LANES), 1) // DH
    ).astype(jnp.bfloat16)
    head_scale = 1.0 / math.sqrt(DH)
    here = pl.ds(pl.multiple_of(step * LANES, LANES), LANES)
    is_own = lax.rem(step // (pl.num_programs(0) // 2) + place_ref[1], 2) == 0
    gm = jnp.where(is_own, gm_own_ref[...], gm_other_ref[...])
    seg_query = jnp.concatenate([seg_query_ref[...], seg_query_ref[...]], axis=1)
    all_lanes = [slice(pair * LANES, (pair + 1) * LANES) for pair in range(pairs)]
    length = k_ref.shape[0]

    def window(size):
        start = 0 if size == length else pl.multiple_of(place_ref[2 + step], LANES)
        keys = pl.ds(start, size)
        seg_key = seg_key_ref[keys]
        same = jnp.concatenate([seg_key, seg_key], axis=1) == seg_query
        queries, grads, centres, probs, grad_probs = [], [], [], [], []
        for lanes in all_lanes:
            queries.append(stacked_heads(q_ref[:, lanes], lane_is_low))
            grads.append(stacked_heads(gm[:, lanes], lane_is_low))
            high, low = split_bf16(
                gm[:, lanes].astype(jnp.float32) * mixed_ref[:, lanes].astype(jnp.float32)
            )
            sums = dot_nt(head_of_lane, high) + dot_nt(head_of_lane, low)
            centres.append(jnp.concatenate([sums[0:1], sums[1:2]], axis=1))
        for pair, lanes in enumerate(all_lanes):
            log_total = jnp.concatenate(
                [log_ref[2 * pair : 2 * pair + 1], log_ref[2 * pair + 1 : 2 * pair + 2]], axis=1
            )
            scores = dot_nt(k_ref[keys, lanes], queries[pair])
            probs.append(jnp.exp(jnp.where(same, scores - log_total, MASKED)))
            grad_probs.append(dot_nt(v_ref[keys, lanes], grads[pair]))
        for pair, lanes in enumerate(all_lanes):
            grad_scores = (probs[pair] * (grad_probs[pair] - centres[pair])).astype(jnp.bfloat16)
            grad_value[keys, lanes] += dot_nn(probs[pair].astype(jnp.bfloat16), grads[pair])
            grad_key[keys, lanes] += dot_nn(grad_scores, queries[pair])
            grad_query = own_blocks(dot_nn(key_t[lanes, keys], grad_scores)).astype(jnp.bfloat16)
            grad_ref[0, here, lanes] = (grad_query.astype(jnp.float32) * head_scale).astype(
                jnp.bfloat16
            )

    for number, size in enumerate(window_sizes(length)):
        pl.when(place_ref[2 + pl.num_programs(0) + step] == number)(partial(window, size))

    @pl.when(step == pl.num_programs(0) - 1)
    def _():
        grad_ref[1] = grad_key[...].astype(jnp.bfloat16)
        low_value = grad_value[...].astype(jnp.bfloat16)
        grad_ref[2] = low_value
        sums_ref[0:1] = jnp.sum(grad_ref[0].astype(jnp.float32), axis=0, keepdims=True)
        sums_ref[1:2] = jnp.sum(low_value.astype(jnp.float32), axis=0, keepdims=True)


def attend_back(projected, seg_keys, seg_queries, grad_own, grad_other, mixed, logs, slot, bounds,
                old, place, core):
    length = seg_keys.shape[1]
    slab = projected.shape[2]
    blocks = length // LANES
    half = blocks // 2
    at = jnp.concatenate(
        [
            jnp.stack([place, core]),
            windows_of(bounds[2 * slot : 2 * slot + 2, :blocks], length),
        ]
    )
    grid_spec = pltpu.PrefetchScalarGridSpec(
        num_scalar_prefetch=1,
        grid=(blocks,),
        in_specs=[
            pl.BlockSpec((None, LANES, slab), lambda i, at: (0, at[0] * blocks + i, 0)),
            pl.BlockSpec((None, length, slab), lambda i, at: (1, at[0], 0)),
            pl.BlockSpec((None, length, slab), lambda i, at: (2, at[0], 0)),
            pl.BlockSpec((None, length, LANES), lambda i, at: (at[0], 0, 0)),
            pl.BlockSpec((None, 1, LANES), lambda i, at: (at[0], 0, i)),
            pl.BlockSpec((None, LANES, slab), lambda i, at: (grad_own[1], lax.rem(i, half), 0)),
            pl.BlockSpec((None, LANES, slab), lambda i, at: (grad_other[1], lax.rem(i, half), 0)),
            pl.BlockSpec((None, LANES, slab), lambda i, at: (slot, i, 0)),
            pl.BlockSpec((None, slab // DH, LANES), lambda i, at: (slot, 0, i)),
            pl.BlockSpec(memory_space=pl.ANY),
        ],
        out_specs=[
            pl.BlockSpec((3, length, slab), lambda i, at: (0, at[0], 0)),
            pl.BlockSpec((2, slab), lambda i, at: (0, 0)),
        ],
        scratch_shapes=[
            pltpu.VMEM((slab, length), jnp.bfloat16),
            pltpu.VMEM((length, slab), jnp.float32),
            pltpu.VMEM((length, slab), jnp.float32),
        ],
    )
    return pl.pallas_call(
        attend_back_kernel,
        grid_spec=grid_spec,
        out_shape=[
            jax.ShapeDtypeStruct(projected.shape, jnp.bfloat16),
            jax.ShapeDtypeStruct((2, slab), jnp.float32),
        ],
        input_output_aliases={} if old is None else {10: 0},
        compiler_params=pltpu.CompilerParams(vmem_limit_bytes=24 << 20),
        cost_estimate=BRIEF,
        name="attend_back",
    )(at, projected, projected, projected, seg_keys, seg_queries, grad_own[0],
      grad_other[0], mixed, logs, seg_keys if old is None else old)


def row_mean(values):
    return jnp.mean(values, axis=-1, keepdims=True)


def layer_kernel(tokens, cotangent, w_qkv_ref, out_ref, in_ref, down_ref,
                 factor_in_ref, factor_down_ref, head_ref, bias_ref, vec_ref, segments,
                 projected_out, log_out, mixed_out, in_two, down_two, out_rest, bias_two,
                 result_out, low_out, active_out, branch_out, hidden_out, norm_out, near_out,
                 far_one_out, far_two_out, keys_out, rows_out, down_near, down_part_out, down_rest, in_part_out, in_head,
                 far_in_out, far_down_out, out_sum,
                 out_far, unit_ref, unit_two, sums_ref, bounds_ref,
                 rows_in, w_qkv, projected, value_t, log_total, mixed, pieces,
                 w_out, w_in, w_down, bias, tok, cot, first, normed, inverse, low, slope, active,
                 part, other, acc, wide, branch, result, down_part, near, far_mixed, outs_two,
                 seg_keys, seg_queries, load_sem, store_sem, send_sem, recv_sem):
    dp_place = lax.axis_index("dp")
    tensor_place = lax.axis_index("tensor")
    core = lax.rem(tensor_place, 2)
    seq = tensor_place // 2
    far = 1 - seq
    side = lax.rem(dp_place, 2)
    depth = lax.rem(dp_place // 2, 2)
    here = 2 * depth + side
    sibling = (dp_place, tensor_place + 1 - 2 * core)
    opposite = (dp_place, core + 2 * far)
    diagonal = (dp_place, 1 - core + 2 * far)
    beside = (dp_place + 1 - 2 * side, tensor_place)
    behind = (dp_place + 2 - 4 * depth, tensor_place)
    share, width = tok.shape
    slab = in_ref.shape[1]
    length = rows_in.shape[1]
    head_slab = w_qkv.shape[2]
    head_count = head_slab // DH
    stores = []
    sends = []
    numbers = iter(range(send_sem.shape[0]))

    def load_later(number, source, target):
        return pltpu.make_async_copy(source, target, load_sem.at[number])

    def load(number, source, target):
        copy = load_later(number, source, target)
        copy.start()
        return copy

    def store(source, target):
        copy = pltpu.make_async_copy(source, target, store_sem.at[len(stores)])
        copy.start()
        stores.append(copy)

    def send_later(source, target, device):
        number = next(numbers)
        copy = pltpu.make_async_remote_copy(
            src_ref=source,
            dst_ref=target,
            send_sem=send_sem.at[number],
            recv_sem=recv_sem.at[number],
            device_id=device,
            device_id_type=MESH,
        )
        sends.append(copy)
        return copy

    def send(source, target, device):
        copy = send_later(source, target, device)
        copy.start()
        return copy

    def rows_of(number, size):
        return pl.ds(pl.multiple_of(number * size, LANES), size)

    load_qkv = load(0, w_qkv_ref, w_qkv)
    load_far = load(1, tokens.at[rows_of(far, length)], rows_in.at[0])
    load_near = load(2, tokens.at[rows_of(seq, length)], rows_in.at[1])
    load_out = load(3, out_ref, w_out.at[0])
    load_in = load(4, in_ref, w_in.at[0])
    load_down = load(5, down_ref, w_down.at[pl.ds(0, slab)])
    load_tok = load(6, tokens.at[rows_of(tensor_place, share)], tok)
    load_cot = load(7, cotangent.at[rows_of(tensor_place, share)], cot)

    barrier = pltpu.get_barrier_semaphore()
    for device in (sibling, opposite, diagonal, beside, behind):
        pl.semaphore_signal(barrier, inc=1, device_id=device, device_id_type=MESH)
    pl.semaphore_wait(barrier, 5)
    sums_ref[...] = jnp.zeros_like(sums_ref)
    unit_ref[...] = jnp.zeros_like(unit_ref)

    def rows_part(whole, number, parts):
        size = whole.shape[0] // parts
        return whole.at[pl.ds(pl.multiple_of(number * size, size), size)]

    class Fetch:
        def __init__(self, source, whole):
            own = rows_part(whole, here, 4)
            half_one = rows_part(whole, 2 * (here + 1 - 2 * side), 8)
            half_two = rows_part(whole, 2 * (here + 2 - 4 * depth) + 1, 8)
            self.over_y = send_later(rows_part(source, here, 4), own, opposite)
            self.over_x = send_later(own, own, beside)
            self.over_z = send_later(own, own, behind)
            self.half_z = send_later(half_one, half_one, behind)
            self.half_x = send_later(half_two, half_two, beside)

        def start(self):
            self.over_y.start()

        def pass_on(self):
            self.over_y.wait_recv()
            self.over_x.start()
            self.over_z.start()

        def pass_halves(self):
            self.over_x.wait_recv()
            self.half_z.start()
            self.over_z.wait_recv()
            self.half_x.start()

        def wait(self):
            self.half_z.wait_recv()
            self.half_x.wait_recv()

    bias_send = send(bias_ref, bias_two, opposite)
    factor_sends = [
        send(factor_in_ref, far_in_out, opposite), send(factor_down_ref, far_down_out, opposite)
    ]
    fetch_out = Fetch(out_ref, out_rest.at[1])
    upper, lower = pl.ds(0, width // 2), pl.ds(width // 2, width // 2)
    fetch_in = [Fetch(in_ref.at[rows], in_two.at[rows]) for rows in (upper, lower)]
    upper, lower = pl.ds(0, slab // 2), pl.ds(slab // 2, slab // 2)
    fetch_down = [Fetch(down_ref.at[rows], down_two.at[rows]) for rows in (upper, lower)]
    fetch_out.start()
    fetch_in[0].start()
    fetch_in[1].start()
    fetch_down[0].start()

    chunk = 256
    scale = 1.0 / math.sqrt(DH)

    def project(slot):
        def rows_step(step, carry):
            rows = rows_of(step, chunk)
            values = rows_in[slot, rows]
            projected[slot, 0, rows] = (
                (dot_nn(values, w_qkv[0]) + head_ref[0:1]) * scale
            ).astype(jnp.bfloat16)
            projected[slot, 1, rows] = dot_nn(values, w_qkv[1]).astype(jnp.bfloat16)
            projected[slot, 2, rows] = (dot_nn(values, w_qkv[2]) + head_ref[1:2]).astype(
                jnp.bfloat16
            )
            return carry

        lax.fori_loop(0, length // chunk, rows_step, 0)
        value_t[...] = projected[slot, 2].T

    lane_is_low = lax.broadcasted_iota(jnp.int32, (1, LANES), 1) < DH

    def attend_rows(slot, place, tasks):
        def block(step):
            rows = rows_of(step, LANES)
            same = seg_keys[place] == seg_queries[place, :, rows]
            mask = jnp.where(same, 0.0, MASKED)
            mask = jnp.concatenate([mask, mask], axis=1)
            all_lanes = [slice(at, at + LANES) for at in range(0, head_slab, LANES)]
            all_scores = [
                dot_nt(
                    projected[slot, 1, :, lanes],
                    stacked_heads(projected[slot, 0, rows, lanes], lane_is_low),
                )
                + mask
                for lanes in all_lanes
            ]
            for pair, (lanes, scores) in enumerate(zip(all_lanes, all_scores)):
                highest = jnp.max(scores, axis=0, keepdims=True)
                powers = jnp.exp(scores - highest)
                denominator = jnp.sum(powers, axis=0, keepdims=True)
                blend = dot_nn(value_t[lanes], powers.astype(jnp.bfloat16))
                mixed[slot, rows, lanes] = own_blocks(blend * (1.0 / denominator)).astype(
                    jnp.bfloat16
                )
                total = highest + jnp.log(denominator)
                log_total[slot, 2 * pair : 2 * pair + 1, rows] = total[:, :LANES]
                log_total[slot, 2 * pair + 1 : 2 * pair + 2, rows] = total[:, LANES:]

        def two_blocks(step, carry):
            for number, task in tasks:
                pl.when(step == number)(task)
            block(2 * step)
            block(2 * step + 1)
            return carry

        lax.fori_loop(0, length // LANES // 2, two_blocks, 0)

    for number in range(segments.shape[0]):
        documents = segments[number : number + 1].astype(jnp.float32)
        seg_queries[number] = documents
        seg_keys[number] = jnp.broadcast_to(documents, (LANES, length)).T
    store(seg_keys, keys_out)
    store(seg_queries, rows_out)
    load_qkv.wait()
    load_far.wait()
    project(0)
    attend_rows(0, far, [(2, fetch_out.pass_on)])
    fetch_in[0].pass_on()
    own_rows = rows_of(core, share)
    sibling_rows = rows_of(1 - core, share)
    piece_two = send(mixed.at[0, own_rows], pieces.at[1], opposite)
    piece_three = send(mixed.at[0, sibling_rows], pieces.at[2], diagonal)
    fetch_down[1].start()
    store(projected.at[0, 0], projected_out.at[0, rows_of(far, length)])
    store(projected.at[0, 1], projected_out.at[1, rows_of(far, length)])
    store(projected.at[0, 2], projected_out.at[2, rows_of(far, length)])
    load_near.wait()
    project(1)
    out_pass = [
        send_later(out_ref, out_rest.at[0], sibling),
        send_later(out_rest.at[1], out_rest.at[2], sibling),
    ]
    load_two = load_later(8, out_rest.at[1], w_out.at[2])

    def pass_in():
        fetch_in[1].pass_on()
        fetch_in[0].pass_halves()

    def pass_out():
        fetch_out.wait()
        for copy in out_pass:
            copy.start()
        load_two.start()

    attend_rows(1, seq, [(0, fetch_out.pass_halves), (2, pass_in), (3, pass_out)])
    piece_one = send(mixed.at[1, sibling_rows], pieces.at[0], sibling)
    store(projected.at[1, 0], projected_out.at[0, rows_of(seq, length)])
    store(projected.at[1, 1], projected_out.at[1, rows_of(seq, length)])
    store(projected.at[1, 2], projected_out.at[2, rows_of(seq, length)])
    store(log_total, log_out)
    for copy in out_pass:
        copy.wait_recv()
    load_one = load(9, out_rest.at[0], w_out.at[1])
    load_three = load(10, out_rest.at[2], w_out.at[3])
    store(mixed, mixed_out)
    fetch_down[0].pass_on()
    fetch_in[1].pass_halves()
    for copy in (load_out, load_tok, load_one, load_two, load_three):
        copy.wait()
    for copy in (piece_two, piece_three, piece_one):
        copy.wait_recv()
    small = 64

    def attn_rows(step, carry):
        rows = rows_of(step, chunk)
        total = dot_nn(mixed[1, pl.ds(pl.multiple_of(core * share + step * chunk, LANES), chunk)],
                       w_out[0])
        for piece in range(3):
            total += dot_nn(pieces[piece, rows], w_out[piece + 1])
        acc[rows] = total
        return carry

    def first_rows(step, carry):
        rows = pl.ds(pl.multiple_of(step * small, small), small)
        values = tok[rows].astype(jnp.float32) + (acc[rows] + vec_ref[0:1])
        centred = values - row_mean(values)
        spread = lax.rsqrt(row_mean(centred * centred) + EPS_NORM)
        unit = centred * spread
        normed[rows] = unit
        inverse[rows] = spread
        shifted = unit * vec_ref[2:3] + vec_ref[3:4]
        first[rows] = shifted
        low[rows] = shifted.astype(jnp.bfloat16)
        return carry

    lax.fori_loop(0, share // chunk, attn_rows, 0)
    lax.fori_loop(0, share // small, first_rows, 0)
    slots = [slice(0, share), slice(share, 2 * share)]
    low_send = send(low.at[slots[0]], low.at[slots[1]], sibling)
    fetch_down[0].pass_halves()
    load_in.wait()

    def hidden_of(slot, owner):
        def units(step, carry):
            inner = rows_of(step, chunk)
            values = dot_nn(low[slots[slot]], w_in[owner, :, inner]) + bias[owner, :, inner]
            share_of = 0.5 * (1.0 + lax.erf(values * math.sqrt(0.5)))
            density = jnp.exp(-0.5 * values * values) * (1.0 / math.sqrt(2.0 * math.pi))
            active[owner, slots[slot], inner] = (values * share_of).astype(jnp.bfloat16)
            slope[owner, slots[slot], inner] = (share_of - 0.5 + values * density).astype(jnp.bfloat16)
            return carry

        lax.fori_loop(0, slab // chunk, units, 0)

    def branch_of(slot, owner, target, start, size):
        units = slice(owner * slab, (owner + 1) * slab)

        def columns(step, carry):
            at = pl.ds(pl.multiple_of(start + step * chunk, chunk), chunk)
            values = dot_nn(active[owner, slots[slot]], w_down[units, at])
            target[:, at] = values if owner == 0 else target[:, at] + values
            return carry

        lax.fori_loop(0, size // chunk, columns, 0)

    bias_send.wait_recv()
    bias[0] = bias_ref[...]
    load_bias = load(11, bias_two, bias.at[1])
    hidden_of(0, 0)
    low_send.wait_recv()
    store(low, low_out)
    fetch_down[1].pass_on()
    hidden_of(1, 0)
    for fetch in fetch_in:
        fetch.wait()
    load_in_two = load(12, in_two, w_in.at[1])
    load_down.wait()
    branch_of(1, 0, part, 0, width)
    branch_of(0, 0, acc, 0, width)
    load_bias.wait()
    load_in_two.wait()
    fetch_down[1].pass_halves()
    hidden_of(1, 1)
    hidden_of(0, 1)
    store(active.at[0], active_out)
    lane = lax.broadcasted_iota(jnp.int32, (1, LANES), 1)
    for slot, place in ((0, far), (1, seq)):
        firsts = jnp.zeros((1, LANES), jnp.float32)
        lasts = jnp.zeros((1, LANES), jnp.float32)
        for block in range(length // LANES):
            start = block * LANES
            firsts = jnp.where(lane == block, seg_keys[place, start : start + 1], firsts)
            lasts = jnp.where(
                lane == block, seg_keys[place, start + LANES - 1 : start + LANES], lasts
            )
        documents = seg_keys[place]
        bounds_ref[2 * slot : 2 * slot + 1] = jnp.sum(
            jnp.where(documents < firsts, 1.0, 0.0), axis=0, keepdims=True
        ).astype(jnp.int32)
        bounds_ref[2 * slot + 1 : 2 * slot + 2] = jnp.sum(
            jnp.where(documents <= lasts, 1.0, 0.0), axis=0, keepdims=True
        ).astype(jnp.int32)
    for fetch in fetch_down:
        fetch.wait()
    load_down_two = load(13, down_two, w_down.at[pl.ds(slab, slab)])
    load_down_two.wait()
    half = width // 2
    part_sends = []
    for number in range(2):
        branch_of(1, 1, part, number * half, half)
        columns = slice(number * half, (number + 1) * half)
        part_sends.append(send(part.at[:, columns], other.at[:, columns], sibling))
    branch_of(0, 1, acc, 0, width)
    load_cot.wait()
    for copy in part_sends:
        copy.wait_recv()

    def second_rows(step, carry):
        rows = pl.ds(pl.multiple_of(step * small, small), small)
        values = first[rows] + (acc[rows] + other[rows]) + vec_ref[1:2]
        centred = values - row_mean(values)
        spread = lax.rsqrt(row_mean(centred * centred) + EPS_NORM)
        unit = centred * spread
        result[rows] = (unit * vec_ref[4:5] + vec_ref[5:6]).astype(jnp.bfloat16)
        upper = cot[rows].astype(jnp.float32)
        scaled = upper * vec_ref[4:5]
        grad = spread * (scaled - row_mean(scaled) - unit * row_mean(scaled * unit))
        wide[rows] = grad
        grad_low = grad.astype(jnp.bfloat16)
        branch[rows] = grad_low
        sums_ref[1:2] += jnp.sum(grad_low.astype(jnp.float32), axis=0, keepdims=True)
        sums_ref[4:5] += jnp.sum(upper * unit, axis=0, keepdims=True)
        sums_ref[5:6] += jnp.sum(upper, axis=0, keepdims=True)
        return carry

    branch_sends = []
    for number in range(2):
        steps = share // small // 2
        lax.fori_loop(number * steps, (number + 1) * steps, second_rows, 0)
        rows = slice(number * steps * small, (number + 1) * steps * small)
        there = slice(share + rows.start, share + rows.stop)
        branch_sends.append(send(branch.at[rows], branch.at[there], sibling))
    store(result, result_out)
    hidden = rows_in

    def grad_hidden_of(slot, owner):
        def units(step, carry):
            inner = rows_of(step, chunk)
            outer = pl.ds(pl.multiple_of(owner * slab + step * chunk, chunk), chunk)
            grad = dot_nt(branch[slots[slot]], w_down[outer]) * (
                0.5 + slope[owner, slots[slot], inner].astype(jnp.float32)
            )
            grad_low = grad.astype(jnp.bfloat16)
            hidden[owner, slots[slot], inner] = grad_low
            unit_ref[:, outer] += jnp.sum(grad_low.astype(jnp.float32), axis=0, keepdims=True)
            return carry

        lax.fori_loop(0, slab // chunk, units, 0)

    def grad_first_of(slot, target, start, size):
        def columns(step, carry):
            at = pl.ds(pl.multiple_of(start + step * chunk, chunk), chunk)
            target[:, at] = dot_nt(hidden[0, slots[slot]], w_in[0, at]) + dot_nt(
                hidden[1, slots[slot]], w_in[1, at]
            )
            return carry

        lax.fori_loop(0, size // chunk, columns, 0)

    def far_product(left_side, right_side, target, start, stop):
        def rows_step(step, carry):
            at = rows_of(step, LANES)
            target[at] = dot_tn(left_side[:, at], right_side[...]).astype(jnp.bfloat16)
            return carry

        lax.fori_loop(start // LANES, stop // LANES, rows_step, 0)

    grad_hidden_of(0, 0)
    grad_hidden_of(0, 1)
    for copy in branch_sends:
        copy.wait_recv()
    store(branch, branch_out)
    early = down_near.shape[0]
    far_product(active.at[1], branch, down_part, 0, early)
    down_send = send(down_part.at[pl.ds(0, early)], down_near, opposite)
    far_product(active.at[1], branch, down_part, early, slab)
    store(down_part, down_part_out)
    store(down_part.at[pl.ds(early, slab - early)], down_rest)
    grad_hidden_of(1, 0)
    grad_hidden_of(1, 1)
    unit_send = send(unit_ref.at[:, pl.ds(slab, slab)], unit_two, opposite)
    store(hidden.at[0], hidden_out)
    for copy in part_sends:
        copy.wait_send()
    sends[:] = [one for one in sends if all(one is not copy for copy in part_sends)]
    first_sends = []
    for number in range(2):
        grad_first_of(1, part, number * half, half)
        columns = slice(number * half, (number + 1) * half)
        first_sends.append(send(part.at[:, columns], other.at[:, columns], sibling))
    grad_first_of(0, acc, 0, width)
    for copy in first_sends:
        copy.wait_recv()

    def back_rows(step, carry):
        rows = pl.ds(pl.multiple_of(step * small, small), small)
        grad = acc[rows] + other[rows] + wide[rows]
        unit = normed[rows]
        scaled = grad * vec_ref[2:3]
        back = inverse[rows] * (scaled - row_mean(scaled) - unit * row_mean(scaled * unit))
        acc[rows] = back
        back_low = back.astype(jnp.bfloat16)
        tok[rows] = back_low
        sums_ref[0:1] += jnp.sum(back_low.astype(jnp.float32), axis=0, keepdims=True)
        sums_ref[2:3] += jnp.sum(grad * unit, axis=0, keepdims=True)
        sums_ref[3:4] += jnp.sum(grad, axis=0, keepdims=True)
        return carry

    lax.fori_loop(0, share // small, back_rows, 0)
    store(acc, norm_out)
    attn = tok[...]
    near[1] = dot_nt(attn, w_out[1]).astype(jnp.bfloat16)
    near_send = send(near.at[1], near.at[2], sibling)
    out_one = slice(0, head_slab)
    out_three = slice(head_slab, 2 * head_slab)
    first[out_one] = dot_tn(pieces[0], attn)
    first[out_three] = dot_tn(pieces[2], attn)
    outs_send = send(first.at[pl.ds(0, 2 * head_slab)], outs_two, sibling)
    far_mixed[0] = dot_nt(attn, w_out[2]).astype(jnp.bfloat16)
    far_mixed[1] = dot_nt(attn, w_out[3]).astype(jnp.bfloat16)
    store(far_mixed.at[0], far_one_out.at[0])
    store(far_mixed.at[1], far_two_out.at[0])
    near[0] = dot_nt(attn, w_out[0]).astype(jnp.bfloat16)
    store(near.at[0], near_out.at[0])
    far_product(low, hidden.at[1], active.at[1], 0, width)
    store(active.at[1], in_part_out)
    store(active.at[1, pl.ds(0, in_head.shape[0])], in_head)
    near_send.wait_recv()
    store(near.at[2], near_out.at[1])
    outs_send.wait_recv()
    out_sum[...] = dot_tn(mixed[1, own_rows], attn) + outs_two[out_one]
    out_far[...] = (dot_tn(pieces[1], attn) + outs_two[out_three]).astype(jnp.bfloat16)
    unit_send.wait_recv()
    down_send.wait_recv()
    for copy in factor_sends:
        copy.wait_recv()
    for copy in sends:
        copy.wait_send()
    for copy in stores:
        copy.wait()


def layer_call(tokens, cotangent, planes, w_out, w_in, w_down, factor_in, factor_down, head_bias,
               unit_bias, vectors, segments):
    token_count, width = tokens.shape
    seq_count, length = segments.shape
    share = token_count // (2 * seq_count)
    head_slab = planes.shape[2]
    slab = w_in.shape[1]
    early = slab // 2
    low_type, full_type = jnp.bfloat16, jnp.float32
    vmem = pl.BlockSpec(memory_space=pltpu.VMEM)
    anywhere = pl.BlockSpec(memory_space=pl.ANY)
    shapes = [
        jax.ShapeDtypeStruct((3, token_count, head_slab), low_type),
        jax.ShapeDtypeStruct((2, head_slab // DH, length), full_type),
        jax.ShapeDtypeStruct((2, length, head_slab), low_type),
        jax.ShapeDtypeStruct(w_in.shape, low_type),
        jax.ShapeDtypeStruct(w_down.shape, low_type),
        jax.ShapeDtypeStruct((3,) + w_out.shape, low_type),
        jax.ShapeDtypeStruct((1, slab), full_type),
        jax.ShapeDtypeStruct((share, width), low_type),
        jax.ShapeDtypeStruct((2 * share, width), low_type),
        jax.ShapeDtypeStruct((2 * share, slab), low_type),
        jax.ShapeDtypeStruct((2 * share, width), low_type),
        jax.ShapeDtypeStruct((2 * share, slab), low_type),
        jax.ShapeDtypeStruct((share, width), full_type),
        jax.ShapeDtypeStruct((2, share, head_slab), low_type),
        jax.ShapeDtypeStruct((1, share, head_slab), low_type),
        jax.ShapeDtypeStruct((1, share, head_slab), low_type),
        jax.ShapeDtypeStruct((seq_count, length, LANES), full_type),
        jax.ShapeDtypeStruct((seq_count, 1, length), full_type),
        jax.ShapeDtypeStruct((early, width), low_type),
        jax.ShapeDtypeStruct((slab, width), low_type),
        jax.ShapeDtypeStruct((slab - early, width), low_type),
        jax.ShapeDtypeStruct(w_in.shape, low_type),
        jax.ShapeDtypeStruct((early, slab), low_type),
        jax.ShapeDtypeStruct(factor_in.shape, full_type),
        jax.ShapeDtypeStruct(factor_down.shape, full_type),
        jax.ShapeDtypeStruct((head_slab, width), full_type),
        jax.ShapeDtypeStruct((head_slab, width), low_type),
        jax.ShapeDtypeStruct((1, 2 * slab), full_type),
        jax.ShapeDtypeStruct((1, slab), full_type),
        jax.ShapeDtypeStruct((6, width), full_type),
        jax.ShapeDtypeStruct((4, LANES), jnp.int32),
    ]
    return pl.pallas_call(
        layer_kernel,
        in_specs=[anywhere] * 8 + [vmem] * 4,
        out_specs=[anywhere] * 25 + [vmem] * 6,
        out_shape=shapes,
        scratch_shapes=[
            pltpu.VMEM((2, length, width), low_type),
            pltpu.VMEM(planes.shape, low_type),
            pltpu.VMEM((2, 3, length, head_slab), low_type),
            pltpu.VMEM((head_slab, length), low_type),
            pltpu.VMEM((2, head_slab // DH, length), full_type),
            pltpu.VMEM((2, length, head_slab), low_type),
            pltpu.VMEM((3, share, head_slab), low_type),
            pltpu.VMEM((4,) + w_out.shape, low_type),
            pltpu.VMEM((2,) + w_in.shape, low_type),
            pltpu.VMEM((2 * slab, width), low_type),
            pltpu.VMEM((2, 1, slab), full_type),
            pltpu.VMEM((share, width), low_type),
            pltpu.VMEM((share, width), low_type),
            pltpu.VMEM((share, width), full_type),
            pltpu.VMEM((share, width), full_type),
            pltpu.VMEM((share, 1), full_type),
            pltpu.VMEM((2 * share, width), low_type),
            pltpu.VMEM((2, 2 * share, slab), low_type),
            pltpu.VMEM((2, 2 * share, slab), low_type),
            pltpu.VMEM((share, width), full_type),
            pltpu.VMEM((share, width), full_type),
            pltpu.VMEM((share, width), full_type),
            pltpu.VMEM((share, width), full_type),
            pltpu.VMEM((2 * share, width), low_type),
            pltpu.VMEM((share, width), low_type),
            pltpu.VMEM((slab, width), low_type),
            pltpu.VMEM((3, share, head_slab), low_type),
            pltpu.VMEM((2, share, head_slab), low_type),
            pltpu.VMEM((2 * head_slab, width), full_type),
            pltpu.VMEM((seq_count, length, LANES), full_type),
            pltpu.VMEM((seq_count, 1, length), full_type),
            pltpu.SemaphoreType.DMA((14,)),
            pltpu.SemaphoreType.DMA((28,)),
            pltpu.SemaphoreType.DMA((46,)),
            pltpu.SemaphoreType.DMA((46,)),
        ],
        compiler_params=pltpu.CompilerParams(
            collective_id=3, has_side_effects=True, vmem_limit_bytes=VMEM_GRANT
        ),
        name="layer",
    )(tokens, cotangent, planes, w_out, w_in, w_down, factor_in, factor_down, head_bias, unit_bias,
      vectors, segments)


def layer_general(tokens, segments, w_qkv, head_bias, w_out, w_in, unit_bias, w_down, vectors,
                  cotangent, errors, factors):
    token_count, model_width = tokens.shape
    seq_count, length = segments.shape
    head_slab = w_qkv.shape[2]
    head_count = head_slab // DH
    tensor_size = lax.axis_size("tensor")
    share_rows = token_count // tensor_size
    tensor_place = lax.axis_index("tensor")
    row_start = tensor_place * share_rows
    head_scale = 1.0 / math.sqrt(DH)

    def own_rows(values):
        return lax.dynamic_slice_in_dim(values, row_start, share_rows, 0)

    flat_qkv = w_qkv.reshape(model_width, 3 * head_slab)
    projected = jnp.dot(tokens, flat_qkv, preferred_element_type=jnp.float32).reshape(
        token_count, 3, head_slab
    )
    head_shape = (seq_count, length, head_count, DH)
    queries = (
        ((projected[:, 0] + head_bias[0]) * head_scale).astype(jnp.bfloat16).reshape(head_shape)
    )
    key_heads = projected[:, 1].astype(jnp.bfloat16).reshape(head_shape)
    value_heads = (projected[:, 2] + head_bias[1]).astype(jnp.bfloat16).reshape(head_shape)
    mixed_heads, log_total = lax.map(attend_forward, (queries, key_heads, value_heads, segments))
    mixed_flat = mixed_heads.reshape(token_count, head_slab)
    attn_out = (
        lax.psum(jnp.dot(mixed_flat, w_out, preferred_element_type=jnp.float32), "tensor")
        + vectors[0]
    )
    first_norm, first_normed, first_inverse = norm_forward(
        tokens.astype(jnp.float32) + attn_out, vectors[2], vectors[3]
    )
    first_low = first_norm.astype(jnp.bfloat16)
    hidden = jnp.dot(first_low, w_in, preferred_element_type=jnp.float32) + unit_bias
    active, gelu_back = jax.vjp(partial(jax.nn.gelu, approximate=False), hidden)
    active_low = active.astype(jnp.bfloat16)
    grad_out_share = own_rows(cotangent).astype(jnp.float32)
    summed_input = (
        first_norm
        + lax.psum(jnp.dot(active_low, w_down, preferred_element_type=jnp.float32), "tensor")
        + vectors[1]
    )
    second_norm, second_normed, second_inverse = norm_forward(summed_input, vectors[4], vectors[5])
    layer_out = own_rows(second_norm).astype(jnp.bfloat16)
    grad_sum = norm_backward(
        cotangent.astype(jnp.float32), second_normed, second_inverse, vectors[4]
    )
    grad_branch = grad_sum.astype(jnp.bfloat16)
    second_share = own_rows(second_normed)
    grad_w_down = trans_times(active_low, grad_branch)
    grad_active = times_trans(grad_branch, w_down)
    grad_hidden = gelu_back(grad_active)[0].astype(jnp.bfloat16)
    grad_w_in = trans_times(first_low, grad_hidden)
    grad_units = jnp.sum(grad_hidden.astype(jnp.float32), axis=0)
    grad_first = lax.psum(times_trans(grad_hidden, w_in), "tensor") + grad_sum
    grad_h1 = norm_backward(grad_first, first_normed, first_inverse, vectors[2])
    grad_attn = grad_h1.astype(jnp.bfloat16)
    grad_first_share = own_rows(grad_first)
    first_normed_share = own_rows(first_normed)
    grad_h1_share = own_rows(grad_h1)
    grad_w_out = trans_times(mixed_flat, grad_attn)
    grad_mixed = times_trans(grad_attn, w_out).astype(jnp.bfloat16).reshape(head_shape)
    grad_query, grad_key, grad_value = lax.map(
        attend_backward, (queries, key_heads, value_heads, segments, grad_mixed, log_total)
    )
    grad_query = (
        grad_query.reshape(token_count, head_slab).astype(jnp.float32) * head_scale
    ).astype(jnp.bfloat16)
    grad_key = grad_key.reshape(token_count, head_slab)
    grad_value = grad_value.reshape(token_count, head_slab)
    grad_projected = jnp.stack([grad_query, grad_key, grad_value], axis=1).reshape(
        token_count, 3 * head_slab
    )
    grad_w_qkv = trans_times(tokens, grad_projected)
    grad_heads = jnp.stack(
        [
            jnp.sum(grad_query.astype(jnp.float32), axis=0),
            jnp.sum(grad_value.astype(jnp.float32), axis=0),
        ]
    )
    grad_tokens = (
        lax.psum_scatter(
            times_trans(grad_projected, flat_qkv).astype(jnp.bfloat16),
            "tensor",
            scatter_dimension=0,
            tiled=True,
        ).astype(jnp.float32)
        + grad_h1_share
    )
    local_vectors = jnp.stack(
        [
            jnp.sum(own_rows(grad_attn).astype(jnp.float32), axis=0),
            jnp.sum(own_rows(grad_branch).astype(jnp.float32), axis=0),
            jnp.sum(grad_first_share * first_normed_share, axis=0),
            jnp.sum(grad_first_share, axis=0),
            jnp.sum(grad_out_share * second_share, axis=0),
            jnp.sum(grad_out_share, axis=0),
        ]
    )
    grads = (
        grad_w_qkv.reshape(model_width, 3, head_slab).transpose(1, 0, 2),
        grad_w_out,
        grad_w_in,
        grad_w_down,
    )
    matrices = tuple(grad + error for grad, error in zip(grads, errors))

    def left_of(equation, number):
        return jnp.einsum(equation, factors[number], matrices[number], precision=PRECISE)

    lefts = (
        left_of("gkn,gmn->km", 0), factors[1], left_of("kn,mn->km", 2), left_of("kn,mn->km", 3)
    )
    return (
        layer_out,
        lambda after: grad_tokens,
        matrices,
        lefts,
        local_vectors,
        grad_heads,
        grad_units,
        (),
        (),
    )


def layer_split(tokens, segments, w_qkv, head_bias, w_out, w_in, unit_bias, w_down, vectors,
                cotangent, errors, factors):
    token_count, model_width = tokens.shape
    unit_slab = w_in.shape[1]
    tensor_size = lax.axis_size("tensor")
    share = token_count // tensor_size
    tensor_place = lax.axis_index("tensor")
    core = lax.rem(tensor_place, 2)
    seq = tensor_place // 2

    def to(values, step):
        return lax.ppermute(
            values, "tensor", [(place, place ^ step) for place in range(tensor_size)]
        )

    def rows_at(values, number, size):
        return lax.dynamic_slice_in_dim(values, number * size, size, 0)

    planes = w_qkv.transpose(1, 0, 2)
    (projected, logs, mixed, _, _, _, _, layer_out, low, active, grad_branch, grad_hidden, grad_h1,
     grad_near, far_one, far_two, seg_keys, seg_queries, down_near, down_part, down_rest, in_part, in_head, far_in, far_down,
     out_sum, out_far, units, unit_two, sums, bounds) = layer_call(
        tokens, cotangent, planes, w_out, w_in, w_down, factors[2], factors[3], head_bias,
        unit_bias[None], vectors, segments,
    )
    far_own = to(far_one, 2)
    far_other = to(far_two, 3)
    down_rest = to(down_rest, 2)
    in_near = to(in_head, 2)
    out_back = to(out_far, 2)

    grad_projected, heads_near = attend_back(
        projected, seg_keys, seg_queries, (grad_near, 0), (grad_near, 1), mixed, logs, 1,
        bounds, None, seq, core,
    )
    grad_projected, heads_far = attend_back(
        projected, seg_keys, seg_queries, (far_own, 0), (far_other, 0), mixed, logs, 0,
        bounds, grad_projected, 1 - seq, core,
    )
    token_part = jnp.einsum(
        "gtn,gdn->td", grad_projected, planes, preferred_element_type=jnp.float32
    ).astype(jnp.bfloat16)
    other_one = to(
        jnp.stack([rows_at(token_part, 2 * at + 1 - core, share) for at in (seq, 1 - seq)]), 1
    )
    across_part = rows_at(token_part, 2 * (1 - seq) + core, share).astype(jnp.float32)
    across_part = (across_part + other_one[1].astype(jnp.float32)).astype(jnp.bfloat16)
    own_part = rows_at(token_part, 2 * seq + core, share)

    def finish_tokens(after):
        from_two = to(lax.optimization_barrier((across_part, after))[0], 2)
        return (
            own_part.astype(jnp.float32)
            + other_one[0].astype(jnp.float32)
            + from_two.astype(jnp.float32)
            + grad_h1
        )

    matrix_qkv, left_qkv = product(tokens, grad_projected, errors[0], factors[0])
    matrix_down, left_down = product(active, grad_branch, errors[3], factors[3])
    matrix_in, left_in = product(low, grad_hidden, errors[2], factors[2])
    out_sum, in_near = lax.optimization_barrier((out_sum, in_near))
    matrix_out = out_sum + out_back.astype(jnp.float32) + errors[1]
    return (
        layer_out,
        finish_tokens,
        (matrix_qkv, matrix_out, matrix_in, matrix_down),
        (left_qkv, factors[1], left_in, left_down),
        sums,
        heads_near + heads_far,
        units[0, :unit_slab] + unit_two[0],
        (in_part, down_part, far_in, far_down),
        (in_near, down_near, down_rest),
    )


def local(
    tokens,
    segments,
    w_qkv,
    head_bias,
    w_out,
    w_in,
    unit_bias,
    w_down,
    vectors,
    cotangent,
    err_qkv,
    err_out,
    err_in,
    err_down,
    basis_qkv,
    basis_out,
    basis_in,
    basis_down,
    mom_qkv,
    mom_head_bias,
    mom_out,
    mom_in,
    mom_unit_bias,
    mom_down,
    mom_vectors,
):
    token_count, model_width = tokens.shape
    head_slab = w_qkv.shape[2]
    unit_slab = w_in.shape[1]
    tensor_size = lax.axis_size("tensor")
    replicas = lax.axis_size("dp")
    one_sequence_per_chip = 2 * segments.shape[0] == tensor_size and replicas % 4 == 0
    layer = layer_split if one_sequence_per_chip else layer_general
    planes = (1, 0, 2)
    layer_out, finish_tokens, matrices, lefts, local_vectors, grad_heads, grad_units, far, late = (
        layer(
            tokens, segments, w_qkv, head_bias, w_out, w_in, unit_bias, w_down, vectors, cotangent,
            (err_qkv[0].transpose(planes), err_out[0], err_in[0], err_down[0]),
            (basis_qkv.transpose(planes), basis_out, basis_in, basis_down),
        )
    )
    small = jnp.concatenate(
        [
            local_vectors,
            jnp.pad(grad_units, (0, model_width - unit_slab))[None],
            jnp.pad(grad_heads.reshape(1, 2 * head_slab), ((0, 0), (0, model_width - 2 * head_slab))),
        ],
        axis=0,
    )
    bases, rights, small_sum, late_rest = compress(
        matrices,
        lefts,
        small,
        replicas,
        tensor_size,
        far,
    )
    grad_tokens = finish_tokens(small_sum)
    if late:
        late = (late[0], late_rest[0]) + late[1:]
    step_rate = 0.3 * math.sqrt(replicas / token_count)
    grads, errors, moments, news = update(
        matrices,
        (mom_qkv.transpose(planes), mom_out, mom_in, mom_down),
        (w_qkv.transpose(planes), w_out, w_in, w_down),
        bases,
        rights,
        late,
        step_rate,
    )
    reduced_qkv, rank_out, rank_in, rank_down = (grads[0].transpose(planes),) + tuple(grads[1:])
    new_err_qkv, new_err_out, new_err_in, new_err_down = (
        errors[0].transpose(planes)[None],
        errors[1][None],
        errors[2][None],
        errors[3][None],
    )
    new_mom_qkv, new_mom_out, new_mom_in, new_mom_down = (moments[0].transpose(planes),) + tuple(
        moments[1:]
    )
    new_w_qkv, new_w_out, new_w_in, new_w_down = (news[0].transpose(planes),) + tuple(news[1:])
    right_qkv, right_out, right_in, right_down = rights
    new_basis_qkv = right_qkv.transpose(planes)
    grad_vectors = small_sum[:6]
    grad_unit_bias = small_sum[6, :unit_slab]
    grad_head_bias = small_sum[7, : 2 * head_slab].reshape(2, head_slab)
    new_mom_head_bias = 0.9 * mom_head_bias + grad_head_bias
    new_mom_unit_bias = 0.9 * mom_unit_bias + grad_unit_bias
    new_mom_vectors = 0.9 * mom_vectors + grad_vectors
    new_head_bias = head_bias - step_rate * new_mom_head_bias
    new_unit_bias = unit_bias - step_rate * new_mom_unit_bias
    new_vectors = vectors - step_rate * new_mom_vectors
    return (
        layer_out,
        grad_tokens,
        reduced_qkv,
        grad_head_bias,
        rank_out,
        rank_in,
        grad_unit_bias,
        rank_down,
        grad_vectors,
        new_err_qkv,
        new_err_out,
        new_err_in,
        new_err_down,
        new_basis_qkv,
        right_out,
        right_in,
        right_down,
        new_mom_qkv,
        new_mom_head_bias,
        new_mom_out,
        new_mom_in,
        new_mom_unit_bias,
        new_mom_down,
        new_mom_vectors,
        new_w_qkv,
        new_head_bias,
        new_w_out,
        new_w_in,
        new_unit_bias,
        new_w_down,
        new_vectors,
    )


def solution(mesh):
    in_specs = (
        P("dp", None),
        P("dp", None),
        P(None, None, "tensor"),
        P(None, "tensor"),
        P("tensor", None),
        P(None, "tensor"),
        P("tensor"),
        P("tensor", None),
        P(),
        P("dp", None),
        P("dp", None, None, "tensor"),
        P("dp", "tensor", None),
        P("dp", None, "tensor"),
        P("dp", "tensor", None),
        P(None, None, "tensor"),
        P("tensor", None),
        P(None, "tensor"),
        P("tensor", None),
        P(None, None, "tensor"),
        P(None, "tensor"),
        P("tensor", None),
        P(None, "tensor"),
        P("tensor"),
        P("tensor", None),
        P(),
    )
    out_specs = (
        P(("dp", "tensor"), None),
        P(("dp", "tensor"), None),
        P(None, None, "tensor"),
        P(None, "tensor"),
        P("tensor", None),
        P(None, "tensor"),
        P("tensor"),
        P("tensor", None),
        P(),
        P("dp", None, None, "tensor"),
        P("dp", "tensor", None),
        P("dp", None, "tensor"),
        P("dp", "tensor", None),
        P(None, None, "tensor"),
        P("tensor", None),
        P(None, "tensor"),
        P("tensor", None),
        P(None, None, "tensor"),
        P(None, "tensor"),
        P("tensor", None),
        P(None, "tensor"),
        P("tensor"),
        P("tensor", None),
        P(),
        P(None, None, "tensor"),
        P(None, "tensor"),
        P("tensor", None),
        P(None, "tensor"),
        P("tensor"),
        P("tensor", None),
        P(),
    )
    return jax.shard_map(local, mesh=mesh, in_specs=in_specs, out_specs=out_specs, check_vma=False)
```

```python
from functools import partial
import math

import jax
import jax.numpy as jnp
from jax import lax
from jax.experimental import pallas as pl
from jax.experimental.pallas import tpu as pltpu
from jax.sharding import PartitionSpec as P

DH = 64
LANES = 128
MESH = pl.DeviceIdType.MESH
VMEM_GRANT = 60 << 20
BRIEF = pl.CostEstimate(flops=1, bytes_accessed=1, transcendentals=1)


PRECISE = lax.Precision.HIGHEST
EPS_NORM = 1e-05
EPS_BASIS = 1e-08
MASKED = -1000000000.0


def norm_forward(values, gain, shift):
    row_mean = jnp.mean(values, axis=-1, keepdims=True)
    centred = values - row_mean
    variance = jnp.mean(centred * centred, axis=-1, keepdims=True)
    inverse = lax.rsqrt(variance + EPS_NORM)
    normed = centred * inverse
    return (normed * gain + shift, normed, inverse)


def norm_backward(grad_norm, normed, inverse, gain):
    scaled_grad = grad_norm * gain
    grad_mean = jnp.mean(scaled_grad, axis=-1, keepdims=True)
    along_norm = jnp.mean(scaled_grad * normed, axis=-1, keepdims=True)
    return inverse * (scaled_grad - grad_mean - normed * along_norm)


def times_trans(left_side, right_side):
    return lax.dot_general(
        left_side, right_side, (((1,), (1,)), ((), ())), preferred_element_type=jnp.float32
    )


def trans_times(left_side, right_side):
    return lax.dot_general(
        left_side, right_side, (((0,), (0,)), ((), ())), preferred_element_type=jnp.float32
    )


def split_bf16(values):
    high = values.astype(jnp.bfloat16)
    low = (values - high.astype(jnp.float32)).astype(jnp.bfloat16)
    return high, low


def dot_nt(left_side, right_side):
    return lax.dot_general(
        left_side, right_side, (((1,), (1,)), ((), ())), preferred_element_type=jnp.float32
    )


def dot_nn(left_side, right_side):
    return lax.dot_general(
        left_side, right_side, (((1,), (0,)), ((), ())), preferred_element_type=jnp.float32
    )


def dot_tn(left_side, right_side):
    return lax.dot_general(
        left_side, right_side, (((0,), (0,)), ((), ())), preferred_element_type=jnp.float32
    )


def low_left(factor, matrix):
    both = dot_nt(jnp.concatenate(split_bf16(factor), axis=0), matrix)
    return both[: factor.shape[0]] + both[factor.shape[0] :]


def low_right(basis_rows, matrix):
    both = dot_nn(jnp.concatenate(split_bf16(basis_rows), axis=0), matrix)
    return both[: basis_rows.shape[0]] + both[basis_rows.shape[0] :]


def left_factor(factor, matrix):
    rank_size = factor.shape[0]
    factor_high, factor_low = split_bf16(factor)
    matrix_high, matrix_low = split_bf16(matrix)
    both = dot_nt(jnp.concatenate([factor_high, factor_low], axis=0), matrix_high)
    return both[:rank_size] + both[rank_size:] + dot_nt(factor_high, matrix_low)


def right_factor(basis_rows, matrix):
    rank_size = basis_rows.shape[0]
    basis_high, basis_low = split_bf16(basis_rows)
    matrix_high, matrix_low = split_bf16(matrix)
    both = dot_nn(jnp.concatenate([basis_high, basis_low], axis=0), matrix_high)
    return both[:rank_size] + both[rank_size:] + dot_nn(basis_high, matrix_low)


def place_tiles(target, offset, values):
    per_chunk = target.shape[2] // LANES
    for tile in range(values.shape[1] // LANES):
        spot = offset + tile
        target[spot // per_chunk, :, pl.ds(spot % per_chunk * LANES, LANES)] = values[
            :, tile * LANES : (tile + 1) * LANES
        ]
    return offset + values.shape[1] // LANES


def add_tiles(target, offset, values):
    per_chunk = target.shape[2] // LANES
    for tile in range(values.shape[1] // LANES):
        spot = offset + tile
        target[spot // per_chunk, :, pl.ds(spot % per_chunk * LANES, LANES)] += values[
            :, tile * LANES : (tile + 1) * LANES
        ]


def take_tiles(source, offset, size):
    per_chunk = source.shape[2] // LANES
    pieces = []
    for tile in range(size // LANES):
        spot = offset + tile
        piece = source[spot // per_chunk, :, pl.ds(spot % per_chunk * LANES, LANES)]
        pieces.append(piece.astype(jnp.float32))
    return jnp.concatenate(pieces, axis=1) if len(pieces) > 1 else pieces[0]


def orthonormal_rows(rows):
    rank_size = rows.shape[0]
    row_number = lax.broadcasted_iota(jnp.int32, (rank_size, 1), 0)
    for position in range(rank_size):
        row = rows[position : position + 1]
        length = jnp.sqrt(jnp.sum(row * row, axis=1, keepdims=True)) + EPS_BASIS
        unit = row / length
        along = jnp.sum(rows * unit, axis=1, keepdims=True)
        later = jnp.where(row_number > position, along, 0.0)
        rows = jnp.where(row_number == position, unit, rows - later * unit)
    return rows


def dp_exchange(replicas, mine, wire, arrived, total, sems, meanwhile=None):
    send_one, recv_one, send_two, recv_two = sems
    dp_place = lax.axis_index("dp")
    tensor_place = lax.axis_index("tensor")

    def peer_of(step):
        return lax.rem(dp_place + step, replicas)

    def scatter(step, slot):
        return pltpu.make_async_remote_copy(
            src_ref=wire.at[peer_of(step)],
            dst_ref=arrived.at[slot],
            send_sem=send_one.at[step],
            recv_sem=recv_one.at[slot],
            device_id=(peer_of(step), tensor_place),
            device_id_type=MESH,
        )

    def gather(step, slot):
        return pltpu.make_async_remote_copy(
            src_ref=total.at[dp_place],
            dst_ref=total.at[slot],
            send_sem=send_two.at[step],
            recv_sem=recv_two.at[slot],
            device_id=(peer_of(step), tensor_place),
            device_id_type=MESH,
        )

    def start_scatter(step, carry):
        scatter(step, dp_place).start()
        return carry

    def add_arrived(step, carry):
        scatter(step, peer_of(step)).wait_recv()
        return carry + arrived[peer_of(step)].astype(jnp.float32)

    def start_gather(step, carry):
        gather(step, dp_place).start()
        return carry

    def finish(step, carry):
        gather(step, peer_of(step)).wait_recv()
        return carry

    wire[...] = mine[...].astype(wire.dtype)
    lax.fori_loop(1, replicas, start_scatter, 0)
    total[dp_place] = lax.fori_loop(1, replicas, add_arrived, mine[dp_place]).astype(total.dtype)
    lax.fori_loop(1, replicas, start_gather, 0)
    lax.fori_loop(1, replicas, finish, 0)

    def drain(step, carry):
        scatter(step, dp_place).wait_send()
        gather(step, dp_place).wait_send()
        return carry

    return lambda: lax.fori_loop(1, replicas, drain, 0)


def product_kernel(left_ref, right_ref, err_ref, factor_ref, matrix_ref, factor_out):
    if len(matrix_ref.shape) == 2:
        matrix = dot_tn(left_ref[...], right_ref[...]) + err_ref[...]
        matrix_ref[...] = matrix
        factor_out[...] = left_factor(factor_ref[...], matrix)
    else:
        total = None
        left_rows = left_ref[...].T
        for part in range(matrix_ref.shape[0]):
            matrix = dot_nn(left_rows, right_ref[part]) + err_ref[part]
            matrix_ref[part] = matrix
            piece = left_factor(factor_ref[part], matrix)
            total = piece if total is None else total + piece
        factor_out[...] = total


def product(left_side, right_side, err, factor):
    block = 2 * LANES
    length, rows = left_side.shape
    lead = err.shape[:-2]
    zeros = (0,) * len(lead)

    def whole(array):
        return pl.BlockSpec(array.shape, lambda i: (0,) * array.ndim)

    by_rows = pl.BlockSpec(lead + (block, err.shape[-1]), lambda i: zeros + (i, 0))
    return pl.pallas_call(
        product_kernel,
        grid=(rows // block,),
        in_specs=[
            pl.BlockSpec((length, block), lambda i: (0, i)),
            whole(right_side),
            by_rows,
            whole(factor),
        ],
        out_specs=[by_rows, pl.BlockSpec((factor.shape[-2], block), lambda i: (0, i))],
        out_shape=[
            jax.ShapeDtypeStruct(err.shape, jnp.float32),
            jax.ShapeDtypeStruct((factor.shape[-2], rows), jnp.float32),
        ],
        compiler_params=pltpu.CompilerParams(vmem_limit_bytes=VMEM_GRANT),
        cost_estimate=pl.CostEstimate(flops=10**10, bytes_accessed=10**8, transcendentals=1),
        name="product",
    )(left_side, right_side, err, factor)


def compress_kernel(replicas, tensor_size, has_far, *refs):
    if has_far:
        far_refs, refs, late_ref = refs[:4], refs[4:13] + refs[14:], refs[13]
        compress_body(replicas, tensor_size, far_refs, late_ref, *refs)
    else:
        compress_body(replicas, tensor_size, None, None, *refs)


def compress_body(replicas, tensor_size, far_refs, late_ref, qkv_ref, out_ref, in_ref, down_ref,
                    lq_ref, fo_ref, li_ref, ld_ref, small_ref,
                    bq_ref, bo_ref, bi_ref, bd_ref, rq_ref, ro_ref, ri_ref, rd_ref, sum_ref,
                    qkv, out, inw, down, mine, wire, arrived, total,
                    mine_two, wire_two, arrived_two, total_two, small_slots,
                    load_sem, *sems):
    first_sems, second_sems, (send_small, recv_small) = sems[:4], sems[4:8], sems[8:10]
    dp_place = lax.axis_index("dp")
    tensor_place = lax.axis_index("tensor")
    loads = [
        pltpu.make_async_copy(source, target, load_sem.at[number])
        for number, (source, target) in enumerate(
            [(out_ref, out), (qkv_ref, qkv), (down_ref, down), (in_ref, inw)]
        )
    ]
    if far_refs:
        far_in_ref, far_down_ref, far_factor_in, far_factor_down = far_refs
        far_in, far_down, sent, got, far_send, far_recv = sems[10:]
        opposite = (dp_place, tensor_place + 2 - 4 * (tensor_place // 2))
        head = far_in_ref.shape[0] - late_ref.shape[0]
        cut = head + 2 * LANES

        def bulk(number, start, stop):
            return pltpu.make_async_remote_copy(
                src_ref=far_in_ref.at[pl.ds(start, stop - start)],
                dst_ref=late_ref.at[pl.ds(start - head, stop - start)],
                send_sem=far_send.at[number],
                recv_sem=far_recv.at[number],
                device_id=opposite,
                device_id_type=MESH,
            )

        bulks = [bulk(3, head, cut), bulk(4, cut, far_in_ref.shape[0])]
        far_loads = [
            pltpu.make_async_copy(far_in_ref, far_in, load_sem.at[4]),
            pltpu.make_async_copy(far_down_ref, far_down, load_sem.at[5]),
        ]
        for load in far_loads:
            load.start()

        def far_copy(number):
            return pltpu.make_async_remote_copy(
                src_ref=sent.at[number],
                dst_ref=got.at[number],
                send_sem=far_send.at[number],
                recv_sem=far_recv.at[number],
                device_id=opposite,
                device_id_type=MESH,
            )

    for load in loads:
        load.start()
    barrier = pltpu.get_barrier_semaphore()

    def greet_dp(step, carry):
        pl.semaphore_signal(
            barrier,
            inc=1,
            device_id=(lax.rem(dp_place + step, replicas), tensor_place),
            device_id_type=MESH,
        )
        return carry

    def greet_tensor(step, carry):
        pl.semaphore_signal(
            barrier,
            inc=1,
            device_id=(dp_place, lax.rem(tensor_place + step, tensor_size)),
            device_id_type=MESH,
        )
        return carry

    lax.fori_loop(1, replicas, greet_dp, 0)
    lax.fori_loop(1, tensor_size, greet_tensor, 0)
    mine[...] = jnp.zeros_like(mine)
    mine_two[...] = jnp.zeros_like(mine_two)
    block = 2 * LANES
    if far_refs:
        for number, (factor_ref, matrix) in enumerate(
            ((far_factor_down, far_down), (far_factor_in, far_in))
        ):
            far_loads[1 - number].wait()
            for start in range(0, matrix.shape[0], block):
                rows = slice(start, start + block)
                sent[0, number, :, rows] = low_left(factor_ref[...], matrix[rows])
        pl.semaphore_wait(barrier, replicas - 1 + tensor_size - 1)
        far_copy(0).start()
        bulks[0].start()
    offset = place_tiles(mine, 0, lq_ref[...])
    loads[0].wait()
    offset = place_tiles(mine, offset, left_factor(fo_ref[...], out[...]))
    offset = place_tiles(mine, offset, ld_ref[...])
    offset = place_tiles(mine, offset, li_ref[...])
    place_tiles(mine, offset, small_ref[...])
    if far_refs:
        far_copy(0).wait_recv()
        add_tiles(mine, offset - 2 * down.shape[0] // LANES, got[0, 0])
        add_tiles(mine, offset - inw.shape[0] // LANES, got[0, 1])
    else:
        pl.semaphore_wait(barrier, replicas - 1 + tensor_size - 1)
    drain_one = dp_exchange(replicas, mine, wire, arrived, total, first_sems)

    def slot_copy(step, slot):
        peer = lax.rem(tensor_place + step, tensor_size)
        return pltpu.make_async_remote_copy(
            src_ref=small_slots.at[tensor_place],
            dst_ref=small_slots.at[slot],
            send_sem=send_small.at[step],
            recv_sem=recv_small.at[slot],
            device_id=(dp_place, peer),
            device_id_type=MESH,
        )

    def start_small(step, carry):
        slot_copy(step, tensor_place).start()
        return carry

    own_small = take_tiles(total, offset, small_ref.shape[1])
    small_slots[tensor_place] = own_small
    lax.fori_loop(1, tensor_size, start_small, 0)
    offset = 0
    offset_two = 0
    offsets = []
    for basis_ref in (bq_ref, bo_ref, bd_ref, bi_ref):
        offsets.append(offset)
        offset += basis_ref.shape[1] // LANES
    for number in (2, 3, 0, 1):
        basis_ref = (bq_ref, bo_ref, bd_ref, bi_ref)[number]
        rows = take_tiles(total, offsets[number], basis_ref.shape[1]) * (1.0 / replicas)
        basis_ref[...] = orthonormal_rows(rows)
        if far_refs and number >= 2:
            sent[1, number - 2] = basis_ref[...]
        if far_refs and number == 3:
            far_copy(1).start()
    drain_one()
    for load in loads[1:]:
        load.wait()
    for part in range(3):
        right = right_factor(bq_ref[:, :block], qkv[part, :block])
        for start in range(block, qkv.shape[1], block):
            rows = slice(start, start + block)
            right += right_factor(bq_ref[:, rows], qkv[part, rows])
        offset_two = place_tiles(mine_two, offset_two, right)
    for basis_ref, matrix in zip((bo_ref, bd_ref, bi_ref), (out, down, inw)):
        rows_of = min(block, matrix.shape[0])
        right = right_factor(basis_ref[:, :rows_of], matrix[:rows_of])
        for start in range(rows_of, matrix.shape[0], rows_of):
            rows = slice(start, start + rows_of)
            right += right_factor(basis_ref[:, rows], matrix[rows])
        offset_two = place_tiles(mine_two, offset_two, right)
    if far_refs:
        far_copy(1).wait_recv()
        sent[2, 0] = low_right(got[1, 0], far_down[...])
        sent[2, 1] = low_right(got[1, 1], far_in[...])
        far_copy(2).start()
        bulks[1].start()
        far_copy(2).wait_recv()
        add_tiles(mine_two, offset_two - (down.shape[1] + inw.shape[1]) // LANES, got[2, 0])
        add_tiles(mine_two, offset_two - inw.shape[1] // LANES, got[2, 1])
    drain_two = dp_exchange(
        replicas, mine_two, wire_two, arrived_two, total_two, second_sems
    )

    def collect(step, carry):
        peer = lax.rem(tensor_place + step, tensor_size)
        slot_copy(step, peer).wait_recv()
        slot_copy(step, tensor_place).wait_send()
        return carry + small_slots[peer]

    everyone = lax.fori_loop(1, tensor_size, collect, own_small)
    row_number = lax.broadcasted_iota(jnp.int32, everyone.shape, 0)
    sum_ref[...] = jnp.where(row_number < 6, everyone, own_small) * (1.0 / replicas)
    offset = 0
    for part in range(3):
        rq_ref[part] = take_tiles(total_two, offset, rq_ref.shape[2]) * (1.0 / replicas)
        offset += rq_ref.shape[2] // LANES
    for ref in (ro_ref, rd_ref, ri_ref):
        ref[...] = take_tiles(total_two, offset, ref.shape[1]) * (1.0 / replicas)
        offset += ref.shape[1] // LANES
    drain_two()
    if far_refs:
        for number in range(3):
            far_copy(number).wait_send()
        for copy in bulks:
            copy.wait()


def compress(matrices, lefts, small, replicas, tensor_size, far):
    qkv, out, inw, down = matrices
    rank_size = small.shape[0]
    sizes = (qkv.shape[1], out.shape[0], inw.shape[0], down.shape[0])
    right_shapes = [(3, rank_size, qkv.shape[2])] + [(rank_size, one.shape[1]) for one in matrices[1:]]
    lanes_one = sum(sizes) + small.shape[1]
    lanes_two = 3 * qkv.shape[2] + sum(one.shape[1] for one in matrices[1:])
    scratch = [pltpu.VMEM(one.shape, jnp.float32) for one in matrices]
    for lanes in (lanes_one, lanes_two):
        shape = (replicas, rank_size, -(-lanes // (LANES * replicas)) * LANES)
        scratch += [
            pltpu.VMEM(shape, jnp.float32),
            pltpu.VMEM(shape, jnp.bfloat16),
            pltpu.VMEM(shape, jnp.bfloat16),
            pltpu.VMEM(shape, jnp.bfloat16),
        ]
    scratch += [pltpu.VMEM((tensor_size,) + small.shape, jnp.float32), pltpu.SemaphoreType.DMA((6,))]
    scratch += [pltpu.SemaphoreType.DMA((replicas,))] * 8
    scratch += [pltpu.SemaphoreType.DMA((tensor_size,))] * 2
    if far:
        scratch += [pltpu.VMEM(one.shape, one.dtype) for one in far[:2]]
        scratch += [pltpu.VMEM((3, 2, rank_size, inw.shape[0]), jnp.float32)] * 2
        scratch += [pltpu.SemaphoreType.DMA((5,))] * 2
    vmem = pl.BlockSpec(memory_space=pltpu.VMEM)
    shapes = [(rank_size, size) for size in sizes] + right_shapes + [small.shape]
    shapes = [jax.ShapeDtypeStruct(shape, jnp.float32) for shape in shapes]
    late_shape = []
    if far:
        late_shape = [jax.ShapeDtypeStruct((inw.shape[0] // 2, inw.shape[1]), far[0].dtype)]
    outputs = pl.pallas_call(
        partial(compress_kernel, replicas, tensor_size, bool(far)),
        in_specs=([pl.BlockSpec(memory_space=pl.ANY)] * 2 + [vmem] * 2 if far else [])
        + [pl.BlockSpec(memory_space=pl.ANY)] * 4
        + [vmem] * 5,
        out_specs=[pl.BlockSpec(memory_space=pl.ANY)] * len(late_shape) + [vmem] * 9,
        out_shape=late_shape + shapes,
        scratch_shapes=scratch,
        compiler_params=pltpu.CompilerParams(
            collective_id=1, has_side_effects=True, vmem_limit_bytes=VMEM_GRANT
        ),
        name="compress",
    )(*far, *matrices, *lefts, small)
    late, outputs = outputs[:-9], outputs[-9:]
    return outputs[:4], outputs[4:8], outputs[8], late


def outer_of(basis_rows, right):
    basis_high, basis_low = split_bf16(basis_rows)
    right_high, right_low = split_bf16(right)
    return dot_tn(
        jnp.concatenate([basis_high, basis_low, basis_high], axis=0),
        jnp.concatenate([right_high, right_high, right_low], axis=0),
    )


def update_kernel(step_rate, out_steps, near_steps, *refs):
    (mq, mo, mi, md, oq, oo, oi, od, wq, wo, wi, wd, bq, bo, bi, bd, rq, ro, ri, rd,
     gq, go, gi, gd, eq, eo, ei, ed, nq, no, ni, nd, vq, vo, vi, vd) = refs[:20] + refs[-16:]
    step = pl.program_id(0)
    whole_in, whole_down = mi[...], md[...]
    if len(refs) > 36:
        near_in, rest_in, near_down, rest_down = refs[20:24]
        whole_in += jnp.where(step < near_steps, near_in[...], rest_in[...]).astype(jnp.float32)
        whole_down += jnp.where(step < near_steps, near_down[...], rest_down[...]).astype(
            jnp.float32
        )

    def one(matrix, old, weight, rank, grad_ref, err_ref, mom_ref, new_ref, place):
        moment = 0.9 * old + rank
        grad_ref[place] = rank
        err_ref[place] = matrix - rank
        mom_ref[place] = moment
        new_ref[place] = weight.astype(jnp.float32) - step_rate * moment

    def lanes_of(ref, rows):
        return ref[:, pl.ds(pl.multiple_of(step * rows, LANES), rows)]

    rows = mq.shape[1]
    for part in range(3):
        rank = outer_of(lanes_of(bq, rows), rq[part])
        one(mq[part], oq[part], wq[part], rank, gq, eq, nq, vq, part)
    rank = outer_of(lanes_of(bi, mi.shape[0]), ri[...])
    one(whole_in, oi[...], wi[...], rank, gi, ei, ni, vi, slice(None))
    rank = outer_of(lanes_of(bd, md.shape[0]), rd[...])
    one(whole_down, od[...], wd[...], rank, gd, ed, nd, vd, slice(None))

    @pl.when(step < out_steps)
    def _():
        rank = outer_of(lanes_of(bo, mo.shape[0]), ro[...])
        one(mo[...], oo[...], wo[...], rank, go, eo, no, vo, slice(None))


def update(matrices, momenta, weights, bases, rights, late, step_rate):
    qkv, out, inw, down = matrices
    rows = LANES
    steps = inw.shape[0] // rows
    down_rows = down.shape[0] // steps
    if down_rows < LANES:
        steps = down.shape[0] // LANES
        rows, down_rows = inw.shape[0] // steps, LANES
    out_steps = out.shape[0] // LANES
    near_steps = late[0].shape[0] // rows if late else 0
    late_specs = [
        pl.BlockSpec((rows, inw.shape[1]), lambda i: (jnp.minimum(i, near_steps - 1), 0)),
        pl.BlockSpec((rows, inw.shape[1]), lambda i: (jnp.maximum(i - near_steps, 0), 0)),
        pl.BlockSpec((down_rows, down.shape[1]), lambda i: (jnp.minimum(i, near_steps - 1), 0)),
        pl.BlockSpec((down_rows, down.shape[1]), lambda i: (jnp.maximum(i - near_steps, 0), 0)),
    ]

    def whole(array):
        return pl.BlockSpec(array.shape, lambda i: (0,) * array.ndim)

    def specs():
        return [
            pl.BlockSpec((3, rows, qkv.shape[2]), lambda i: (0, i, 0)),
            pl.BlockSpec((LANES, out.shape[1]), lambda i: (jnp.minimum(i, out_steps - 1), 0)),
            pl.BlockSpec((rows, inw.shape[1]), lambda i: (i, 0)),
            pl.BlockSpec((down_rows, down.shape[1]), lambda i: (i, 0)),
        ]

    shapes = [jax.ShapeDtypeStruct(one.shape, jnp.float32) for one in matrices]
    outputs = pl.pallas_call(
        partial(update_kernel, step_rate, out_steps, near_steps),
        grid=(steps,),
        in_specs=specs() * 3
        + [whole(one) for one in bases]
        + [whole(one) for one in rights]
        + late_specs[: len(late)],
        out_specs=specs() * 4,
        out_shape=shapes * 4,
        compiler_params=pltpu.CompilerParams(vmem_limit_bytes=VMEM_GRANT),
        name="update",
    )(*matrices, *momenta, *weights, *bases, *rights, *late)
    return outputs[0:4], outputs[4:8], outputs[8:12], outputs[12:16]


def masked_scores(queries, key_heads, seg_ids):
    scores = jnp.einsum("qhd,khd->hqk", queries, key_heads, preferred_element_type=jnp.float32)
    same_doc = seg_ids[:, None] == seg_ids[None, :]
    return jnp.where(same_doc[None], scores, MASKED)


def attend_forward(inputs_of):
    queries, key_heads, value_heads, seg_ids = inputs_of
    scores = masked_scores(queries, key_heads, seg_ids)
    highest = jnp.max(scores, axis=-1, keepdims=True)
    powers = jnp.exp(scores - highest)
    denominator = jnp.sum(powers, axis=-1, keepdims=True)
    weights = (powers / denominator).astype(jnp.bfloat16)
    mixed_heads = jnp.einsum(
        "hqk,khd->qhd", weights, value_heads, preferred_element_type=jnp.float32
    )
    return (mixed_heads.astype(jnp.bfloat16), highest[..., 0] + jnp.log(denominator[..., 0]))


def attend_backward(inputs_of):
    queries, key_heads, value_heads, seg_ids, grad_mixed, log_total = inputs_of
    scores = masked_scores(queries, key_heads, seg_ids)
    probability = jnp.exp(scores - log_total[..., None])
    grad_probs = jnp.einsum(
        "qhd,khd->hqk", grad_mixed, value_heads, preferred_element_type=jnp.float32
    )
    centre = jnp.sum(probability * grad_probs, axis=-1, keepdims=True)
    grad_scores = (probability * (grad_probs - centre)).astype(jnp.bfloat16)
    grad_query = jnp.einsum(
        "hqk,khd->qhd", grad_scores, key_heads, preferred_element_type=jnp.float32
    )
    grad_key = jnp.einsum("hqk,qhd->khd", grad_scores, queries, preferred_element_type=jnp.float32)
    grad_value = jnp.einsum(
        "hqk,qhd->khd",
        probability.astype(jnp.bfloat16),
        grad_mixed,
        preferred_element_type=jnp.float32,
    )
    return (
        grad_query.astype(jnp.bfloat16),
        grad_key.astype(jnp.bfloat16),
        grad_value.astype(jnp.bfloat16),
    )


def stacked_heads(pair, lane_is_low):
    zero = jnp.zeros_like(pair)
    return jnp.concatenate(
        [jnp.where(lane_is_low, pair, zero), jnp.where(lane_is_low, zero, pair)], axis=0
    )


def own_blocks(both):
    rows = both.shape[1] // 2
    return jnp.concatenate([both[:DH, :rows], both[DH:, rows:]], axis=0).T


def window_sizes(length):
    return (length * 3 // 8, length * 5 // 8, length)


def windows_of(bounds, length):
    first = bounds[0] // LANES * LANES
    need = bounds[1] - first
    small, large, whole = window_sizes(length)
    number = jnp.where(need <= small, 0, jnp.where(need <= large, 1, 2))
    room = jnp.where(need <= small, length - small, jnp.where(need <= large, length - large, 0))
    return jnp.concatenate([jnp.minimum(first, room), number])


def attend_back_kernel(place_ref, q_ref, k_ref, v_ref, seg_key_ref, seg_query_ref, gm_own_ref,
                       gm_other_ref, mixed_ref, log_ref, old_ref, grad_ref, sums_ref, key_t, grad_key,
                       grad_value):
    del old_ref
    step = pl.program_id(0)

    @pl.when(step == 0)
    def _():
        key_t[...] = k_ref[...].T
        grad_key[...] = jnp.zeros_like(grad_key)
        grad_value[...] = jnp.zeros_like(grad_value)

    pairs = q_ref.shape[1] // LANES
    lane = lax.broadcasted_iota(jnp.int32, (1, LANES), 1)
    lane_is_low = lane < DH
    head_of_lane = (
        lax.broadcasted_iota(jnp.int32, (8, LANES), 0)
        == lax.broadcasted_iota(jnp.int32, (8, LANES), 1) // DH
    ).astype(jnp.bfloat16)
    head_scale = 1.0 / math.sqrt(DH)
    here = pl.ds(pl.multiple_of(step * LANES, LANES), LANES)
    is_own = lax.rem(step // (pl.num_programs(0) // 2) + place_ref[1], 2) == 0
    gm = jnp.where(is_own, gm_own_ref[...], gm_other_ref[...])
    seg_query = jnp.concatenate([seg_query_ref[...], seg_query_ref[...]], axis=1)
    all_lanes = [slice(pair * LANES, (pair + 1) * LANES) for pair in range(pairs)]
    length = k_ref.shape[0]

    def window(size):
        start = 0 if size == length else pl.multiple_of(place_ref[2 + step], LANES)
        keys = pl.ds(start, size)
        seg_key = seg_key_ref[keys]
        same = jnp.concatenate([seg_key, seg_key], axis=1) == seg_query
        queries, grads, centres, probs, grad_probs = [], [], [], [], []
        for lanes in all_lanes:
            queries.append(stacked_heads(q_ref[:, lanes], lane_is_low))
            grads.append(stacked_heads(gm[:, lanes], lane_is_low))
            high, low = split_bf16(
                gm[:, lanes].astype(jnp.float32) * mixed_ref[:, lanes].astype(jnp.float32)
            )
            sums = dot_nt(head_of_lane, high) + dot_nt(head_of_lane, low)
            centres.append(jnp.concatenate([sums[0:1], sums[1:2]], axis=1))
        for pair, lanes in enumerate(all_lanes):
            log_total = jnp.concatenate(
                [log_ref[2 * pair : 2 * pair + 1], log_ref[2 * pair + 1 : 2 * pair + 2]], axis=1
            )
            scores = dot_nt(k_ref[keys, lanes], queries[pair])
            probs.append(jnp.exp(jnp.where(same, scores - log_total, MASKED)))
            grad_probs.append(dot_nt(v_ref[keys, lanes], grads[pair]))
        for pair, lanes in enumerate(all_lanes):
            grad_scores = (probs[pair] * (grad_probs[pair] - centres[pair])).astype(jnp.bfloat16)
            grad_value[keys, lanes] += dot_nn(probs[pair].astype(jnp.bfloat16), grads[pair])
            grad_key[keys, lanes] += dot_nn(grad_scores, queries[pair])
            grad_query = own_blocks(dot_nn(key_t[lanes, keys], grad_scores)).astype(jnp.bfloat16)
            grad_ref[0, here, lanes] = (grad_query.astype(jnp.float32) * head_scale).astype(
                jnp.bfloat16
            )

    for number, size in enumerate(window_sizes(length)):
        pl.when(place_ref[2 + pl.num_programs(0) + step] == number)(partial(window, size))

    @pl.when(step == pl.num_programs(0) - 1)
    def _():
        grad_ref[1] = grad_key[...].astype(jnp.bfloat16)
        low_value = grad_value[...].astype(jnp.bfloat16)
        grad_ref[2] = low_value
        sums_ref[0:1] = jnp.sum(grad_ref[0].astype(jnp.float32), axis=0, keepdims=True)
        sums_ref[1:2] = jnp.sum(low_value.astype(jnp.float32), axis=0, keepdims=True)


def attend_back(projected, seg_keys, seg_queries, grad_own, grad_other, mixed, logs, slot, bounds,
                old, place, core):
    length = seg_keys.shape[1]
    slab = projected.shape[2]
    blocks = length // LANES
    half = blocks // 2
    at = jnp.concatenate(
        [
            jnp.stack([place, core]),
            windows_of(bounds[2 * slot : 2 * slot + 2, :blocks], length),
        ]
    )
    grid_spec = pltpu.PrefetchScalarGridSpec(
        num_scalar_prefetch=1,
        grid=(blocks,),
        in_specs=[
            pl.BlockSpec((None, LANES, slab), lambda i, at: (0, at[0] * blocks + i, 0)),
            pl.BlockSpec((None, length, slab), lambda i, at: (1, at[0], 0)),
            pl.BlockSpec((None, length, slab), lambda i, at: (2, at[0], 0)),
            pl.BlockSpec((None, length, LANES), lambda i, at: (at[0], 0, 0)),
            pl.BlockSpec((None, 1, LANES), lambda i, at: (at[0], 0, i)),
            pl.BlockSpec((None, LANES, slab), lambda i, at: (grad_own[1], lax.rem(i, half), 0)),
            pl.BlockSpec((None, LANES, slab), lambda i, at: (grad_other[1], lax.rem(i, half), 0)),
            pl.BlockSpec((None, LANES, slab), lambda i, at: (slot, i, 0)),
            pl.BlockSpec((None, slab // DH, LANES), lambda i, at: (slot, 0, i)),
            pl.BlockSpec(memory_space=pl.ANY),
        ],
        out_specs=[
            pl.BlockSpec((3, length, slab), lambda i, at: (0, at[0], 0)),
            pl.BlockSpec((2, slab), lambda i, at: (0, 0)),
        ],
        scratch_shapes=[
            pltpu.VMEM((slab, length), jnp.bfloat16),
            pltpu.VMEM((length, slab), jnp.float32),
            pltpu.VMEM((length, slab), jnp.float32),
        ],
    )
    return pl.pallas_call(
        attend_back_kernel,
        grid_spec=grid_spec,
        out_shape=[
            jax.ShapeDtypeStruct(projected.shape, jnp.bfloat16),
            jax.ShapeDtypeStruct((2, slab), jnp.float32),
        ],
        input_output_aliases={} if old is None else {10: 0},
        compiler_params=pltpu.CompilerParams(vmem_limit_bytes=24 << 20),
        cost_estimate=BRIEF,
        name="attend_back",
    )(at, projected, projected, projected, seg_keys, seg_queries, grad_own[0],
      grad_other[0], mixed, logs, seg_keys if old is None else old)


def row_mean(values):
    return jnp.mean(values, axis=-1, keepdims=True)


def layer_kernel(tokens, cotangent, w_qkv_ref, out_ref, in_ref, down_ref,
                 factor_in_ref, factor_down_ref, head_ref, bias_ref, vec_ref, segments,
                 projected_out, log_out, mixed_out, in_two, down_two, out_rest, bias_two,
                 result_out, low_out, active_out, branch_out, hidden_out, norm_out, near_out,
                 far_one_out, far_two_out, keys_out, rows_out, down_near, down_part_out, down_rest, in_part_out, in_head,
                 far_in_out, far_down_out, out_sum,
                 out_far, unit_ref, unit_two, sums_ref, bounds_ref,
                 rows_in, w_qkv, projected, value_t, log_total, mixed, pieces,
                 w_out, w_in, w_down, bias, tok, cot, first, normed, inverse, low, slope, active,
                 part, other, acc, wide, branch, result, down_part, near, far_mixed, outs_two,
                 seg_keys, seg_queries, load_sem, store_sem, send_sem, recv_sem):
    dp_place = lax.axis_index("dp")
    tensor_place = lax.axis_index("tensor")
    core = lax.rem(tensor_place, 2)
    seq = tensor_place // 2
    far = 1 - seq
    side = lax.rem(dp_place, 2)
    depth = lax.rem(dp_place // 2, 2)
    here = 2 * depth + side
    sibling = (dp_place, tensor_place + 1 - 2 * core)
    opposite = (dp_place, core + 2 * far)
    diagonal = (dp_place, 1 - core + 2 * far)
    beside = (dp_place + 1 - 2 * side, tensor_place)
    behind = (dp_place + 2 - 4 * depth, tensor_place)
    share, width = tok.shape
    slab = in_ref.shape[1]
    length = rows_in.shape[1]
    head_slab = w_qkv.shape[2]
    head_count = head_slab // DH
    stores = []
    sends = []
    numbers = iter(range(send_sem.shape[0]))

    def load_later(number, source, target):
        return pltpu.make_async_copy(source, target, load_sem.at[number])

    def load(number, source, target):
        copy = load_later(number, source, target)
        copy.start()
        return copy

    def store(source, target):
        copy = pltpu.make_async_copy(source, target, store_sem.at[len(stores)])
        copy.start()
        stores.append(copy)

    def send_later(source, target, device):
        number = next(numbers)
        copy = pltpu.make_async_remote_copy(
            src_ref=source,
            dst_ref=target,
            send_sem=send_sem.at[number],
            recv_sem=recv_sem.at[number],
            device_id=device,
            device_id_type=MESH,
        )
        sends.append(copy)
        return copy

    def send(source, target, device):
        copy = send_later(source, target, device)
        copy.start()
        return copy

    def rows_of(number, size):
        return pl.ds(pl.multiple_of(number * size, LANES), size)

    load_qkv = load(0, w_qkv_ref, w_qkv)
    load_far = load(1, tokens.at[rows_of(far, length)], rows_in.at[0])
    load_near = load(2, tokens.at[rows_of(seq, length)], rows_in.at[1])
    load_out = load(3, out_ref, w_out.at[0])
    load_in = load(4, in_ref, w_in.at[0])
    load_down = load(5, down_ref, w_down.at[pl.ds(0, slab)])
    load_tok = load(6, tokens.at[rows_of(tensor_place, share)], tok)
    load_cot = load(7, cotangent.at[rows_of(tensor_place, share)], cot)

    barrier = pltpu.get_barrier_semaphore()
    for device in (sibling, opposite, diagonal, beside, behind):
        pl.semaphore_signal(barrier, inc=1, device_id=device, device_id_type=MESH)
    pl.semaphore_wait(barrier, 5)
    sums_ref[...] = jnp.zeros_like(sums_ref)
    unit_ref[...] = jnp.zeros_like(unit_ref)

    def rows_part(whole, number, parts):
        size = whole.shape[0] // parts
        return whole.at[pl.ds(pl.multiple_of(number * size, size), size)]

    class Fetch:
        def __init__(self, source, whole):
            own = rows_part(whole, here, 4)
            half_one = rows_part(whole, 2 * (here + 1 - 2 * side), 8)
            half_two = rows_part(whole, 2 * (here + 2 - 4 * depth) + 1, 8)
            self.over_y = send_later(rows_part(source, here, 4), own, opposite)
            self.over_x = send_later(own, own, beside)
            self.over_z = send_later(own, own, behind)
            self.half_z = send_later(half_one, half_one, behind)
            self.half_x = send_later(half_two, half_two, beside)

        def start(self):
            self.over_y.start()

        def pass_on(self):
            self.over_y.wait_recv()
            self.over_x.start()
            self.over_z.start()

        def pass_halves(self):
            self.over_x.wait_recv()
            self.half_z.start()
            self.over_z.wait_recv()
            self.half_x.start()

        def wait(self):
            self.half_z.wait_recv()
            self.half_x.wait_recv()

    bias_send = send(bias_ref, bias_two, opposite)
    factor_sends = [
        send(factor_in_ref, far_in_out, opposite), send(factor_down_ref, far_down_out, opposite)
    ]
    fetch_out = Fetch(out_ref, out_rest.at[1])
    upper, lower = pl.ds(0, width // 2), pl.ds(width // 2, width // 2)
    fetch_in = [Fetch(in_ref.at[rows], in_two.at[rows]) for rows in (upper, lower)]
    upper, lower = pl.ds(0, slab // 2), pl.ds(slab // 2, slab // 2)
    fetch_down = [Fetch(down_ref.at[rows], down_two.at[rows]) for rows in (upper, lower)]
    fetch_out.start()
    fetch_in[0].start()
    fetch_in[1].start()
    fetch_down[0].start()

    chunk = 256
    scale = 1.0 / math.sqrt(DH)

    def project(slot):
        def rows_step(step, carry):
            rows = rows_of(step, chunk)
            values = rows_in[slot, rows]
            projected[slot, 0, rows] = (
                (dot_nn(values, w_qkv[0]) + head_ref[0:1]) * scale
            ).astype(jnp.bfloat16)
            projected[slot, 1, rows] = dot_nn(values, w_qkv[1]).astype(jnp.bfloat16)
            projected[slot, 2, rows] = (dot_nn(values, w_qkv[2]) + head_ref[1:2]).astype(
                jnp.bfloat16
            )
            return carry

        lax.fori_loop(0, length // chunk, rows_step, 0)
        value_t[...] = projected[slot, 2].T

    lane_is_low = lax.broadcasted_iota(jnp.int32, (1, LANES), 1) < DH

    def attend_rows(slot, place, tasks):
        def block(step):
            rows = rows_of(step, LANES)
            same = seg_keys[place] == seg_queries[place, :, rows]
            mask = jnp.where(same, 0.0, MASKED)
            mask = jnp.concatenate([mask, mask], axis=1)
            all_lanes = [slice(at, at + LANES) for at in range(0, head_slab, LANES)]
            all_scores = [
                dot_nt(
                    projected[slot, 1, :, lanes],
                    stacked_heads(projected[slot, 0, rows, lanes], lane_is_low),
                )
                + mask
                for lanes in all_lanes
            ]
            for pair, (lanes, scores) in enumerate(zip(all_lanes, all_scores)):
                highest = jnp.max(scores, axis=0, keepdims=True)
                powers = jnp.exp(scores - highest)
                denominator = jnp.sum(powers, axis=0, keepdims=True)
                blend = dot_nn(value_t[lanes], powers.astype(jnp.bfloat16))
                mixed[slot, rows, lanes] = own_blocks(blend * (1.0 / denominator)).astype(
                    jnp.bfloat16
                )
                total = highest + jnp.log(denominator)
                log_total[slot, 2 * pair : 2 * pair + 1, rows] = total[:, :LANES]
                log_total[slot, 2 * pair + 1 : 2 * pair + 2, rows] = total[:, LANES:]

        def two_blocks(step, carry):
            for number, task in tasks:
                pl.when(step == number)(task)
            block(2 * step)
            block(2 * step + 1)
            return carry

        lax.fori_loop(0, length // LANES // 2, two_blocks, 0)

    for number in range(segments.shape[0]):
        documents = segments[number : number + 1].astype(jnp.float32)
        seg_queries[number] = documents
        seg_keys[number] = jnp.broadcast_to(documents, (LANES, length)).T
    store(seg_keys, keys_out)
    store(seg_queries, rows_out)
    load_qkv.wait()
    load_far.wait()
    project(0)
    attend_rows(0, far, [(2, fetch_out.pass_on)])
    fetch_in[0].pass_on()
    own_rows = rows_of(core, share)
    sibling_rows = rows_of(1 - core, share)
    piece_two = send(mixed.at[0, own_rows], pieces.at[1], opposite)
    piece_three = send(mixed.at[0, sibling_rows], pieces.at[2], diagonal)
    fetch_down[1].start()
    store(projected.at[0, 0], projected_out.at[0, rows_of(far, length)])
    store(projected.at[0, 1], projected_out.at[1, rows_of(far, length)])
    store(projected.at[0, 2], projected_out.at[2, rows_of(far, length)])
    load_near.wait()
    project(1)
    out_pass = [
        send_later(out_ref, out_rest.at[0], sibling),
        send_later(out_rest.at[1], out_rest.at[2], sibling),
    ]
    load_two = load_later(8, out_rest.at[1], w_out.at[2])

    def pass_in():
        fetch_in[1].pass_on()
        fetch_in[0].pass_halves()

    def pass_out():
        fetch_out.wait()
        for copy in out_pass:
            copy.start()
        load_two.start()

    attend_rows(1, seq, [(0, fetch_out.pass_halves), (2, pass_in), (3, pass_out)])
    piece_one = send(mixed.at[1, sibling_rows], pieces.at[0], sibling)
    store(projected.at[1, 0], projected_out.at[0, rows_of(seq, length)])
    store(projected.at[1, 1], projected_out.at[1, rows_of(seq, length)])
    store(projected.at[1, 2], projected_out.at[2, rows_of(seq, length)])
    store(log_total, log_out)
    for copy in out_pass:
        copy.wait_recv()
    load_one = load(9, out_rest.at[0], w_out.at[1])
    load_three = load(10, out_rest.at[2], w_out.at[3])
    store(mixed, mixed_out)
    fetch_down[0].pass_on()
    fetch_in[1].pass_halves()
    for copy in (load_out, load_tok, load_one, load_two, load_three):
        copy.wait()
    for copy in (piece_two, piece_three, piece_one):
        copy.wait_recv()
    small = 64

    def attn_rows(step, carry):
        rows = rows_of(step, chunk)
        total = dot_nn(mixed[1, pl.ds(pl.multiple_of(core * share + step * chunk, LANES), chunk)],
                       w_out[0])
        for piece in range(3):
            total += dot_nn(pieces[piece, rows], w_out[piece + 1])
        acc[rows] = total
        return carry

    def first_rows(step, carry):
        rows = pl.ds(pl.multiple_of(step * small, small), small)
        values = tok[rows].astype(jnp.float32) + (acc[rows] + vec_ref[0:1])
        centred = values - row_mean(values)
        spread = lax.rsqrt(row_mean(centred * centred) + EPS_NORM)
        unit = centred * spread
        normed[rows] = unit
        inverse[rows] = spread
        shifted = unit * vec_ref[2:3] + vec_ref[3:4]
        first[rows] = shifted
        low[rows] = shifted.astype(jnp.bfloat16)
        return carry

    lax.fori_loop(0, share // chunk, attn_rows, 0)
    lax.fori_loop(0, share // small, first_rows, 0)
    slots = [slice(0, share), slice(share, 2 * share)]
    low_send = send(low.at[slots[0]], low.at[slots[1]], sibling)
    fetch_down[0].pass_halves()
    load_in.wait()

    def hidden_of(slot, owner):
        def units(step, carry):
            inner = rows_of(step, chunk)
            values = dot_nn(low[slots[slot]], w_in[owner, :, inner]) + bias[owner, :, inner]
            share_of = 0.5 * (1.0 + lax.erf(values * math.sqrt(0.5)))
            density = jnp.exp(-0.5 * values * values) * (1.0 / math.sqrt(2.0 * math.pi))
            active[owner, slots[slot], inner] = (values * share_of).astype(jnp.bfloat16)
            slope[owner, slots[slot], inner] = (share_of - 0.5 + values * density).astype(jnp.bfloat16)
            return carry

        lax.fori_loop(0, slab // chunk, units, 0)

    def branch_of(slot, owner, target, start, size):
        units = slice(owner * slab, (owner + 1) * slab)

        def columns(step, carry):
            at = pl.ds(pl.multiple_of(start + step * chunk, chunk), chunk)
            values = dot_nn(active[owner, slots[slot]], w_down[units, at])
            target[:, at] = values if owner == 0 else target[:, at] + values
            return carry

        lax.fori_loop(0, size // chunk, columns, 0)

    bias_send.wait_recv()
    bias[0] = bias_ref[...]
    load_bias = load(11, bias_two, bias.at[1])
    hidden_of(0, 0)
    low_send.wait_recv()
    store(low, low_out)
    fetch_down[1].pass_on()
    hidden_of(1, 0)
    for fetch in fetch_in:
        fetch.wait()
    load_in_two = load(12, in_two, w_in.at[1])
    load_down.wait()
    branch_of(1, 0, part, 0, width)
    branch_of(0, 0, acc, 0, width)
    load_bias.wait()
    load_in_two.wait()
    fetch_down[1].pass_halves()
    hidden_of(1, 1)
    hidden_of(0, 1)
    store(active.at[0], active_out)
    lane = lax.broadcasted_iota(jnp.int32, (1, LANES), 1)
    for slot, place in ((0, far), (1, seq)):
        firsts = jnp.zeros((1, LANES), jnp.float32)
        lasts = jnp.zeros((1, LANES), jnp.float32)
        for block in range(length // LANES):
            start = block * LANES
            firsts = jnp.where(lane == block, seg_keys[place, start : start + 1], firsts)
            lasts = jnp.where(
                lane == block, seg_keys[place, start + LANES - 1 : start + LANES], lasts
            )
        documents = seg_keys[place]
        bounds_ref[2 * slot : 2 * slot + 1] = jnp.sum(
            jnp.where(documents < firsts, 1.0, 0.0), axis=0, keepdims=True
        ).astype(jnp.int32)
        bounds_ref[2 * slot + 1 : 2 * slot + 2] = jnp.sum(
            jnp.where(documents <= lasts, 1.0, 0.0), axis=0, keepdims=True
        ).astype(jnp.int32)
    for fetch in fetch_down:
        fetch.wait()
    load_down_two = load(13, down_two, w_down.at[pl.ds(slab, slab)])
    load_down_two.wait()
    half = width // 2
    part_sends = []
    for number in range(2):
        branch_of(1, 1, part, number * half, half)
        columns = slice(number * half, (number + 1) * half)
        part_sends.append(send(part.at[:, columns], other.at[:, columns], sibling))
    branch_of(0, 1, acc, 0, width)
    load_cot.wait()
    for copy in part_sends:
        copy.wait_recv()

    def second_rows(step, carry):
        rows = pl.ds(pl.multiple_of(step * small, small), small)
        values = first[rows] + (acc[rows] + other[rows]) + vec_ref[1:2]
        centred = values - row_mean(values)
        spread = lax.rsqrt(row_mean(centred * centred) + EPS_NORM)
        unit = centred * spread
        result[rows] = (unit * vec_ref[4:5] + vec_ref[5:6]).astype(jnp.bfloat16)
        upper = cot[rows].astype(jnp.float32)
        scaled = upper * vec_ref[4:5]
        grad = spread * (scaled - row_mean(scaled) - unit * row_mean(scaled * unit))
        wide[rows] = grad
        grad_low = grad.astype(jnp.bfloat16)
        branch[rows] = grad_low
        sums_ref[1:2] += jnp.sum(grad_low.astype(jnp.float32), axis=0, keepdims=True)
        sums_ref[4:5] += jnp.sum(upper * unit, axis=0, keepdims=True)
        sums_ref[5:6] += jnp.sum(upper, axis=0, keepdims=True)
        return carry

    branch_sends = []
    for number in range(2):
        steps = share // small // 2
        lax.fori_loop(number * steps, (number + 1) * steps, second_rows, 0)
        rows = slice(number * steps * small, (number + 1) * steps * small)
        there = slice(share + rows.start, share + rows.stop)
        branch_sends.append(send(branch.at[rows], branch.at[there], sibling))
    store(result, result_out)
    hidden = rows_in

    def grad_hidden_of(slot, owner):
        def units(step, carry):
            inner = rows_of(step, chunk)
            outer = pl.ds(pl.multiple_of(owner * slab + step * chunk, chunk), chunk)
            grad = dot_nt(branch[slots[slot]], w_down[outer]) * (
                0.5 + slope[owner, slots[slot], inner].astype(jnp.float32)
            )
            grad_low = grad.astype(jnp.bfloat16)
            hidden[owner, slots[slot], inner] = grad_low
            unit_ref[:, outer] += jnp.sum(grad_low.astype(jnp.float32), axis=0, keepdims=True)
            return carry

        lax.fori_loop(0, slab // chunk, units, 0)

    def grad_first_of(slot, target, start, size):
        def columns(step, carry):
            at = pl.ds(pl.multiple_of(start + step * chunk, chunk), chunk)
            target[:, at] = dot_nt(hidden[0, slots[slot]], w_in[0, at]) + dot_nt(
                hidden[1, slots[slot]], w_in[1, at]
            )
            return carry

        lax.fori_loop(0, size // chunk, columns, 0)

    def far_product(left_side, right_side, target, start, stop):
        def rows_step(step, carry):
            at = rows_of(step, LANES)
            target[at] = dot_tn(left_side[:, at], right_side[...]).astype(jnp.bfloat16)
            return carry

        lax.fori_loop(start // LANES, stop // LANES, rows_step, 0)

    grad_hidden_of(0, 0)
    grad_hidden_of(0, 1)
    for copy in branch_sends:
        copy.wait_recv()
    store(branch, branch_out)
    early = down_near.shape[0]
    far_product(active.at[1], branch, down_part, 0, early)
    down_send = send(down_part.at[pl.ds(0, early)], down_near, opposite)
    far_product(active.at[1], branch, down_part, early, slab)
    store(down_part, down_part_out)
    store(down_part.at[pl.ds(early, slab - early)], down_rest)
    grad_hidden_of(1, 0)
    grad_hidden_of(1, 1)
    unit_send = send(unit_ref.at[:, pl.ds(slab, slab)], unit_two, opposite)
    store(hidden.at[0], hidden_out)
    for copy in part_sends:
        copy.wait_send()
    sends[:] = [one for one in sends if all(one is not copy for copy in part_sends)]
    first_sends = []
    for number in range(2):
        grad_first_of(1, part, number * half, half)
        columns = slice(number * half, (number + 1) * half)
        first_sends.append(send(part.at[:, columns], other.at[:, columns], sibling))
    grad_first_of(0, acc, 0, width)
    for copy in first_sends:
        copy.wait_recv()

    def back_rows(step, carry):
        rows = pl.ds(pl.multiple_of(step * small, small), small)
        grad = acc[rows] + other[rows] + wide[rows]
        unit = normed[rows]
        scaled = grad * vec_ref[2:3]
        back = inverse[rows] * (scaled - row_mean(scaled) - unit * row_mean(scaled * unit))
        acc[rows] = back
        back_low = back.astype(jnp.bfloat16)
        tok[rows] = back_low
        sums_ref[0:1] += jnp.sum(back_low.astype(jnp.float32), axis=0, keepdims=True)
        sums_ref[2:3] += jnp.sum(grad * unit, axis=0, keepdims=True)
        sums_ref[3:4] += jnp.sum(grad, axis=0, keepdims=True)
        return carry

    lax.fori_loop(0, share // small, back_rows, 0)
    store(acc, norm_out)
    attn = tok[...]
    near[1] = dot_nt(attn, w_out[1]).astype(jnp.bfloat16)
    near_send = send(near.at[1], near.at[2], sibling)
    out_one = slice(0, head_slab)
    out_three = slice(head_slab, 2 * head_slab)
    first[out_one] = dot_tn(pieces[0], attn)
    first[out_three] = dot_tn(pieces[2], attn)
    outs_send = send(first.at[pl.ds(0, 2 * head_slab)], outs_two, sibling)
    far_mixed[0] = dot_nt(attn, w_out[2]).astype(jnp.bfloat16)
    far_mixed[1] = dot_nt(attn, w_out[3]).astype(jnp.bfloat16)
    store(far_mixed.at[0], far_one_out.at[0])
    store(far_mixed.at[1], far_two_out.at[0])
    near[0] = dot_nt(attn, w_out[0]).astype(jnp.bfloat16)
    store(near.at[0], near_out.at[0])
    far_product(low, hidden.at[1], active.at[1], 0, width)
    store(active.at[1], in_part_out)
    store(active.at[1, pl.ds(0, in_head.shape[0])], in_head)
    near_send.wait_recv()
    store(near.at[2], near_out.at[1])
    outs_send.wait_recv()
    out_sum[...] = dot_tn(mixed[1, own_rows], attn) + outs_two[out_one]
    out_far[...] = (dot_tn(pieces[1], attn) + outs_two[out_three]).astype(jnp.bfloat16)
    unit_send.wait_recv()
    down_send.wait_recv()
    for copy in factor_sends:
        copy.wait_recv()
    for copy in sends:
        copy.wait_send()
    for copy in stores:
        copy.wait()


def layer_call(tokens, cotangent, planes, w_out, w_in, w_down, factor_in, factor_down, head_bias,
               unit_bias, vectors, segments):
    token_count, width = tokens.shape
    seq_count, length = segments.shape
    share = token_count // (2 * seq_count)
    head_slab = planes.shape[2]
    slab = w_in.shape[1]
    early = slab // 2
    low_type, full_type = jnp.bfloat16, jnp.float32
    vmem = pl.BlockSpec(memory_space=pltpu.VMEM)
    anywhere = pl.BlockSpec(memory_space=pl.ANY)
    shapes = [
        jax.ShapeDtypeStruct((3, token_count, head_slab), low_type),
        jax.ShapeDtypeStruct((2, head_slab // DH, length), full_type),
        jax.ShapeDtypeStruct((2, length, head_slab), low_type),
        jax.ShapeDtypeStruct(w_in.shape, low_type),
        jax.ShapeDtypeStruct(w_down.shape, low_type),
        jax.ShapeDtypeStruct((3,) + w_out.shape, low_type),
        jax.ShapeDtypeStruct((1, slab), full_type),
        jax.ShapeDtypeStruct((share, width), low_type),
        jax.ShapeDtypeStruct((2 * share, width), low_type),
        jax.ShapeDtypeStruct((2 * share, slab), low_type),
        jax.ShapeDtypeStruct((2 * share, width), low_type),
        jax.ShapeDtypeStruct((2 * share, slab), low_type),
        jax.ShapeDtypeStruct((share, width), full_type),
        jax.ShapeDtypeStruct((2, share, head_slab), low_type),
        jax.ShapeDtypeStruct((1, share, head_slab), low_type),
        jax.ShapeDtypeStruct((1, share, head_slab), low_type),
        jax.ShapeDtypeStruct((seq_count, length, LANES), full_type),
        jax.ShapeDtypeStruct((seq_count, 1, length), full_type),
        jax.ShapeDtypeStruct((early, width), low_type),
        jax.ShapeDtypeStruct((slab, width), low_type),
        jax.ShapeDtypeStruct((slab - early, width), low_type),
        jax.ShapeDtypeStruct(w_in.shape, low_type),
        jax.ShapeDtypeStruct((early, slab), low_type),
        jax.ShapeDtypeStruct(factor_in.shape, full_type),
        jax.ShapeDtypeStruct(factor_down.shape, full_type),
        jax.ShapeDtypeStruct((head_slab, width), full_type),
        jax.ShapeDtypeStruct((head_slab, width), low_type),
        jax.ShapeDtypeStruct((1, 2 * slab), full_type),
        jax.ShapeDtypeStruct((1, slab), full_type),
        jax.ShapeDtypeStruct((6, width), full_type),
        jax.ShapeDtypeStruct((4, LANES), jnp.int32),
    ]
    return pl.pallas_call(
        layer_kernel,
        in_specs=[anywhere] * 8 + [vmem] * 4,
        out_specs=[anywhere] * 25 + [vmem] * 6,
        out_shape=shapes,
        scratch_shapes=[
            pltpu.VMEM((2, length, width), low_type),
            pltpu.VMEM(planes.shape, low_type),
            pltpu.VMEM((2, 3, length, head_slab), low_type),
            pltpu.VMEM((head_slab, length), low_type),
            pltpu.VMEM((2, head_slab // DH, length), full_type),
            pltpu.VMEM((2, length, head_slab), low_type),
            pltpu.VMEM((3, share, head_slab), low_type),
            pltpu.VMEM((4,) + w_out.shape, low_type),
            pltpu.VMEM((2,) + w_in.shape, low_type),
            pltpu.VMEM((2 * slab, width), low_type),
            pltpu.VMEM((2, 1, slab), full_type),
            pltpu.VMEM((share, width), low_type),
            pltpu.VMEM((share, width), low_type),
            pltpu.VMEM((share, width), full_type),
            pltpu.VMEM((share, width), full_type),
            pltpu.VMEM((share, 1), full_type),
            pltpu.VMEM((2 * share, width), low_type),
            pltpu.VMEM((2, 2 * share, slab), low_type),
            pltpu.VMEM((2, 2 * share, slab), low_type),
            pltpu.VMEM((share, width), full_type),
            pltpu.VMEM((share, width), full_type),
            pltpu.VMEM((share, width), full_type),
            pltpu.VMEM((share, width), full_type),
            pltpu.VMEM((2 * share, width), low_type),
            pltpu.VMEM((share, width), low_type),
            pltpu.VMEM((slab, width), low_type),
            pltpu.VMEM((3, share, head_slab), low_type),
            pltpu.VMEM((2, share, head_slab), low_type),
            pltpu.VMEM((2 * head_slab, width), full_type),
            pltpu.VMEM((seq_count, length, LANES), full_type),
            pltpu.VMEM((seq_count, 1, length), full_type),
            pltpu.SemaphoreType.DMA((14,)),
            pltpu.SemaphoreType.DMA((28,)),
            pltpu.SemaphoreType.DMA((46,)),
            pltpu.SemaphoreType.DMA((46,)),
        ],
        compiler_params=pltpu.CompilerParams(
            collective_id=3, has_side_effects=True, vmem_limit_bytes=VMEM_GRANT
        ),
        name="layer",
    )(tokens, cotangent, planes, w_out, w_in, w_down, factor_in, factor_down, head_bias, unit_bias,
      vectors, segments)


def layer_general(tokens, segments, w_qkv, head_bias, w_out, w_in, unit_bias, w_down, vectors,
                  cotangent, errors, factors):
    token_count, model_width = tokens.shape
    seq_count, length = segments.shape
    head_slab = w_qkv.shape[2]
    head_count = head_slab // DH
    tensor_size = lax.axis_size("tensor")
    share_rows = token_count // tensor_size
    tensor_place = lax.axis_index("tensor")
    row_start = tensor_place * share_rows
    head_scale = 1.0 / math.sqrt(DH)

    def own_rows(values):
        return lax.dynamic_slice_in_dim(values, row_start, share_rows, 0)

    flat_qkv = w_qkv.reshape(model_width, 3 * head_slab)
    projected = jnp.dot(tokens, flat_qkv, preferred_element_type=jnp.float32).reshape(
        token_count, 3, head_slab
    )
    head_shape = (seq_count, length, head_count, DH)
    queries = (
        ((projected[:, 0] + head_bias[0]) * head_scale).astype(jnp.bfloat16).reshape(head_shape)
    )
    key_heads = projected[:, 1].astype(jnp.bfloat16).reshape(head_shape)
    value_heads = (projected[:, 2] + head_bias[1]).astype(jnp.bfloat16).reshape(head_shape)
    mixed_heads, log_total = lax.map(attend_forward, (queries, key_heads, value_heads, segments))
    mixed_flat = mixed_heads.reshape(token_count, head_slab)
    attn_out = (
        lax.psum(jnp.dot(mixed_flat, w_out, preferred_element_type=jnp.float32), "tensor")
        + vectors[0]
    )
    first_norm, first_normed, first_inverse = norm_forward(
        tokens.astype(jnp.float32) + attn_out, vectors[2], vectors[3]
    )
    first_low = first_norm.astype(jnp.bfloat16)
    hidden = jnp.dot(first_low, w_in, preferred_element_type=jnp.float32) + unit_bias
    active, gelu_back = jax.vjp(partial(jax.nn.gelu, approximate=False), hidden)
    active_low = active.astype(jnp.bfloat16)
    grad_out_share = own_rows(cotangent).astype(jnp.float32)
    summed_input = (
        first_norm
        + lax.psum(jnp.dot(active_low, w_down, preferred_element_type=jnp.float32), "tensor")
        + vectors[1]
    )
    second_norm, second_normed, second_inverse = norm_forward(summed_input, vectors[4], vectors[5])
    layer_out = own_rows(second_norm).astype(jnp.bfloat16)
    grad_sum = norm_backward(
        cotangent.astype(jnp.float32), second_normed, second_inverse, vectors[4]
    )
    grad_branch = grad_sum.astype(jnp.bfloat16)
    second_share = own_rows(second_normed)
    grad_w_down = trans_times(active_low, grad_branch)
    grad_active = times_trans(grad_branch, w_down)
    grad_hidden = gelu_back(grad_active)[0].astype(jnp.bfloat16)
    grad_w_in = trans_times(first_low, grad_hidden)
    grad_units = jnp.sum(grad_hidden.astype(jnp.float32), axis=0)
    grad_first = lax.psum(times_trans(grad_hidden, w_in), "tensor") + grad_sum
    grad_h1 = norm_backward(grad_first, first_normed, first_inverse, vectors[2])
    grad_attn = grad_h1.astype(jnp.bfloat16)
    grad_first_share = own_rows(grad_first)
    first_normed_share = own_rows(first_normed)
    grad_h1_share = own_rows(grad_h1)
    grad_w_out = trans_times(mixed_flat, grad_attn)
    grad_mixed = times_trans(grad_attn, w_out).astype(jnp.bfloat16).reshape(head_shape)
    grad_query, grad_key, grad_value = lax.map(
        attend_backward, (queries, key_heads, value_heads, segments, grad_mixed, log_total)
    )
    grad_query = (
        grad_query.reshape(token_count, head_slab).astype(jnp.float32) * head_scale
    ).astype(jnp.bfloat16)
    grad_key = grad_key.reshape(token_count, head_slab)
    grad_value = grad_value.reshape(token_count, head_slab)
    grad_projected = jnp.stack([grad_query, grad_key, grad_value], axis=1).reshape(
        token_count, 3 * head_slab
    )
    grad_w_qkv = trans_times(tokens, grad_projected)
    grad_heads = jnp.stack(
        [
            jnp.sum(grad_query.astype(jnp.float32), axis=0),
            jnp.sum(grad_value.astype(jnp.float32), axis=0),
        ]
    )
    grad_tokens = (
        lax.psum_scatter(
            times_trans(grad_projected, flat_qkv).astype(jnp.bfloat16),
            "tensor",
            scatter_dimension=0,
            tiled=True,
        ).astype(jnp.float32)
        + grad_h1_share
    )
    local_vectors = jnp.stack(
        [
            jnp.sum(own_rows(grad_attn).astype(jnp.float32), axis=0),
            jnp.sum(own_rows(grad_branch).astype(jnp.float32), axis=0),
            jnp.sum(grad_first_share * first_normed_share, axis=0),
            jnp.sum(grad_first_share, axis=0),
            jnp.sum(grad_out_share * second_share, axis=0),
            jnp.sum(grad_out_share, axis=0),
        ]
    )
    grads = (
        grad_w_qkv.reshape(model_width, 3, head_slab).transpose(1, 0, 2),
        grad_w_out,
        grad_w_in,
        grad_w_down,
    )
    matrices = tuple(grad + error for grad, error in zip(grads, errors))

    def left_of(equation, number):
        return jnp.einsum(equation, factors[number], matrices[number], precision=PRECISE)

    lefts = (
        left_of("gkn,gmn->km", 0), factors[1], left_of("kn,mn->km", 2), left_of("kn,mn->km", 3)
    )
    return (
        layer_out,
        lambda after: grad_tokens,
        matrices,
        lefts,
        local_vectors,
        grad_heads,
        grad_units,
        (),
        (),
    )


def layer_split(tokens, segments, w_qkv, head_bias, w_out, w_in, unit_bias, w_down, vectors,
                cotangent, errors, factors):
    token_count, model_width = tokens.shape
    unit_slab = w_in.shape[1]
    tensor_size = lax.axis_size("tensor")
    share = token_count // tensor_size
    tensor_place = lax.axis_index("tensor")
    core = lax.rem(tensor_place, 2)
    seq = tensor_place // 2

    def to(values, step):
        return lax.ppermute(
            values, "tensor", [(place, place ^ step) for place in range(tensor_size)]
        )

    def rows_at(values, number, size):
        return lax.dynamic_slice_in_dim(values, number * size, size, 0)

    planes = w_qkv.transpose(1, 0, 2)
    (projected, logs, mixed, _, _, _, _, layer_out, low, active, grad_branch, grad_hidden, grad_h1,
     grad_near, far_one, far_two, seg_keys, seg_queries, down_near, down_part, down_rest, in_part, in_head, far_in, far_down,
     out_sum, out_far, units, unit_two, sums, bounds) = layer_call(
        tokens, cotangent, planes, w_out, w_in, w_down, factors[2], factors[3], head_bias,
        unit_bias[None], vectors, segments,
    )
    far_own = to(far_one, 2)
    far_other = to(far_two, 3)
    down_rest = to(down_rest, 2)
    in_near = to(in_head, 2)
    out_back = to(out_far, 2)

    grad_projected, heads_near = attend_back(
        projected, seg_keys, seg_queries, (grad_near, 0), (grad_near, 1), mixed, logs, 1,
        bounds, None, seq, core,
    )
    grad_projected, heads_far = attend_back(
        projected, seg_keys, seg_queries, (far_own, 0), (far_other, 0), mixed, logs, 0,
        bounds, grad_projected, 1 - seq, core,
    )
    token_part = jnp.einsum(
        "gtn,gdn->td", grad_projected, planes, preferred_element_type=jnp.float32
    ).astype(jnp.bfloat16)
    other_one = to(
        jnp.stack([rows_at(token_part, 2 * at + 1 - core, share) for at in (seq, 1 - seq)]), 1
    )
    across_part = rows_at(token_part, 2 * (1 - seq) + core, share).astype(jnp.float32)
    across_part = (across_part + other_one[1].astype(jnp.float32)).astype(jnp.bfloat16)
    own_part = rows_at(token_part, 2 * seq + core, share)

    def finish_tokens(after):
        from_two = to(lax.optimization_barrier((across_part, after))[0], 2)
        return (
            own_part.astype(jnp.float32)
            + other_one[0].astype(jnp.float32)
            + from_two.astype(jnp.float32)
            + grad_h1
        )

    matrix_qkv, left_qkv = product(tokens, grad_projected, errors[0], factors[0])
    matrix_down, left_down = product(active, grad_branch, errors[3], factors[3])
    matrix_in, left_in = product(low, grad_hidden, errors[2], factors[2])
    out_sum, in_near = lax.optimization_barrier((out_sum, in_near))
    matrix_out = out_sum + out_back.astype(jnp.float32) + errors[1]
    return (
        layer_out,
        finish_tokens,
        (matrix_qkv, matrix_out, matrix_in, matrix_down),
        (left_qkv, factors[1], left_in, left_down),
        sums,
        heads_near + heads_far,
        units[0, :unit_slab] + unit_two[0],
        (in_part, down_part, far_in, far_down),
        (in_near, down_near, down_rest),
    )


def local(
    tokens,
    segments,
    w_qkv,
    head_bias,
    w_out,
    w_in,
    unit_bias,
    w_down,
    vectors,
    cotangent,
    err_qkv,
    err_out,
    err_in,
    err_down,
    basis_qkv,
    basis_out,
    basis_in,
    basis_down,
    mom_qkv,
    mom_head_bias,
    mom_out,
    mom_in,
    mom_unit_bias,
    mom_down,
    mom_vectors,
):
    token_count, model_width = tokens.shape
    head_slab = w_qkv.shape[2]
    unit_slab = w_in.shape[1]
    tensor_size = lax.axis_size("tensor")
    replicas = lax.axis_size("dp")
    one_sequence_per_chip = 2 * segments.shape[0] == tensor_size and replicas % 4 == 0
    layer = layer_split if one_sequence_per_chip else layer_general
    planes = (1, 0, 2)
    layer_out, finish_tokens, matrices, lefts, local_vectors, grad_heads, grad_units, far, late = (
        layer(
            tokens, segments, w_qkv, head_bias, w_out, w_in, unit_bias, w_down, vectors, cotangent,
            (err_qkv[0].transpose(planes), err_out[0], err_in[0], err_down[0]),
            (basis_qkv.transpose(planes), basis_out, basis_in, basis_down),
        )
    )
    small = jnp.concatenate(
        [
            local_vectors,
            jnp.pad(grad_units, (0, model_width - unit_slab))[None],
            jnp.pad(grad_heads.reshape(1, 2 * head_slab), ((0, 0), (0, model_width - 2 * head_slab))),
        ],
        axis=0,
    )
    bases, rights, small_sum, late_rest = compress(
        matrices,
        lefts,
        small,
        replicas,
        tensor_size,
        far,
    )
    grad_tokens = finish_tokens(small_sum)
    if late:
        late = (late[0], late_rest[0]) + late[1:]
    step_rate = 0.3 * math.sqrt(replicas / token_count)
    grads, errors, moments, news = update(
        matrices,
        (mom_qkv.transpose(planes), mom_out, mom_in, mom_down),
        (w_qkv.transpose(planes), w_out, w_in, w_down),
        bases,
        rights,
        late,
        step_rate,
    )
    reduced_qkv, rank_out, rank_in, rank_down = (grads[0].transpose(planes),) + tuple(grads[1:])
    new_err_qkv, new_err_out, new_err_in, new_err_down = (
        errors[0].transpose(planes)[None],
        errors[1][None],
        errors[2][None],
        errors[3][None],
    )
    new_mom_qkv, new_mom_out, new_mom_in, new_mom_down = (moments[0].transpose(planes),) + tuple(
        moments[1:]
    )
    new_w_qkv, new_w_out, new_w_in, new_w_down = (news[0].transpose(planes),) + tuple(news[1:])
    right_qkv, right_out, right_in, right_down = rights
    new_basis_qkv = right_qkv.transpose(planes)
    grad_vectors = small_sum[:6]
    grad_unit_bias = small_sum[6, :unit_slab]
    grad_head_bias = small_sum[7, : 2 * head_slab].reshape(2, head_slab)
    new_mom_head_bias = 0.9 * mom_head_bias + grad_head_bias
    new_mom_unit_bias = 0.9 * mom_unit_bias + grad_unit_bias
    new_mom_vectors = 0.9 * mom_vectors + grad_vectors
    new_head_bias = head_bias - step_rate * new_mom_head_bias
    new_unit_bias = unit_bias - step_rate * new_mom_unit_bias
    new_vectors = vectors - step_rate * new_mom_vectors
    return (
        layer_out,
        grad_tokens,
        reduced_qkv,
        grad_head_bias,
        rank_out,
        rank_in,
        grad_unit_bias,
        rank_down,
        grad_vectors,
        new_err_qkv,
        new_err_out,
        new_err_in,
        new_err_down,
        new_basis_qkv,
        right_out,
        right_in,
        right_down,
        new_mom_qkv,
        new_mom_head_bias,
        new_mom_out,
        new_mom_in,
        new_mom_unit_bias,
        new_mom_down,
        new_mom_vectors,
        new_w_qkv,
        new_head_bias,
        new_w_out,
        new_w_in,
        new_unit_bias,
        new_w_down,
        new_vectors,
    )


def solution(mesh):
    in_specs = (
        P("dp", None),
        P("dp", None),
        P(None, None, "tensor"),
        P(None, "tensor"),
        P("tensor", None),
        P(None, "tensor"),
        P("tensor"),
        P("tensor", None),
        P(),
        P("dp", None),
        P("dp", None, None, "tensor"),
        P("dp", "tensor", None),
        P("dp", None, "tensor"),
        P("dp", "tensor", None),
        P(None, None, "tensor"),
        P("tensor", None),
        P(None, "tensor"),
        P("tensor", None),
        P(None, None, "tensor"),
        P(None, "tensor"),
        P("tensor", None),
        P(None, "tensor"),
        P("tensor"),
        P("tensor", None),
        P(),
    )
    out_specs = (
        P(("dp", "tensor"), None),
        P(("dp", "tensor"), None),
        P(None, None, "tensor"),
        P(None, "tensor"),
        P("tensor", None),
        P(None, "tensor"),
        P("tensor"),
        P("tensor", None),
        P(),
        P("dp", None, None, "tensor"),
        P("dp", "tensor", None),
        P("dp", None, "tensor"),
        P("dp", "tensor", None),
        P(None, None, "tensor"),
        P("tensor", None),
        P(None, "tensor"),
        P("tensor", None),
        P(None, None, "tensor"),
        P(None, "tensor"),
        P("tensor", None),
        P(None, "tensor"),
        P("tensor"),
        P("tensor", None),
        P(),
        P(None, None, "tensor"),
        P(None, "tensor"),
        P("tensor", None),
        P(None, "tensor"),
        P("tensor"),
        P("tensor", None),
        P(),
    )
    return jax.shard_map(local, mesh=mesh, in_specs=in_specs, out_specs=out_specs, check_vma=False)
```

```python
from functools import partial
import math

import jax
import jax.numpy as jnp
from jax import lax
from jax.experimental import pallas as pl
from jax.experimental.pallas import tpu as pltpu
from jax.sharding import PartitionSpec as P

DH = 64
LANES = 128
MESH = pl.DeviceIdType.MESH
VMEM_GRANT = 60 << 20
BRIEF = pl.CostEstimate(flops=1, bytes_accessed=1, transcendentals=1)


PRECISE = lax.Precision.HIGHEST
EPS_NORM = 1e-05
EPS_BASIS = 1e-08
MASKED = -1000000000.0


def norm_forward(values, gain, shift):
    row_mean = jnp.mean(values, axis=-1, keepdims=True)
    centred = values - row_mean
    variance = jnp.mean(centred * centred, axis=-1, keepdims=True)
    inverse = lax.rsqrt(variance + EPS_NORM)
    normed = centred * inverse
    return (normed * gain + shift, normed, inverse)


def norm_backward(grad_norm, normed, inverse, gain):
    scaled_grad = grad_norm * gain
    grad_mean = jnp.mean(scaled_grad, axis=-1, keepdims=True)
    along_norm = jnp.mean(scaled_grad * normed, axis=-1, keepdims=True)
    return inverse * (scaled_grad - grad_mean - normed * along_norm)


def times_trans(left_side, right_side):
    return lax.dot_general(
        left_side, right_side, (((1,), (1,)), ((), ())), preferred_element_type=jnp.float32
    )


def trans_times(left_side, right_side):
    return lax.dot_general(
        left_side, right_side, (((0,), (0,)), ((), ())), preferred_element_type=jnp.float32
    )


def split_bf16(values):
    high = values.astype(jnp.bfloat16)
    low = (values - high.astype(jnp.float32)).astype(jnp.bfloat16)
    return high, low


def dot_nt(left_side, right_side):
    return lax.dot_general(
        left_side, right_side, (((1,), (1,)), ((), ())), preferred_element_type=jnp.float32
    )


def dot_nn(left_side, right_side):
    return lax.dot_general(
        left_side, right_side, (((1,), (0,)), ((), ())), preferred_element_type=jnp.float32
    )


def dot_tn(left_side, right_side):
    return lax.dot_general(
        left_side, right_side, (((0,), (0,)), ((), ())), preferred_element_type=jnp.float32
    )


def low_left(factor, matrix):
    both = dot_nt(jnp.concatenate(split_bf16(factor), axis=0), matrix)
    return both[: factor.shape[0]] + both[factor.shape[0] :]


def low_right(basis_rows, matrix):
    both = dot_nn(jnp.concatenate(split_bf16(basis_rows), axis=0), matrix)
    return both[: basis_rows.shape[0]] + both[basis_rows.shape[0] :]


def left_factor(factor, matrix):
    rank_size = factor.shape[0]
    factor_high, factor_low = split_bf16(factor)
    matrix_high, matrix_low = split_bf16(matrix)
    both = dot_nt(jnp.concatenate([factor_high, factor_low], axis=0), matrix_high)
    return both[:rank_size] + both[rank_size:] + dot_nt(factor_high, matrix_low)


def right_factor(basis_rows, matrix):
    rank_size = basis_rows.shape[0]
    basis_high, basis_low = split_bf16(basis_rows)
    matrix_high, matrix_low = split_bf16(matrix)
    both = dot_nn(jnp.concatenate([basis_high, basis_low], axis=0), matrix_high)
    return both[:rank_size] + both[rank_size:] + dot_nn(basis_high, matrix_low)


def place_tiles(target, offset, values):
    per_chunk = target.shape[2] // LANES
    for tile in range(values.shape[1] // LANES):
        spot = offset + tile
        target[spot // per_chunk, :, pl.ds(spot % per_chunk * LANES, LANES)] = values[
            :, tile * LANES : (tile + 1) * LANES
        ]
    return offset + values.shape[1] // LANES


def add_tiles(target, offset, values):
    per_chunk = target.shape[2] // LANES
    for tile in range(values.shape[1] // LANES):
        spot = offset + tile
        target[spot // per_chunk, :, pl.ds(spot % per_chunk * LANES, LANES)] += values[
            :, tile * LANES : (tile + 1) * LANES
        ]


def take_tiles(source, offset, size):
    per_chunk = source.shape[2] // LANES
    pieces = []
    for tile in range(size // LANES):
        spot = offset + tile
        piece = source[spot // per_chunk, :, pl.ds(spot % per_chunk * LANES, LANES)]
        pieces.append(piece.astype(jnp.float32))
    return jnp.concatenate(pieces, axis=1) if len(pieces) > 1 else pieces[0]


def orthonormal_rows(rows):
    rank_size = rows.shape[0]
    row_number = lax.broadcasted_iota(jnp.int32, (rank_size, 1), 0)
    for position in range(rank_size):
        row = rows[position : position + 1]
        length = jnp.sqrt(jnp.sum(row * row, axis=1, keepdims=True)) + EPS_BASIS
        unit = row / length
        along = jnp.sum(rows * unit, axis=1, keepdims=True)
        later = jnp.where(row_number > position, along, 0.0)
        rows = jnp.where(row_number == position, unit, rows - later * unit)
    return rows


def dp_exchange(replicas, mine, wire, arrived, total, sems, meanwhile=None):
    send_one, recv_one, send_two, recv_two = sems
    dp_place = lax.axis_index("dp")
    tensor_place = lax.axis_index("tensor")

    def peer_of(step):
        return lax.rem(dp_place + step, replicas)

    def scatter(step, slot):
        return pltpu.make_async_remote_copy(
            src_ref=wire.at[peer_of(step)],
            dst_ref=arrived.at[slot],
            send_sem=send_one.at[step],
            recv_sem=recv_one.at[slot],
            device_id=(peer_of(step), tensor_place),
            device_id_type=MESH,
        )

    def gather(step, slot):
        return pltpu.make_async_remote_copy(
            src_ref=total.at[dp_place],
            dst_ref=total.at[slot],
            send_sem=send_two.at[step],
            recv_sem=recv_two.at[slot],
            device_id=(peer_of(step), tensor_place),
            device_id_type=MESH,
        )

    def start_scatter(step, carry):
        scatter(step, dp_place).start()
        return carry

    def add_arrived(step, carry):
        scatter(step, peer_of(step)).wait_recv()
        return carry + arrived[peer_of(step)].astype(jnp.float32)

    def start_gather(step, carry):
        gather(step, dp_place).start()
        return carry

    def finish(step, carry):
        gather(step, peer_of(step)).wait_recv()
        return carry

    wire[...] = mine[...].astype(wire.dtype)
    lax.fori_loop(1, replicas, start_scatter, 0)
    total[dp_place] = lax.fori_loop(1, replicas, add_arrived, mine[dp_place]).astype(total.dtype)
    lax.fori_loop(1, replicas, start_gather, 0)
    lax.fori_loop(1, replicas, finish, 0)

    def drain(step, carry):
        scatter(step, dp_place).wait_send()
        gather(step, dp_place).wait_send()
        return carry

    return lambda: lax.fori_loop(1, replicas, drain, 0)


def product_kernel(left_ref, right_ref, err_ref, factor_ref, matrix_ref, factor_out):
    if len(matrix_ref.shape) == 2:
        matrix = dot_tn(left_ref[...], right_ref[...]) + err_ref[...]
        matrix_ref[...] = matrix
        factor_out[...] = left_factor(factor_ref[...], matrix)
    else:
        left_rows = left_ref[...].T
        parts = range(matrix_ref.shape[0])
        matrices = [dot_nn(left_rows, right_ref[part]) + err_ref[part] for part in parts]
        for part in parts:
            matrix_ref[part] = matrices[part]
        factor_out[...] = left_factor(
            jnp.concatenate([factor_ref[part] for part in parts], axis=1),
            jnp.concatenate(matrices, axis=1),
        )


def product(left_side, right_side, err, factor):
    block = 2 * LANES
    length, rows = left_side.shape
    lead = err.shape[:-2]
    zeros = (0,) * len(lead)

    def whole(array):
        return pl.BlockSpec(array.shape, lambda i: (0,) * array.ndim)

    by_rows = pl.BlockSpec(lead + (block, err.shape[-1]), lambda i: zeros + (i, 0))
    return pl.pallas_call(
        product_kernel,
        grid=(rows // block,),
        in_specs=[
            pl.BlockSpec((length, block), lambda i: (0, i)),
            whole(right_side),
            by_rows,
            whole(factor),
        ],
        out_specs=[by_rows, pl.BlockSpec((factor.shape[-2], block), lambda i: (0, i))],
        out_shape=[
            jax.ShapeDtypeStruct(err.shape, jnp.float32),
            jax.ShapeDtypeStruct((factor.shape[-2], rows), jnp.float32),
        ],
        compiler_params=pltpu.CompilerParams(vmem_limit_bytes=VMEM_GRANT),
        cost_estimate=pl.CostEstimate(flops=10**10, bytes_accessed=10**8, transcendentals=1),
        name="product",
    )(left_side, right_side, err, factor)


def compress_kernel(replicas, tensor_size, has_far, *refs):
    if has_far:
        far_refs, refs, late_ref = refs[:4], refs[4:13] + refs[14:], refs[13]
        compress_body(replicas, tensor_size, far_refs, late_ref, *refs)
    else:
        compress_body(replicas, tensor_size, None, None, *refs)


def compress_body(replicas, tensor_size, far_refs, late_ref, qkv_ref, out_ref, in_ref, down_ref,
                    lq_ref, fo_ref, li_ref, ld_ref, small_ref,
                    bq_ref, bo_ref, bi_ref, bd_ref, rq_ref, ro_ref, ri_ref, rd_ref, sum_ref,
                    qkv, out, inw, down, mine, wire, arrived, total,
                    mine_two, wire_two, arrived_two, total_two, small_slots,
                    load_sem, *sems):
    first_sems, second_sems, (send_small, recv_small) = sems[:4], sems[4:8], sems[8:10]
    dp_place = lax.axis_index("dp")
    tensor_place = lax.axis_index("tensor")
    loads = [
        pltpu.make_async_copy(source, target, load_sem.at[number])
        for number, (source, target) in enumerate(
            [(out_ref, out), (qkv_ref, qkv), (down_ref, down), (in_ref, inw)]
        )
    ]
    if far_refs:
        far_in_ref, far_down_ref, far_factor_in, far_factor_down = far_refs
        far_in, far_down, sent, got, far_send, far_recv = sems[10:]
        opposite = (dp_place, tensor_place + 2 - 4 * (tensor_place // 2))
        head = far_in_ref.shape[0] - late_ref.shape[0]
        cut = head + 2 * LANES

        def bulk(number, start, stop):
            return pltpu.make_async_remote_copy(
                src_ref=far_in_ref.at[pl.ds(start, stop - start)],
                dst_ref=late_ref.at[pl.ds(start - head, stop - start)],
                send_sem=far_send.at[number],
                recv_sem=far_recv.at[number],
                device_id=opposite,
                device_id_type=MESH,
            )

        bulks = [bulk(3, head, cut), bulk(4, cut, far_in_ref.shape[0])]
        far_loads = [
            pltpu.make_async_copy(far_in_ref, far_in, load_sem.at[4]),
            pltpu.make_async_copy(far_down_ref, far_down, load_sem.at[5]),
        ]
        for load in far_loads:
            load.start()

        def far_copy(number):
            return pltpu.make_async_remote_copy(
                src_ref=sent.at[number],
                dst_ref=got.at[number],
                send_sem=far_send.at[number],
                recv_sem=far_recv.at[number],
                device_id=opposite,
                device_id_type=MESH,
            )

    for load in loads:
        load.start()
    barrier = pltpu.get_barrier_semaphore()

    def greet_dp(step, carry):
        pl.semaphore_signal(
            barrier,
            inc=1,
            device_id=(lax.rem(dp_place + step, replicas), tensor_place),
            device_id_type=MESH,
        )
        return carry

    def greet_tensor(step, carry):
        pl.semaphore_signal(
            barrier,
            inc=1,
            device_id=(dp_place, lax.rem(tensor_place + step, tensor_size)),
            device_id_type=MESH,
        )
        return carry

    lax.fori_loop(1, replicas, greet_dp, 0)
    lax.fori_loop(1, tensor_size, greet_tensor, 0)
    mine[...] = jnp.zeros_like(mine)
    mine_two[...] = jnp.zeros_like(mine_two)
    block = 2 * LANES
    if far_refs:
        for number, (factor_ref, matrix) in enumerate(
            ((far_factor_down, far_down), (far_factor_in, far_in))
        ):
            far_loads[1 - number].wait()
            for start in range(0, matrix.shape[0], block):
                rows = slice(start, start + block)
                sent[0, number, :, rows] = low_left(factor_ref[...], matrix[rows])
        pl.semaphore_wait(barrier, replicas - 1 + tensor_size - 1)
        far_copy(0).start()
        bulks[0].start()
    offset = place_tiles(mine, 0, lq_ref[...])
    loads[0].wait()
    offset = place_tiles(mine, offset, left_factor(fo_ref[...], out[...]))
    offset = place_tiles(mine, offset, ld_ref[...])
    offset = place_tiles(mine, offset, li_ref[...])
    place_tiles(mine, offset, small_ref[...])
    if far_refs:
        far_copy(0).wait_recv()
        add_tiles(mine, offset - 2 * down.shape[0] // LANES, got[0, 0])
        add_tiles(mine, offset - inw.shape[0] // LANES, got[0, 1])
    else:
        pl.semaphore_wait(barrier, replicas - 1 + tensor_size - 1)
    drain_one = dp_exchange(replicas, mine, wire, arrived, total, first_sems)

    def slot_copy(step, slot):
        peer = lax.rem(tensor_place + step, tensor_size)
        return pltpu.make_async_remote_copy(
            src_ref=small_slots.at[tensor_place],
            dst_ref=small_slots.at[slot],
            send_sem=send_small.at[step],
            recv_sem=recv_small.at[slot],
            device_id=(dp_place, peer),
            device_id_type=MESH,
        )

    def start_small(step, carry):
        slot_copy(step, tensor_place).start()
        return carry

    own_small = take_tiles(total, offset, small_ref.shape[1])
    small_slots[tensor_place] = own_small
    lax.fori_loop(1, tensor_size, start_small, 0)
    offset = 0
    offset_two = 0
    offsets = []
    for basis_ref in (bq_ref, bo_ref, bd_ref, bi_ref):
        offsets.append(offset)
        offset += basis_ref.shape[1] // LANES
    for number in (2, 3, 0, 1):
        basis_ref = (bq_ref, bo_ref, bd_ref, bi_ref)[number]
        rows = take_tiles(total, offsets[number], basis_ref.shape[1]) * (1.0 / replicas)
        basis_ref[...] = orthonormal_rows(rows)
        if far_refs and number >= 2:
            sent[1, number - 2] = basis_ref[...]
        if far_refs and number == 3:
            far_copy(1).start()
    drain_one()
    for load in loads[1:]:
        load.wait()
    for part in range(3):
        right = right_factor(bq_ref[:, :block], qkv[part, :block])
        for start in range(block, qkv.shape[1], block):
            rows = slice(start, start + block)
            right += right_factor(bq_ref[:, rows], qkv[part, rows])
        offset_two = place_tiles(mine_two, offset_two, right)
    for basis_ref, matrix in zip((bo_ref, bd_ref, bi_ref), (out, down, inw)):
        rows_of = min(block, matrix.shape[0])
        right = right_factor(basis_ref[:, :rows_of], matrix[:rows_of])
        for start in range(rows_of, matrix.shape[0], rows_of):
            rows = slice(start, start + rows_of)
            right += right_factor(basis_ref[:, rows], matrix[rows])
        offset_two = place_tiles(mine_two, offset_two, right)
    if far_refs:
        far_copy(1).wait_recv()
        sent[2, 0] = low_right(got[1, 0], far_down[...])
        sent[2, 1] = low_right(got[1, 1], far_in[...])
        far_copy(2).start()
        bulks[1].start()
        far_copy(2).wait_recv()
        add_tiles(mine_two, offset_two - (down.shape[1] + inw.shape[1]) // LANES, got[2, 0])
        add_tiles(mine_two, offset_two - inw.shape[1] // LANES, got[2, 1])
    drain_two = dp_exchange(
        replicas, mine_two, wire_two, arrived_two, total_two, second_sems
    )

    def collect(step, carry):
        peer = lax.rem(tensor_place + step, tensor_size)
        slot_copy(step, peer).wait_recv()
        slot_copy(step, tensor_place).wait_send()
        return carry + small_slots[peer]

    everyone = lax.fori_loop(1, tensor_size, collect, own_small)
    row_number = lax.broadcasted_iota(jnp.int32, everyone.shape, 0)
    sum_ref[...] = jnp.where(row_number < 6, everyone, own_small) * (1.0 / replicas)
    offset = 0
    for part in range(3):
        rq_ref[part] = take_tiles(total_two, offset, rq_ref.shape[2]) * (1.0 / replicas)
        offset += rq_ref.shape[2] // LANES
    for ref in (ro_ref, rd_ref, ri_ref):
        ref[...] = take_tiles(total_two, offset, ref.shape[1]) * (1.0 / replicas)
        offset += ref.shape[1] // LANES
    drain_two()
    if far_refs:
        for number in range(3):
            far_copy(number).wait_send()
        for copy in bulks:
            copy.wait()


def compress(matrices, lefts, small, replicas, tensor_size, far):
    qkv, out, inw, down = matrices
    rank_size = small.shape[0]
    sizes = (qkv.shape[1], out.shape[0], inw.shape[0], down.shape[0])
    right_shapes = [(3, rank_size, qkv.shape[2])] + [(rank_size, one.shape[1]) for one in matrices[1:]]
    lanes_one = sum(sizes) + small.shape[1]
    lanes_two = 3 * qkv.shape[2] + sum(one.shape[1] for one in matrices[1:])
    scratch = [pltpu.VMEM(one.shape, jnp.float32) for one in matrices]
    for lanes in (lanes_one, lanes_two):
        shape = (replicas, rank_size, -(-lanes // (LANES * replicas)) * LANES)
        scratch += [
            pltpu.VMEM(shape, jnp.float32),
            pltpu.VMEM(shape, jnp.bfloat16),
            pltpu.VMEM(shape, jnp.bfloat16),
            pltpu.VMEM(shape, jnp.bfloat16),
        ]
    scratch += [pltpu.VMEM((tensor_size,) + small.shape, jnp.float32), pltpu.SemaphoreType.DMA((6,))]
    scratch += [pltpu.SemaphoreType.DMA((replicas,))] * 8
    scratch += [pltpu.SemaphoreType.DMA((tensor_size,))] * 2
    if far:
        scratch += [pltpu.VMEM(one.shape, one.dtype) for one in far[:2]]
        scratch += [pltpu.VMEM((3, 2, rank_size, inw.shape[0]), jnp.float32)] * 2
        scratch += [pltpu.SemaphoreType.DMA((5,))] * 2
    vmem = pl.BlockSpec(memory_space=pltpu.VMEM)
    shapes = [(rank_size, size) for size in sizes] + right_shapes + [small.shape]
    shapes = [jax.ShapeDtypeStruct(shape, jnp.float32) for shape in shapes]
    late_shape = []
    if far:
        late_shape = [jax.ShapeDtypeStruct((inw.shape[0] // 2, inw.shape[1]), far[0].dtype)]
    outputs = pl.pallas_call(
        partial(compress_kernel, replicas, tensor_size, bool(far)),
        in_specs=([pl.BlockSpec(memory_space=pl.ANY)] * 2 + [vmem] * 2 if far else [])
        + [pl.BlockSpec(memory_space=pl.ANY)] * 4
        + [vmem] * 5,
        out_specs=[pl.BlockSpec(memory_space=pl.ANY)] * len(late_shape) + [vmem] * 9,
        out_shape=late_shape + shapes,
        scratch_shapes=scratch,
        compiler_params=pltpu.CompilerParams(
            collective_id=1, has_side_effects=True, vmem_limit_bytes=VMEM_GRANT
        ),
        name="compress",
    )(*far, *matrices, *lefts, small)
    late, outputs = outputs[:-9], outputs[-9:]
    return outputs[:4], outputs[4:8], outputs[8], late


def outer_of(basis_rows, right):
    basis_high, basis_low = split_bf16(basis_rows)
    right_high, right_low = split_bf16(right)
    return dot_tn(
        jnp.concatenate([basis_high, basis_low, basis_high], axis=0),
        jnp.concatenate([right_high, right_high, right_low], axis=0),
    )


def update_kernel(step_rate, out_steps, near_steps, *refs):
    (mq, mo, mi, md, oq, oo, oi, od, wq, wo, wi, wd, bq, bo, bi, bd, rq, ro, ri, rd,
     gq, go, gi, gd, eq, eo, ei, ed, nq, no, ni, nd, vq, vo, vi, vd) = refs[:20] + refs[-16:]
    step = pl.program_id(0)
    whole_in, whole_down = mi[...], md[...]
    if len(refs) > 36:
        near_in, rest_in, near_down, rest_down = refs[20:24]
        whole_in += jnp.where(step < near_steps, near_in[...], rest_in[...]).astype(jnp.float32)
        whole_down += jnp.where(step < near_steps, near_down[...], rest_down[...]).astype(
            jnp.float32
        )

    def one(matrix, old, weight, rank, grad_ref, err_ref, mom_ref, new_ref, place):
        moment = 0.9 * old + rank
        grad_ref[place] = rank
        err_ref[place] = matrix - rank
        mom_ref[place] = moment
        new_ref[place] = weight.astype(jnp.float32) - step_rate * moment

    def lanes_of(ref, rows):
        return ref[:, pl.ds(pl.multiple_of(step * rows, LANES), rows)]

    rows = mq.shape[1]
    for part in range(3):
        rank = outer_of(lanes_of(bq, rows), rq[part])
        one(mq[part], oq[part], wq[part], rank, gq, eq, nq, vq, part)
    rank = outer_of(lanes_of(bi, mi.shape[0]), ri[...])
    one(whole_in, oi[...], wi[...], rank, gi, ei, ni, vi, slice(None))
    rank = outer_of(lanes_of(bd, md.shape[0]), rd[...])
    one(whole_down, od[...], wd[...], rank, gd, ed, nd, vd, slice(None))

    @pl.when(step < out_steps)
    def _():
        rank = outer_of(lanes_of(bo, mo.shape[0]), ro[...])
        one(mo[...], oo[...], wo[...], rank, go, eo, no, vo, slice(None))


def update(matrices, momenta, weights, bases, rights, late, step_rate):
    qkv, out, inw, down = matrices
    rows = LANES
    steps = inw.shape[0] // rows
    down_rows = down.shape[0] // steps
    if down_rows < LANES:
        steps = down.shape[0] // LANES
        rows, down_rows = inw.shape[0] // steps, LANES
    out_steps = out.shape[0] // LANES
    near_steps = late[0].shape[0] // rows if late else 0
    late_specs = [
        pl.BlockSpec((rows, inw.shape[1]), lambda i: (jnp.minimum(i, near_steps - 1), 0)),
        pl.BlockSpec((rows, inw.shape[1]), lambda i: (jnp.maximum(i - near_steps, 0), 0)),
        pl.BlockSpec((down_rows, down.shape[1]), lambda i: (jnp.minimum(i, near_steps - 1), 0)),
        pl.BlockSpec((down_rows, down.shape[1]), lambda i: (jnp.maximum(i - near_steps, 0), 0)),
    ]

    def whole(array):
        return pl.BlockSpec(array.shape, lambda i: (0,) * array.ndim)

    def specs():
        return [
            pl.BlockSpec((3, rows, qkv.shape[2]), lambda i: (0, i, 0)),
            pl.BlockSpec((LANES, out.shape[1]), lambda i: (jnp.minimum(i, out_steps - 1), 0)),
            pl.BlockSpec((rows, inw.shape[1]), lambda i: (i, 0)),
            pl.BlockSpec((down_rows, down.shape[1]), lambda i: (i, 0)),
        ]

    shapes = [jax.ShapeDtypeStruct(one.shape, jnp.float32) for one in matrices]
    outputs = pl.pallas_call(
        partial(update_kernel, step_rate, out_steps, near_steps),
        grid=(steps,),
        in_specs=specs() * 3
        + [whole(one) for one in bases]
        + [whole(one) for one in rights]
        + late_specs[: len(late)],
        out_specs=specs() * 4,
        out_shape=shapes * 4,
        compiler_params=pltpu.CompilerParams(vmem_limit_bytes=VMEM_GRANT),
        name="update",
    )(*matrices, *momenta, *weights, *bases, *rights, *late)
    return outputs[0:4], outputs[4:8], outputs[8:12], outputs[12:16]


def masked_scores(queries, key_heads, seg_ids):
    scores = jnp.einsum("qhd,khd->hqk", queries, key_heads, preferred_element_type=jnp.float32)
    same_doc = seg_ids[:, None] == seg_ids[None, :]
    return jnp.where(same_doc[None], scores, MASKED)


def attend_forward(inputs_of):
    queries, key_heads, value_heads, seg_ids = inputs_of
    scores = masked_scores(queries, key_heads, seg_ids)
    highest = jnp.max(scores, axis=-1, keepdims=True)
    powers = jnp.exp(scores - highest)
    denominator = jnp.sum(powers, axis=-1, keepdims=True)
    weights = (powers / denominator).astype(jnp.bfloat16)
    mixed_heads = jnp.einsum(
        "hqk,khd->qhd", weights, value_heads, preferred_element_type=jnp.float32
    )
    return (mixed_heads.astype(jnp.bfloat16), highest[..., 0] + jnp.log(denominator[..., 0]))


def attend_backward(inputs_of):
    queries, key_heads, value_heads, seg_ids, grad_mixed, log_total = inputs_of
    scores = masked_scores(queries, key_heads, seg_ids)
    probability = jnp.exp(scores - log_total[..., None])
    grad_probs = jnp.einsum(
        "qhd,khd->hqk", grad_mixed, value_heads, preferred_element_type=jnp.float32
    )
    centre = jnp.sum(probability * grad_probs, axis=-1, keepdims=True)
    grad_scores = (probability * (grad_probs - centre)).astype(jnp.bfloat16)
    grad_query = jnp.einsum(
        "hqk,khd->qhd", grad_scores, key_heads, preferred_element_type=jnp.float32
    )
    grad_key = jnp.einsum("hqk,qhd->khd", grad_scores, queries, preferred_element_type=jnp.float32)
    grad_value = jnp.einsum(
        "hqk,qhd->khd",
        probability.astype(jnp.bfloat16),
        grad_mixed,
        preferred_element_type=jnp.float32,
    )
    return (
        grad_query.astype(jnp.bfloat16),
        grad_key.astype(jnp.bfloat16),
        grad_value.astype(jnp.bfloat16),
    )


def stacked_heads(pair, lane_is_low):
    zero = jnp.zeros_like(pair)
    return jnp.concatenate(
        [jnp.where(lane_is_low, pair, zero), jnp.where(lane_is_low, zero, pair)], axis=0
    )


def own_blocks(both):
    rows = both.shape[1] // 2
    return jnp.concatenate([both[:DH, :rows], both[DH:, rows:]], axis=0).T


def window_sizes(length):
    return (length * 3 // 8, length * 5 // 8, length)


def windows_of(bounds, length):
    first = bounds[0] // LANES * LANES
    need = bounds[1] - first
    small, large, whole = window_sizes(length)
    number = jnp.where(need <= small, 0, jnp.where(need <= large, 1, 2))
    room = jnp.where(need <= small, length - small, jnp.where(need <= large, length - large, 0))
    return jnp.concatenate([jnp.minimum(first, room), number])


def attend_back_kernel(place_ref, q_ref, k_ref, v_ref, seg_key_ref, seg_query_ref, gm_own_ref,
                       gm_other_ref, mixed_ref, log_ref, old_ref, grad_ref, sums_ref, key_t, grad_key,
                       grad_value):
    del old_ref
    step = pl.program_id(0)

    @pl.when(step == 0)
    def _():
        key_t[...] = k_ref[...].T
        grad_key[...] = jnp.zeros_like(grad_key)
        grad_value[...] = jnp.zeros_like(grad_value)

    pairs = q_ref.shape[1] // LANES
    lane = lax.broadcasted_iota(jnp.int32, (1, LANES), 1)
    lane_is_low = lane < DH
    head_of_lane = (
        lax.broadcasted_iota(jnp.int32, (8, LANES), 0)
        == lax.broadcasted_iota(jnp.int32, (8, LANES), 1) // DH
    ).astype(jnp.bfloat16)
    head_scale = 1.0 / math.sqrt(DH)
    here = pl.ds(pl.multiple_of(step * LANES, LANES), LANES)
    is_own = lax.rem(step // (pl.num_programs(0) // 2) + place_ref[1], 2) == 0
    gm = jnp.where(is_own, gm_own_ref[...], gm_other_ref[...])
    seg_query = jnp.concatenate([seg_query_ref[...], seg_query_ref[...]], axis=1)
    all_lanes = [slice(pair * LANES, (pair + 1) * LANES) for pair in range(pairs)]
    length = k_ref.shape[0]

    def window(size):
        start = 0 if size == length else pl.multiple_of(place_ref[2 + step], LANES)
        keys = pl.ds(start, size)
        seg_key = seg_key_ref[keys]
        same = jnp.concatenate([seg_key, seg_key], axis=1) == seg_query
        queries, grads, centres, probs, grad_probs = [], [], [], [], []
        for lanes in all_lanes:
            queries.append(stacked_heads(q_ref[:, lanes], lane_is_low))
            grads.append(stacked_heads(gm[:, lanes], lane_is_low))
            high, low = split_bf16(
                gm[:, lanes].astype(jnp.float32) * mixed_ref[:, lanes].astype(jnp.float32)
            )
            sums = dot_nt(head_of_lane, high) + dot_nt(head_of_lane, low)
            centres.append(jnp.concatenate([sums[0:1], sums[1:2]], axis=1))
        for pair, lanes in enumerate(all_lanes):
            log_total = jnp.concatenate(
                [log_ref[2 * pair : 2 * pair + 1], log_ref[2 * pair + 1 : 2 * pair + 2]], axis=1
            )
            scores = dot_nt(k_ref[keys, lanes], queries[pair])
            probs.append(jnp.exp(jnp.where(same, scores - log_total, MASKED)))
            grad_probs.append(dot_nt(v_ref[keys, lanes], grads[pair]))
        for pair, lanes in enumerate(all_lanes):
            grad_scores = (probs[pair] * (grad_probs[pair] - centres[pair])).astype(jnp.bfloat16)
            grad_value[keys, lanes] += dot_nn(probs[pair].astype(jnp.bfloat16), grads[pair])
            grad_key[keys, lanes] += dot_nn(grad_scores, queries[pair])
            grad_query = own_blocks(dot_nn(key_t[lanes, keys], grad_scores)).astype(jnp.bfloat16)
            grad_ref[0, here, lanes] = (grad_query.astype(jnp.float32) * head_scale).astype(
                jnp.bfloat16
            )

    for number, size in enumerate(window_sizes(length)):
        pl.when(place_ref[2 + pl.num_programs(0) + step] == number)(partial(window, size))

    @pl.when(step == pl.num_programs(0) - 1)
    def _():
        grad_ref[1] = grad_key[...].astype(jnp.bfloat16)
        low_value = grad_value[...].astype(jnp.bfloat16)
        grad_ref[2] = low_value
        sums_ref[0:1] = jnp.sum(grad_ref[0].astype(jnp.float32), axis=0, keepdims=True)
        sums_ref[1:2] = jnp.sum(low_value.astype(jnp.float32), axis=0, keepdims=True)


def attend_back(projected, seg_keys, seg_queries, grad_own, grad_other, mixed, logs, slot, bounds,
                old, place, core):
    length = seg_keys.shape[1]
    slab = projected.shape[2]
    blocks = length // LANES
    half = blocks // 2
    at = jnp.concatenate(
        [
            jnp.stack([place, core]),
            windows_of(bounds[2 * slot : 2 * slot + 2, :blocks], length),
        ]
    )
    grid_spec = pltpu.PrefetchScalarGridSpec(
        num_scalar_prefetch=1,
        grid=(blocks,),
        in_specs=[
            pl.BlockSpec((None, LANES, slab), lambda i, at: (0, at[0] * blocks + i, 0)),
            pl.BlockSpec((None, length, slab), lambda i, at: (1, at[0], 0)),
            pl.BlockSpec((None, length, slab), lambda i, at: (2, at[0], 0)),
            pl.BlockSpec((None, length, LANES), lambda i, at: (at[0], 0, 0)),
            pl.BlockSpec((None, 1, LANES), lambda i, at: (at[0], 0, i)),
            pl.BlockSpec((None, LANES, slab), lambda i, at: (grad_own[1], lax.rem(i, half), 0)),
            pl.BlockSpec((None, LANES, slab), lambda i, at: (grad_other[1], lax.rem(i, half), 0)),
            pl.BlockSpec((None, LANES, slab), lambda i, at: (slot, i, 0)),
            pl.BlockSpec((None, slab // DH, LANES), lambda i, at: (slot, 0, i)),
            pl.BlockSpec(memory_space=pl.ANY),
        ],
        out_specs=[
            pl.BlockSpec((3, length, slab), lambda i, at: (0, at[0], 0)),
            pl.BlockSpec((2, slab), lambda i, at: (0, 0)),
        ],
        scratch_shapes=[
            pltpu.VMEM((slab, length), jnp.bfloat16),
            pltpu.VMEM((length, slab), jnp.float32),
            pltpu.VMEM((length, slab), jnp.float32),
        ],
    )
    return pl.pallas_call(
        attend_back_kernel,
        grid_spec=grid_spec,
        out_shape=[
            jax.ShapeDtypeStruct(projected.shape, jnp.bfloat16),
            jax.ShapeDtypeStruct((2, slab), jnp.float32),
        ],
        input_output_aliases={} if old is None else {10: 0},
        compiler_params=pltpu.CompilerParams(vmem_limit_bytes=24 << 20),
        cost_estimate=BRIEF,
        name="attend_back",
    )(at, projected, projected, projected, seg_keys, seg_queries, grad_own[0],
      grad_other[0], mixed, logs, seg_keys if old is None else old)


def row_mean(values):
    return jnp.mean(values, axis=-1, keepdims=True)


def layer_kernel(tokens, cotangent, w_qkv_ref, out_ref, in_ref, down_ref,
                 factor_in_ref, factor_down_ref, head_ref, bias_ref, vec_ref, segments,
                 projected_out, log_out, mixed_out, in_two, down_two, out_rest, bias_two,
                 result_out, low_out, active_out, branch_out, hidden_out, norm_out, near_out,
                 far_one_out, far_two_out, keys_out, rows_out, down_near, down_part_out, down_rest, in_part_out, in_head,
                 far_in_out, far_down_out, out_sum,
                 out_far, unit_ref, unit_two, sums_ref, bounds_ref,
                 rows_in, w_qkv, projected, value_t, log_total, mixed, pieces,
                 w_out, w_in, w_down, bias, tok, cot, first, normed, inverse, low, slope, active,
                 part, other, acc, wide, branch, result, down_part, near, far_mixed, outs_two,
                 seg_keys, seg_queries, load_sem, store_sem, send_sem, recv_sem):
    dp_place = lax.axis_index("dp")
    tensor_place = lax.axis_index("tensor")
    core = lax.rem(tensor_place, 2)
    seq = tensor_place // 2
    far = 1 - seq
    side = lax.rem(dp_place, 2)
    depth = lax.rem(dp_place // 2, 2)
    here = 2 * depth + side
    sibling = (dp_place, tensor_place + 1 - 2 * core)
    opposite = (dp_place, core + 2 * far)
    diagonal = (dp_place, 1 - core + 2 * far)
    beside = (dp_place + 1 - 2 * side, tensor_place)
    behind = (dp_place + 2 - 4 * depth, tensor_place)
    share, width = tok.shape
    slab = in_ref.shape[1]
    length = rows_in.shape[1]
    head_slab = w_qkv.shape[2]
    head_count = head_slab // DH
    stores = []
    sends = []
    numbers = iter(range(send_sem.shape[0]))

    def load_later(number, source, target):
        return pltpu.make_async_copy(source, target, load_sem.at[number])

    def load(number, source, target):
        copy = load_later(number, source, target)
        copy.start()
        return copy

    def store(source, target):
        copy = pltpu.make_async_copy(source, target, store_sem.at[len(stores)])
        copy.start()
        stores.append(copy)

    def send_later(source, target, device):
        number = next(numbers)
        copy = pltpu.make_async_remote_copy(
            src_ref=source,
            dst_ref=target,
            send_sem=send_sem.at[number],
            recv_sem=recv_sem.at[number],
            device_id=device,
            device_id_type=MESH,
        )
        sends.append(copy)
        return copy

    def send(source, target, device):
        copy = send_later(source, target, device)
        copy.start()
        return copy

    def rows_of(number, size):
        return pl.ds(pl.multiple_of(number * size, LANES), size)

    load_qkv = load(0, w_qkv_ref, w_qkv)
    load_far = load(1, tokens.at[rows_of(far, length)], rows_in.at[0])
    load_near = load(2, tokens.at[rows_of(seq, length)], rows_in.at[1])
    load_out = load(3, out_ref, w_out.at[0])
    load_in = load(4, in_ref, w_in.at[0])
    load_down = load(5, down_ref, w_down.at[pl.ds(0, slab)])
    load_tok = load(6, tokens.at[rows_of(tensor_place, share)], tok)
    load_cot = load(7, cotangent.at[rows_of(tensor_place, share)], cot)

    barrier = pltpu.get_barrier_semaphore()
    for device in (sibling, opposite, diagonal, beside, behind):
        pl.semaphore_signal(barrier, inc=1, device_id=device, device_id_type=MESH)
    pl.semaphore_wait(barrier, 5)
    sums_ref[...] = jnp.zeros_like(sums_ref)
    unit_ref[...] = jnp.zeros_like(unit_ref)

    def rows_part(whole, number, parts):
        size = whole.shape[0] // parts
        return whole.at[pl.ds(pl.multiple_of(number * size, size), size)]

    class Fetch:
        def __init__(self, source, whole):
            own = rows_part(whole, here, 4)
            half_one = rows_part(whole, 2 * (here + 1 - 2 * side), 8)
            half_two = rows_part(whole, 2 * (here + 2 - 4 * depth) + 1, 8)
            self.over_y = send_later(rows_part(source, here, 4), own, opposite)
            self.over_x = send_later(own, own, beside)
            self.over_z = send_later(own, own, behind)
            self.half_z = send_later(half_one, half_one, behind)
            self.half_x = send_later(half_two, half_two, beside)

        def start(self):
            self.over_y.start()

        def pass_on(self):
            self.over_y.wait_recv()
            self.over_x.start()
            self.over_z.start()

        def pass_halves(self):
            self.over_x.wait_recv()
            self.half_z.start()
            self.over_z.wait_recv()
            self.half_x.start()

        def wait(self):
            self.half_z.wait_recv()
            self.half_x.wait_recv()

    bias_send = send(bias_ref, bias_two, opposite)
    factor_sends = [
        send(factor_in_ref, far_in_out, opposite), send(factor_down_ref, far_down_out, opposite)
    ]
    fetch_out = Fetch(out_ref, out_rest.at[1])
    upper, lower = pl.ds(0, width // 2), pl.ds(width // 2, width // 2)
    fetch_in = [Fetch(in_ref.at[rows], in_two.at[rows]) for rows in (upper, lower)]
    upper, lower = pl.ds(0, slab // 2), pl.ds(slab // 2, slab // 2)
    fetch_down = [Fetch(down_ref.at[rows], down_two.at[rows]) for rows in (upper, lower)]
    fetch_out.start()
    fetch_in[0].start()
    fetch_in[1].start()
    fetch_down[0].start()

    chunk = 256
    scale = 1.0 / math.sqrt(DH)

    def project(slot):
        def rows_step(step, carry):
            rows = rows_of(step, chunk)
            values = rows_in[slot, rows]
            projected[slot, 0, rows] = (
                (dot_nn(values, w_qkv[0]) + head_ref[0:1]) * scale
            ).astype(jnp.bfloat16)
            projected[slot, 1, rows] = dot_nn(values, w_qkv[1]).astype(jnp.bfloat16)
            projected[slot, 2, rows] = (dot_nn(values, w_qkv[2]) + head_ref[1:2]).astype(
                jnp.bfloat16
            )
            return carry

        lax.fori_loop(0, length // chunk, rows_step, 0)
        value_t[...] = projected[slot, 2].T

    lane_is_low = lax.broadcasted_iota(jnp.int32, (1, LANES), 1) < DH

    def attend_rows(slot, place, tasks):
        def block(step):
            rows = rows_of(step, LANES)
            same = seg_keys[place] == seg_queries[place, :, rows]
            mask = jnp.where(same, 0.0, MASKED)
            mask = jnp.concatenate([mask, mask], axis=1)
            all_lanes = [slice(at, at + LANES) for at in range(0, head_slab, LANES)]
            all_scores = [
                dot_nt(
                    projected[slot, 1, :, lanes],
                    stacked_heads(projected[slot, 0, rows, lanes], lane_is_low),
                )
                + mask
                for lanes in all_lanes
            ]
            for pair, (lanes, scores) in enumerate(zip(all_lanes, all_scores)):
                highest = jnp.max(scores, axis=0, keepdims=True)
                powers = jnp.exp(scores - highest)
                denominator = jnp.sum(powers, axis=0, keepdims=True)
                blend = dot_nn(value_t[lanes], powers.astype(jnp.bfloat16))
                mixed[slot, rows, lanes] = own_blocks(blend * (1.0 / denominator)).astype(
                    jnp.bfloat16
                )
                total = highest + jnp.log(denominator)
                log_total[slot, 2 * pair : 2 * pair + 1, rows] = total[:, :LANES]
                log_total[slot, 2 * pair + 1 : 2 * pair + 2, rows] = total[:, LANES:]

        def two_blocks(step, carry):
            for number, task in tasks:
                pl.when(step == number)(task)
            block(2 * step)
            block(2 * step + 1)
            return carry

        lax.fori_loop(0, length // LANES // 2, two_blocks, 0)

    for number in range(segments.shape[0]):
        documents = segments[number : number + 1].astype(jnp.float32)
        seg_queries[number] = documents
        seg_keys[number] = jnp.broadcast_to(documents, (LANES, length)).T
    store(seg_keys, keys_out)
    store(seg_queries, rows_out)
    load_qkv.wait()
    load_far.wait()
    project(0)
    attend_rows(0, far, [(2, fetch_out.pass_on)])
    fetch_in[0].pass_on()
    own_rows = rows_of(core, share)
    sibling_rows = rows_of(1 - core, share)
    piece_two = send(mixed.at[0, own_rows], pieces.at[1], opposite)
    piece_three = send(mixed.at[0, sibling_rows], pieces.at[2], diagonal)
    fetch_down[1].start()
    store(projected.at[0, 0], projected_out.at[0, rows_of(far, length)])
    store(projected.at[0, 1], projected_out.at[1, rows_of(far, length)])
    store(projected.at[0, 2], projected_out.at[2, rows_of(far, length)])
    load_near.wait()
    project(1)
    out_pass = [
        send_later(out_ref, out_rest.at[0], sibling),
        send_later(out_rest.at[1], out_rest.at[2], sibling),
    ]
    load_two = load_later(8, out_rest.at[1], w_out.at[2])

    def pass_in():
        fetch_in[1].pass_on()
        fetch_in[0].pass_halves()

    def pass_out():
        fetch_out.wait()
        for copy in out_pass:
            copy.start()
        load_two.start()

    attend_rows(1, seq, [(0, fetch_out.pass_halves), (2, pass_in), (3, pass_out)])
    piece_one = send(mixed.at[1, sibling_rows], pieces.at[0], sibling)
    store(projected.at[1, 0], projected_out.at[0, rows_of(seq, length)])
    store(projected.at[1, 1], projected_out.at[1, rows_of(seq, length)])
    store(projected.at[1, 2], projected_out.at[2, rows_of(seq, length)])
    store(log_total, log_out)
    for copy in out_pass:
        copy.wait_recv()
    load_one = load(9, out_rest.at[0], w_out.at[1])
    load_three = load(10, out_rest.at[2], w_out.at[3])
    store(mixed, mixed_out)
    fetch_down[0].pass_on()
    fetch_in[1].pass_halves()
    for copy in (load_out, load_tok, load_one, load_two, load_three):
        copy.wait()
    for copy in (piece_two, piece_three, piece_one):
        copy.wait_recv()
    small = 64

    def attn_rows(step, carry):
        rows = rows_of(step, chunk)
        total = dot_nn(mixed[1, pl.ds(pl.multiple_of(core * share + step * chunk, LANES), chunk)],
                       w_out[0])
        for piece in range(3):
            total += dot_nn(pieces[piece, rows], w_out[piece + 1])
        acc[rows] = total
        return carry

    def first_rows(step, carry):
        rows = pl.ds(pl.multiple_of(step * small, small), small)
        values = tok[rows].astype(jnp.float32) + (acc[rows] + vec_ref[0:1])
        centred = values - row_mean(values)
        spread = lax.rsqrt(row_mean(centred * centred) + EPS_NORM)
        unit = centred * spread
        normed[rows] = unit
        inverse[rows] = spread
        shifted = unit * vec_ref[2:3] + vec_ref[3:4]
        first[rows] = shifted
        low[rows] = shifted.astype(jnp.bfloat16)
        return carry

    lax.fori_loop(0, share // chunk, attn_rows, 0)
    lax.fori_loop(0, share // small, first_rows, 0)
    slots = [slice(0, share), slice(share, 2 * share)]
    low_send = send(low.at[slots[0]], low.at[slots[1]], sibling)
    fetch_down[0].pass_halves()
    load_in.wait()

    per_slab = slab // chunk

    def hidden_of(slot, owner, count=1):
        def units(step, carry):
            inner = rows_of(lax.rem(step, per_slab), chunk)
            rows = rows_of(lax.rem(slot + step // per_slab, 2), share)
            values = dot_nn(low[rows], w_in[owner, :, inner]) + bias[owner, :, inner]
            share_of = 0.5 * (1.0 + lax.erf(values * math.sqrt(0.5)))
            density = jnp.exp(-0.5 * values * values) * (1.0 / math.sqrt(2.0 * math.pi))
            active[owner, rows, inner] = (values * share_of).astype(jnp.bfloat16)
            slope[owner, rows, inner] = (share_of - 0.5 + values * density).astype(jnp.bfloat16)
            return carry

        lax.fori_loop(0, count * per_slab, units, 0)

    def branch_of(slot, owner, target, start, size):
        units = slice(owner * slab, (owner + 1) * slab)

        def columns(step, carry):
            at = pl.ds(pl.multiple_of(start + step * chunk, chunk), chunk)
            values = dot_nn(active[owner, slots[slot]], w_down[units, at])
            target[:, at] = values if owner == 0 else target[:, at] + values
            return carry

        lax.fori_loop(0, size // chunk, columns, 0)

    bias_send.wait_recv()
    bias[0] = bias_ref[...]
    load_bias = load(11, bias_two, bias.at[1])
    hidden_of(0, 0)
    low_send.wait_recv()
    store(low, low_out)
    fetch_down[1].pass_on()
    hidden_of(1, 0)
    for fetch in fetch_in:
        fetch.wait()
    load_in_two = load(12, in_two, w_in.at[1])
    load_down.wait()
    branch_of(1, 0, part, 0, width)
    branch_of(0, 0, acc, 0, width)
    load_bias.wait()
    load_in_two.wait()
    fetch_down[1].pass_halves()
    hidden_of(1, 1, 2)
    store(active.at[0], active_out)
    lane = lax.broadcasted_iota(jnp.int32, (1, LANES), 1)
    for slot, place in ((0, far), (1, seq)):
        firsts = jnp.zeros((1, LANES), jnp.float32)
        lasts = jnp.zeros((1, LANES), jnp.float32)
        for block in range(length // LANES):
            start = block * LANES
            firsts = jnp.where(lane == block, seg_keys[place, start : start + 1], firsts)
            lasts = jnp.where(
                lane == block, seg_keys[place, start + LANES - 1 : start + LANES], lasts
            )
        documents = seg_keys[place]
        bounds_ref[2 * slot : 2 * slot + 1] = jnp.sum(
            jnp.where(documents < firsts, 1.0, 0.0), axis=0, keepdims=True
        ).astype(jnp.int32)
        bounds_ref[2 * slot + 1 : 2 * slot + 2] = jnp.sum(
            jnp.where(documents <= lasts, 1.0, 0.0), axis=0, keepdims=True
        ).astype(jnp.int32)
    for fetch in fetch_down:
        fetch.wait()
    load_down_two = load(13, down_two, w_down.at[pl.ds(slab, slab)])
    load_down_two.wait()
    half = width // 2
    part_sends = []
    for number in range(2):
        branch_of(1, 1, part, number * half, half)
        columns = slice(number * half, (number + 1) * half)
        part_sends.append(send(part.at[:, columns], other.at[:, columns], sibling))
    branch_of(0, 1, acc, 0, width)
    load_cot.wait()
    for copy in part_sends:
        copy.wait_recv()

    def second_rows(step, carry):
        rows = pl.ds(pl.multiple_of(step * small, small), small)
        values = first[rows] + (acc[rows] + other[rows]) + vec_ref[1:2]
        centred = values - row_mean(values)
        spread = lax.rsqrt(row_mean(centred * centred) + EPS_NORM)
        unit = centred * spread
        result[rows] = (unit * vec_ref[4:5] + vec_ref[5:6]).astype(jnp.bfloat16)
        upper = cot[rows].astype(jnp.float32)
        scaled = upper * vec_ref[4:5]
        grad = spread * (scaled - row_mean(scaled) - unit * row_mean(scaled * unit))
        wide[rows] = grad
        grad_low = grad.astype(jnp.bfloat16)
        branch[rows] = grad_low
        sums_ref[1:2] += jnp.sum(grad_low.astype(jnp.float32), axis=0, keepdims=True)
        sums_ref[4:5] += jnp.sum(upper * unit, axis=0, keepdims=True)
        sums_ref[5:6] += jnp.sum(upper, axis=0, keepdims=True)
        return carry

    branch_sends = []
    for number in range(2):
        steps = share // small // 2
        lax.fori_loop(number * steps, (number + 1) * steps, second_rows, 0)
        rows = slice(number * steps * small, (number + 1) * steps * small)
        there = slice(share + rows.start, share + rows.stop)
        branch_sends.append(send(branch.at[rows], branch.at[there], sibling))
    store(result, result_out)
    hidden = rows_in

    def grad_hidden_of(slot):
        def units(step, carry):
            owner = step // per_slab
            inner = rows_of(lax.rem(step, per_slab), chunk)
            outer = rows_of(step, chunk)
            grad = dot_nt(branch[slots[slot]], w_down[outer]) * (
                0.5 + slope[owner, slots[slot], inner].astype(jnp.float32)
            )
            grad_low = grad.astype(jnp.bfloat16)
            hidden[owner, slots[slot], inner] = grad_low
            unit_ref[:, outer] += jnp.sum(grad_low.astype(jnp.float32), axis=0, keepdims=True)
            return carry

        lax.fori_loop(0, 2 * per_slab, units, 0)

    def grad_first_of(slot, target, start, size):
        def columns(step, carry):
            at = pl.ds(pl.multiple_of(start + step * chunk, chunk), chunk)
            target[:, at] = dot_nt(hidden[0, slots[slot]], w_in[0, at]) + dot_nt(
                hidden[1, slots[slot]], w_in[1, at]
            )
            return carry

        lax.fori_loop(0, size // chunk, columns, 0)

    def far_product(left_side, right_side, target, copy=None, ready=0):
        def rows_step(step, carry):
            if copy is not None:
                pl.when(step == ready // LANES)(copy.start)
            at = rows_of(step, LANES)
            target[at] = dot_tn(left_side[:, at], right_side[...]).astype(jnp.bfloat16)
            return carry

        lax.fori_loop(0, target.shape[0] // LANES, rows_step, 0)

    grad_hidden_of(0)
    for copy in branch_sends:
        copy.wait_recv()
    store(branch, branch_out)
    early = down_near.shape[0]
    down_send = send_later(down_part.at[pl.ds(0, early)], down_near, opposite)
    far_product(active.at[1], branch, down_part, down_send, early)
    store(down_part, down_part_out)
    store(down_part.at[pl.ds(early, slab - early)], down_rest)
    grad_hidden_of(1)
    unit_send = send(unit_ref.at[:, pl.ds(slab, slab)], unit_two, opposite)
    store(hidden.at[0], hidden_out)
    for copy in part_sends:
        copy.wait_send()
    sends[:] = [one for one in sends if all(one is not copy for copy in part_sends)]
    first_sends = []
    for number in range(2):
        grad_first_of(1, part, number * half, half)
        columns = slice(number * half, (number + 1) * half)
        first_sends.append(send(part.at[:, columns], other.at[:, columns], sibling))
    grad_first_of(0, acc, 0, width)
    for copy in first_sends:
        copy.wait_recv()

    def back_rows(step, carry):
        rows = pl.ds(pl.multiple_of(step * small, small), small)
        grad = acc[rows] + other[rows] + wide[rows]
        unit = normed[rows]
        scaled = grad * vec_ref[2:3]
        back = inverse[rows] * (scaled - row_mean(scaled) - unit * row_mean(scaled * unit))
        acc[rows] = back
        back_low = back.astype(jnp.bfloat16)
        tok[rows] = back_low
        sums_ref[0:1] += jnp.sum(back_low.astype(jnp.float32), axis=0, keepdims=True)
        sums_ref[2:3] += jnp.sum(grad * unit, axis=0, keepdims=True)
        sums_ref[3:4] += jnp.sum(grad, axis=0, keepdims=True)
        return carry

    lax.fori_loop(0, share // small, back_rows, 0)
    store(acc, norm_out)
    attn = tok[...]
    near[1] = dot_nt(attn, w_out[1]).astype(jnp.bfloat16)
    near_send = send(near.at[1], near.at[2], sibling)
    out_one = slice(0, head_slab)
    out_three = slice(head_slab, 2 * head_slab)
    first[out_one] = dot_tn(pieces[0], attn)
    first[out_three] = dot_tn(pieces[2], attn)
    outs_send = send(first.at[pl.ds(0, 2 * head_slab)], outs_two, sibling)
    far_mixed[0] = dot_nt(attn, w_out[2]).astype(jnp.bfloat16)
    far_mixed[1] = dot_nt(attn, w_out[3]).astype(jnp.bfloat16)
    store(far_mixed.at[0], far_one_out.at[0])
    store(far_mixed.at[1], far_two_out.at[0])
    near[0] = dot_nt(attn, w_out[0]).astype(jnp.bfloat16)
    store(near.at[0], near_out.at[0])
    far_product(low, hidden.at[1], active.at[1])
    store(active.at[1], in_part_out)
    store(active.at[1, pl.ds(0, in_head.shape[0])], in_head)
    near_send.wait_recv()
    store(near.at[2], near_out.at[1])
    outs_send.wait_recv()
    out_sum[...] = dot_tn(mixed[1, own_rows], attn) + outs_two[out_one]
    out_far[...] = (dot_tn(pieces[1], attn) + outs_two[out_three]).astype(jnp.bfloat16)
    unit_send.wait_recv()
    down_send.wait_recv()
    for copy in factor_sends:
        copy.wait_recv()
    for copy in sends:
        copy.wait_send()
    for copy in stores:
        copy.wait()


def layer_call(tokens, cotangent, planes, w_out, w_in, w_down, factor_in, factor_down, head_bias,
               unit_bias, vectors, segments):
    token_count, width = tokens.shape
    seq_count, length = segments.shape
    share = token_count // (2 * seq_count)
    head_slab = planes.shape[2]
    slab = w_in.shape[1]
    early = slab // 2
    low_type, full_type = jnp.bfloat16, jnp.float32
    vmem = pl.BlockSpec(memory_space=pltpu.VMEM)
    anywhere = pl.BlockSpec(memory_space=pl.ANY)
    shapes = [
        jax.ShapeDtypeStruct((3, token_count, head_slab), low_type),
        jax.ShapeDtypeStruct((2, head_slab // DH, length), full_type),
        jax.ShapeDtypeStruct((2, length, head_slab), low_type),
        jax.ShapeDtypeStruct(w_in.shape, low_type),
        jax.ShapeDtypeStruct(w_down.shape, low_type),
        jax.ShapeDtypeStruct((3,) + w_out.shape, low_type),
        jax.ShapeDtypeStruct((1, slab), full_type),
        jax.ShapeDtypeStruct((share, width), low_type),
        jax.ShapeDtypeStruct((2 * share, width), low_type),
        jax.ShapeDtypeStruct((2 * share, slab), low_type),
        jax.ShapeDtypeStruct((2 * share, width), low_type),
        jax.ShapeDtypeStruct((2 * share, slab), low_type),
        jax.ShapeDtypeStruct((share, width), full_type),
        jax.ShapeDtypeStruct((2, share, head_slab), low_type),
        jax.ShapeDtypeStruct((1, share, head_slab), low_type),
        jax.ShapeDtypeStruct((1, share, head_slab), low_type),
        jax.ShapeDtypeStruct((seq_count, length, LANES), full_type),
        jax.ShapeDtypeStruct((seq_count, 1, length), full_type),
        jax.ShapeDtypeStruct((early, width), low_type),
        jax.ShapeDtypeStruct((slab, width), low_type),
        jax.ShapeDtypeStruct((slab - early, width), low_type),
        jax.ShapeDtypeStruct(w_in.shape, low_type),
        jax.ShapeDtypeStruct((early, slab), low_type),
        jax.ShapeDtypeStruct(factor_in.shape, full_type),
        jax.ShapeDtypeStruct(factor_down.shape, full_type),
        jax.ShapeDtypeStruct((head_slab, width), full_type),
        jax.ShapeDtypeStruct((head_slab, width), low_type),
        jax.ShapeDtypeStruct((1, 2 * slab), full_type),
        jax.ShapeDtypeStruct((1, slab), full_type),
        jax.ShapeDtypeStruct((6, width), full_type),
        jax.ShapeDtypeStruct((4, LANES), jnp.int32),
    ]
    return pl.pallas_call(
        layer_kernel,
        in_specs=[anywhere] * 8 + [vmem] * 4,
        out_specs=[anywhere] * 25 + [vmem] * 6,
        out_shape=shapes,
        scratch_shapes=[
            pltpu.VMEM((2, length, width), low_type),
            pltpu.VMEM(planes.shape, low_type),
            pltpu.VMEM((2, 3, length, head_slab), low_type),
            pltpu.VMEM((head_slab, length), low_type),
            pltpu.VMEM((2, head_slab // DH, length), full_type),
            pltpu.VMEM((2, length, head_slab), low_type),
            pltpu.VMEM((3, share, head_slab), low_type),
            pltpu.VMEM((4,) + w_out.shape, low_type),
            pltpu.VMEM((2,) + w_in.shape, low_type),
            pltpu.VMEM((2 * slab, width), low_type),
            pltpu.VMEM((2, 1, slab), full_type),
            pltpu.VMEM((share, width), low_type),
            pltpu.VMEM((share, width), low_type),
            pltpu.VMEM((share, width), full_type),
            pltpu.VMEM((share, width), full_type),
            pltpu.VMEM((share, 1), full_type),
            pltpu.VMEM((2 * share, width), low_type),
            pltpu.VMEM((2, 2 * share, slab), low_type),
            pltpu.VMEM((2, 2 * share, slab), low_type),
            pltpu.VMEM((share, width), full_type),
            pltpu.VMEM((share, width), full_type),
            pltpu.VMEM((share, width), full_type),
            pltpu.VMEM((share, width), full_type),
            pltpu.VMEM((2 * share, width), low_type),
            pltpu.VMEM((share, width), low_type),
            pltpu.VMEM((slab, width), low_type),
            pltpu.VMEM((3, share, head_slab), low_type),
            pltpu.VMEM((2, share, head_slab), low_type),
            pltpu.VMEM((2 * head_slab, width), full_type),
            pltpu.VMEM((seq_count, length, LANES), full_type),
            pltpu.VMEM((seq_count, 1, length), full_type),
            pltpu.SemaphoreType.DMA((14,)),
            pltpu.SemaphoreType.DMA((28,)),
            pltpu.SemaphoreType.DMA((46,)),
            pltpu.SemaphoreType.DMA((46,)),
        ],
        compiler_params=pltpu.CompilerParams(
            collective_id=3, has_side_effects=True, vmem_limit_bytes=VMEM_GRANT
        ),
        name="layer",
    )(tokens, cotangent, planes, w_out, w_in, w_down, factor_in, factor_down, head_bias, unit_bias,
      vectors, segments)


def layer_general(tokens, segments, w_qkv, head_bias, w_out, w_in, unit_bias, w_down, vectors,
                  cotangent, errors, factors):
    token_count, model_width = tokens.shape
    seq_count, length = segments.shape
    head_slab = w_qkv.shape[2]
    head_count = head_slab // DH
    tensor_size = lax.axis_size("tensor")
    share_rows = token_count // tensor_size
    tensor_place = lax.axis_index("tensor")
    row_start = tensor_place * share_rows
    head_scale = 1.0 / math.sqrt(DH)

    def own_rows(values):
        return lax.dynamic_slice_in_dim(values, row_start, share_rows, 0)

    flat_qkv = w_qkv.reshape(model_width, 3 * head_slab)
    projected = jnp.dot(tokens, flat_qkv, preferred_element_type=jnp.float32).reshape(
        token_count, 3, head_slab
    )
    head_shape = (seq_count, length, head_count, DH)
    queries = (
        ((projected[:, 0] + head_bias[0]) * head_scale).astype(jnp.bfloat16).reshape(head_shape)
    )
    key_heads = projected[:, 1].astype(jnp.bfloat16).reshape(head_shape)
    value_heads = (projected[:, 2] + head_bias[1]).astype(jnp.bfloat16).reshape(head_shape)
    mixed_heads, log_total = lax.map(attend_forward, (queries, key_heads, value_heads, segments))
    mixed_flat = mixed_heads.reshape(token_count, head_slab)
    attn_out = (
        lax.psum(jnp.dot(mixed_flat, w_out, preferred_element_type=jnp.float32), "tensor")
        + vectors[0]
    )
    first_norm, first_normed, first_inverse = norm_forward(
        tokens.astype(jnp.float32) + attn_out, vectors[2], vectors[3]
    )
    first_low = first_norm.astype(jnp.bfloat16)
    hidden = jnp.dot(first_low, w_in, preferred_element_type=jnp.float32) + unit_bias
    active, gelu_back = jax.vjp(partial(jax.nn.gelu, approximate=False), hidden)
    active_low = active.astype(jnp.bfloat16)
    grad_out_share = own_rows(cotangent).astype(jnp.float32)
    summed_input = (
        first_norm
        + lax.psum(jnp.dot(active_low, w_down, preferred_element_type=jnp.float32), "tensor")
        + vectors[1]
    )
    second_norm, second_normed, second_inverse = norm_forward(summed_input, vectors[4], vectors[5])
    layer_out = own_rows(second_norm).astype(jnp.bfloat16)
    grad_sum = norm_backward(
        cotangent.astype(jnp.float32), second_normed, second_inverse, vectors[4]
    )
    grad_branch = grad_sum.astype(jnp.bfloat16)
    second_share = own_rows(second_normed)
    grad_w_down = trans_times(active_low, grad_branch)
    grad_active = times_trans(grad_branch, w_down)
    grad_hidden = gelu_back(grad_active)[0].astype(jnp.bfloat16)
    grad_w_in = trans_times(first_low, grad_hidden)
    grad_units = jnp.sum(grad_hidden.astype(jnp.float32), axis=0)
    grad_first = lax.psum(times_trans(grad_hidden, w_in), "tensor") + grad_sum
    grad_h1 = norm_backward(grad_first, first_normed, first_inverse, vectors[2])
    grad_attn = grad_h1.astype(jnp.bfloat16)
    grad_first_share = own_rows(grad_first)
    first_normed_share = own_rows(first_normed)
    grad_h1_share = own_rows(grad_h1)
    grad_w_out = trans_times(mixed_flat, grad_attn)
    grad_mixed = times_trans(grad_attn, w_out).astype(jnp.bfloat16).reshape(head_shape)
    grad_query, grad_key, grad_value = lax.map(
        attend_backward, (queries, key_heads, value_heads, segments, grad_mixed, log_total)
    )
    grad_query = (
        grad_query.reshape(token_count, head_slab).astype(jnp.float32) * head_scale
    ).astype(jnp.bfloat16)
    grad_key = grad_key.reshape(token_count, head_slab)
    grad_value = grad_value.reshape(token_count, head_slab)
    grad_projected = jnp.stack([grad_query, grad_key, grad_value], axis=1).reshape(
        token_count, 3 * head_slab
    )
    grad_w_qkv = trans_times(tokens, grad_projected)
    grad_heads = jnp.stack(
        [
            jnp.sum(grad_query.astype(jnp.float32), axis=0),
            jnp.sum(grad_value.astype(jnp.float32), axis=0),
        ]
    )
    grad_tokens = (
        lax.psum_scatter(
            times_trans(grad_projected, flat_qkv).astype(jnp.bfloat16),
            "tensor",
            scatter_dimension=0,
            tiled=True,
        ).astype(jnp.float32)
        + grad_h1_share
    )
    local_vectors = jnp.stack(
        [
            jnp.sum(own_rows(grad_attn).astype(jnp.float32), axis=0),
            jnp.sum(own_rows(grad_branch).astype(jnp.float32), axis=0),
            jnp.sum(grad_first_share * first_normed_share, axis=0),
            jnp.sum(grad_first_share, axis=0),
            jnp.sum(grad_out_share * second_share, axis=0),
            jnp.sum(grad_out_share, axis=0),
        ]
    )
    grads = (
        grad_w_qkv.reshape(model_width, 3, head_slab).transpose(1, 0, 2),
        grad_w_out,
        grad_w_in,
        grad_w_down,
    )
    matrices = tuple(grad + error for grad, error in zip(grads, errors))

    def left_of(equation, number):
        return jnp.einsum(equation, factors[number], matrices[number], precision=PRECISE)

    lefts = (
        left_of("gkn,gmn->km", 0), factors[1], left_of("kn,mn->km", 2), left_of("kn,mn->km", 3)
    )
    return (
        layer_out,
        lambda after: grad_tokens,
        matrices,
        lefts,
        local_vectors,
        grad_heads,
        grad_units,
        (),
        (),
    )


def layer_split(tokens, segments, w_qkv, head_bias, w_out, w_in, unit_bias, w_down, vectors,
                cotangent, errors, factors):
    token_count, model_width = tokens.shape
    unit_slab = w_in.shape[1]
    tensor_size = lax.axis_size("tensor")
    share = token_count // tensor_size
    tensor_place = lax.axis_index("tensor")
    core = lax.rem(tensor_place, 2)
    seq = tensor_place // 2

    def to(values, step):
        return lax.ppermute(
            values, "tensor", [(place, place ^ step) for place in range(tensor_size)]
        )

    def rows_at(values, number, size):
        return lax.dynamic_slice_in_dim(values, number * size, size, 0)

    planes = w_qkv.transpose(1, 0, 2)
    (projected, logs, mixed, _, _, _, _, layer_out, low, active, grad_branch, grad_hidden, grad_h1,
     grad_near, far_one, far_two, seg_keys, seg_queries, down_near, down_part, down_rest, in_part, in_head, far_in, far_down,
     out_sum, out_far, units, unit_two, sums, bounds) = layer_call(
        tokens, cotangent, planes, w_out, w_in, w_down, factors[2], factors[3], head_bias,
        unit_bias[None], vectors, segments,
    )
    far_own = to(far_one, 2)
    far_other = to(far_two, 3)
    down_rest = to(down_rest, 2)
    in_near = to(in_head, 2)
    out_back = to(out_far, 2)

    grad_projected, heads_near = attend_back(
        projected, seg_keys, seg_queries, (grad_near, 0), (grad_near, 1), mixed, logs, 1,
        bounds, None, seq, core,
    )
    grad_projected, heads_far = attend_back(
        projected, seg_keys, seg_queries, (far_own, 0), (far_other, 0), mixed, logs, 0,
        bounds, grad_projected, 1 - seq, core,
    )
    token_part = jnp.einsum(
        "gtn,gdn->td", grad_projected, planes, preferred_element_type=jnp.float32
    ).astype(jnp.bfloat16)
    other_one = to(
        jnp.stack([rows_at(token_part, 2 * at + 1 - core, share) for at in (seq, 1 - seq)]), 1
    )
    across_part = rows_at(token_part, 2 * (1 - seq) + core, share).astype(jnp.float32)
    across_part = (across_part + other_one[1].astype(jnp.float32)).astype(jnp.bfloat16)
    own_part = rows_at(token_part, 2 * seq + core, share)

    def finish_tokens(after):
        from_two = to(lax.optimization_barrier((across_part, after))[0], 2)
        return (
            own_part.astype(jnp.float32)
            + other_one[0].astype(jnp.float32)
            + from_two.astype(jnp.float32)
            + grad_h1
        )

    matrix_qkv, left_qkv = product(tokens, grad_projected, errors[0], factors[0])
    matrix_down, left_down = product(active, grad_branch, errors[3], factors[3])
    matrix_in, left_in = product(low, grad_hidden, errors[2], factors[2])
    out_sum, in_near = lax.optimization_barrier((out_sum, in_near))
    matrix_out = out_sum + out_back.astype(jnp.float32) + errors[1]
    return (
        layer_out,
        finish_tokens,
        (matrix_qkv, matrix_out, matrix_in, matrix_down),
        (left_qkv, factors[1], left_in, left_down),
        sums,
        heads_near + heads_far,
        units[0, :unit_slab] + unit_two[0],
        (in_part, down_part, far_in, far_down),
        (in_near, down_near, down_rest),
    )


def local(
    tokens,
    segments,
    w_qkv,
    head_bias,
    w_out,
    w_in,
    unit_bias,
    w_down,
    vectors,
    cotangent,
    err_qkv,
    err_out,
    err_in,
    err_down,
    basis_qkv,
    basis_out,
    basis_in,
    basis_down,
    mom_qkv,
    mom_head_bias,
    mom_out,
    mom_in,
    mom_unit_bias,
    mom_down,
    mom_vectors,
):
    token_count, model_width = tokens.shape
    head_slab = w_qkv.shape[2]
    unit_slab = w_in.shape[1]
    tensor_size = lax.axis_size("tensor")
    replicas = lax.axis_size("dp")
    one_sequence_per_chip = 2 * segments.shape[0] == tensor_size and replicas % 4 == 0
    layer = layer_split if one_sequence_per_chip else layer_general
    planes = (1, 0, 2)
    layer_out, finish_tokens, matrices, lefts, local_vectors, grad_heads, grad_units, far, late = (
        layer(
            tokens, segments, w_qkv, head_bias, w_out, w_in, unit_bias, w_down, vectors, cotangent,
            (err_qkv[0].transpose(planes), err_out[0], err_in[0], err_down[0]),
            (basis_qkv.transpose(planes), basis_out, basis_in, basis_down),
        )
    )
    small = jnp.concatenate(
        [
            local_vectors,
            jnp.pad(grad_units, (0, model_width - unit_slab))[None],
            jnp.pad(grad_heads.reshape(1, 2 * head_slab), ((0, 0), (0, model_width - 2 * head_slab))),
        ],
        axis=0,
    )
    bases, rights, small_sum, late_rest = compress(
        matrices,
        lefts,
        small,
        replicas,
        tensor_size,
        far,
    )
    grad_tokens = finish_tokens(small_sum)
    if late:
        late = (late[0], late_rest[0]) + late[1:]
    step_rate = 0.3 * math.sqrt(replicas / token_count)
    grads, errors, moments, news = update(
        matrices,
        (mom_qkv.transpose(planes), mom_out, mom_in, mom_down),
        (w_qkv.transpose(planes), w_out, w_in, w_down),
        bases,
        rights,
        late,
        step_rate,
    )
    reduced_qkv, rank_out, rank_in, rank_down = (grads[0].transpose(planes),) + tuple(grads[1:])
    new_err_qkv, new_err_out, new_err_in, new_err_down = (
        errors[0].transpose(planes)[None],
        errors[1][None],
        errors[2][None],
        errors[3][None],
    )
    new_mom_qkv, new_mom_out, new_mom_in, new_mom_down = (moments[0].transpose(planes),) + tuple(
        moments[1:]
    )
    new_w_qkv, new_w_out, new_w_in, new_w_down = (news[0].transpose(planes),) + tuple(news[1:])
    right_qkv, right_out, right_in, right_down = rights
    new_basis_qkv = right_qkv.transpose(planes)
    grad_vectors = small_sum[:6]
    grad_unit_bias = small_sum[6, :unit_slab]
    grad_head_bias = small_sum[7, : 2 * head_slab].reshape(2, head_slab)
    new_mom_head_bias = 0.9 * mom_head_bias + grad_head_bias
    new_mom_unit_bias = 0.9 * mom_unit_bias + grad_unit_bias
    new_mom_vectors = 0.9 * mom_vectors + grad_vectors
    new_head_bias = head_bias - step_rate * new_mom_head_bias
    new_unit_bias = unit_bias - step_rate * new_mom_unit_bias
    new_vectors = vectors - step_rate * new_mom_vectors
    return (
        layer_out,
        grad_tokens,
        reduced_qkv,
        grad_head_bias,
        rank_out,
        rank_in,
        grad_unit_bias,
        rank_down,
        grad_vectors,
        new_err_qkv,
        new_err_out,
        new_err_in,
        new_err_down,
        new_basis_qkv,
        right_out,
        right_in,
        right_down,
        new_mom_qkv,
        new_mom_head_bias,
        new_mom_out,
        new_mom_in,
        new_mom_unit_bias,
        new_mom_down,
        new_mom_vectors,
        new_w_qkv,
        new_head_bias,
        new_w_out,
        new_w_in,
        new_unit_bias,
        new_w_down,
        new_vectors,
    )


def solution(mesh):
    in_specs = (
        P("dp", None),
        P("dp", None),
        P(None, None, "tensor"),
        P(None, "tensor"),
        P("tensor", None),
        P(None, "tensor"),
        P("tensor"),
        P("tensor", None),
        P(),
        P("dp", None),
        P("dp", None, None, "tensor"),
        P("dp", "tensor", None),
        P("dp", None, "tensor"),
        P("dp", "tensor", None),
        P(None, None, "tensor"),
        P("tensor", None),
        P(None, "tensor"),
        P("tensor", None),
        P(None, None, "tensor"),
        P(None, "tensor"),
        P("tensor", None),
        P(None, "tensor"),
        P("tensor"),
        P("tensor", None),
        P(),
    )
    out_specs = (
        P(("dp", "tensor"), None),
        P(("dp", "tensor"), None),
        P(None, None, "tensor"),
        P(None, "tensor"),
        P("tensor", None),
        P(None, "tensor"),
        P("tensor"),
        P("tensor", None),
        P(),
        P("dp", None, None, "tensor"),
        P("dp", "tensor", None),
        P("dp", None, "tensor"),
        P("dp", "tensor", None),
        P(None, None, "tensor"),
        P("tensor", None),
        P(None, "tensor"),
        P("tensor", None),
        P(None, None, "tensor"),
        P(None, "tensor"),
        P("tensor", None),
        P(None, "tensor"),
        P("tensor"),
        P("tensor", None),
        P(),
        P(None, None, "tensor"),
        P(None, "tensor"),
        P("tensor", None),
        P(None, "tensor"),
        P("tensor"),
        P("tensor", None),
        P(),
    )
    return jax.shard_map(local, mesh=mesh, in_specs=in_specs, out_specs=out_specs, check_vma=False)
```
